32 devices in a mesh: dp: 4 (over z), seq: 8 (over y, x, core).
Axes of the slice: x: 2, y: 2, z: 4, core: 2. Of those that a mesh axis runs over, the one named last changes fastest.
Arguments:
- patches: bfloat16 [12, 16, 64, 1152], P('dp', 'seq'), may hold values from -6 to 6
- valid: int32 [12, 2], P('dp'), may hold values from 1 to 64, as said below
- labels: int32 [12], P('dp'), may hold values from 0 to 999
- partners: int32 [12], P('dp'), may hold values from 0 to 11
- mix: float32 [12], P('dp'), may hold values from 0.5 to 1
- embed_w: float32 [1152, 320], P('dp'), may hold values from -0.1875 to 0.1875
- in_proj: float32 [6, 320, 2560], P(None, 'dp'), may hold values from -0.3125 to 0.3125
- down_proj: float32 [6, 2, 1280, 320], P(None, None, 'dp'), may hold values from -0.15625 to 0.15625
- dw_kernel: float32 [6, 9, 1280], P(None, None, 'dp'), may hold values from -2 to 2
- head_w: float32 [320, 1000], P('dp'), may hold values from -0.3125 to 0.3125
- norm_gain: float32 [20, 320], P(None, 'dp'), may hold values from 0.5 to 1.5
- norm_bias: float32 [20, 320], P(None, 'dp'), may hold values from -1.5 to 1.5
- m_embed: float32 [1152, 320], P('dp'), may hold values from -5.340576e-05 to 5.340576e-05
- m_proj: float32 [6, 320, 2560], P(None, 'dp'), may hold values from -5.340576e-05 to 5.340576e-05
- m_down: float32 [6, 2, 1280, 320], P(None, None, 'dp'), may hold values from -5.340576e-05 to 5.340576e-05
- m_taps: float32 [6, 9, 1280], P(None, None, 'dp'), may hold values from -5.340576e-05 to 5.340576e-05
- m_head: float32 [320, 1000], P('dp'), may hold values from -5.340576e-05 to 5.340576e-05
- m_gain: float32 [20, 320], P(None, 'dp'), may hold values from -5.340576e-05 to 5.340576e-05
- m_bias: float32 [20, 320], P(None, 'dp'), may hold values from -5.340576e-05 to 5.340576e-05
- v_embed: float32 [1152, 320], P('dp'), may hold values from 9.433108e-13 to 3.773243e-12
- v_proj: float32 [6, 320, 2560], P(None, 'dp'), may hold values from 9.433108e-13 to 3.773243e-12
- v_down: float32 [6, 2, 1280, 320], P(None, None, 'dp'), may hold values from 9.433108e-13 to 3.773243e-12
- v_taps: float32 [6, 9, 1280], P(None, None, 'dp'), may hold values from 9.433108e-13 to 3.773243e-12
- v_head: float32 [320, 1000], P('dp'), may hold values from 9.433108e-13 to 3.773243e-12
- v_gain: float32 [20, 320], P(None, 'dp'), may hold values from 9.433108e-13 to 3.773243e-12
- v_bias: float32 [20, 320], P(None, 'dp'), may hold values from 9.433108e-13 to 3.773243e-12
Outputs:
- loss: float32 [], replicated
- grad_norm: float32 [], replicated
- stats: float32 [2, 22], replicated
- trust: float32 [22], replicated
- new_embed: float32 [1152, 320], P('dp')
- new_proj: float32 [6, 320, 2560], P(None, 'dp')
- new_down: float32 [6, 2, 1280, 320], P(None, None, 'dp')
- new_taps: float32 [6, 9, 1280], P(None, None, 'dp')
- new_head: float32 [320, 1000], P('dp')
- new_gain: float32 [20, 320], P(None, 'dp')
- new_bias: float32 [20, 320], P(None, 'dp')
- m_embed_out: float32 [1152, 320], P('dp')
- m_proj_out: float32 [6, 320, 2560], P(None, 'dp')
- m_down_out: float32 [6, 2, 1280, 320], P(None, None, 'dp')
- m_taps_out: float32 [6, 9, 1280], P(None, None, 'dp')
- m_head_out: float32 [320, 1000], P('dp')
- m_gain_out: float32 [20, 320], P(None, 'dp')
- m_bias_out: float32 [20, 320], P(None, 'dp')
- v_embed_out: float32 [1152, 320], P('dp')
- v_proj_out: float32 [6, 320, 2560], P(None, 'dp')
- v_down_out: float32 [6, 2, 1280, 320], P(None, None, 'dp')
- v_taps_out: float32 [6, 9, 1280], P(None, None, 'dp')
- v_head_out: float32 [320, 1000], P('dp')
- v_gain_out: float32 [20, 320], P(None, 'dp')
- v_bias_out: float32 [20, 320], P(None, 'dp')
The draws below stay inside these ranges and needn't reach their ends.
Inputs may be any that keep to these rules, and one draw needn't show every extreme that they name: Each image's valid rows are at least 8 and valid columns at least 32; the first image fills the whole grid.
All inputs are finite; a program needn't handle non-finite values.
Results may differ from the reference program's by a relative error of at most 0.006.
The reference program's roundings to bfloat16 on the way count: a program that leaves them out, or rounds other values in their place, can miss the bound.
Values may be sent and summed in bfloat16 or wider, within the bound.
No kernel may reach another device: no remote copies, remote signals or barrier semaphores. Data moves between devices by JAX's collectives and lax.ppermute only.
A program may use at most 512 MiB of HBM per device.

```python
import math
import jax
import jax.numpy as jnp
from jax import lax

D = 320
HEADS = 5
HD = 64
FF = 1280
PIN = 1152
CLS = 1000
W = 64
LAYERS = 6
STEP = 5
IMAGES = 12
H = 16
KEYS = 256
NG = 20
PARAMS = 10600960


def draw_patches(key, part):
    first, second = jax.random.split(key)
    common = jax.random.normal(first, (IMAGES, 1, 1, PIN), jnp.float32)
    noise = jax.random.normal(second, (IMAGES, H, W, PIN), jnp.float32)
    return jnp.clip(0.6 * common + 0.8 * noise, -6.0, 6.0).astype(jnp.bfloat16)


def draw_valid(key, part):
    first, second = jax.random.split(jax.random.fold_in(key, 7))
    rows = jax.random.randint(first, (IMAGES,), H // 2, H + 1)
    cols = jax.random.randint(second, (IMAGES,), W // 2, W + 1)
    leading = jnp.arange(IMAGES) == 0
    rows = jnp.where(leading, H, rows)
    cols = jnp.where(leading, W, cols)
    return jnp.stack([rows, cols], 1).astype(jnp.int32)


def set_ends(drawn, key, least, largest):
    place = [jax.random.randint(jax.random.fold_in(key, axis), (), 0, length) for axis, length in enumerate(drawn.shape)]
    main_axis = drawn.shape.index(max(drawn.shape))
    neighbour = place[:main_axis] + [(place[main_axis] + 1) % drawn.shape[main_axis]] + place[main_axis + 1:]
    return drawn.at[tuple(place)].set(least).at[tuple(neighbour)].set(largest)


def steps_of(rng, extent, shards, smallest, largest):
    level = 1.0
    for dim, parts in shards:
        heights = jax.random.uniform(jax.random.fold_in(jax.random.fold_in(rng, 6), dim), (parts,), jnp.float32, smallest / len(shards), largest / len(shards))
        level = level * jnp.repeat(jnp.exp(heights), extent[dim] // parts).reshape((-1,) + (1,) * (len(extent) - 1 - dim))
    return level


def centred(rng, shape, deviation, reach, pieces=(), dtype=jnp.bfloat16):
    drawn = deviation * jax.random.normal(rng, shape, jnp.float32)
    if pieces:
        drawn = drawn * steps_of(rng, shape, pieces, -0.22, 0.18)
    return jnp.clip(drawn, -reach, reach).astype(dtype)


def setup_inputs(seed: int = 0) -> dict:
    keys = jax.random.split(jax.random.key(seed), 27)
    return {
        "patches": draw_patches(jax.random.fold_in(keys[26], 71), 0),
        "valid": draw_valid(jax.random.fold_in(keys[26], 71), 0),
        "labels": set_ends(jax.random.randint(keys[2], (IMAGES,), 0, CLS), jax.random.fold_in(keys[2], 1), 0, CLS - 1).astype(jnp.int32),
        "partners": set_ends(jax.random.randint(keys[3], (IMAGES,), 0, IMAGES), jax.random.fold_in(keys[3], 1), 0, IMAGES - 1).astype(jnp.int32),
        "mix": jnp.clip(0.5 + 0.5 * jax.random.uniform(keys[4], (IMAGES,), jnp.float32) ** steps_of(keys[4], (IMAGES,), ((0, 4),), -0.2, 0.2), 0.5, 1.0),
        "embed_w": centred(keys[5], (PIN, D), PIN ** -0.5, 0.1875, ((0, 4),), jnp.float32),
        "in_proj": centred(keys[6], (LAYERS, D, 4 * D + FF), D ** -0.5, 0.3125, ((1, 4),), jnp.float32),
        "down_proj": centred(keys[7], (LAYERS, 2, FF, D), FF ** -0.5, 0.15625, ((2, 4),), jnp.float32),
        "dw_kernel": centred(keys[8], (LAYERS, 9, FF), 9 ** -0.5, 2.0, ((2, 4),), jnp.float32),
        "head_w": centred(keys[9], (D, CLS), D ** -0.5, 0.3125, ((0, 4),), jnp.float32),
        "norm_gain": jnp.clip(1.0 + 0.1 * jax.random.normal(keys[10], (NG, D), jnp.float32), 0.5, 1.5),
        "norm_bias": centred(keys[11], (NG, D), 0.3, 1.5, ((1, 4),), jnp.float32),
        "m_embed": centred(keys[12], (PIN, D), (0.0111 / PARAMS ** 0.5), 5.340576171875e-05, ((0, 4),), jnp.float32),
        "m_proj": centred(keys[13], (LAYERS, D, 4 * D + FF), (0.0111 / PARAMS ** 0.5), 5.340576171875e-05, ((1, 4),), jnp.float32),
        "m_down": centred(keys[14], (LAYERS, 2, FF, D), (0.0111 / PARAMS ** 0.5), 5.340576171875e-05, ((2, 4),), jnp.float32),
        "m_taps": centred(keys[15], (LAYERS, 9, FF), (0.0111 / PARAMS ** 0.5), 5.340576171875e-05, ((2, 4),), jnp.float32),
        "m_head": centred(keys[16], (D, CLS), (0.0111 / PARAMS ** 0.5), 5.340576171875e-05, ((0, 4),), jnp.float32),
        "m_gain": centred(keys[17], (NG, D), (0.0111 / PARAMS ** 0.5), 5.340576171875e-05, ((1, 4),), jnp.float32),
        "m_bias": centred(keys[18], (NG, D), (0.0111 / PARAMS ** 0.5), 5.340576171875e-05, ((1, 4),), jnp.float32),
        "v_embed": jnp.clip(jnp.exp(math.log(3.7732430027692665e-12) - 1.3862944 * jax.random.uniform(keys[19], (PIN, D), jnp.float32) ** steps_of(keys[19], (PIN, D), ((0, 4),), -0.2, 0.2)), 9.433107506923166e-13, 3.7732430027692665e-12),
        "v_proj": jnp.clip(jnp.exp(math.log(3.7732430027692665e-12) - 1.3862944 * jax.random.uniform(keys[20], (LAYERS, D, 4 * D + FF), jnp.float32) ** steps_of(keys[20], (LAYERS, D, 4 * D + FF), ((1, 4),), -0.2, 0.2)), 9.433107506923166e-13, 3.7732430027692665e-12),
        "v_down": jnp.clip(jnp.exp(math.log(3.7732430027692665e-12) - 1.3862944 * jax.random.uniform(keys[21], (LAYERS, 2, FF, D), jnp.float32) ** steps_of(keys[21], (LAYERS, 2, FF, D), ((2, 4),), -0.2, 0.2)), 9.433107506923166e-13, 3.7732430027692665e-12),
        "v_taps": jnp.clip(jnp.exp(math.log(3.7732430027692665e-12) - 1.3862944 * jax.random.uniform(keys[22], (LAYERS, 9, FF), jnp.float32) ** steps_of(keys[22], (LAYERS, 9, FF), ((2, 4),), -0.2, 0.2)), 9.433107506923166e-13, 3.7732430027692665e-12),
        "v_head": jnp.clip(jnp.exp(math.log(3.7732430027692665e-12) - 1.3862944 * jax.random.uniform(keys[23], (D, CLS), jnp.float32) ** steps_of(keys[23], (D, CLS), ((0, 4),), -0.2, 0.2)), 9.433107506923166e-13, 3.7732430027692665e-12),
        "v_gain": jnp.clip(jnp.exp(math.log(3.7732430027692665e-12) - 1.3862944 * jax.random.uniform(keys[24], (NG, D), jnp.float32) ** steps_of(keys[24], (NG, D), ((1, 4),), -0.2, 0.2)), 9.433107506923166e-13, 3.7732430027692665e-12),
        "v_bias": jnp.clip(jnp.exp(math.log(3.7732430027692665e-12) - 1.3862944 * jax.random.uniform(keys[25], (NG, D), jnp.float32) ** steps_of(keys[25], (NG, D), ((1, 4),), -0.2, 0.2)), 9.433107506923166e-13, 3.7732430027692665e-12),
    }


@jax.custom_vjp
def low(v):
    return lax.optimization_barrier(v.astype(jnp.bfloat16)).astype(jnp.float32)

@jax.custom_vjp
def low_back(v):
    return v

def low_keep(v):
    return (low(v), None)

def low_pass(kept, grad):
    return (grad,)

def back_keep(v):
    return (v, None)

def back_low(kept, grad):
    return (low(grad),)
low.defvjp(low_keep, low_pass)
low_back.defvjp(back_keep, back_low)
precise = lax.Precision.HIGHEST
norm_eps = 1e-06
scale_qk = 0.125
big_neg = -1e+30
beta_one = 0.9
beta_two = 0.999
lamb_eps = 1e-06
decay_rate = 0.01
learn_rate = 0.3
clip_limit = 0.1

def matmul(a, b):
    return jnp.dot(a, b, precision=precise, preferred_element_type=jnp.float32)

def layer_norm(v, gain, bias):
    center = v - lax.optimization_barrier(jnp.mean(v, -1, keepdims=True))
    spread = lax.optimization_barrier(jnp.mean(center * center, -1, keepdims=True))
    return center * lax.rsqrt(spread + norm_eps) * gain + bias

def image_loss(params, patch, valid, label, partner, lam):
    embed, proj, downs, taps, head, gains, biases = [low(p) for p in params]
    rows = lax.broadcasted_iota(jnp.int32, (H, W), 0).reshape(-1)
    cols = lax.broadcasted_iota(jnp.int32, (H, W), 1).reshape(-1)
    kid = lax.broadcasted_iota(jnp.int32, (KEYS,), 0)
    key_ok = (2 * (kid // (W // 2)) < valid[0]) & (2 * (kid % (W // 2)) < valid[1])
    embedded = low_back(matmul(patch.reshape(H * W, PIN), embed))
    x = layer_norm(embedded, gains[0], biases[0])
    for layer in range(LAYERS):
        base = 1 + 3 * layer
        wmat = proj[layer]
        a = low(layer_norm(x, gains[base], biases[base]))
        q = low(low_back(matmul(a, wmat[:, :D])))
        grid = a.reshape(H // 2, 2, W // 2, 2, D).transpose(0, 2, 1, 3, 4).reshape(KEYS, 4 * D)
        r = low_back(matmul(grid, downs[layer, 0]))
        rn = low(layer_norm(r, gains[base + 1], biases[base + 1]))
        kv = low(matmul(rn, wmat[:, D:3 * D]))
        qh = q.reshape(H * W, HEADS, HD)
        kh = kv[:, :D].reshape(KEYS, HEADS, HD)
        vh = kv[:, D:].reshape(KEYS, HEADS, HD)
        s = low_back(scale_qk * jnp.einsum('qhd,khd->hqk', qh, kh, precision=precise))
        s = jnp.where(key_ok[None, None, :], s, big_neg)
        expo = jnp.exp(s - lax.optimization_barrier(jnp.max(s, -1, keepdims=True)))
        prob = low(expo / lax.optimization_barrier(jnp.sum(expo, -1, keepdims=True)))
        att = jnp.einsum('hqk,khd->qhd', prob, vh, precision=precise).reshape(H * W, D)
        o = low(low_back(att))
        x = x + low_back(matmul(o, wmat[:, 3 * D:4 * D]))
        b = low(layer_norm(x, gains[base + 2], biases[base + 2]))
        h = low(low_back(matmul(b, wmat[:, 4 * D:]))).reshape(H, W, FF)
        padded = jnp.pad(h, ((1, 1), (1, 1), (0, 0)))
        z = jnp.zeros((H, W, FF), jnp.float32)
        for i in range(3):
            for j in range(3):
                z = z + taps[layer, 3 * i + j] * padded[i:i + H, j:j + W]
        g = low(low_back(jax.nn.gelu(low_back(z), approximate=False))).reshape(H * W, FF)
        x = x + low_back(matmul(g, downs[layer, 1]))
    fin = layer_norm(x, gains[NG - 1], biases[NG - 1])
    okay = ((rows < valid[0]) & (cols < valid[1])).astype(jnp.float32)
    count = (valid[0] * valid[1]).astype(jnp.float32)
    pooled = low(lax.optimization_barrier(jnp.sum(fin * okay[:, None], 0)) / count)
    logits = low_back(matmul(pooled[None, :], head))[0]
    shifted = logits - jnp.max(logits)
    logp = shifted - jnp.log(jnp.sum(jnp.exp(shifted)))
    classes = lax.broadcasted_iota(jnp.int32, (CLS,), 0)
    target = lam * (classes == label) + (1.0 - lam) * (classes == partner)
    return -jnp.sum(target * logp) / IMAGES

def group_sums(arrs):
    embed, proj, downs, taps, head, gains, biases = arrs
    first = jnp.stack([jnp.sum(embed), jnp.sum(head), jnp.sum(gains), jnp.sum(biases)])
    rest = [lax.optimization_barrier(jnp.sum(a.reshape(a.shape[0], -1), 1)) for a in (proj, downs, taps)]
    return jnp.concatenate([first] + rest)

def spread_ratio(ratio):
    return (ratio[0], ratio[4:4 + LAYERS].reshape(LAYERS, 1, 1), ratio[4 + LAYERS:4 + 2 * LAYERS].reshape(LAYERS, 1, 1, 1), ratio[4 + 2 * LAYERS:4 + 3 * LAYERS].reshape(LAYERS, 1, 1), ratio[1], ratio[2], ratio[3])

def reference(patches, valid, labels, partners, mix, embed_w, in_proj, down_proj, dw_kernel, head_w, norm_gain, norm_bias, m_embed, m_proj, m_down, m_taps, m_head, m_gain, m_bias, v_embed, v_proj, v_down, v_taps, v_head, v_gain, v_bias):
    params = (embed_w, in_proj, down_proj, dw_kernel, head_w, norm_gain, norm_bias)
    firsts = (m_embed, m_proj, m_down, m_taps, m_head, m_gain, m_bias)
    seconds = (v_embed, v_proj, v_down, v_taps, v_head, v_gain, v_bias)
    partner_labels = labels[partners]

    def one(carry, item):
        patch, val, lab, plab, lam = item
        patch = patch.astype(jnp.float32)

        def loss_of(*ps):
            return image_loss(ps, patch, val, lab, plab, lam)
        value, pull = jax.vjp(loss_of, *params)
        grads = pull(jnp.ones_like(value))
        return ((carry[0] + value, tuple((a + g for a, g in zip(carry[1], grads)))), None)
    init = (jnp.zeros((), jnp.float32), tuple((jnp.zeros_like(p) for p in params)))
    (loss, grads), _ = lax.scan(one, init, (patches, valid, labels, partner_labels, mix))
    gsq = sum((jnp.sum(g * g) for g in grads))
    grad_norm = jnp.sqrt(gsq)
    factor = jnp.minimum(1.0, clip_limit / grad_norm)
    new_m, new_v, updates = ([], [], [])
    for w, g, m, v in zip(params, grads, firsts, seconds):
        g = g * factor
        m2 = beta_one * m + (1.0 - beta_one) * g
        v2 = beta_two * v + (1.0 - beta_two) * g * g
        u = m2 / (1.0 - beta_one ** STEP) / (jnp.sqrt(v2 / (1.0 - beta_two ** STEP)) + lamb_eps) + decay_rate * w
        new_m.append(m2)
        new_v.append(v2)
        updates.append(u)
    wnorm = jnp.sqrt(group_sums(tuple((w * w for w in params))))
    unorm = jnp.sqrt(group_sums(tuple((u * u for u in updates))))
    ratio = wnorm / unorm
    spreads = spread_ratio(ratio)
    new_w = [w - learn_rate * r * u for w, r, u in zip(params, spreads, updates)]
    stats = jnp.stack([wnorm, unorm])
    return (loss, grad_norm, stats, ratio, new_w[0], new_w[1], new_w[2], new_w[3], new_w[4], new_w[5], new_w[6], new_m[0], new_m[1], new_m[2], new_m[3], new_m[4], new_m[5], new_m[6], new_v[0], new_v[1], new_v[2], new_v[3], new_v[4], new_v[5], new_v[6])
```

```python
import functools

import jax
import jax.numpy as jnp
from jax import lax
from jax.experimental import pallas as pl
from jax.experimental.pallas import tpu as pltpu
from jax.sharding import PartitionSpec as P

D = 320
HEADS = 5
HD = 64
FF = 1280
CLS = 1000
W = 64
HALF = W // 2
LAYERS = 6
STEP = 5
LANES = 128


norm_eps = 1e-06
scale_qk = 0.125
big_neg = -1e30
beta_one = 0.9
beta_two = 0.999
lamb_eps = 1e-06
decay_rate = 0.01
learn_rate = 0.3
clip_limit = 0.1
root_half = 0.7071067811865476
root_two_pi = 0.3989422804014327
precise = lax.Precision.HIGHEST

f32 = jnp.float32
bf16 = jnp.bfloat16


def to_bf(v):
    return v.astype(bf16)


def dot(a, b):
    return jnp.dot(a, b, preferred_element_type=f32)


def dot_nt(a, b, precision=None):
    return lax.dot_general(
        a, b, (((1,), (1,)), ((), ())), precision=precision, preferred_element_type=f32
    )


def contract(a, b, precision=None):
    return lax.dot_general(
        a, b, (((0,), (0,)), ((), ())), precision=precision, preferred_element_type=f32
    )


def norm_parts(v):
    center = v - jnp.mean(v, -1, keepdims=True)
    spread = jnp.mean(center * center, -1, keepdims=True)
    scale = lax.rsqrt(spread + norm_eps)
    return center * scale, scale


def layer_norm(v, gain, bias):
    return norm_parts(v)[0] * gain + bias


def norm_back(v, gain, grad):
    unit, scale = norm_parts(v)
    dgain = jnp.sum(grad * unit, 0, keepdims=True)
    dbias = jnp.sum(grad, 0, keepdims=True)
    t = grad * gain
    dv = scale * (
        t - jnp.mean(t, -1, keepdims=True) - unit * jnp.mean(t * unit, -1, keepdims=True)
    )
    return dv, dgain, dbias


def run(body, outs, *args):
    vm = pl.BlockSpec(memory_space=pltpu.VMEM)
    return pl.pallas_call(
        body,
        out_shape=[jax.ShapeDtypeStruct(s, d) for s, d in outs],
        in_specs=[vm] * len(args),
        out_specs=[vm] * len(outs),
        compiler_params=pltpu.CompilerParams(vmem_limit_bytes=48 << 20),
    )(*args)


def cells_of(v):
    rows = v.shape[0] // W
    split = v.reshape(rows // 2, 2, 2, HALF, v.shape[1])
    return [split[:, k // 2, k % 2].reshape(-1, v.shape[1]) for k in range(4)]


def attention_inputs(x, gain, bias, wq, wsr, wkv, a_ref, q_ref, r_ref, rn_ref, kv_ref):
    a = to_bf(layer_norm(x, gain[0:1], bias[0:1]))
    a_ref[...] = a
    q_ref[...] = to_bf(dot(a, wq[...]))
    total = None
    for k, cell in enumerate(cells_of(a)):
        part = dot(cell, wsr[k * D : (k + 1) * D, :])
        total = part if total is None else total + part
    r_ref[...] = total
    rn = to_bf(layer_norm(total, gain[1:2], bias[1:2]))
    rn_ref[...] = rn
    kv_ref[...] = to_bf(dot(rn, wkv[...]))


def first_body(e_ref, ln_ref, gain, bias, wq, wsr, wkv, x_ref, *outs):
    x = layer_norm(e_ref[...], ln_ref[0:1], ln_ref[1:2])
    x_ref[...] = x
    attention_inputs(x, gain, bias, wq, wsr, wkv, *outs)


def middle_body(q_ref, kv_ref, ok_ref, x_ref, gain, bias, wo, w1, o_ref, lse_ref, x2_ref, b_ref, h_ref):
    q = q_ref[...] * jnp.asarray(scale_qk, bf16)
    keys = kv_ref.shape[0]
    kv = kv_ref[...]
    shut = jnp.broadcast_to(ok_ref[...], (keys, q.shape[0]))
    q_t = q.T
    v_t = kv[:, D:].T
    parts = []
    for head in range(HEADS):
        low, high = head * HD, (head + 1) * HD
        s = dot(kv[:, low:high], q_t[low:high, :]) + shut
        top = jnp.max(s, 0, keepdims=True)
        expo = jnp.exp(s - top)
        total = jnp.sum(expo, 0, keepdims=True)
        lse_ref[head : head + 1, :] = top + jnp.log(total)
        p = to_bf(expo * (1.0 / total))
        parts.append(dot(v_t[low:high, :], p))
    o = to_bf(jnp.concatenate(parts, 0).T)
    o_ref[...] = o
    x2 = x_ref[...] + dot(o, wo[...])
    x2_ref[...] = x2
    b = to_bf(layer_norm(x2, gain[2:3], bias[2:3]))
    b_ref[...] = b
    h_ref[...] = to_bf(dot(b, w1[...]))


def shift_down(v):
    index = lax.broadcasted_iota(jnp.int32, v.shape, 0)
    return jnp.where(index == 0, 0.0, pltpu.roll(v, 1, 0))


def shift_up(v):
    index = lax.broadcasted_iota(jnp.int32, v.shape, 0)
    return jnp.where(index == v.shape[0] - 1, 0.0, pltpu.roll(v, v.shape[0] - 1, 0))


def from_left(v):
    return jnp.concatenate([shift_down(v[HALF:]), v[:HALF]], 0)


def from_right(v):
    return jnp.concatenate([v[HALF:], shift_up(v[:HALF])], 0)


def row_of(main, low, high, i, rows, lanes):
    if i < 0:
        return low[:, lanes].astype(f32)
    if i >= rows:
        return high[:, lanes].astype(f32)
    return main[i * W : (i + 1) * W, lanes].astype(f32)


def conv_gelu(h_ref, low_ref, high_ref, taps_ref, g_ref, slope_ref):
    rows = h_ref.shape[0] // W

    def chunk(c, carry):
        lanes = pl.ds(pl.multiple_of(c * LANES, LANES), LANES)
        taps = [taps_ref[k : k + 1, lanes] for k in range(9)]
        near = [row_of(h_ref, low_ref, high_ref, i, rows, lanes) for i in (-1, 0)]
        for i in range(rows):
            near.append(row_of(h_ref, low_ref, high_ref, i + 1, rows, lanes))
            sums = [
                taps[j] * near[0] + taps[3 + j] * near[1] + taps[6 + j] * near[2] for j in range(3)
            ]
            z = sums[1] + from_left(sums[0]) + from_right(sums[2])
            phi = 0.5 + 0.5 * lax.erf(z * root_half)
            here = slice(i * W, (i + 1) * W)
            g_ref[here, lanes] = to_bf(z * phi)
            slope_ref[here, lanes] = phi + z * (jnp.exp(-0.5 * z * z) * root_two_pi)
            near = near[1:]
        return carry

    lax.fori_loop(0, FF // LANES, chunk, 0)


def last_body(h_ref, low_ref, high_ref, taps_ref, x2_ref, w2, ln_ref, ok_ref, g_ref, slope_ref, x_ref, sum_ref):
    conv_gelu(h_ref, low_ref, high_ref, taps_ref, g_ref, slope_ref)
    x = x2_ref[...] + dot(g_ref[...], w2[...])
    x_ref[...] = x
    fin = layer_norm(x, ln_ref[0:1], ln_ref[1:2])
    sum_ref[...] = jnp.sum(fin * ok_ref[...], 0, keepdims=True)


def join_body(
    h_ref, low_ref, high_ref, taps_ref, x2_ref, w2, gain, bias, wq, wsr, wkv, g_ref, slope_ref, x_ref, *outs
):
    conv_gelu(h_ref, low_ref, high_ref, taps_ref, g_ref, slope_ref)
    x = x2_ref[...] + dot(g_ref[...], w2[...])
    x_ref[...] = x
    attention_inputs(x, gain, bias, wq, wsr, wkv, *outs)


def gelu_back(dx, w2, slope_ref, dy_ref, dz_ref):
    dy = to_bf(dx)
    dy_ref[...] = dy
    dg = to_bf(dot_nt(dy, w2[...])).astype(f32)
    dz_ref[...] = to_bf(dg * slope_ref[...])


def head_body(
    images,
    pool_ref,
    count_ref,
    head_ref,
    target_ref,
    x_ref,
    ln_ref,
    ok_ref,
    w2,
    slope_ref,
    loss_ref,
    pooled_ref,
    dlog_ref,
    dln_ref,
    dx_ref,
    dy_ref,
    dz_ref,
):
    count = count_ref[...]
    pooled = to_bf(pool_ref[...] / count)
    pooled_ref[...] = pooled
    logits = dot(jnp.broadcast_to(pooled.astype(f32), (16, D)).astype(bf16), head_ref[...])[0:1]
    shifted = logits - jnp.max(logits, -1, keepdims=True)
    logp = shifted - jnp.log(jnp.sum(jnp.exp(shifted), -1, keepdims=True))
    target = target_ref[...]
    loss_ref[...] = jnp.sum(target * logp, -1, keepdims=True) * (-1.0 / images)
    dlog = to_bf((jnp.exp(logp) - target) * (1.0 / images))
    dlog_ref[...] = dlog
    wide = jnp.broadcast_to(dlog.astype(f32), (16, CLS)).astype(bf16)
    dpool = dot_nt(wide, head_ref[...])[0:1] / count
    dx, dgain, dbias = norm_back(x_ref[...], ln_ref[0:1], ok_ref[...] * dpool)
    dln_ref[0:1, :] = dgain
    dln_ref[1:2, :] = dbias
    dx_ref[...] = dx
    gelu_back(dx, w2, slope_ref, dy_ref, dz_ref)


def conv_back(h_ref, hlow_ref, hhigh_ref, dz_ref, zlow_ref, zhigh_ref, taps_ref, dh_ref, dtaps_ref):
    rows = h_ref.shape[0] // W

    def chunk(c, carry):
        lanes = pl.ds(pl.multiple_of(c * LANES, LANES), LANES)
        taps = [taps_ref[k : k + 1, lanes] for k in range(9)]
        acc = [jnp.zeros((8, LANES), f32) for _ in range(9)]

        def views(i):
            v = row_of(dz_ref, zlow_ref, zhigh_ref, i, rows, lanes)
            return [from_right(v), v, from_left(v)]

        near = [views(-1), views(0)]
        hear = [row_of(h_ref, hlow_ref, hhigh_ref, i, rows, lanes) for i in (-1, 0)]
        for i in range(rows):
            near.append(views(i + 1))
            hear.append(row_of(h_ref, hlow_ref, hhigh_ref, i + 1, rows, lanes))
            dh = None
            for di in range(3):
                for dj in range(3):
                    part = taps[3 * di + dj] * near[2 - di][dj]
                    dh = part if dh is None else dh + part
            dh_ref[i * W : (i + 1) * W, lanes] = to_bf(dh)
            for di in range(3):
                for dj in range(3):
                    prod = (hear[di] * near[1][dj]).reshape(W // 8, 8, LANES)
                    acc[3 * di + dj] = acc[3 * di + dj] + jnp.sum(prod, 0)
            near = near[1:]
            hear = hear[1:]
        for k in range(9):
            dtaps_ref[k : k + 1, lanes] = jnp.sum(acc[k], 0, keepdims=True)
        return carry

    lax.fori_loop(0, FF // LANES, chunk, 0)


def block_back_body(
    h_ref,
    hlow_ref,
    hhigh_ref,
    dz_ref,
    zlow_ref,
    zhigh_ref,
    taps_ref,
    w1,
    x2_ref,
    gain,
    dx_ref,
    wo,
    q_ref,
    kv_ref,
    ok_ref,
    lse_ref,
    dh_ref,
    dtaps_ref,
    dln_ref,
    dx2_ref,
    dy_ref,
    dq_ref,
    dkv_ref,
):
    conv_back(h_ref, hlow_ref, hhigh_ref, dz_ref, zlow_ref, zhigh_ref, taps_ref, dh_ref, dtaps_ref)
    db = dot_nt(dh_ref[...], w1[...])
    dln, dgain, dbias = norm_back(x2_ref[...], gain[2:3], db)
    dln_ref[0:1, :] = dgain
    dln_ref[1:2, :] = dbias
    dx2 = dx_ref[...] + dln
    dx2_ref[...] = dx2
    dy = to_bf(dx2)
    dy_ref[...] = dy
    do_t = to_bf(dot_nt(wo[...], dy))
    q = q_ref[...] * jnp.asarray(scale_qk, bf16)
    q_t = q.T
    keys = kv_ref.shape[0]
    kv = kv_ref[...]
    k_t = (kv[:, :D] * jnp.asarray(scale_qk, bf16)).T
    shut = jnp.broadcast_to(ok_ref[...], (keys, q.shape[0]))
    dq_parts, dk_parts, dv_parts = ([], [], [])
    for head in range(HEADS):
        low, high = head * HD, (head + 1) * HD
        s = dot(kv[:, low:high], q_t[low:high, :]) + shut
        p = jnp.exp(s - lse_ref[head : head + 1, :])
        dp = dot(kv[:, D + low : D + high], do_t[low:high, :])
        dv_parts.append(dot_nt(do_t[low:high, :], to_bf(p)))
        ds = to_bf(p * (dp - jnp.sum(p * dp, 0, keepdims=True)))
        dq_parts.append(dot(k_t[low:high, :], ds))
        dk_parts.append(dot_nt(q_t[low:high, :], ds))
    dq_ref[...] = to_bf(jnp.concatenate(dq_parts, 0).T)
    dkv_ref[...] = jnp.concatenate(dk_parts + dv_parts, 0).T


def inputs_back(dkv, wkv, r_ref, gain, dq_ref, wq, wsr, x_ref, dx2_ref, dr_ref, dln_ref):
    w_kv = wkv[...].astype(f32)
    drn = dot_nt(dkv, w_kv, precise)
    dr, dgain1, dbias1 = norm_back(r_ref[...], gain[1:2], drn)
    dr = to_bf(dr)
    dr_ref[...] = dr
    rows = x_ref.shape[0] // W
    cells = [
        dot_nt(dr, wsr[k * D : (k + 1) * D, :]).reshape(rows // 2, 1, 1, HALF, D) for k in range(4)
    ]
    placed = jnp.concatenate(
        [jnp.concatenate(cells[0:2], 2), jnp.concatenate(cells[2:4], 2)], 1
    ).reshape(rows * W, D)
    da = dot_nt(dq_ref[...], wq[...]) + placed
    dln, dgain0, dbias0 = norm_back(x_ref[...], gain[0:1], da)
    for k, row in enumerate((dgain0, dgain1, dbias0, dbias1)):
        dln_ref[k : k + 1, :] = row
    return dx2_ref[...] + dln


def join_back_body(
    dkv_ref, wkv, r_ref, gain, dq_ref, wq, wsr, x_ref, dx2_ref, w2, slope_ref, dr_ref, dln_ref, dx_ref, dy_ref, dz_ref
):
    dx = inputs_back(dkv_ref[...], wkv, r_ref, gain, dq_ref, wq, wsr, x_ref, dx2_ref, dr_ref, dln_ref)
    dx_ref[...] = dx
    gelu_back(dx, w2, slope_ref, dy_ref, dz_ref)


def first_back_body(
    dkv_ref, wkv, r_ref, gain, dq_ref, wq, wsr, x_ref, dx2_ref, e_ref, ln_ref, dr_ref, dln_ref, de_ref, dle_ref
):
    dx = inputs_back(dkv_ref[...], wkv, r_ref, gain, dq_ref, wq, wsr, x_ref, dx2_ref, dr_ref, dln_ref)
    de, dgain, dbias = norm_back(e_ref[...], ln_ref[0:1], dx)
    de_ref[...] = to_bf(de)
    dle_ref[0:1, :] = dgain
    dle_ref[1:2, :] = dbias


def weight_grads_body(
    n_dp, cols, subs, core_ref, a_ref, dq_ref, rn_ref, dkv_ref, o_ref, dy2_ref, b_ref, dh_ref, dr_ref, g_ref, dy_ref, *refs
):
    outs, (proj, down) = refs[:-2], refs[-2:]
    a = a_ref[...]
    proj[:, :D] = contract(a, dq_ref[...])
    proj[:, D : 3 * D] = contract(rn_ref[...].astype(f32), dkv_ref[...], precise)
    proj[:, 3 * D : 4 * D] = contract(o_ref[...], dy2_ref[...])
    proj[:, 4 * D :] = contract(b_ref[...], dh_ref[...])
    dr = dr_ref[...]
    for k, cell in enumerate(cells_of(a)):
        down[k * D : (k + 1) * D, :D] = contract(cell, dr)
    down[:, D:] = contract(g_ref[...], dy_ref[...])
    rows = D // n_dp
    sub = rows // subs
    wide = (4 * D + FF) // cols
    down_rows = FF // n_dp
    for c in range(cols):
        for d in range(n_dp):
            for n, out in enumerate(outs):
                for j in range(subs) if len(outs) == 1 else (None,):
                    if j is None:
                        k = core_ref[0] if n == 0 else 1 - core_ref[0]
                        at = (c, d)
                    else:
                        k = j
                        at = (c, j, d)
                    start = d * rows + k * sub
                    low = d * down_rows + (c * subs + k) * (down_rows // (cols * subs))
                    if j is None:
                        start = pl.multiple_of(start, 8)
                        low = pl.multiple_of(low, 8)
                    out[(*at, slice(0, sub))] = proj[pl.ds(start, sub), c * wide : (c + 1) * wide]
                    out[(*at, slice(sub, 2 * sub))] = down[pl.ds(low, sub), :]


def group_sums(arrs):
    embed, proj, downs, taps, head, gains, biases = arrs
    first = jnp.stack([jnp.sum(embed), jnp.sum(head), jnp.sum(gains), jnp.sum(biases)])
    rest = [jnp.sum(a.reshape(a.shape[0], -1), 1) for a in (proj, downs, taps)]
    return jnp.concatenate([first] + rest)


def spread_ratio(ratio):
    return (
        ratio[0],
        ratio[4 : 4 + LAYERS].reshape(LAYERS, 1, 1),
        ratio[4 + LAYERS : 4 + 2 * LAYERS].reshape(LAYERS, 1, 1, 1),
        ratio[4 + 2 * LAYERS : 4 + 3 * LAYERS].reshape(LAYERS, 1, 1),
        ratio[1],
        ratio[2],
        ratio[3],
    )


def per_device(
    patches,
    valid,
    labels,
    partners,
    mix,
    embed_w,
    in_proj,
    down_proj,
    dw_kernel,
    head_w,
    norm_gain,
    norm_bias,
    m_embed,
    m_proj,
    m_down,
    m_taps,
    m_head,
    m_gain,
    m_bias,
    v_embed,
    v_proj,
    v_down,
    v_taps,
    v_head,
    v_gain,
    v_bias,
):
    masters = (embed_w, in_proj, down_proj, dw_kernel, head_w, norm_gain, norm_bias)
    firsts = (m_embed, m_proj, m_down, m_taps, m_head, m_gain, m_bias)
    seconds = (v_embed, v_proj, v_down, v_taps, v_head, v_gain, v_bias)
    n_seq = lax.axis_size("seq")
    n_dp = lax.axis_size("dp")
    seq_pos = lax.axis_index("seq")
    img_dev, rows = (patches.shape[0], patches.shape[1])
    images = img_dev * n_dp

    team = n_seq
    while team * img_dev > n_seq:
        team //= 2
    blocks = n_seq // team
    rows_own = rows * blocks
    tok = rows_own * W
    keys_own = tok // 4
    image = jnp.minimum(seq_pos // team, img_dev - 1)
    busy = seq_pos // team < img_dev
    place = seq_pos % team

    def between(shift, wrap):
        pairs = []
        for base in range(0, n_seq, team):
            for h in range(team):
                if wrap or 0 <= h + shift < team:
                    pairs.append((base + (h + shift) % team, base + h))
        return pairs

    def edges(v):
        low = lax.ppermute(v[-W:], "seq", between(-1, False))
        high = lax.ppermute(v[:W], "seq", between(1, False))
        return low, high

    def all_keys(v):
        return jnp.concatenate(
            [v] + [lax.ppermute(v, "seq", between(j, True)) for j in range(1, team)], 0
        )

    def own_keys(v):
        total = v[:keys_own]
        for j in range(1, team):
            part = v[j * keys_own : (j + 1) * keys_own]
            total = total + lax.ppermute(part, "seq", between(-j, True))
        return total

    back_block = seq_pos % blocks
    routes = [
        [
            (blocks * h + (i + r) % blocks, team * i + h)
            for i in range(img_dev)
            for h in range(team)
        ]
        for r in range(blocks)
    ]

    def to_team(v):
        got = []
        for r, pairs in enumerate(routes):
            send = lax.dynamic_index_in_dim(
                v, jnp.minimum((back_block - r) % blocks, img_dev - 1), 0, keepdims=False
            )
            got.append(lax.ppermute(send, "seq", pairs))
        twice = jnp.stack(got + got)
        own = lax.dynamic_slice_in_dim(twice, (blocks - image) % blocks, blocks, 0)
        return own.reshape(tok, -1)

    def from_team(v):
        parts = v.reshape(blocks, rows * W, -1)
        got = []
        for r, pairs in enumerate(routes):
            send = lax.dynamic_index_in_dim(parts, (image + r) % blocks, 0, keepdims=False)
            got.append(lax.ppermute(send, "seq", [(b, a) for a, b in pairs]))
        got = jnp.stack(got)
        return jnp.stack(
            [
                lax.dynamic_index_in_dim(got, (back_block - i) % blocks, 0, keepdims=False)
                for i in range(img_dev)
            ]
        )

    cols = 4
    subs = n_seq // cols
    row_in = D // n_dp
    sub_in = row_in // subs
    wide = in_proj.shape[2] // cols
    down_rows = down_proj.shape[2] // n_seq
    core = seq_pos % subs

    def part_of(flat):
        size = -(-flat.shape[0] // (wide * n_seq)) * wide * n_seq
        flat = jnp.pad(flat, (0, size - flat.shape[0])).reshape(n_seq, -1, wide)
        return lax.dynamic_index_in_dim(flat, seq_pos, 0, keepdims=False)

    def layer_part(l):
        block = lax.dynamic_slice(
            in_proj[l], (core * sub_in, (seq_pos // subs) * wide), (sub_in, wide)
        )
        lower = lax.dynamic_slice_in_dim(down_proj[l], seq_pos * down_rows, down_rows, 1)
        return [to_bf(block), to_bf(jnp.concatenate([lower[0], lower[1]], 1))]

    def gathered(parts):
        sizes = [p.shape[0] for p in parts]
        got = lax.all_gather(jnp.concatenate(parts, 0), ("dp", "seq"), axis=0, tiled=False)
        got = got.reshape(n_dp, n_seq, sum(sizes), wide)
        starts = [sum(sizes[:i]) for i in range(len(sizes))]
        return [got[:, :, a : a + n] for a, n in zip(starts, sizes)]

    def proj_of(got):
        got = got.reshape(n_dp, cols, subs, sub_in, wide).transpose(0, 2, 3, 1, 4)
        return got.reshape(D, cols * wide)

    small = jnp.concatenate(
        [to_bf(dw_kernel).reshape(-1), to_bf(norm_gain).reshape(-1), to_bf(norm_bias).reshape(-1)]
    )
    groups = [[0], [1, 2], [3, 4, 5]]
    extra = [[part_of(to_bf(embed_w).reshape(-1)), part_of(small)], [], [part_of(to_bf(head_w).reshape(-1))]]
    layers16, extras = ([], [])
    for members, more in zip(groups, extra):
        parts = more + [p for l in members for p in layer_part(l)]
        got = gathered(parts)
        extras += [g.reshape(n_dp, -1) for g in got[: len(more)]]
        got = got[len(more) :]
        layers16 += [(proj_of(got[2 * i]), got[2 * i + 1].reshape(FF, 2 * D)) for i in range(len(members))]
    embed16 = extras[0][:, : embed_w.size].reshape(-1, D)
    head16 = extras[2][:, : head_w.size].reshape(D, CLS)
    small = extras[1].astype(f32)
    n_taps = dw_kernel.size
    n_gain = norm_gain.size
    taps32 = small[:, :n_taps].reshape(n_dp, LAYERS * 9, -1).transpose(1, 0, 2)
    taps32 = taps32.reshape(LAYERS, 9, FF)
    gain32 = small[:, n_taps : n_taps + n_gain].reshape(n_dp, -1, row_in).transpose(1, 0, 2)
    gain32 = gain32.reshape(-1, D)
    bias32 = small[:, n_taps + n_gain : n_taps + 2 * n_gain].reshape(n_dp, -1, row_in)
    bias32 = bias32.transpose(1, 0, 2).reshape(-1, D)

    def own(v):
        return lax.dynamic_index_in_dim(v, image, 0, keepdims=False)

    dp_pos = lax.axis_index("dp")
    wanted = own(partners)
    partner_label = jnp.zeros((), jnp.int32)
    for j in range(n_dp):
        other = labels
        if j:
            other = lax.ppermute(labels, "dp", [((d + j) % n_dp, d) for d in range(n_dp)])
        index = ((dp_pos + j) % n_dp) * img_dev + jnp.arange(img_dev)
        partner_label = partner_label + jnp.sum(jnp.where(index == wanted, other, 0))
    valid_own = own(valid)
    tid = lax.broadcasted_iota(jnp.int32, (tok, 1), 0)
    within = tid % W
    row_id = place * rows_own + tid // W
    col_id = 2 * (within % HALF) + within // HALF
    okay = ((row_id < valid_own[0]) & (col_id < valid_own[1]) & busy).astype(f32)
    kid = lax.broadcasted_iota(jnp.int32, (team * keys_own, 1), 0)
    segment = (place + kid // keys_own) % team
    key_row = segment * (rows_own // 2) + (kid % keys_own) // HALF
    key_ok = (2 * key_row < valid_own[0]) & (2 * (kid % HALF) < valid_own[1])
    shut = jnp.where(key_ok, 0.0, big_neg).astype(f32)
    count = (valid_own[0] * valid_own[1]).astype(f32).reshape(1, 1)
    classes = lax.broadcasted_iota(jnp.int32, (1, CLS), 1)
    mix_own = own(mix)
    target = mix_own * (classes == own(labels)).astype(f32) + (1.0 - mix_own) * (
        classes == partner_label
    ).astype(f32)

    def weights(l):
        base = 1 + 3 * l
        return dict(
            wq=layers16[l][0][:, :D],
            wkv=layers16[l][0][:, D : 3 * D],
            wo=layers16[l][0][:, 3 * D : 4 * D],
            w1=layers16[l][0][:, 4 * D :],
            wsr=layers16[l][1][:, :D],
            w2=layers16[l][1][:, D:],
            taps=taps32[l],
            gain=gain32[base : base + 3],
            bias=bias32[base : base + 3],
        )

    wts = [weights(l) for l in range(LAYERS)]
    ln_first = jnp.stack([gain32[0], bias32[0]])
    ln_last = jnp.stack([gain32[-1], bias32[-1]])

    full = ((tok, D), f32)
    half = ((tok, D), bf16)
    wide16 = ((tok, FF), bf16)
    input_outs = [half, half, ((keys_own, D), f32), ((keys_own, D), bf16), ((keys_own, 2 * D), bf16)]
    ln_out = ((2, D), f32)

    embedded = dot(patches.reshape(-1, patches.shape[-1]), embed16)
    embedded = embedded.reshape(img_dev, rows, HALF, 2, D).transpose(0, 1, 3, 2, 4)
    e = to_team(embedded.reshape(img_dev, rows * W, D))
    w = wts[0]
    x, a16, q16, r, rn16, kv16 = run(
        first_body, [full] + input_outs, e, ln_first, w["gain"], w["bias"], w["wq"], w["wsr"], w["wkv"]
    )
    kept = []
    for l in range(LAYERS):
        w = wts[l]
        kv_all = all_keys(kv16)
        o16, lse, x2, b16, h16 = run(
            middle_body,
            [half, ((HEADS, tok), f32), full, half, wide16],
            q16,
            kv_all,
            shut,
            x,
            w["gain"],
            w["bias"],
            w["wo"],
            w["w1"],
        )
        hlow, hhigh = edges(h16)
        keep = dict(
            x=x, a16=a16, q16=q16, r=r, rn16=rn16, kv=kv_all, o16=o16, lse=lse, x2=x2, b16=b16,
            h16=h16, hlow=hlow, hhigh=hhigh,
        )
        shared = (h16, hlow, hhigh, w["taps"], x2, w["w2"])
        if l + 1 < LAYERS:
            n = wts[l + 1]
            keep["g16"], keep["slope"], x, a16, q16, r, rn16, kv16 = run(
                join_body,
                [wide16, ((tok, FF), f32), full] + input_outs,
                *shared,
                n["gain"],
                n["bias"],
                n["wq"],
                n["wsr"],
                n["wkv"],
            )
        else:
            keep["g16"], keep["slope"], x, pool = run(
                last_body,
                [wide16, ((tok, FF), f32), full, ((1, D), f32)],
                *shared,
                ln_last,
                okay,
            )
        kept.append(keep)

    whole = pool
    for j in range(1, team):
        whole = whole + lax.ppermute(pool, "seq", between(j, True))
    loss_own, pooled16, dlog16, dln_last, dx, dy16, dz16 = run(
        functools.partial(head_body, images),
        [((1, 1), f32), ((1, D), bf16), ((1, CLS), bf16), ln_out, full, half, wide16],
        whole,
        count,
        head16,
        target,
        x,
        ln_last,
        okay,
        wts[-1]["w2"],
        kept[-1]["slope"],
    )
    chosen = ((place == 0) & busy).astype(f32)
    d_head = pooled16.astype(f32).reshape(D, 1) * dlog16.astype(f32) * chosen
    loss_local = loss_own[0, 0] * busy.astype(f32)
    teams = n_seq // team
    loss_parts = jnp.zeros((teams,), f32)
    for j in range(teams):
        other = loss_local
        if j:
            other = lax.ppermute(
                loss_local, "seq", [((d + j * team) % n_seq, d) for d in range(n_seq)]
            )
        loss_parts = jnp.where(jnp.arange(teams) == (seq_pos // team + j) % teams, other, loss_parts)
    loss_seq = jnp.sum(loss_parts)

    piece = ((cols, n_dp, 2 * sub_in, wide), f32)
    paired = subs == 2

    def weight_grads(*args):
        vm = pl.BlockSpec(memory_space=pltpu.VMEM)
        outs = [piece] * 2 if paired else [((cols, subs) + piece[0][1:], f32)]
        got = pl.pallas_call(
            functools.partial(weight_grads_body, n_dp, cols, subs),
            out_shape=[jax.ShapeDtypeStruct(s, d) for s, d in outs],
            in_specs=[pl.BlockSpec(memory_space=pltpu.SMEM)] + [vm] * len(args),
            out_specs=[vm] * len(outs),
            scratch_shapes=[pltpu.VMEM((D, cols * wide), f32), pltpu.VMEM((FF, 2 * D), f32)],
            compiler_params=pltpu.CompilerParams(vmem_limit_bytes=48 << 20),
        )(core.reshape(1), *args)
        if paired:
            return got[0] + lax.ppermute(got[1], "seq", [(d ^ 1, d) for d in range(n_seq)])
        return got[0]

    grads = [None] * LAYERS
    for l in reversed(range(LAYERS)):
        w, k = wts[l], kept[l]
        zlow, zhigh = edges(dz16)
        dh16, d_taps, dln2, dx2, dy2, dq16, dkv = run(
            block_back_body,
            [wide16, ((9, FF), f32), ln_out, full, half, half, ((team * keys_own, 2 * D), f32)],
            k["h16"], k["hlow"], k["hhigh"], dz16, zlow, zhigh, w["taps"], w["w1"], k["x2"], w["gain"], dx,
            w["wo"], k["q16"], k["kv"], shut, k["lse"],
        )
        dkv_own = own_keys(dkv)
        upper = dy16
        shared = (dkv_own, w["wkv"], k["r"], w["gain"], dq16, w["wq"], w["wsr"], k["x"], dx2)
        if l:
            dr16, dln, dx, dy16, dz16 = run(
                join_back_body,
                [((keys_own, D), bf16), ((4, D), f32), full, half, wide16],
                *shared,
                wts[l - 1]["w2"],
                kept[l - 1]["slope"],
            )
        else:
            dr16, dln, de16, dln_first = run(
                first_back_body,
                [((keys_own, D), bf16), ((4, D), f32), half, ln_out],
                *shared,
                e,
                ln_first,
            )
        grads[l] = (
            weight_grads(
                k["a16"], dq16, k["rn16"], dkv_own, k["o16"], dy2, k["b16"], dh16, dr16, k["g16"], upper
            ),
            None,
            d_taps,
            jnp.concatenate([dln[0:2], dln2[0:1]], 0),
            jnp.concatenate([dln[2:4], dln2[1:2]], 0),
        )
    de = from_team(de16).reshape(img_dev, rows, 2, HALF, D).transpose(0, 1, 3, 2, 4)
    d_embed = contract(patches.reshape(-1, patches.shape[-1]), de.reshape(-1, D))
    d_gain = jnp.concatenate([dln_first[0:1]] + [g[3] for g in grads] + [dln_last[0:1]], 0)
    d_bias = jnp.concatenate([dln_first[1:2]] + [g[4] for g in grads] + [dln_last[1:2]], 0)

    d_taps = jnp.stack([g[2] for g in grads])
    rest = [
        d_embed.reshape(n_dp, -1),
        d_head.reshape(n_dp, -1),
        d_taps.reshape(LAYERS * 9, n_dp, -1).transpose(1, 0, 2).reshape(n_dp, -1),
        d_gain.reshape(-1, n_dp, row_in).transpose(1, 0, 2).reshape(n_dp, -1),
        d_bias.reshape(-1, n_dp, row_in).transpose(1, 0, 2).reshape(n_dp, -1),
    ]
    cuts = [0]
    for part in rest:
        cuts.append(cuts[-1] + part.shape[1])
    size = -(-cuts[-1] // (8 * wide * n_seq)) * 8 * wide * n_seq
    rest = jnp.pad(jnp.concatenate(rest, 1), ((0, 0), (0, size - cuts[-1])))
    rest = rest.reshape(n_dp, cols, subs, -1, wide).transpose(1, 2, 0, 3, 4)
    if paired:
        mine = lax.dynamic_index_in_dim(rest, core, 1, keepdims=False)
        send = lax.dynamic_index_in_dim(rest, 1 - core, 1, keepdims=False)
        rest = mine + lax.ppermute(send, "seq", [(d ^ 1, d) for d in range(n_seq)])

    def scattered(parts):
        both = jnp.concatenate([to_bf(p) for p in parts], -2)
        both = both.reshape(-1, wide)
        if paired:
            chips = [[c * subs + k for c in range(cols)] for k in range(subs)]
            both = lax.psum_scatter(
                both, "seq", scatter_dimension=0, tiled=True, axis_index_groups=chips
            )
        else:
            both = lax.psum_scatter(both, "seq", scatter_dimension=0, tiled=True)
        return lax.psum_scatter(both.astype(f32), "dp", scatter_dimension=0, tiled=True)

    chunks = [
        scattered([grads[5][0], grads[4][0]]),
        scattered([grads[3][0], grads[2][0]]),
        scattered([grads[1][0], grads[0][0], rest]),
    ]
    got = lax.all_gather(jnp.concatenate(chunks, 0), "seq", axis=0, tiled=False)
    proj_sums, down_sums = ([], [])
    for n in range(LAYERS):
        block = got[:, 2 * sub_in * n : 2 * sub_in * (n + 1)]
        g_proj = block[:, :sub_in].reshape(cols, subs, sub_in, wide).transpose(1, 2, 0, 3)
        proj_sums.append(g_proj.reshape(row_in, cols * wide))
        g_down = block[:, sub_in:].reshape(-1, 2, D).transpose(1, 0, 2)
        down_sums.append(g_down)
    got = got[:, 2 * sub_in * LAYERS :].reshape(-1)
    got = [got[a:b] for a, b in zip(cuts, cuts[1:])]
    shards = (
        got[0].reshape(embed_w.shape),
        jnp.stack(proj_sums[::-1]),
        jnp.stack(down_sums[::-1]),
        got[2].reshape(dw_kernel.shape),
        got[1].reshape(head_w.shape),
        got[3].reshape(norm_gain.shape),
        got[4].reshape(norm_bias.shape),
    )

    gsq_local = sum((jnp.sum(g * g) for g in shards))
    wsq_local = group_sums(tuple((w * w for w in masters)))
    gsq, wsq, loss = lax.psum((gsq_local, wsq_local, loss_seq), "dp")
    grad_norm = jnp.sqrt(gsq)
    factor = jnp.minimum(1.0, clip_limit / grad_norm)
    new_m, new_v, updates = ([], [], [])
    for w, g, m, v in zip(masters, shards, firsts, seconds):
        g = g * factor
        m2 = beta_one * m + (1.0 - beta_one) * g
        v2 = beta_two * v + (1.0 - beta_two) * g * g
        u = (
            m2 / (1.0 - beta_one**STEP) / (jnp.sqrt(v2 / (1.0 - beta_two**STEP)) + lamb_eps)
            + decay_rate * w
        )
        new_m.append(m2)
        new_v.append(v2)
        updates.append(u)
    usq = lax.psum(group_sums(tuple((u * u for u in updates))), "dp")
    wnorm = jnp.sqrt(wsq)
    unorm = jnp.sqrt(usq)
    ratio = wnorm / unorm
    spreads = spread_ratio(ratio)
    new_w = [w - learn_rate * r * u for w, r, u in zip(masters, spreads, updates)]
    stats = jnp.stack([wnorm, unorm])
    return (loss, grad_norm, stats, ratio, *new_w, *new_m, *new_v)


def solution(mesh):
    placed = (
        P("dp", None),
        P(None, "dp", None),
        P(None, None, "dp", None),
        P(None, None, "dp"),
        P("dp", None),
        P(None, "dp"),
        P(None, "dp"),
    )
    in_specs = (
        P("dp", "seq", None, None),
        P("dp", None),
        P("dp"),
        P("dp"),
        P("dp"),
    ) + placed * 3
    out_specs = (P(), P(), P(), P()) + placed * 3
    return jax.shard_map(
        per_device, mesh=mesh, in_specs=in_specs, out_specs=out_specs, check_vma=False
    )
```

```python
import functools

import jax
import jax.numpy as jnp
from jax import lax
from jax.experimental import pallas as pl
from jax.experimental.pallas import tpu as pltpu
from jax.sharding import PartitionSpec as P

D = 320
HEADS = 5
HD = 64
FF = 1280
CLS = 1000
W = 64
HALF = W // 2
LAYERS = 6
STEP = 5
LANES = 128


norm_eps = 1e-06
scale_qk = 0.125
big_neg = -1e30
beta_one = 0.9
beta_two = 0.999
lamb_eps = 1e-06
decay_rate = 0.01
learn_rate = 0.3
clip_limit = 0.1
root_half = 0.7071067811865476
root_two_pi = 0.3989422804014327
precise = lax.Precision.HIGHEST

f32 = jnp.float32
bf16 = jnp.bfloat16


def to_bf(v):
    return v.astype(bf16)


def dot(a, b):
    return jnp.dot(a, b, preferred_element_type=f32)


def dot_nt(a, b, precision=None):
    return lax.dot_general(
        a, b, (((1,), (1,)), ((), ())), precision=precision, preferred_element_type=f32
    )


def contract(a, b, precision=None):
    return lax.dot_general(
        a, b, (((0,), (0,)), ((), ())), precision=precision, preferred_element_type=f32
    )


def norm_parts(v):
    center = v - jnp.mean(v, -1, keepdims=True)
    spread = jnp.mean(center * center, -1, keepdims=True)
    scale = lax.rsqrt(spread + norm_eps)
    return center * scale, scale


def layer_norm(v, gain, bias):
    return norm_parts(v)[0] * gain + bias


def norm_back(v, gain, grad):
    unit, scale = norm_parts(v)
    dgain = jnp.sum(grad * unit, 0, keepdims=True)
    dbias = jnp.sum(grad, 0, keepdims=True)
    t = grad * gain
    dv = scale * (
        t - jnp.mean(t, -1, keepdims=True) - unit * jnp.mean(t * unit, -1, keepdims=True)
    )
    return dv, dgain, dbias


def cost(us):
    return pl.CostEstimate(flops=int(us * 1e9), bytes_accessed=int(us * 3e6), transcendentals=0)


def run(us, body, outs, *args):
    vm = pl.BlockSpec(memory_space=pltpu.VMEM)
    return pl.pallas_call(
        body,
        out_shape=[jax.ShapeDtypeStruct(s, d) for s, d in outs],
        in_specs=[vm] * len(args),
        out_specs=[vm] * len(outs),
        compiler_params=pltpu.CompilerParams(vmem_limit_bytes=48 << 20),
        cost_estimate=cost(us),
    )(*args)


def cells_of(v):
    rows = v.shape[0] // W
    split = v.reshape(rows // 2, 2, 2, HALF, v.shape[1])
    return [split[:, k // 2, k % 2].reshape(-1, v.shape[1]) for k in range(4)]


def attention_inputs(x, gain, bias, wq, wsr, wkv, a_ref, q_ref, r_ref, rn_ref, kv_ref):
    a = to_bf(layer_norm(x, gain[0:1], bias[0:1]))
    a_ref[...] = a
    q_ref[...] = to_bf(dot(a, wq[...]))
    total = None
    for k, cell in enumerate(cells_of(a)):
        part = dot(cell, wsr[k * D : (k + 1) * D, :])
        total = part if total is None else total + part
    r_ref[...] = total
    rn = to_bf(layer_norm(total, gain[1:2], bias[1:2]))
    rn_ref[...] = rn
    kv_ref[...] = to_bf(dot(rn, wkv[...]))


def embed_body(p_ref, w_ref, ln_ref, e_ref, x_ref):
    e = dot(p_ref[...], w_ref[...])
    e_ref[...] = e
    x_ref[...] = layer_norm(e, ln_ref[0:1], ln_ref[1:2])


def embed_back_body(p_ref, de_ref, dw_ref):
    dw_ref[...] = contract(p_ref[...], de_ref[...])


def first_body(x_ref, gain, bias, wq, wsr, wkv, *outs):
    attention_inputs(x_ref[...], gain, bias, wq, wsr, wkv, *outs)


def middle_body(q_ref, kv_ref, ok_ref, x_ref, gain, bias, wo, w1, o_ref, lse_ref, x2_ref, b_ref, h_ref):
    q = q_ref[...] * jnp.asarray(scale_qk, bf16)
    keys = kv_ref.shape[0]
    kv = kv_ref[...]
    shut = jnp.broadcast_to(ok_ref[...], (keys, q.shape[0]))
    q_t = q.T
    v_t = kv[:, D:].T
    parts = []
    for head in range(HEADS):
        low, high = head * HD, (head + 1) * HD
        s = dot(kv[:, low:high], q_t[low:high, :]) + shut
        top = jnp.max(s, 0, keepdims=True)
        expo = jnp.exp(s - top)
        total = jnp.sum(expo, 0, keepdims=True)
        lse_ref[head : head + 1, :] = top + jnp.log(total)
        p = to_bf(expo * (1.0 / total))
        parts.append(dot(v_t[low:high, :], p))
    o = to_bf(jnp.concatenate(parts, 0).T)
    o_ref[...] = o
    x2 = x_ref[...] + dot(o, wo[...])
    x2_ref[...] = x2
    b = to_bf(layer_norm(x2, gain[2:3], bias[2:3]))
    b_ref[...] = b
    h_ref[...] = to_bf(dot(b, w1[...]))


def shift_down(v):
    index = lax.broadcasted_iota(jnp.int32, v.shape, 0)
    return jnp.where(index == 0, 0.0, pltpu.roll(v, 1, 0))


def shift_up(v):
    index = lax.broadcasted_iota(jnp.int32, v.shape, 0)
    return jnp.where(index == v.shape[0] - 1, 0.0, pltpu.roll(v, v.shape[0] - 1, 0))


def from_left(v):
    return jnp.concatenate([shift_down(v[HALF:]), v[:HALF]], 0)


def from_right(v):
    return jnp.concatenate([v[HALF:], shift_up(v[:HALF])], 0)


def row_of(main, low, high, i, rows, lanes):
    if i < 0:
        return low[:, lanes].astype(f32)
    if i >= rows:
        return high[:, lanes].astype(f32)
    return main[i * W : (i + 1) * W, lanes].astype(f32)


def conv_gelu(h_ref, low_ref, high_ref, taps_ref, g_ref, slope_ref):
    rows = h_ref.shape[0] // W

    def chunk(c, carry):
        lanes = pl.ds(pl.multiple_of(c * LANES, LANES), LANES)
        taps = [taps_ref[k : k + 1, lanes] for k in range(9)]
        near = [row_of(h_ref, low_ref, high_ref, i, rows, lanes) for i in (-1, 0)]
        for i in range(rows):
            near.append(row_of(h_ref, low_ref, high_ref, i + 1, rows, lanes))
            sums = [
                taps[j] * near[0] + taps[3 + j] * near[1] + taps[6 + j] * near[2] for j in range(3)
            ]
            z = sums[1] + from_left(sums[0]) + from_right(sums[2])
            phi = 0.5 + 0.5 * lax.erf(z * root_half)
            here = slice(i * W, (i + 1) * W)
            g_ref[here, lanes] = to_bf(z * phi)
            slope_ref[here, lanes] = phi + z * (jnp.exp(-0.5 * z * z) * root_two_pi)
            near = near[1:]
        return carry

    lax.fori_loop(0, FF // LANES, chunk, 0)


def last_body(h_ref, low_ref, high_ref, taps_ref, x2_ref, w2, ln_ref, ok_ref, g_ref, slope_ref, x_ref, sum_ref):
    conv_gelu(h_ref, low_ref, high_ref, taps_ref, g_ref, slope_ref)
    x = x2_ref[...] + dot(g_ref[...], w2[...])
    x_ref[...] = x
    fin = layer_norm(x, ln_ref[0:1], ln_ref[1:2])
    sum_ref[...] = jnp.sum(fin * ok_ref[...], 0, keepdims=True)


def join_body(
    h_ref, low_ref, high_ref, taps_ref, x2_ref, w2, gain, bias, wq, wsr, wkv, g_ref, slope_ref, x_ref, *outs
):
    conv_gelu(h_ref, low_ref, high_ref, taps_ref, g_ref, slope_ref)
    x = x2_ref[...] + dot(g_ref[...], w2[...])
    x_ref[...] = x
    attention_inputs(x, gain, bias, wq, wsr, wkv, *outs)


def gelu_back(dx, w2, slope_ref, dy_ref, dz_ref):
    dy = to_bf(dx)
    dy_ref[...] = dy
    dg = to_bf(dot_nt(dy, w2[...])).astype(f32)
    dz_ref[...] = to_bf(dg * slope_ref[...])


def head_body(
    images,
    pool_ref,
    count_ref,
    head_ref,
    target_ref,
    x_ref,
    ln_ref,
    ok_ref,
    w2,
    slope_ref,
    loss_ref,
    pooled_ref,
    dlog_ref,
    dln_ref,
    dx_ref,
    dy_ref,
    dz_ref,
):
    count = count_ref[...]
    pooled = to_bf(pool_ref[...] / count)
    pooled_ref[...] = pooled
    logits = dot(jnp.broadcast_to(pooled.astype(f32), (16, D)).astype(bf16), head_ref[...])[0:1]
    shifted = logits - jnp.max(logits, -1, keepdims=True)
    logp = shifted - jnp.log(jnp.sum(jnp.exp(shifted), -1, keepdims=True))
    target = target_ref[...]
    loss_ref[...] = jnp.sum(target * logp, -1, keepdims=True) * (-1.0 / images)
    dlog = to_bf((jnp.exp(logp) - target) * (1.0 / images))
    dlog_ref[...] = dlog
    wide = jnp.broadcast_to(dlog.astype(f32), (16, CLS)).astype(bf16)
    dpool = dot_nt(wide, head_ref[...])[0:1] / count
    dx, dgain, dbias = norm_back(x_ref[...], ln_ref[0:1], ok_ref[...] * dpool)
    dln_ref[0:1, :] = dgain
    dln_ref[1:2, :] = dbias
    dx_ref[...] = dx
    gelu_back(dx, w2, slope_ref, dy_ref, dz_ref)


def conv_back(h_ref, hlow_ref, hhigh_ref, dz_ref, zlow_ref, zhigh_ref, taps_ref, dh_ref, dtaps_ref):
    rows = h_ref.shape[0] // W

    def chunk(c, carry):
        lanes = pl.ds(pl.multiple_of(c * LANES, LANES), LANES)
        taps = [taps_ref[k : k + 1, lanes] for k in range(9)]
        acc = [jnp.zeros((8, LANES), f32) for _ in range(9)]

        def views(i):
            v = row_of(dz_ref, zlow_ref, zhigh_ref, i, rows, lanes)
            return [from_right(v), v, from_left(v)]

        near = [views(-1), views(0)]
        hear = [row_of(h_ref, hlow_ref, hhigh_ref, i, rows, lanes) for i in (-1, 0)]
        for i in range(rows):
            near.append(views(i + 1))
            hear.append(row_of(h_ref, hlow_ref, hhigh_ref, i + 1, rows, lanes))
            dh = None
            for di in range(3):
                for dj in range(3):
                    part = taps[3 * di + dj] * near[2 - di][dj]
                    dh = part if dh is None else dh + part
            dh_ref[i * W : (i + 1) * W, lanes] = to_bf(dh)
            for di in range(3):
                for dj in range(3):
                    prod = (hear[di] * near[1][dj]).reshape(W // 8, 8, LANES)
                    acc[3 * di + dj] = acc[3 * di + dj] + jnp.sum(prod, 0)
            near = near[1:]
            hear = hear[1:]
        for k in range(9):
            dtaps_ref[k : k + 1, lanes] = jnp.sum(acc[k], 0, keepdims=True)
        return carry

    lax.fori_loop(0, FF // LANES, chunk, 0)


def block_back_body(
    h_ref,
    hlow_ref,
    hhigh_ref,
    dz_ref,
    zlow_ref,
    zhigh_ref,
    taps_ref,
    w1,
    x2_ref,
    gain,
    dx_ref,
    wo,
    q_ref,
    kv_ref,
    ok_ref,
    lse_ref,
    dh_ref,
    dtaps_ref,
    dln_ref,
    dx2_ref,
    dy_ref,
    dq_ref,
    dkv_ref,
):
    conv_back(h_ref, hlow_ref, hhigh_ref, dz_ref, zlow_ref, zhigh_ref, taps_ref, dh_ref, dtaps_ref)
    db = dot_nt(dh_ref[...], w1[...])
    dln, dgain, dbias = norm_back(x2_ref[...], gain[2:3], db)
    dln_ref[0:1, :] = dgain
    dln_ref[1:2, :] = dbias
    dx2 = dx_ref[...] + dln
    dx2_ref[...] = dx2
    dy = to_bf(dx2)
    dy_ref[...] = dy
    do_t = to_bf(dot_nt(wo[...], dy))
    q = q_ref[...] * jnp.asarray(scale_qk, bf16)
    q_t = q.T
    keys = kv_ref.shape[0]
    kv = kv_ref[...]
    k_t = (kv[:, :D] * jnp.asarray(scale_qk, bf16)).T
    shut = jnp.broadcast_to(ok_ref[...], (keys, q.shape[0]))
    dq_parts, dk_parts, dv_parts = ([], [], [])
    for head in range(HEADS):
        low, high = head * HD, (head + 1) * HD
        s = dot(kv[:, low:high], q_t[low:high, :]) + shut
        p = jnp.exp(s - lse_ref[head : head + 1, :])
        dp = dot(kv[:, D + low : D + high], do_t[low:high, :])
        dv_parts.append(dot_nt(do_t[low:high, :], to_bf(p)))
        ds = to_bf(p * (dp - jnp.sum(p * dp, 0, keepdims=True)))
        dq_parts.append(dot(k_t[low:high, :], ds))
        dk_parts.append(dot_nt(q_t[low:high, :], ds))
    dq_ref[...] = to_bf(jnp.concatenate(dq_parts, 0).T)
    dkv_ref[...] = jnp.concatenate(dk_parts + dv_parts, 0).T


def inputs_back(dkv, wkv, r_ref, gain, dq_ref, wq, wsr, x_ref, dx2_ref, dr_ref, dln_ref):
    w_kv = wkv[...].astype(f32)
    drn = dot_nt(dkv, w_kv, precise)
    dr, dgain1, dbias1 = norm_back(r_ref[...], gain[1:2], drn)
    dr = to_bf(dr)
    dr_ref[...] = dr
    rows = x_ref.shape[0] // W
    cells = [
        dot_nt(dr, wsr[k * D : (k + 1) * D, :]).reshape(rows // 2, 1, 1, HALF, D) for k in range(4)
    ]
    placed = jnp.concatenate(
        [jnp.concatenate(cells[0:2], 2), jnp.concatenate(cells[2:4], 2)], 1
    ).reshape(rows * W, D)
    da = dot_nt(dq_ref[...], wq[...]) + placed
    dln, dgain0, dbias0 = norm_back(x_ref[...], gain[0:1], da)
    for k, row in enumerate((dgain0, dgain1, dbias0, dbias1)):
        dln_ref[k : k + 1, :] = row
    return dx2_ref[...] + dln


def join_back_body(
    dkv_ref, wkv, r_ref, gain, dq_ref, wq, wsr, x_ref, dx2_ref, w2, slope_ref, dr_ref, dln_ref, dx_ref, dy_ref, dz_ref
):
    dx = inputs_back(dkv_ref[...], wkv, r_ref, gain, dq_ref, wq, wsr, x_ref, dx2_ref, dr_ref, dln_ref)
    dx_ref[...] = dx
    gelu_back(dx, w2, slope_ref, dy_ref, dz_ref)


def first_back_body(
    dkv_ref, wkv, r_ref, gain, dq_ref, wq, wsr, x_ref, dx2_ref, e_ref, ln_ref, dr_ref, dln_ref, de_ref, dle_ref
):
    dx = inputs_back(dkv_ref[...], wkv, r_ref, gain, dq_ref, wq, wsr, x_ref, dx2_ref, dr_ref, dln_ref)
    de, dgain, dbias = norm_back(e_ref[...], ln_ref[0:1], dx)
    de_ref[...] = to_bf(de)
    dle_ref[0:1, :] = dgain
    dle_ref[1:2, :] = dbias


def weight_grads_body(
    n_dp, cols, subs, core_ref, a_ref, dq_ref, rn_ref, dkv_ref, o_ref, dy2_ref, b_ref, dh_ref, dr_ref, g_ref, dy_ref, *refs
):
    outs, (proj, down) = refs[:-2], refs[-2:]
    a = a_ref[...]
    proj[:, :D] = contract(a, dq_ref[...])
    proj[:, D : 3 * D] = contract(rn_ref[...].astype(f32), dkv_ref[...], precise)
    proj[:, 3 * D : 4 * D] = contract(o_ref[...], dy2_ref[...])
    proj[:, 4 * D :] = contract(b_ref[...], dh_ref[...])
    dr = dr_ref[...]
    for k, cell in enumerate(cells_of(a)):
        down[k * D : (k + 1) * D, :D] = contract(cell, dr)
    down[:, D:] = contract(g_ref[...], dy_ref[...])
    rows = D // n_dp
    sub = rows // subs
    wide = (4 * D + FF) // cols
    down_rows = FF // n_dp
    for c in range(cols):
        for d in range(n_dp):
            for n, out in enumerate(outs):
                for j in range(subs) if len(outs) == 1 else (None,):
                    if j is None:
                        k = core_ref[0] if n == 0 else 1 - core_ref[0]
                        at = (c ^ core_ref[1], lax.rem(d + n_dp - core_ref[2], n_dp))
                    else:
                        k = j
                        at = (c, j, d)
                    start = d * rows + k * sub
                    low = d * down_rows + (c * subs + k) * (down_rows // (cols * subs))
                    if j is None:
                        start = pl.multiple_of(start, 8)
                        low = pl.multiple_of(low, 8)
                    out[(*at, slice(0, sub))] = proj[pl.ds(start, sub), c * wide : (c + 1) * wide]
                    out[(*at, slice(sub, 2 * sub))] = down[pl.ds(low, sub), :]


def moments(w, g, m, v):
    m2 = beta_one * m + (1.0 - beta_one) * g
    v2 = beta_two * v + (1.0 - beta_two) * g * g
    u = (
        m2 / (1.0 - beta_one**STEP) / (jnp.sqrt(v2 / (1.0 - beta_two**STEP)) + lamb_eps)
        + decay_rate * w
    )
    return m2, v2, u


def update_body(
    cols, subs, late, factor_ref, early_ref, late_ref, wp, mp, vp, wd, md, vd, mp2, vp2, up, md2, vd2, ud, sums
):
    factor = factor_ref[0]
    layer = pl.program_id(0)
    sub = wp.shape[1] // subs
    wide = wp.shape[2] // cols

    def go(g_ref):
        squares = [0.0, 0.0]

        def put(n, at, refs, outs, g):
            new = moments(refs[0][at], g * factor, refs[1][at], refs[2][at])
            for out, value in zip(outs, new):
                out[at] = value
            squares[n] = squares[n] + jnp.sum(new[2] * new[2], 0, keepdims=True)

        for c in range(cols):
            for k in range(subs):
                g = g_ref[c * subs + k].astype(f32).reshape(2 * sub, wide)
                at = (0, slice(k * sub, (k + 1) * sub), slice(c * wide, (c + 1) * wide))
                put(0, at, (wp, mp, vp), (mp2, vp2, up), g[:sub])
                rows = slice((c * subs + k) * sub, (c * subs + k + 1) * sub)
                for half in range(2):
                    at = (0, half, rows, slice(0, D))
                    put(1, at, (wd, md, vd), (md2, vd2, ud), g[sub:, half * D : (half + 1) * D])
        for n in range(2):
            sums[0, n : n + 1, :] = jnp.broadcast_to(jnp.sum(squares[n], 1, keepdims=True), (1, LANES))

    pl.when(layer >= late)(lambda: go(early_ref))
    pl.when(layer < late)(lambda: go(late_ref))


def group_sums(arrs, layered=None):
    embed, proj, downs, taps, head, gains, biases = arrs
    first = jnp.stack([jnp.sum(embed), jnp.sum(head), jnp.sum(gains), jnp.sum(biases)])
    if layered is None:
        layered = [jnp.sum(a.reshape(a.shape[0], -1), 1) for a in (proj, downs)]
    return jnp.concatenate([first, *layered, jnp.sum(taps.reshape(taps.shape[0], -1), 1)])


def spread_ratio(ratio):
    return (
        ratio[0],
        ratio[4 : 4 + LAYERS].reshape(LAYERS, 1, 1),
        ratio[4 + LAYERS : 4 + 2 * LAYERS].reshape(LAYERS, 1, 1, 1),
        ratio[4 + 2 * LAYERS : 4 + 3 * LAYERS].reshape(LAYERS, 1, 1),
        ratio[1],
        ratio[2],
        ratio[3],
    )


def per_device(
    patches,
    valid,
    labels,
    partners,
    mix,
    embed_w,
    in_proj,
    down_proj,
    dw_kernel,
    head_w,
    norm_gain,
    norm_bias,
    m_embed,
    m_proj,
    m_down,
    m_taps,
    m_head,
    m_gain,
    m_bias,
    v_embed,
    v_proj,
    v_down,
    v_taps,
    v_head,
    v_gain,
    v_bias,
):
    masters = (embed_w, in_proj, down_proj, dw_kernel, head_w, norm_gain, norm_bias)
    firsts = (m_embed, m_proj, m_down, m_taps, m_head, m_gain, m_bias)
    seconds = (v_embed, v_proj, v_down, v_taps, v_head, v_gain, v_bias)
    n_seq = lax.axis_size("seq")
    n_dp = lax.axis_size("dp")
    seq_pos = lax.axis_index("seq")
    img_dev, rows = (patches.shape[0], patches.shape[1])
    images = img_dev * n_dp

    team = n_seq
    while team * img_dev > n_seq:
        team //= 2
    blocks = n_seq // team
    rows_own = rows * blocks
    tok = rows_own * W
    keys_own = tok // 4
    image = jnp.minimum(seq_pos // team, img_dev - 1)
    busy = seq_pos // team < img_dev
    place = seq_pos % team

    def between(shift, wrap):
        pairs = []
        for base in range(0, n_seq, team):
            for h in range(team):
                if wrap or 0 <= h + shift < team:
                    pairs.append((base + (h + shift) % team, base + h))
        return pairs

    def edges(v):
        low = lax.ppermute(v[-W:], "seq", between(-1, False))
        high = lax.ppermute(v[:W], "seq", between(1, False))
        return low, high

    def all_keys(v):
        return jnp.concatenate(
            [v] + [lax.ppermute(v, "seq", between(j, True)) for j in range(1, team)], 0
        )

    def own_keys(v):
        total = v[:keys_own]
        for j in range(1, team):
            part = v[j * keys_own : (j + 1) * keys_own]
            total = total + lax.ppermute(part, "seq", between(-j, True))
        return total

    back_block = seq_pos % blocks
    routes = [
        [
            (blocks * h + (i + r) % blocks, team * i + h)
            for i in range(img_dev)
            for h in range(team)
        ]
        for r in range(blocks)
    ]

    def to_team(v):
        got = []
        for r, pairs in enumerate(routes):
            send = lax.dynamic_index_in_dim(
                v, jnp.minimum((back_block - r) % blocks, img_dev - 1), 0, keepdims=False
            )
            got.append(lax.ppermute(send, "seq", pairs))
        twice = jnp.stack(got + got)
        own = lax.dynamic_slice_in_dim(twice, (blocks - image) % blocks, blocks, 0)
        return own.reshape(tok, -1)

    cols = 4
    subs = n_seq // cols
    row_in = D // n_dp
    sub_in = row_in // subs
    wide = in_proj.shape[2] // cols
    down_rows = down_proj.shape[2] // n_seq
    core = seq_pos % subs

    def part_of(flat):
        size = -(-flat.shape[0] // (wide * n_seq)) * wide * n_seq
        flat = jnp.pad(flat, (0, size - flat.shape[0])).reshape(n_seq, -1, wide)
        return lax.dynamic_index_in_dim(flat, seq_pos, 0, keepdims=False)

    def layer_part(l):
        block = lax.dynamic_slice(
            in_proj[l], (core * sub_in, (seq_pos // subs) * wide), (sub_in, wide)
        )
        lower = lax.dynamic_slice_in_dim(down_proj[l], seq_pos * down_rows, down_rows, 1)
        return [to_bf(block), to_bf(jnp.concatenate([lower[0], lower[1]], 1))]

    def gathered(parts):
        sizes = [p.shape[0] for p in parts]
        got = lax.all_gather(jnp.concatenate(parts, 0), ("dp", "seq"), axis=0, tiled=False)
        got = got.reshape(n_dp, n_seq, sum(sizes), wide)
        starts = [sum(sizes[:i]) for i in range(len(sizes))]
        return [got[:, :, a : a + n] for a, n in zip(starts, sizes)]

    def proj_of(got):
        got = got.reshape(n_dp, cols, subs, sub_in, wide).transpose(0, 2, 3, 1, 4)
        return got.reshape(D, cols * wide)

    dp_pos = lax.axis_index("dp")

    def over_dp(v):
        got = [v] + [
            lax.ppermute(v, "dp", [((d + j) % n_dp, d) for d in range(n_dp)])
            for j in range(1, n_dp)
        ]
        return lax.dynamic_slice_in_dim(jnp.stack(got + got), (n_dp - dp_pos) % n_dp, n_dp, 0)

    embed16 = over_dp(to_bf(embed_w)).reshape(-1, D)
    taps16 = over_dp(to_bf(dw_kernel).reshape(LAYERS * 9, -1))
    norms16 = over_dp(to_bf(jnp.stack([norm_gain, norm_bias])))
    taps32 = taps16.transpose(1, 0, 2).reshape(LAYERS, 9, FF).astype(f32)
    norms32 = norms16.transpose(1, 2, 0, 3).reshape(2, -1, D).astype(f32)
    gain32, bias32 = norms32[0], norms32[1]
    groups = [[0, 1, 2, 3], [4, 5]]
    extra = [[], [part_of(to_bf(head_w).reshape(-1))]]
    layers16, extras = ([], [])
    for members, more in zip(groups, extra):
        parts = more + [p for l in members for p in layer_part(l)]
        got = gathered(parts)
        extras += [g.reshape(n_dp, -1) for g in got[: len(more)]]
        got = got[len(more) :]
        layers16 += [(proj_of(got[2 * i]), got[2 * i + 1].reshape(FF, 2 * D)) for i in range(len(members))]
    head16 = extras[0][:, : head_w.size].reshape(D, CLS)

    def own(v):
        return lax.dynamic_index_in_dim(v, image, 0, keepdims=False)

    wanted = own(partners)
    partner_label = jnp.zeros((), jnp.int32)
    for j in range(n_dp):
        other = labels
        if j:
            other = lax.ppermute(labels, "dp", [((d + j) % n_dp, d) for d in range(n_dp)])
        index = ((dp_pos + j) % n_dp) * img_dev + jnp.arange(img_dev)
        partner_label = partner_label + jnp.sum(jnp.where(index == wanted, other, 0))
    valid_own = own(valid)
    tid = lax.broadcasted_iota(jnp.int32, (tok, 1), 0)
    within = tid % W
    row_id = place * rows_own + tid // W
    col_id = 2 * (within % HALF) + within // HALF
    okay = ((row_id < valid_own[0]) & (col_id < valid_own[1]) & busy).astype(f32)
    kid = lax.broadcasted_iota(jnp.int32, (team * keys_own, 1), 0)
    segment = (place + kid // keys_own) % team
    key_row = segment * (rows_own // 2) + (kid % keys_own) // HALF
    key_ok = (2 * key_row < valid_own[0]) & (2 * (kid % HALF) < valid_own[1])
    shut = jnp.where(key_ok, 0.0, big_neg).astype(f32)
    count = (valid_own[0] * valid_own[1]).astype(f32).reshape(1, 1)
    classes = lax.broadcasted_iota(jnp.int32, (1, CLS), 1)
    mix_own = own(mix)
    target = mix_own * (classes == own(labels)).astype(f32) + (1.0 - mix_own) * (
        classes == partner_label
    ).astype(f32)

    def weights(l):
        base = 1 + 3 * l
        return dict(
            wq=layers16[l][0][:, :D],
            wkv=layers16[l][0][:, D : 3 * D],
            wo=layers16[l][0][:, 3 * D : 4 * D],
            w1=layers16[l][0][:, 4 * D :],
            wsr=layers16[l][1][:, :D],
            w2=layers16[l][1][:, D:],
            taps=taps32[l],
            gain=gain32[base : base + 3],
            bias=bias32[base : base + 3],
        )

    wts = [weights(l) for l in range(LAYERS)]
    ln_first = jnp.stack([gain32[0], bias32[0]])
    ln_last = jnp.stack([gain32[-1], bias32[-1]])

    full = ((tok, D), f32)
    half = ((tok, D), bf16)
    wide16 = ((tok, FF), bf16)
    input_outs = [half, half, ((keys_own, D), f32), ((keys_own, D), bf16), ((keys_own, 2 * D), bf16)]
    ln_out = ((2, D), f32)

    spread = patches.reshape(img_dev, rows, HALF, 2, -1).transpose(0, 1, 3, 2, 4)
    patch_own = to_team(spread.reshape(img_dev, rows * W, -1))
    e, x = run(2, embed_body, [full, full], patch_own, embed16, ln_first)
    w = wts[0]
    a16, q16, r, rn16, kv16 = run(
        2, first_body, input_outs, x, w["gain"], w["bias"], w["wq"], w["wsr"], w["wkv"]
    )
    kept = []
    for l in range(LAYERS):
        w = wts[l]
        kv_all = all_keys(kv16)
        o16, lse, x2, b16, h16 = run(
            4,
            middle_body,
            [half, ((HEADS, tok), f32), full, half, wide16],
            q16,
            kv_all,
            shut,
            x,
            w["gain"],
            w["bias"],
            w["wo"],
            w["w1"],
        )
        hlow, hhigh = edges(h16)
        keep = dict(
            x=x, a16=a16, q16=q16, r=r, rn16=rn16, kv=kv_all, o16=o16, lse=lse, x2=x2, b16=b16,
            h16=h16, hlow=hlow, hhigh=hhigh,
        )
        shared = (h16, hlow, hhigh, w["taps"], x2, w["w2"])
        if l + 1 < LAYERS:
            n = wts[l + 1]
            keep["g16"], keep["slope"], x, a16, q16, r, rn16, kv16 = run(
                8,
                join_body,
                [wide16, ((tok, FF), f32), full] + input_outs,
                *shared,
                n["gain"],
                n["bias"],
                n["wq"],
                n["wsr"],
                n["wkv"],
            )
        else:
            keep["g16"], keep["slope"], x, pool = run(
                7,
                last_body,
                [wide16, ((tok, FF), f32), full, ((1, D), f32)],
                *shared,
                ln_last,
                okay,
            )
        kept.append(keep)

    whole = pool
    for j in range(1, team):
        whole = whole + lax.ppermute(pool, "seq", between(j, True))
    loss_own, pooled16, dlog16, dln_last, dx, dy16, dz16 = run(
        4,
        functools.partial(head_body, images),
        [((1, 1), f32), ((1, D), bf16), ((1, CLS), bf16), ln_out, full, half, wide16],
        whole,
        count,
        head16,
        target,
        x,
        ln_last,
        okay,
        wts[-1]["w2"],
        kept[-1]["slope"],
    )
    chosen = ((place == 0) & busy).astype(f32)
    d_head = pooled16.astype(f32).reshape(D, 1) * dlog16.astype(f32) * chosen
    loss_local = loss_own[0, 0] * busy.astype(f32)
    teams = n_seq // team
    loss_parts = jnp.zeros((teams,), f32)
    for j in range(teams):
        other = loss_local
        if j:
            other = lax.ppermute(
                loss_local, "seq", [((d + j * team) % n_seq, d) for d in range(n_seq)]
            )
        loss_parts = jnp.where(jnp.arange(teams) == (seq_pos // team + j) % teams, other, loss_parts)
    loss_seq = jnp.sum(loss_parts)

    piece = ((cols, n_dp, 2 * sub_in, wide), f32)
    paired = subs == 2 and cols == 4
    chip = seq_pos // subs
    where = jnp.stack([core, chip, dp_pos]).astype(jnp.int32)

    def weight_grads(*args):
        vm = pl.BlockSpec(memory_space=pltpu.VMEM)
        outs = [piece] * 2 if paired else [((cols, subs) + piece[0][1:], f32)]
        return pl.pallas_call(
            functools.partial(weight_grads_body, n_dp, cols, subs),
            out_shape=[jax.ShapeDtypeStruct(s, d) for s, d in outs],
            in_specs=[pl.BlockSpec(memory_space=pltpu.SMEM)] + [vm] * len(args),
            out_specs=[vm] * len(outs),
            scratch_shapes=[pltpu.VMEM((D, cols * wide), f32), pltpu.VMEM((FF, 2 * D), f32)],
            compiler_params=pltpu.CompilerParams(vmem_limit_bytes=48 << 20),
            cost_estimate=cost(6),
        )(where, *args)

    def padded_rest(parts):
        flat = jnp.concatenate(parts, 1)
        size = -(-flat.shape[1] // (8 * wide * n_seq)) * 8 * wide * n_seq
        flat = jnp.pad(flat, ((0, 0), (0, size - flat.shape[1])))
        flat = flat.reshape(n_dp, cols, subs, -1, wide).transpose(1, 2, 0, 3, 4)
        if not paired:
            return [flat]
        flat = jnp.stack([lax.dynamic_index_in_dim(flat, chip ^ j, 0, False) for j in range(cols)])
        twice = jnp.concatenate([flat, flat], 2)
        flat = lax.dynamic_slice_in_dim(twice, dp_pos, n_dp, 2)
        return [lax.dynamic_index_in_dim(flat, k, 1, False) for k in (core, 1 - core)]

    def pair_sum(parts):
        mine, send = parts
        return mine + lax.ppermute(send, "seq", [(d ^ 1, d) for d in range(n_seq)])

    def plane_sum(y):
        total = y[0]
        for j in range(1, cols):
            pairs = [(d ^ (j * subs), d) for d in range(n_seq)]
            total = total + lax.ppermute(to_bf(y[j]), "seq", pairs).astype(f32)
        return total

    def dp_sum(y):
        total = y[0]
        for j in range(1, n_dp):
            pairs = [(d, (d + j) % n_dp) for d in range(n_dp)]
            total = total + lax.ppermute(y[j], "dp", pairs)
        return total

    def whole_sum(parts):
        y = jnp.concatenate([p[0] for p in parts], -2)
        y = lax.psum_scatter(y.reshape(-1, wide), "seq", scatter_dimension=0, tiled=True)
        return lax.psum_scatter(y, "dp", scatter_dimension=0, tiled=True)

    def tied(value, others):
        return lax.optimization_barrier((value, others))

    stages = [pair_sum, plane_sum, dp_sum]
    pieces = []

    def advance(now):
        if not paired:
            return now
        ready = [p for p in pieces if p[0] < len(stages)]
        now, values = tied(now, [p[1] for p in ready])
        for p, v in zip(ready, values):
            p[1] = stages[p[0]](v)
            p[0] += 1
        return now

    grads = [None] * LAYERS
    pieces.append([0, padded_rest([d_head.reshape(n_dp, -1)])])
    waiting = None
    for l in reversed(range(LAYERS)):
        w, k = wts[l], kept[l]
        zlow, zhigh = edges(dz16)
        dh16, d_taps, dln2, dx2, dy2, dq16, dkv = run(
            11,
            block_back_body,
            [wide16, ((9, FF), f32), ln_out, full, half, half, ((team * keys_own, 2 * D), f32)],
            k["h16"], k["hlow"], k["hhigh"], dz16, zlow, zhigh, w["taps"], w["w1"], k["x2"], w["gain"], dx,
            w["wo"], k["q16"], k["kv"], shut, k["lse"],
        )
        if waiting is not None:
            pieces.append([0, weight_grads(*waiting)])
        dkv_own = own_keys(dkv)
        dkv_own = advance(dkv_own)
        upper = dy16
        shared = (dkv_own, w["wkv"], k["r"], w["gain"], dq16, w["wq"], w["wsr"], k["x"], dx2)
        if l:
            dr16, dln, dx, dy16, dz16 = run(
                6,
                join_back_body,
                [((keys_own, D), bf16), ((4, D), f32), full, half, wide16],
                *shared,
                wts[l - 1]["w2"],
                kept[l - 1]["slope"],
            )
        else:
            dr16, dln, de16, dln_first = run(
                3,
                first_back_body,
                [((keys_own, D), bf16), ((4, D), f32), half, ln_out],
                *shared,
                e,
                ln_first,
            )
        waiting = (k["a16"], dq16, k["rn16"], dkv_own, k["o16"], dy2, k["b16"], dh16, dr16, k["g16"], upper)
        grads[l] = (
            d_taps,
            jnp.concatenate([dln[0:2], dln2[0:1]], 0),
            jnp.concatenate([dln[2:4], dln2[1:2]], 0),
        )
    (d_embed,) = run(3, embed_back_body, [((embed16.shape[0], D), f32)], patch_own, de16)
    d_gain = jnp.concatenate([dln_first[0:1]] + [g[1] for g in grads] + [dln_last[0:1]], 0)
    d_bias = jnp.concatenate([dln_first[1:2]] + [g[2] for g in grads] + [dln_last[1:2]], 0)
    d_taps = jnp.stack([g[0] for g in grads])
    rest = [
        d_embed.reshape(n_dp, -1),
        d_taps.reshape(LAYERS * 9, n_dp, -1).transpose(1, 0, 2).reshape(n_dp, -1),
        d_gain.reshape(-1, n_dp, row_in).transpose(1, 0, 2).reshape(n_dp, -1),
        d_bias.reshape(-1, n_dp, row_in).transpose(1, 0, 2).reshape(n_dp, -1),
    ]
    cuts = [0]
    for part in rest:
        cuts.append(cuts[-1] + part.shape[1])
    last = weight_grads(*waiting)
    rest = padded_rest(rest)
    pieces.append([0, [jnp.concatenate([a, b], -2) for a, b in zip(last, rest)]])
    if paired:
        while any(p[0] < len(stages) for p in pieces):
            for p in pieces:
                if p[0] < len(stages):
                    p[1] = stages[p[0]](p[1])
                    p[0] += 1
        sums = [p[1] for p in pieces]
    else:
        sums = [whole_sum([p[1]]) for p in pieces]

    late = 2

    def together(parts):
        return lax.all_gather(to_bf(jnp.concatenate(parts, 0)), "seq", axis=0, tiled=False)

    early_got = together(sums[1 : LAYERS + 1 - late] + sums[:1])
    late_got = together(sums[LAYERS + 1 - late :])
    head_start = (LAYERS - late) * 2 * sub_in
    g_head = early_got[:, head_start:].reshape(-1)[: head_w.size].reshape(head_w.shape).astype(f32)
    flat = late_got[:, late * 2 * sub_in :].reshape(-1).astype(f32)
    flat = [flat[a:b] for a, b in zip(cuts, cuts[1:])]
    shards = (
        flat[0].reshape(embed_w.shape),
        None,
        None,
        flat[1].reshape(dw_kernel.shape),
        g_head,
        flat[2].reshape(norm_gain.shape),
        flat[3].reshape(norm_bias.shape),
    )

    gsq_local = sum(jnp.sum(jnp.square(g.astype(f32))) for g in (early_got, late_got))
    wsq_local = group_sums(tuple((w * w for w in masters)))
    gsq, wsq, loss = lax.psum((gsq_local, wsq_local, loss_seq), "dp")
    grad_norm = jnp.sqrt(gsq)
    factor = jnp.minimum(1.0, clip_limit / grad_norm)

    proj_spec = pl.BlockSpec((1,) + in_proj.shape[1:], lambda l: (l, 0, 0))
    down_spec = pl.BlockSpec((1,) + down_proj.shape[1:], lambda l: (l, 0, 0, 0))
    block = (n_seq, 2 * sub_in, wide)
    blocks_of = [early_got, late_got]
    if 2 * sub_in % 8:
        block = (n_seq, 1, 2 * sub_in, wide)
        counts = (LAYERS - late, late)
        blocks_of = [
            g[:, : n * 2 * sub_in].reshape(n_seq, n, 2 * sub_in, wide)
            for g, n in zip(blocks_of, counts)
        ]
    tail = (0,) * (len(block) - 2)
    got = pl.pallas_call(
        functools.partial(update_body, cols, subs, late),
        grid=(LAYERS,),
        out_shape=[jax.ShapeDtypeStruct(in_proj.shape, f32)] * 3
        + [jax.ShapeDtypeStruct(down_proj.shape, f32)] * 3
        + [jax.ShapeDtypeStruct((LAYERS, 2, LANES), f32)],
        in_specs=[
            pl.BlockSpec(memory_space=pltpu.SMEM),
            pl.BlockSpec(block, lambda l: (0, jnp.minimum(LAYERS - 1 - l, LAYERS - 1 - late), *tail)),
            pl.BlockSpec(block, lambda l: (0, jnp.maximum(late - 1 - l, 0), *tail)),
        ]
        + [proj_spec] * 3
        + [down_spec] * 3,
        out_specs=[proj_spec] * 3 + [down_spec] * 3 + [pl.BlockSpec((1, 2, LANES), lambda l: (l, 0, 0))],
        compiler_params=pltpu.CompilerParams(vmem_limit_bytes=56 << 20),
        cost_estimate=cost(25),
    )(factor.reshape(1), *blocks_of, in_proj, m_proj, v_proj, down_proj, m_down, v_down)
    big = {1: got[0:3], 2: got[3:6]}
    new_m, new_v, updates = ([], [], [])
    for n, (w, g, m, v) in enumerate(zip(masters, shards, firsts, seconds)):
        m2, v2, u = big[n] if n in big else moments(w, g * factor, m, v)
        new_m.append(m2)
        new_v.append(v2)
        updates.append(u)
    usq = lax.psum(
        group_sums(tuple((u * u for u in updates)), [got[6][:, 0, 0], got[6][:, 1, 0]]), "dp"
    )
    wnorm = jnp.sqrt(wsq)
    unorm = jnp.sqrt(usq)
    ratio = wnorm / unorm
    spreads = spread_ratio(ratio)
    new_w = [w - learn_rate * r * u for w, r, u in zip(masters, spreads, updates)]
    stats = jnp.stack([wnorm, unorm])
    return (loss, grad_norm, stats, ratio, *new_w, *new_m, *new_v)


def solution(mesh):
    placed = (
        P("dp", None),
        P(None, "dp", None),
        P(None, None, "dp", None),
        P(None, None, "dp"),
        P("dp", None),
        P(None, "dp"),
        P(None, "dp"),
    )
    in_specs = (
        P("dp", "seq", None, None),
        P("dp", None),
        P("dp"),
        P("dp"),
        P("dp"),
    ) + placed * 3
    out_specs = (P(), P(), P(), P()) + placed * 3
    return jax.shard_map(
        per_device, mesh=mesh, in_specs=in_specs, out_specs=out_specs, check_vma=False
    )
```

```python
import functools

import jax
import jax.numpy as jnp
from jax import lax
from jax.experimental import pallas as pl
from jax.experimental.pallas import tpu as pltpu
from jax.sharding import PartitionSpec as P

D = 320
HEADS = 5
HD = 64
FF = 1280
CLS = 1000
W = 64
HALF = W // 2
LAYERS = 6
STEP = 5
LANES = 128


norm_eps = 1e-06
scale_qk = 0.125
big_neg = -1e30
beta_one = 0.9
beta_two = 0.999
lamb_eps = 1e-06
decay_rate = 0.01
learn_rate = 0.3
clip_limit = 0.1
root_half = 0.7071067811865476
root_two_pi = 0.3989422804014327
precise = lax.Precision.HIGHEST

f32 = jnp.float32
bf16 = jnp.bfloat16


def to_bf(v):
    return v.astype(bf16)


def dot(a, b):
    return jnp.dot(a, b, preferred_element_type=f32)


def dot_nt(a, b, precision=None):
    return lax.dot_general(
        a, b, (((1,), (1,)), ((), ())), precision=precision, preferred_element_type=f32
    )


def contract(a, b, precision=None):
    return lax.dot_general(
        a, b, (((0,), (0,)), ((), ())), precision=precision, preferred_element_type=f32
    )


def norm_parts(v):
    center = v - jnp.mean(v, -1, keepdims=True)
    spread = jnp.mean(center * center, -1, keepdims=True)
    scale = lax.rsqrt(spread + norm_eps)
    return center * scale, scale


def layer_norm(v, gain, bias):
    return norm_parts(v)[0] * gain + bias


def norm_back(v, gain, grad):
    unit, scale = norm_parts(v)
    dgain = jnp.sum(grad * unit, 0, keepdims=True)
    dbias = jnp.sum(grad, 0, keepdims=True)
    t = grad * gain
    dv = scale * (
        t - jnp.mean(t, -1, keepdims=True) - unit * jnp.mean(t * unit, -1, keepdims=True)
    )
    return dv, dgain, dbias


def cost(us):
    return pl.CostEstimate(flops=int(us * 1e8), bytes_accessed=int(us * 1e5), transcendentals=0)


def run(us, body, outs, *args, place=None):
    vm = pl.BlockSpec(memory_space=pltpu.VMEM)
    scalars = [] if place is None else [place]
    return pl.pallas_call(
        body,
        out_shape=[jax.ShapeDtypeStruct(s, d) for s, d in outs],
        in_specs=[pl.BlockSpec(memory_space=pltpu.SMEM)] * len(scalars) + [vm] * len(args),
        out_specs=[vm] * len(outs),
        compiler_params=pltpu.CompilerParams(vmem_limit_bytes=48 << 20),
        cost_estimate=cost(us),
    )(*scalars, *args)


def cells_of(v):
    rows = v.shape[0] // W
    split = v.reshape(rows // 2, 2, 2, HALF, v.shape[1])
    return [split[:, k // 2, k % 2].reshape(-1, v.shape[1]) for k in range(4)]


def attention_inputs(x, gain, bias, wq, wsr, wkv, a_ref, q_ref, r_ref, rn_ref, kv_ref):
    a = to_bf(layer_norm(x, gain[0:1], bias[0:1]))
    a_ref[...] = a
    q_ref[...] = to_bf(dot(a, wq[...]))
    total = None
    for k, cell in enumerate(cells_of(a)):
        part = dot(cell, wsr[k * D : (k + 1) * D, :])
        total = part if total is None else total + part
    r_ref[...] = total
    rn = to_bf(layer_norm(total, gain[1:2], bias[1:2]))
    rn_ref[...] = rn
    kv_ref[...] = to_bf(dot(rn, wkv[...]))


def embed_body(p_ref, w_ref, ln_ref, e_ref, x_ref):
    e = dot(p_ref[...], w_ref[...])
    e_ref[...] = e
    x_ref[...] = layer_norm(e, ln_ref[0:1], ln_ref[1:2])


def embed_back_body(p_ref, de_ref, dw_ref):
    dw_ref[...] = contract(p_ref[...], de_ref[...])


def first_body(x_ref, gain, bias, wq, wsr, wkv, *outs):
    attention_inputs(x_ref[...], gain, bias, wq, wsr, wkv, *outs)


def middle_body(
    place, q_ref, kv_ref, ok_ref, x_ref, gain, bias, wo, w1, o_ref, lse_ref, x2_ref, b_ref, h_ref, edge_ref
):
    q = q_ref[...] * jnp.asarray(scale_qk, bf16)
    keys = kv_ref.shape[0]
    kv = kv_ref[...]
    shut = jnp.broadcast_to(ok_ref[...], (keys, q.shape[0]))
    q_t = q.T
    v_t = kv[:, D:].T
    parts = []
    for head in range(HEADS):
        low, high = head * HD, (head + 1) * HD
        s = dot(kv[:, low:high], q_t[low:high, :]) + shut
        top = jnp.max(s, 0, keepdims=True)
        expo = jnp.exp(s - top)
        total = jnp.sum(expo, 0, keepdims=True)
        lse_ref[head : head + 1, :] = top + jnp.log(total)
        p = to_bf(expo * (1.0 / total))
        parts.append(dot(v_t[low:high, :], p))
    o = to_bf(jnp.concatenate(parts, 0).T)
    o_ref[...] = o
    x2 = x_ref[...] + dot(o, wo[...])
    x2_ref[...] = x2
    b = to_bf(layer_norm(x2, gain[2:3], bias[2:3]))
    b_ref[...] = b
    h_ref[...] = to_bf(dot(b, w1[...]))
    send_edge(place, h_ref, edge_ref)


def shift_down(v):
    index = lax.broadcasted_iota(jnp.int32, v.shape, 0)
    return jnp.where(index == 0, 0.0, pltpu.roll(v, 1, 0))


def shift_up(v):
    index = lax.broadcasted_iota(jnp.int32, v.shape, 0)
    return jnp.where(index == v.shape[0] - 1, 0.0, pltpu.roll(v, v.shape[0] - 1, 0))


def from_left(v):
    return jnp.concatenate([shift_down(v[HALF:]), v[:HALF]], 0)


def from_right(v):
    return jnp.concatenate([v[HALF:], shift_up(v[:HALF])], 0)


def row_of(main, near, i, rows, lanes):
    place, low, high = near
    if i < 0:
        return jnp.where(place[0] > 0, low[:, lanes].astype(f32), 0.0)
    if i >= rows:
        return jnp.where(place[1] > 0, high[:, lanes].astype(f32), 0.0)
    return main[i * W : (i + 1) * W, lanes].astype(f32)


def send_edge(place, main, edge_ref):
    start = pl.multiple_of(jnp.where(place[0] > 0, 0, main.shape[0] - W), W)
    edge_ref[...] = main[pl.ds(start, W), :]


def conv_gelu(h_ref, ends, taps_ref, g_ref, slope_ref):
    rows = h_ref.shape[0] // W

    def chunk(c, carry):
        lanes = pl.ds(pl.multiple_of(c * LANES, LANES), LANES)
        taps = [taps_ref[k : k + 1, lanes] for k in range(9)]
        near = [row_of(h_ref, ends, i, rows, lanes) for i in (-1, 0)]
        for i in range(rows):
            near.append(row_of(h_ref, ends, i + 1, rows, lanes))
            sums = [
                taps[j] * near[0] + taps[3 + j] * near[1] + taps[6 + j] * near[2] for j in range(3)
            ]
            z = sums[1] + from_left(sums[0]) + from_right(sums[2])
            phi = 0.5 + 0.5 * lax.erf(z * root_half)
            here = slice(i * W, (i + 1) * W)
            g_ref[here, lanes] = to_bf(z * phi)
            slope_ref[here, lanes] = phi + z * (jnp.exp(-0.5 * z * z) * root_two_pi)
            near = near[1:]
        return carry

    lax.fori_loop(0, FF // LANES, chunk, 0)


def last_body(place, h_ref, low_ref, high_ref, taps_ref, x2_ref, w2, ln_ref, ok_ref, g_ref, slope_ref, x_ref, sum_ref):
    conv_gelu(h_ref, (place, low_ref, high_ref), taps_ref, g_ref, slope_ref)
    x = x2_ref[...] + dot(g_ref[...], w2[...])
    x_ref[...] = x
    fin = layer_norm(x, ln_ref[0:1], ln_ref[1:2])
    sum_ref[...] = jnp.sum(fin * ok_ref[...], 0, keepdims=True)


def join_body(
    place, h_ref, low_ref, high_ref, taps_ref, x2_ref, w2, gain, bias, wq, wsr, wkv, g_ref, slope_ref, x_ref, *outs
):
    conv_gelu(h_ref, (place, low_ref, high_ref), taps_ref, g_ref, slope_ref)
    x = x2_ref[...] + dot(g_ref[...], w2[...])
    x_ref[...] = x
    attention_inputs(x, gain, bias, wq, wsr, wkv, *outs)


def gelu_back(place, dx, w2, slope_ref, dy_ref, dz_ref, edge_ref):
    dy = to_bf(dx)
    dy_ref[...] = dy
    dg = to_bf(dot_nt(dy, w2[...])).astype(f32)
    dz_ref[...] = to_bf(dg * slope_ref[...])
    send_edge(place, dz_ref, edge_ref)


def head_body(
    images,
    place,
    pool_ref,
    count_ref,
    head_ref,
    target_ref,
    x_ref,
    ln_ref,
    ok_ref,
    w2,
    slope_ref,
    loss_ref,
    pooled_ref,
    dlog_ref,
    dln_ref,
    dx_ref,
    dy_ref,
    dz_ref,
    edge_ref,
):
    count = count_ref[...]
    pooled = to_bf(pool_ref[...] / count)
    pooled_ref[...] = pooled
    logits = dot(jnp.broadcast_to(pooled.astype(f32), (16, D)).astype(bf16), head_ref[...])[0:1]
    shifted = logits - jnp.max(logits, -1, keepdims=True)
    logp = shifted - jnp.log(jnp.sum(jnp.exp(shifted), -1, keepdims=True))
    target = target_ref[...]
    loss_ref[...] = jnp.sum(target * logp, -1, keepdims=True) * (-1.0 / images)
    dlog = to_bf((jnp.exp(logp) - target) * (1.0 / images))
    dlog_ref[...] = dlog
    wide = jnp.broadcast_to(dlog.astype(f32), (16, CLS)).astype(bf16)
    dpool = dot_nt(wide, head_ref[...])[0:1] / count
    dx, dgain, dbias = norm_back(x_ref[...], ln_ref[0:1], ok_ref[...] * dpool)
    dln_ref[0:1, :] = dgain
    dln_ref[1:2, :] = dbias
    dx_ref[...] = dx
    gelu_back(place, dx, w2, slope_ref, dy_ref, dz_ref, edge_ref)


def conv_back(h_ref, hends, dz_ref, zends, taps_ref, dh_ref, dtaps_ref):
    rows = h_ref.shape[0] // W

    def chunk(c, carry):
        lanes = pl.ds(pl.multiple_of(c * LANES, LANES), LANES)
        taps = [taps_ref[k : k + 1, lanes] for k in range(9)]
        acc = [jnp.zeros((8, LANES), f32) for _ in range(9)]

        def views(i):
            v = row_of(dz_ref, zends, i, rows, lanes)
            return [from_right(v), v, from_left(v)]

        near = [views(-1), views(0)]
        hear = [row_of(h_ref, hends, i, rows, lanes) for i in (-1, 0)]
        for i in range(rows):
            near.append(views(i + 1))
            hear.append(row_of(h_ref, hends, i + 1, rows, lanes))
            dh = None
            for di in range(3):
                for dj in range(3):
                    part = taps[3 * di + dj] * near[2 - di][dj]
                    dh = part if dh is None else dh + part
            dh_ref[i * W : (i + 1) * W, lanes] = to_bf(dh)
            for di in range(3):
                for dj in range(3):
                    prod = (hear[di] * near[1][dj]).reshape(W // 8, 8, LANES)
                    acc[3 * di + dj] = acc[3 * di + dj] + jnp.sum(prod, 0)
            near = near[1:]
            hear = hear[1:]
        for k in range(9):
            dtaps_ref[k : k + 1, lanes] = jnp.sum(acc[k], 0, keepdims=True)
        return carry

    lax.fori_loop(0, FF // LANES, chunk, 0)


def block_back_body(
    place,
    h_ref,
    hlow_ref,
    hhigh_ref,
    dz_ref,
    zlow_ref,
    zhigh_ref,
    taps_ref,
    w1,
    x2_ref,
    gain,
    dx_ref,
    wo,
    q_ref,
    kv_ref,
    ok_ref,
    lse_ref,
    dh_ref,
    dtaps_ref,
    dln_ref,
    dx2_ref,
    dy_ref,
    dq_ref,
    dkv_ref,
):
    conv_back(
        h_ref, (place, hlow_ref, hhigh_ref), dz_ref, (place, zlow_ref, zhigh_ref), taps_ref, dh_ref, dtaps_ref
    )
    db = dot_nt(dh_ref[...], w1[...])
    dln, dgain, dbias = norm_back(x2_ref[...], gain[2:3], db)
    dln_ref[0:1, :] = dgain
    dln_ref[1:2, :] = dbias
    dx2 = dx_ref[...] + dln
    dx2_ref[...] = dx2
    dy = to_bf(dx2)
    dy_ref[...] = dy
    do_t = to_bf(dot_nt(wo[...], dy))
    q = q_ref[...] * jnp.asarray(scale_qk, bf16)
    q_t = q.T
    keys = kv_ref.shape[0]
    kv = kv_ref[...]
    k_t = (kv[:, :D] * jnp.asarray(scale_qk, bf16)).T
    shut = jnp.broadcast_to(ok_ref[...], (keys, q.shape[0]))
    dq_parts, dk_parts, dv_parts = ([], [], [])
    for head in range(HEADS):
        low, high = head * HD, (head + 1) * HD
        s = dot(kv[:, low:high], q_t[low:high, :]) + shut
        p = jnp.exp(s - lse_ref[head : head + 1, :])
        dp = dot(kv[:, D + low : D + high], do_t[low:high, :])
        dv_parts.append(dot_nt(do_t[low:high, :], to_bf(p)))
        ds = to_bf(p * (dp - jnp.sum(p * dp, 0, keepdims=True)))
        dq_parts.append(dot(k_t[low:high, :], ds))
        dk_parts.append(dot_nt(q_t[low:high, :], ds))
    dq_ref[...] = to_bf(jnp.concatenate(dq_parts, 0).T)
    dkv_ref[...] = jnp.concatenate(dk_parts + dv_parts, 0).T


def inputs_back(dkv, wkv, r_ref, gain, dq_ref, wq, wsr, x_ref, dx2_ref, dr_ref, dln_ref):
    w_kv = wkv[...].astype(f32)
    drn = dot_nt(dkv, w_kv, precise)
    dr, dgain1, dbias1 = norm_back(r_ref[...], gain[1:2], drn)
    dr = to_bf(dr)
    dr_ref[...] = dr
    rows = x_ref.shape[0] // W
    cells = [
        dot_nt(dr, wsr[k * D : (k + 1) * D, :]).reshape(rows // 2, 1, 1, HALF, D) for k in range(4)
    ]
    placed = jnp.concatenate(
        [jnp.concatenate(cells[0:2], 2), jnp.concatenate(cells[2:4], 2)], 1
    ).reshape(rows * W, D)
    da = dot_nt(dq_ref[...], wq[...]) + placed
    dln, dgain0, dbias0 = norm_back(x_ref[...], gain[0:1], da)
    for k, row in enumerate((dgain0, dgain1, dbias0, dbias1)):
        dln_ref[k : k + 1, :] = row
    return dx2_ref[...] + dln


def join_back_body(
    place, dkv_ref, wkv, r_ref, gain, dq_ref, wq, wsr, x_ref, dx2_ref, w2, slope_ref,
    dr_ref, dln_ref, dx_ref, dy_ref, dz_ref, edge_ref
):
    dx = inputs_back(dkv_ref[...], wkv, r_ref, gain, dq_ref, wq, wsr, x_ref, dx2_ref, dr_ref, dln_ref)
    dx_ref[...] = dx
    gelu_back(place, dx, w2, slope_ref, dy_ref, dz_ref, edge_ref)


def first_back_body(
    dkv_ref, wkv, r_ref, gain, dq_ref, wq, wsr, x_ref, dx2_ref, e_ref, ln_ref, dr_ref, dln_ref, de_ref, dle_ref
):
    dx = inputs_back(dkv_ref[...], wkv, r_ref, gain, dq_ref, wq, wsr, x_ref, dx2_ref, dr_ref, dln_ref)
    de, dgain, dbias = norm_back(e_ref[...], ln_ref[0:1], dx)
    de_ref[...] = to_bf(de)
    dle_ref[0:1, :] = dgain
    dle_ref[1:2, :] = dbias


def weight_grads_body(
    n_dp, cols, subs, core_ref, a_ref, dq_ref, rn_ref, dkv_ref, o_ref, dy2_ref, b_ref, dh_ref, dr_ref, g_ref, dy_ref, *refs
):
    outs, (proj, down) = refs[:-2], refs[-2:]
    a = a_ref[...]
    proj[:, :D] = contract(a, dq_ref[...])
    proj[:, D : 3 * D] = contract(rn_ref[...].astype(f32), dkv_ref[...], precise)
    proj[:, 3 * D : 4 * D] = contract(o_ref[...], dy2_ref[...])
    proj[:, 4 * D :] = contract(b_ref[...], dh_ref[...])
    dr = dr_ref[...]
    for k, cell in enumerate(cells_of(a)):
        down[k * D : (k + 1) * D, :D] = contract(cell, dr)
    down[:, D:] = contract(g_ref[...], dy_ref[...])
    rows = D // n_dp
    sub = rows // subs
    wide = (4 * D + FF) // cols
    down_rows = FF // n_dp
    for c in range(cols):
        for d in range(n_dp):
            for n, out in enumerate(outs):
                for j in range(subs) if len(outs) == 1 else (None,):
                    if j is None:
                        k = core_ref[0] if n == 0 else 1 - core_ref[0]
                        at = (c ^ core_ref[1], lax.rem(d + n_dp - core_ref[2], n_dp))
                    else:
                        k = j
                        at = (c, j, d)
                    start = d * rows + k * sub
                    low = d * down_rows + (c * subs + k) * (down_rows // (cols * subs))
                    if j is None:
                        start = pl.multiple_of(start, 8)
                        low = pl.multiple_of(low, 8)
                    out[(*at, slice(0, sub))] = proj[pl.ds(start, sub), c * wide : (c + 1) * wide]
                    out[(*at, slice(sub, 2 * sub))] = down[pl.ds(low, sub), :]


def moments(w, g, m, v):
    m2 = beta_one * m + (1.0 - beta_one) * g
    v2 = beta_two * v + (1.0 - beta_two) * g * g
    u = (
        m2 / (1.0 - beta_one**STEP) / (jnp.sqrt(v2 / (1.0 - beta_two**STEP)) + lamb_eps)
        + decay_rate * w
    )
    return m2, v2, u


def update_body(
    cols, subs, late, factor_ref, early_ref, late_ref, wp, mp, vp, wd, md, vd, mp2, vp2, up, md2, vd2, ud, sums
):
    factor = factor_ref[0]
    layer = pl.program_id(0)
    sub = wp.shape[1] // subs
    wide = wp.shape[2] // cols

    def go(g_ref):
        squares = [0.0, 0.0]

        def put(n, at, refs, outs, g):
            new = moments(refs[0][at], g * factor, refs[1][at], refs[2][at])
            for out, value in zip(outs, new):
                out[at] = value
            squares[n] = squares[n] + jnp.sum(new[2] * new[2], 0, keepdims=True)

        for c in range(cols):
            for k in range(subs):
                g = g_ref[c * subs + k].astype(f32).reshape(2 * sub, wide)
                at = (0, slice(k * sub, (k + 1) * sub), slice(c * wide, (c + 1) * wide))
                put(0, at, (wp, mp, vp), (mp2, vp2, up), g[:sub])
                rows = slice((c * subs + k) * sub, (c * subs + k + 1) * sub)
                for half in range(2):
                    at = (0, half, rows, slice(0, D))
                    put(1, at, (wd, md, vd), (md2, vd2, ud), g[sub:, half * D : (half + 1) * D])
        for n in range(2):
            sums[0, n : n + 1, :] = jnp.broadcast_to(jnp.sum(squares[n], 1, keepdims=True), (1, LANES))

    pl.when(layer >= late)(lambda: go(early_ref))
    pl.when(layer < late)(lambda: go(late_ref))


def group_sums(arrs, layered=None):
    embed, proj, downs, taps, head, gains, biases = arrs
    if layered is None:
        layered = [jnp.sum(a.reshape(a.shape[0], -1), 1) for a in (proj, downs)]
    layered = [*layered, jnp.sum(taps.reshape(taps.shape[0], -1), 1)]
    slot = jnp.arange(4 + 3 * LAYERS)
    total = jnp.zeros((4 + 3 * LAYERS,), f32)
    for n, a in enumerate((embed, head, gains, biases)):
        total = jnp.where(slot == n, jnp.sum(a), total)
    for n, a in enumerate(layered):
        total = total + jnp.pad(a, (4 + LAYERS * n, LAYERS * (2 - n)))
    return total


def spread_ratio(ratio):
    return (
        ratio[0],
        ratio[4 : 4 + LAYERS].reshape(LAYERS, 1, 1),
        ratio[4 + LAYERS : 4 + 2 * LAYERS].reshape(LAYERS, 1, 1, 1),
        ratio[4 + 2 * LAYERS : 4 + 3 * LAYERS].reshape(LAYERS, 1, 1),
        ratio[1],
        ratio[2],
        ratio[3],
    )


def per_device(
    patches,
    valid,
    labels,
    partners,
    mix,
    embed_w,
    in_proj,
    down_proj,
    dw_kernel,
    head_w,
    norm_gain,
    norm_bias,
    m_embed,
    m_proj,
    m_down,
    m_taps,
    m_head,
    m_gain,
    m_bias,
    v_embed,
    v_proj,
    v_down,
    v_taps,
    v_head,
    v_gain,
    v_bias,
):
    masters = (embed_w, in_proj, down_proj, dw_kernel, head_w, norm_gain, norm_bias)
    firsts = (m_embed, m_proj, m_down, m_taps, m_head, m_gain, m_bias)
    seconds = (v_embed, v_proj, v_down, v_taps, v_head, v_gain, v_bias)
    n_seq = lax.axis_size("seq")
    n_dp = lax.axis_size("dp")
    seq_pos = lax.axis_index("seq")
    img_dev, rows = (patches.shape[0], patches.shape[1])
    images = img_dev * n_dp

    team = n_seq
    while team * img_dev > n_seq:
        team //= 2
    blocks = n_seq // team
    rows_own = rows * blocks
    tok = rows_own * W
    keys_own = tok // 4
    image = jnp.minimum(seq_pos // team, img_dev - 1)
    busy = seq_pos // team < img_dev
    place = seq_pos % team

    def between(shift, wrap):
        pairs = []
        for base in range(0, n_seq, team):
            for h in range(team):
                if wrap or 0 <= h + shift < team:
                    pairs.append((base + (h + shift) % team, base + h))
        return pairs

    ends = jnp.stack([place > 0, place < team - 1]).astype(jnp.int32)

    def edges(v, edge):
        if team == 2:
            other = lax.ppermute(edge, "seq", between(1, True))
            return other, other
        low = lax.ppermute(v[-W:], "seq", between(-1, False))
        high = lax.ppermute(v[:W], "seq", between(1, False))
        return low, high

    def all_keys(v):
        return jnp.concatenate(
            [v] + [lax.ppermute(v, "seq", between(j, True)) for j in range(1, team)], 0
        )

    def own_keys(v):
        total = v[:keys_own]
        for j in range(1, team):
            part = v[j * keys_own : (j + 1) * keys_own]
            total = total + lax.ppermute(part, "seq", between(-j, True))
        return total

    back_block = seq_pos % blocks
    routes = [
        [
            (blocks * h + (i + r) % blocks, team * i + h)
            for i in range(img_dev)
            for h in range(team)
        ]
        for r in range(blocks)
    ]

    def to_team(v):
        got = []
        for r, pairs in enumerate(routes):
            send = lax.dynamic_index_in_dim(
                v, jnp.minimum((back_block - r) % blocks, img_dev - 1), 0, keepdims=False
            )
            got.append(lax.ppermute(send, "seq", pairs))
        twice = jnp.stack(got + got)
        own = lax.dynamic_slice_in_dim(twice, (blocks - image) % blocks, blocks, 0)
        return own.reshape(tok, -1)

    cols = 4
    subs = n_seq // cols
    row_in = D // n_dp
    sub_in = row_in // subs
    wide = in_proj.shape[2] // cols
    down_rows = down_proj.shape[2] // n_seq
    core = seq_pos % subs

    def part_of(flat):
        size = -(-flat.shape[0] // (wide * n_seq)) * wide * n_seq
        flat = jnp.pad(flat, (0, size - flat.shape[0])).reshape(n_seq, -1, wide)
        return lax.dynamic_index_in_dim(flat, seq_pos, 0, keepdims=False)

    def layer_part(l):
        block = lax.dynamic_slice(
            in_proj[l], (core * sub_in, (seq_pos // subs) * wide), (sub_in, wide)
        )
        lower = lax.dynamic_slice_in_dim(down_proj[l], seq_pos * down_rows, down_rows, 1)
        return [to_bf(block), to_bf(jnp.concatenate([lower[0], lower[1]], 1))]

    def gathered(parts):
        sizes = [p.shape[0] for p in parts]
        got = lax.all_gather(jnp.concatenate(parts, 0), ("dp", "seq"), axis=0, tiled=False)
        return got, sizes

    def cut(got, sizes):
        got = got.reshape(n_dp, n_seq, sum(sizes), wide)
        starts = [sum(sizes[:i]) for i in range(len(sizes))]
        return [got[:, :, a : a + n] for a, n in zip(starts, sizes)]

    def proj_of(got):
        got = got.reshape(n_dp, cols, subs, sub_in, wide).transpose(0, 2, 3, 1, 4)
        return got.reshape(D, cols * wide)

    dp_pos = lax.axis_index("dp")

    def over_dp(v):
        got = [v] + [
            lax.ppermute(v, "dp", [((d + j) % n_dp, d) for d in range(n_dp)])
            for j in range(1, n_dp)
        ]
        return lax.dynamic_slice_in_dim(jnp.stack(got + got), (n_dp - dp_pos) % n_dp, n_dp, 0)

    embed16 = over_dp(to_bf(embed_w)).reshape(-1, D)
    taps16 = over_dp(to_bf(dw_kernel).reshape(LAYERS * 9, -1))
    norms16 = over_dp(to_bf(jnp.stack([norm_gain, norm_bias])))
    taps32 = taps16.transpose(1, 0, 2).reshape(LAYERS, 9, FF).astype(f32)
    norms32 = norms16.transpose(1, 2, 0, 3).reshape(2, -1, D).astype(f32)
    gain32, bias32 = norms32[0], norms32[1]
    groups = [[0, 1, 2, 3], [4, 5]]
    extra = [[], [part_of(to_bf(head_w).reshape(-1))]]

    def layers_of(got, count):
        return [(proj_of(got[2 * i]), got[2 * i + 1].reshape(FF, 2 * D)) for i in range(count)]

    raw = [
        gathered(more + [p for l in members for p in layer_part(l)])
        for members, more in zip(groups, extra)
    ]
    first_late = groups[1][0]

    def own(v):
        return lax.dynamic_index_in_dim(v, image, 0, keepdims=False)

    wanted = own(partners)
    partner_label = jnp.zeros((), jnp.int32)
    for j in range(n_dp):
        other = labels
        if j:
            other = lax.ppermute(labels, "dp", [((d + j) % n_dp, d) for d in range(n_dp)])
        index = ((dp_pos + j) % n_dp) * img_dev + jnp.arange(img_dev)
        partner_label = partner_label + jnp.sum(jnp.where(index == wanted, other, 0))
    valid_own = own(valid)
    tid = lax.broadcasted_iota(jnp.int32, (tok, 1), 0)
    within = tid % W
    row_id = place * rows_own + tid // W
    col_id = 2 * (within % HALF) + within // HALF
    okay = ((row_id < valid_own[0]) & (col_id < valid_own[1]) & busy).astype(f32)
    kid = lax.broadcasted_iota(jnp.int32, (team * keys_own, 1), 0)
    segment = (place + kid // keys_own) % team
    key_row = segment * (rows_own // 2) + (kid % keys_own) // HALF
    key_ok = (2 * key_row < valid_own[0]) & (2 * (kid % HALF) < valid_own[1])
    shut = jnp.where(key_ok, 0.0, big_neg).astype(f32)
    count = (valid_own[0] * valid_own[1]).astype(f32).reshape(1, 1)
    classes = lax.broadcasted_iota(jnp.int32, (1, CLS), 1)
    mix_own = own(mix)
    target = mix_own * (classes == own(labels)).astype(f32) + (1.0 - mix_own) * (
        classes == partner_label
    ).astype(f32)

    def weights(l, layer):
        base = 1 + 3 * l
        return dict(
            wq=layer[0][:, :D],
            wkv=layer[0][:, D : 3 * D],
            wo=layer[0][:, 3 * D : 4 * D],
            w1=layer[0][:, 4 * D :],
            wsr=layer[1][:, :D],
            w2=layer[1][:, D:],
            taps=taps32[l],
            gain=gain32[base : base + 3],
            bias=bias32[base : base + 3],
        )

    wts = [weights(l, layer) for l, layer in zip(groups[0], layers_of(cut(*raw[0]), len(groups[0])))]
    ln_first = jnp.stack([gain32[0], bias32[0]])
    ln_last = jnp.stack([gain32[-1], bias32[-1]])

    full = ((tok, D), f32)
    half = ((tok, D), bf16)
    wide16 = ((tok, FF), bf16)
    input_outs = [half, half, ((keys_own, D), f32), ((keys_own, D), bf16), ((keys_own, 2 * D), bf16)]
    ln_out = ((2, D), f32)
    row16 = ((W, FF), bf16)

    spread = patches.reshape(img_dev, rows, HALF, 2, -1).transpose(0, 1, 3, 2, 4)
    patch_own = to_team(spread.reshape(img_dev, rows * W, -1))
    e, x = run(2, embed_body, [full, full], patch_own, embed16, ln_first)
    w = wts[0]
    a16, q16, r, rn16, kv16 = run(
        2, first_body, input_outs, x, w["gain"], w["bias"], w["wq"], w["wsr"], w["wkv"]
    )
    kept = []
    for l in range(LAYERS):
        w = wts[l]
        kv_all = all_keys(kv16)
        o16, lse, x2, b16, h16, edge = run(
            4,
            middle_body,
            [half, ((HEADS, tok), f32), full, half, wide16, row16],
            q16,
            kv_all,
            shut,
            x,
            w["gain"],
            w["bias"],
            w["wo"],
            w["w1"],
            place=ends,
        )
        hlow, hhigh = edges(h16, edge)
        keep = dict(
            x=x, a16=a16, q16=q16, r=r, rn16=rn16, kv=kv_all, o16=o16, lse=lse, x2=x2, b16=b16,
            h16=h16, hlow=hlow, hhigh=hhigh,
        )
        shared = (h16, hlow, hhigh, w["taps"], x2, w["w2"])
        if l + 1 == first_late:
            got, _ = lax.optimization_barrier((raw[1][0], kv_all))
            got = cut(got, raw[1][1])
            head16 = got[0].reshape(n_dp, -1)[:, : head_w.size].reshape(D, CLS)
            wts += [weights(m, layer) for m, layer in zip(groups[1], layers_of(got[1:], len(groups[1])))]
        if l + 1 < LAYERS:
            n = wts[l + 1]
            keep["g16"], keep["slope"], x, a16, q16, r, rn16, kv16 = run(
                8,
                join_body,
                [wide16, ((tok, FF), f32), full] + input_outs,
                *shared,
                n["gain"],
                n["bias"],
                n["wq"],
                n["wsr"],
                n["wkv"],
                place=ends,
            )
        else:
            keep["g16"], keep["slope"], x, pool = run(
                7,
                last_body,
                [wide16, ((tok, FF), f32), full, ((1, D), f32)],
                *shared,
                ln_last,
                okay,
                place=ends,
            )
        kept.append(keep)

    whole = pool
    for j in range(1, team):
        whole = whole + lax.ppermute(pool, "seq", between(j, True))
    loss_own, pooled16, dlog16, dln_last, dx, dy16, dz16, edge = run(
        4,
        functools.partial(head_body, images),
        [((1, 1), f32), ((1, D), bf16), ((1, CLS), bf16), ln_out, full, half, wide16, row16],
        whole,
        count,
        head16,
        target,
        x,
        ln_last,
        okay,
        wts[-1]["w2"],
        kept[-1]["slope"],
        place=ends,
    )
    chosen = ((place == 0) & busy).astype(f32)
    d_head = pooled16.astype(f32).reshape(D, 1) * dlog16.astype(f32) * chosen
    loss_local = loss_own[0, 0] * busy.astype(f32)
    teams = n_seq // team
    loss_parts = jnp.zeros((teams,), f32)
    for j in range(teams):
        other = loss_local
        if j:
            other = lax.ppermute(
                loss_local, "seq", [((d + j * team) % n_seq, d) for d in range(n_seq)]
            )
        loss_parts = jnp.where(jnp.arange(teams) == (seq_pos // team + j) % teams, other, loss_parts)
    loss_seq = jnp.sum(loss_parts)

    piece = ((cols, n_dp, 2 * sub_in, wide), f32)
    paired = subs == 2 and cols == 4
    chip = seq_pos // subs
    where = jnp.stack([core, chip, dp_pos]).astype(jnp.int32)

    def weight_grads(*args):
        vm = pl.BlockSpec(memory_space=pltpu.VMEM)
        outs = [piece] * 2 if paired else [((cols, subs) + piece[0][1:], f32)]
        return pl.pallas_call(
            functools.partial(weight_grads_body, n_dp, cols, subs),
            out_shape=[jax.ShapeDtypeStruct(s, d) for s, d in outs],
            in_specs=[pl.BlockSpec(memory_space=pltpu.SMEM)] + [vm] * len(args),
            out_specs=[vm] * len(outs),
            scratch_shapes=[pltpu.VMEM((D, cols * wide), f32), pltpu.VMEM((FF, 2 * D), f32)],
            compiler_params=pltpu.CompilerParams(vmem_limit_bytes=48 << 20),
            cost_estimate=cost(6),
        )(where, *args)

    def padded_rest(parts):
        flat = jnp.concatenate(parts, 1)
        size = -(-flat.shape[1] // (16 * wide * n_seq)) * 16 * wide * n_seq
        flat = jnp.pad(flat, ((0, 0), (0, size - flat.shape[1])))
        flat = flat.reshape(n_dp, cols, subs, -1, wide).transpose(1, 2, 0, 3, 4)
        if not paired:
            return [flat]
        flat = jnp.stack([lax.dynamic_index_in_dim(flat, chip ^ j, 0, False) for j in range(cols)])
        twice = jnp.concatenate([flat, flat], 2)
        flat = lax.dynamic_slice_in_dim(twice, dp_pos, n_dp, 2)
        return [lax.dynamic_index_in_dim(flat, k, 1, False) for k in (core, 1 - core)]

    def pair_sum(parts):
        mine, send = parts
        return mine + lax.ppermute(send, "seq", [(d ^ 1, d) for d in range(n_seq)])

    def over_chips(v, bit):
        return lax.ppermute(v, "seq", [(d ^ (bit * subs), d) for d in range(n_seq)])

    def plane_first(y):
        cut = y.shape[2] // 2
        one, two = y[:, :, :cut], y[:, :, cut:]
        moved = (to_bf(jnp.stack([one[1], one[3]])), to_bf(jnp.stack([two[2], two[3]])))
        got = (over_chips(moved[0], 1).astype(f32), over_chips(moved[1], 2).astype(f32))
        return [one[0] + got[0][0], one[2] + got[0][1], two[0] + got[1][0], two[1] + got[1][1]]

    def plane_second(parts):
        one = parts[0] + over_chips(to_bf(parts[1]), 2).astype(f32)
        two = parts[2] + over_chips(to_bf(parts[3]), 1).astype(f32)
        return jnp.concatenate([one, two], 1)

    def dp_sum(y):
        total = y[0]
        for j in range(1, n_dp):
            pairs = [(d, (d + j) % n_dp) for d in range(n_dp)]
            total = total + lax.ppermute(y[j], "dp", pairs)
        return total

    def whole_sum(parts):
        y = jnp.concatenate([p[0] for p in parts], -2)
        y = lax.psum_scatter(y.reshape(-1, wide), "seq", scatter_dimension=0, tiled=True)
        return lax.psum_scatter(y, "dp", scatter_dimension=0, tiled=True)

    def tied(value, others):
        return lax.optimization_barrier((value, others))

    stages = [pair_sum, plane_first, plane_second, dp_sum]
    pieces = []

    def advance(now, which):
        if not paired:
            return now
        ready = [p for p in pieces if p[0] in which]
        now, values = tied(now, [p[1] for p in ready])
        for p, v in zip(ready, values):
            p[1] = stages[p[0]](v) if p[0] < len(stages) else v
            p[0] += 1
        return now

    grads = [None] * LAYERS
    pieces.append([0, padded_rest([d_head.reshape(n_dp, -1)])])
    waiting = None
    for l in reversed(range(LAYERS)):
        w, k = wts[l], kept[l]
        zlow, zhigh = edges(dz16, edge)
        if waiting is not None:
            pieces.append([0, weight_grads(*waiting)])
        upper = dy16
        dz16 = advance(dz16, (0, 2, 3))
        dh16, d_taps, dln2, dx2, dy2, dq16, dkv = run(
            11,
            block_back_body,
            [wide16, ((9, FF), f32), ln_out, full, half, half, ((team * keys_own, 2 * D), f32)],
            k["h16"], k["hlow"], k["hhigh"], dz16, zlow, zhigh, w["taps"], w["w1"], k["x2"], w["gain"], dx,
            w["wo"], k["q16"], k["kv"], shut, k["lse"],
            place=ends,
        )
        dkv_own = own_keys(dkv)
        dkv_own = advance(dkv_own, (1, 4))
        shared = (dkv_own, w["wkv"], k["r"], w["gain"], dq16, w["wq"], w["wsr"], k["x"], dx2)
        if l:
            dr16, dln, dx, dy16, dz16, edge = run(
                6,
                join_back_body,
                [((keys_own, D), bf16), ((4, D), f32), full, half, wide16, row16],
                *shared,
                wts[l - 1]["w2"],
                kept[l - 1]["slope"],
                place=ends,
            )
        else:
            dr16, dln, de16, dln_first = run(
                3,
                first_back_body,
                [((keys_own, D), bf16), ((4, D), f32), half, ln_out],
                *shared,
                e,
                ln_first,
            )
        waiting = (k["a16"], dq16, k["rn16"], dkv_own, k["o16"], dy2, k["b16"], dh16, dr16, k["g16"], upper)
        grads[l] = (
            d_taps,
            jnp.concatenate([dln[0:2], dln2[0:1]], 0),
            jnp.concatenate([dln[2:4], dln2[1:2]], 0),
        )
    pieces.append([0, weight_grads(*waiting)])
    de16 = advance(de16, (0, 2, 3))
    (d_embed,) = run(3, embed_back_body, [((embed16.shape[0], D), f32)], patch_own, de16)
    d_embed = advance(d_embed, (1, 3, 4))
    d_gain = jnp.concatenate([dln_first[0:1]] + [g[1] for g in grads] + [dln_last[0:1]], 0)
    d_bias = jnp.concatenate([dln_first[1:2]] + [g[2] for g in grads] + [dln_last[1:2]], 0)
    d_taps = jnp.stack([g[0] for g in grads])
    rest = [
        d_embed.reshape(n_dp, -1),
        d_taps.reshape(LAYERS * 9, n_dp, -1).transpose(1, 0, 2).reshape(n_dp, -1),
        d_gain.reshape(-1, n_dp, row_in).transpose(1, 0, 2).reshape(n_dp, -1),
        d_bias.reshape(-1, n_dp, row_in).transpose(1, 0, 2).reshape(n_dp, -1),
    ]
    cuts = [0]
    for part in rest:
        cuts.append(cuts[-1] + part.shape[1])
    rest = padded_rest(rest)

    late = 2

    def together(parts):
        return to_bf(jnp.concatenate(parts, 0))

    if paired:
        assert all(p[0] > len(stages) for p in pieces[: LAYERS + 1 - late])
        early = together([p[1] for p in pieces[1 : LAYERS + 1 - late] + pieces[:1]])
        rest, early = tied(rest, early)
    pieces.append([0, rest])
    if paired:
        while any(p[0] < len(stages) for p in pieces):
            for p in pieces:
                if p[0] < len(stages):
                    p[1] = stages[p[0]](p[1])
                    p[0] += 1
        sums = [p[1] for p in pieces]
    else:
        sums = [whole_sum([p[1]]) for p in pieces]
        early = together(sums[1 : LAYERS + 1 - late] + sums[:1])
    early_got = lax.all_gather(early, "seq", axis=0, tiled=False)
    late_part, early_got = tied(together(sums[LAYERS + 1 - late :]), early_got)
    late_got = lax.all_gather(late_part, "seq", axis=0, tiled=False)
    head_start = (LAYERS - late) * 2 * sub_in
    g_head = early_got[:, head_start:].reshape(-1)[: head_w.size].reshape(head_w.shape).astype(f32)
    flat = late_got[:, late * 2 * sub_in :].reshape(-1).astype(f32)
    flat = [flat[a:b] for a, b in zip(cuts, cuts[1:])]
    shards = (
        flat[0].reshape(embed_w.shape),
        None,
        None,
        flat[1].reshape(dw_kernel.shape),
        g_head,
        flat[2].reshape(norm_gain.shape),
        flat[3].reshape(norm_bias.shape),
    )

    gsq_local = sum(jnp.sum(jnp.square(g.astype(f32))) for g in (early_got, late_got))
    wsq_local = group_sums(tuple((w * w for w in masters)))
    gsq, wsq, loss = lax.psum((gsq_local, wsq_local, loss_seq), "dp")
    grad_norm = jnp.sqrt(gsq)
    factor = jnp.minimum(1.0, clip_limit / grad_norm)

    proj_spec = pl.BlockSpec((1,) + in_proj.shape[1:], lambda l: (l, 0, 0))
    down_spec = pl.BlockSpec((1,) + down_proj.shape[1:], lambda l: (l, 0, 0, 0))
    block = (n_seq, 2 * sub_in, wide)
    blocks_of = [early_got, late_got]
    if 2 * sub_in % 8:
        block = (n_seq, 1, 2 * sub_in, wide)
        counts = (LAYERS - late, late)
        blocks_of = [
            g[:, : n * 2 * sub_in].reshape(n_seq, n, 2 * sub_in, wide)
            for g, n in zip(blocks_of, counts)
        ]
    tail = (0,) * (len(block) - 2)
    got = pl.pallas_call(
        functools.partial(update_body, cols, subs, late),
        grid=(LAYERS,),
        out_shape=[jax.ShapeDtypeStruct(in_proj.shape, f32)] * 3
        + [jax.ShapeDtypeStruct(down_proj.shape, f32)] * 3
        + [jax.ShapeDtypeStruct((LAYERS, 2, LANES), f32)],
        in_specs=[
            pl.BlockSpec(memory_space=pltpu.SMEM),
            pl.BlockSpec(block, lambda l: (0, jnp.minimum(LAYERS - 1 - l, LAYERS - 1 - late), *tail)),
            pl.BlockSpec(block, lambda l: (0, jnp.maximum(late - 1 - l, 0), *tail)),
        ]
        + [proj_spec] * 3
        + [down_spec] * 3,
        out_specs=[proj_spec] * 3 + [down_spec] * 3 + [pl.BlockSpec((1, 2, LANES), lambda l: (l, 0, 0))],
        compiler_params=pltpu.CompilerParams(vmem_limit_bytes=56 << 20),
        cost_estimate=cost(25),
    )(factor.reshape(1), *blocks_of, in_proj, m_proj, v_proj, down_proj, m_down, v_down)
    big = {1: got[0:3], 2: got[3:6]}
    new_m, new_v, updates = ([], [], [])
    for n, (w, g, m, v) in enumerate(zip(masters, shards, firsts, seconds)):
        m2, v2, u = big[n] if n in big else moments(w, g * factor, m, v)
        new_m.append(m2)
        new_v.append(v2)
        updates.append(u)
    usq = lax.psum(
        group_sums(tuple((u * u for u in updates)), [got[6][:, 0, 0], got[6][:, 1, 0]]), "dp"
    )
    wnorm = jnp.sqrt(wsq)
    unorm = jnp.sqrt(usq)
    ratio = wnorm / unorm
    spreads = spread_ratio(ratio)
    new_w = [w - learn_rate * r * u for w, r, u in zip(masters, spreads, updates)]
    stats = jnp.stack([wnorm, unorm])
    return (loss, grad_norm, stats, ratio, *new_w, *new_m, *new_v)


def solution(mesh):
    placed = (
        P("dp", None),
        P(None, "dp", None),
        P(None, None, "dp", None),
        P(None, None, "dp"),
        P("dp", None),
        P(None, "dp"),
        P(None, "dp"),
    )
    in_specs = (
        P("dp", "seq", None, None),
        P("dp", None),
        P("dp"),
        P("dp"),
        P("dp"),
    ) + placed * 3
    out_specs = (P(), P(), P(), P()) + placed * 3
    return jax.shard_map(
        per_device, mesh=mesh, in_specs=in_specs, out_specs=out_specs, check_vma=False
    )
```

```python
import functools

import jax
import jax.numpy as jnp
from jax import lax
from jax.experimental import pallas as pl
from jax.experimental.pallas import tpu as pltpu
from jax.sharding import PartitionSpec as P

D = 320
HEADS = 5
HD = 64
FF = 1280
CLS = 1000
W = 64
HALF = W // 2
LAYERS = 6
STEP = 5
LANES = 128


norm_eps = 1e-06
scale_qk = 0.125
big_neg = -1e30
beta_one = 0.9
beta_two = 0.999
lamb_eps = 1e-06
decay_rate = 0.01
learn_rate = 0.3
clip_limit = 0.1
root_half = 0.7071067811865476
root_two_pi = 0.3989422804014327
precise = lax.Precision.HIGHEST

f32 = jnp.float32
bf16 = jnp.bfloat16


def to_bf(v):
    return v.astype(bf16)


def dot(a, b):
    return jnp.dot(a, b, preferred_element_type=f32)


def dot_nt(a, b, precision=None):
    return lax.dot_general(
        a, b, (((1,), (1,)), ((), ())), precision=precision, preferred_element_type=f32
    )


def contract(a, b, precision=None):
    return lax.dot_general(
        a, b, (((0,), (0,)), ((), ())), precision=precision, preferred_element_type=f32
    )


def norm_parts(v):
    center = v - jnp.mean(v, -1, keepdims=True)
    spread = jnp.mean(center * center, -1, keepdims=True)
    scale = lax.rsqrt(spread + norm_eps)
    return center * scale, scale


def layer_norm(v, gain, bias):
    return norm_parts(v)[0] * gain + bias


def norm_back(v, gain, grad):
    unit, scale = norm_parts(v)
    dgain = jnp.sum(grad * unit, 0, keepdims=True)
    dbias = jnp.sum(grad, 0, keepdims=True)
    t = grad * gain
    dv = scale * (
        t - jnp.mean(t, -1, keepdims=True) - unit * jnp.mean(t * unit, -1, keepdims=True)
    )
    return dv, dgain, dbias


def cost(us):
    return pl.CostEstimate(flops=int(us * 1e8), bytes_accessed=int(us * 1e5), transcendentals=0)


def run(us, body, outs, *args, place=None):
    vm = pl.BlockSpec(memory_space=pltpu.VMEM)
    scalars = [] if place is None else [place]
    return pl.pallas_call(
        body,
        out_shape=[jax.ShapeDtypeStruct(s, d) for s, d in outs],
        in_specs=[pl.BlockSpec(memory_space=pltpu.SMEM)] * len(scalars) + [vm] * len(args),
        out_specs=[vm] * len(outs),
        compiler_params=pltpu.CompilerParams(vmem_limit_bytes=48 << 20),
        cost_estimate=cost(us),
    )(*scalars, *args)


def cells_of(v):
    rows = v.shape[0] // W
    split = v.reshape(rows // 2, 2, 2, HALF, v.shape[1])
    return [split[:, k // 2, k % 2].reshape(-1, v.shape[1]) for k in range(4)]


def attention_inputs(x, gain, bias, wq, wsr, wkv, a_ref, q_ref, r_ref, rn_ref, kv_ref):
    a = to_bf(layer_norm(x, gain[0:1], bias[0:1]))
    a_ref[...] = a
    q_ref[...] = to_bf(dot(a, wq[...]))
    total = None
    for k, cell in enumerate(cells_of(a)):
        part = dot(cell, wsr[k * D : (k + 1) * D, :])
        total = part if total is None else total + part
    r_ref[...] = total
    rn = to_bf(layer_norm(total, gain[1:2], bias[1:2]))
    rn_ref[...] = rn
    kv_ref[...] = to_bf(dot(rn, wkv[...]))


def embed_body(p_ref, w_ref, ln_ref, e_ref, x_ref):
    e = dot(p_ref[...], w_ref[...])
    e_ref[...] = e
    x_ref[...] = layer_norm(e, ln_ref[0:1], ln_ref[1:2])


def embed_back_body(p_ref, de_ref, dw_ref):
    dw_ref[...] = contract(p_ref[...], de_ref[...])


def first_body(x_ref, gain, bias, wq, wsr, wkv, *outs):
    attention_inputs(x_ref[...], gain, bias, wq, wsr, wkv, *outs)


def middle_body(
    place, q_ref, kv_ref, ok_ref, x_ref, gain, bias, wo, w1, o_ref, lse_ref, x2_ref, b_ref, h_ref, edge_ref
):
    q = q_ref[...] * jnp.asarray(scale_qk, bf16)
    keys = kv_ref.shape[0]
    kv = kv_ref[...]
    shut = jnp.broadcast_to(ok_ref[...], (keys, q.shape[0]))
    q_t = q.T
    v_t = kv[:, D:].T
    parts = []
    for head in range(HEADS):
        low, high = head * HD, (head + 1) * HD
        s = dot(kv[:, low:high], q_t[low:high, :]) + shut
        top = jnp.max(s, 0, keepdims=True)
        expo = jnp.exp(s - top)
        total = jnp.sum(expo, 0, keepdims=True)
        lse_ref[head : head + 1, :] = top + jnp.log(total)
        p = to_bf(expo * (1.0 / total))
        parts.append(dot(v_t[low:high, :], p))
    o = to_bf(jnp.concatenate(parts, 0).T)
    o_ref[...] = o
    x2 = x_ref[...] + dot(o, wo[...])
    x2_ref[...] = x2
    b = to_bf(layer_norm(x2, gain[2:3], bias[2:3]))
    b_ref[...] = b
    h_ref[...] = to_bf(dot(b, w1[...]))
    send_edge(place, h_ref, edge_ref)


def shift_down(v):
    index = lax.broadcasted_iota(jnp.int32, v.shape, 0)
    return jnp.where(index == 0, 0.0, pltpu.roll(v, 1, 0))


def shift_up(v):
    index = lax.broadcasted_iota(jnp.int32, v.shape, 0)
    return jnp.where(index == v.shape[0] - 1, 0.0, pltpu.roll(v, v.shape[0] - 1, 0))


def from_left(v):
    return jnp.concatenate([shift_down(v[HALF:]), v[:HALF]], 0)


def from_right(v):
    return jnp.concatenate([v[HALF:], shift_up(v[:HALF])], 0)


def row_of(main, near, i, rows, lanes):
    place, low, high = near
    if i < 0:
        return jnp.where(place[0] > 0, low[:, lanes].astype(f32), 0.0)
    if i >= rows:
        return jnp.where(place[1] > 0, high[:, lanes].astype(f32), 0.0)
    return main[i * W : (i + 1) * W, lanes].astype(f32)


def send_edge(place, main, edge_ref):
    start = pl.multiple_of(jnp.where(place[0] > 0, 0, main.shape[0] - W), W)
    edge_ref[...] = main[pl.ds(start, W), :]


def conv_gelu(h_ref, ends, taps_ref, g_ref, slope_ref):
    rows = h_ref.shape[0] // W

    def chunk(c, carry):
        lanes = pl.ds(pl.multiple_of(c * LANES, LANES), LANES)
        taps = [taps_ref[k : k + 1, lanes] for k in range(9)]
        near = [row_of(h_ref, ends, i, rows, lanes) for i in (-1, 0)]
        for i in range(rows):
            near.append(row_of(h_ref, ends, i + 1, rows, lanes))
            sums = [
                taps[j] * near[0] + taps[3 + j] * near[1] + taps[6 + j] * near[2] for j in range(3)
            ]
            z = sums[1] + from_left(sums[0]) + from_right(sums[2])
            phi = 0.5 + 0.5 * lax.erf(z * root_half)
            here = slice(i * W, (i + 1) * W)
            g_ref[here, lanes] = to_bf(z * phi)
            slope_ref[here, lanes] = phi + z * (jnp.exp(-0.5 * z * z) * root_two_pi)
            near = near[1:]
        return carry

    lax.fori_loop(0, FF // LANES, chunk, 0)


def last_body(place, h_ref, low_ref, high_ref, taps_ref, x2_ref, w2, ln_ref, ok_ref, g_ref, slope_ref, x_ref, sum_ref):
    conv_gelu(h_ref, (place, low_ref, high_ref), taps_ref, g_ref, slope_ref)
    x = x2_ref[...] + dot(g_ref[...], w2[...])
    x_ref[...] = x
    fin = layer_norm(x, ln_ref[0:1], ln_ref[1:2])
    sum_ref[...] = jnp.sum(fin * ok_ref[...], 0, keepdims=True)


def join_body(
    place, h_ref, low_ref, high_ref, taps_ref, x2_ref, w2, gain, bias, wq, wsr, wkv, g_ref, slope_ref, x_ref, *outs
):
    conv_gelu(h_ref, (place, low_ref, high_ref), taps_ref, g_ref, slope_ref)
    x = x2_ref[...] + dot(g_ref[...], w2[...])
    x_ref[...] = x
    attention_inputs(x, gain, bias, wq, wsr, wkv, *outs)


def gelu_back(place, dx, w2, slope_ref, dy_ref, dz_ref, edge_ref):
    dy = to_bf(dx)
    dy_ref[...] = dy
    dg = to_bf(dot_nt(dy, w2[...])).astype(f32)
    dz_ref[...] = to_bf(dg * slope_ref[...])
    send_edge(place, dz_ref, edge_ref)


def head_body(
    images,
    place,
    pool_ref,
    count_ref,
    head_ref,
    target_ref,
    x_ref,
    ln_ref,
    ok_ref,
    w2,
    slope_ref,
    loss_ref,
    pooled_ref,
    dlog_ref,
    dln_ref,
    dx_ref,
    dy_ref,
    dz_ref,
    edge_ref,
):
    count = count_ref[...]
    pooled = to_bf(pool_ref[...] / count)
    pooled_ref[...] = pooled
    logits = dot(jnp.broadcast_to(pooled.astype(f32), (16, D)).astype(bf16), head_ref[...])[0:1]
    shifted = logits - jnp.max(logits, -1, keepdims=True)
    logp = shifted - jnp.log(jnp.sum(jnp.exp(shifted), -1, keepdims=True))
    target = target_ref[...]
    loss_ref[...] = jnp.sum(target * logp, -1, keepdims=True) * (-1.0 / images)
    dlog = to_bf((jnp.exp(logp) - target) * (1.0 / images))
    dlog_ref[...] = dlog
    wide = jnp.broadcast_to(dlog.astype(f32), (16, CLS)).astype(bf16)
    dpool = dot_nt(wide, head_ref[...])[0:1] / count
    dx, dgain, dbias = norm_back(x_ref[...], ln_ref[0:1], ok_ref[...] * dpool)
    dln_ref[0:1, :] = dgain
    dln_ref[1:2, :] = dbias
    dx_ref[...] = dx
    gelu_back(place, dx, w2, slope_ref, dy_ref, dz_ref, edge_ref)


def conv_back(h_ref, hends, dz_ref, zends, taps_ref, dh_ref, dtaps_ref):
    rows = h_ref.shape[0] // W

    def chunk(c, carry):
        lanes = pl.ds(pl.multiple_of(c * LANES, LANES), LANES)
        taps = [taps_ref[k : k + 1, lanes] for k in range(9)]
        acc = [jnp.zeros((8, LANES), f32) for _ in range(9)]

        def views(i):
            v = row_of(dz_ref, zends, i, rows, lanes)
            return [from_right(v), v, from_left(v)]

        near = [views(-1), views(0)]
        hear = [row_of(h_ref, hends, i, rows, lanes) for i in (-1, 0)]
        for i in range(rows):
            near.append(views(i + 1))
            hear.append(row_of(h_ref, hends, i + 1, rows, lanes))
            dh = None
            for di in range(3):
                for dj in range(3):
                    part = taps[3 * di + dj] * near[2 - di][dj]
                    dh = part if dh is None else dh + part
            dh_ref[i * W : (i + 1) * W, lanes] = to_bf(dh)
            for di in range(3):
                for dj in range(3):
                    prod = (hear[di] * near[1][dj]).reshape(W // 8, 8, LANES)
                    acc[3 * di + dj] = acc[3 * di + dj] + jnp.sum(prod, 0)
            near = near[1:]
            hear = hear[1:]
        for k in range(9):
            dtaps_ref[k : k + 1, lanes] = jnp.sum(acc[k], 0, keepdims=True)
        return carry

    lax.fori_loop(0, FF // LANES, chunk, 0)


def block_back_body(
    place,
    h_ref,
    hlow_ref,
    hhigh_ref,
    dz_ref,
    zlow_ref,
    zhigh_ref,
    taps_ref,
    w1,
    x2_ref,
    gain,
    dx_ref,
    wo,
    q_ref,
    kv_ref,
    ok_ref,
    lse_ref,
    dh_ref,
    dtaps_ref,
    dln_ref,
    dx2_ref,
    dy_ref,
    dq_ref,
    dkv_ref,
):
    conv_back(
        h_ref, (place, hlow_ref, hhigh_ref), dz_ref, (place, zlow_ref, zhigh_ref), taps_ref, dh_ref, dtaps_ref
    )
    db = dot_nt(dh_ref[...], w1[...])
    dln, dgain, dbias = norm_back(x2_ref[...], gain[2:3], db)
    dln_ref[0:1, :] = dgain
    dln_ref[1:2, :] = dbias
    dx2 = dx_ref[...] + dln
    dx2_ref[...] = dx2
    dy = to_bf(dx2)
    dy_ref[...] = dy
    do_t = to_bf(dot_nt(wo[...], dy))
    q = q_ref[...] * jnp.asarray(scale_qk, bf16)
    q_t = q.T
    keys = kv_ref.shape[0]
    kv = kv_ref[...]
    k_t = (kv[:, :D] * jnp.asarray(scale_qk, bf16)).T
    shut = jnp.broadcast_to(ok_ref[...], (keys, q.shape[0]))
    dq_parts, dk_parts, dv_parts = ([], [], [])
    for head in range(HEADS):
        low, high = head * HD, (head + 1) * HD
        s = dot(kv[:, low:high], q_t[low:high, :]) + shut
        p = jnp.exp(s - lse_ref[head : head + 1, :])
        dp = dot(kv[:, D + low : D + high], do_t[low:high, :])
        dv_parts.append(dot_nt(do_t[low:high, :], to_bf(p)))
        ds = to_bf(p * (dp - jnp.sum(p * dp, 0, keepdims=True)))
        dq_parts.append(dot(k_t[low:high, :], ds))
        dk_parts.append(dot_nt(q_t[low:high, :], ds))
    dq_ref[...] = to_bf(jnp.concatenate(dq_parts, 0).T)
    dkv_ref[...] = jnp.concatenate(dk_parts + dv_parts, 0).T


def inputs_back(dkv, wkv, r_ref, gain, dq_ref, wq, wsr, x_ref, dx2_ref, dr_ref, dln_ref):
    w_kv = wkv[...].astype(f32)
    drn = dot_nt(dkv, w_kv, precise)
    dr, dgain1, dbias1 = norm_back(r_ref[...], gain[1:2], drn)
    dr = to_bf(dr)
    dr_ref[...] = dr
    rows = x_ref.shape[0] // W
    cells = [
        dot_nt(dr, wsr[k * D : (k + 1) * D, :]).reshape(rows // 2, 1, 1, HALF, D) for k in range(4)
    ]
    placed = jnp.concatenate(
        [jnp.concatenate(cells[0:2], 2), jnp.concatenate(cells[2:4], 2)], 1
    ).reshape(rows * W, D)
    da = dot_nt(dq_ref[...], wq[...]) + placed
    dln, dgain0, dbias0 = norm_back(x_ref[...], gain[0:1], da)
    for k, row in enumerate((dgain0, dgain1, dbias0, dbias1)):
        dln_ref[k : k + 1, :] = row
    return dx2_ref[...] + dln


def join_back_body(
    place, dkv_ref, wkv, r_ref, gain, dq_ref, wq, wsr, x_ref, dx2_ref, w2, slope_ref,
    dr_ref, dln_ref, dx_ref, dy_ref, dz_ref, edge_ref
):
    dx = inputs_back(dkv_ref[...], wkv, r_ref, gain, dq_ref, wq, wsr, x_ref, dx2_ref, dr_ref, dln_ref)
    dx_ref[...] = dx
    gelu_back(place, dx, w2, slope_ref, dy_ref, dz_ref, edge_ref)


def first_back_body(
    dkv_ref, wkv, r_ref, gain, dq_ref, wq, wsr, x_ref, dx2_ref, e_ref, ln_ref, dr_ref, dln_ref, de_ref, dle_ref
):
    dx = inputs_back(dkv_ref[...], wkv, r_ref, gain, dq_ref, wq, wsr, x_ref, dx2_ref, dr_ref, dln_ref)
    de, dgain, dbias = norm_back(e_ref[...], ln_ref[0:1], dx)
    de_ref[...] = to_bf(de)
    dle_ref[0:1, :] = dgain
    dle_ref[1:2, :] = dbias


def weight_grads_body(
    n_dp, cols, subs, core_ref, a_ref, dq_ref, rn_ref, dkv_ref, o_ref, dy2_ref, b_ref, dh_ref, dr_ref, g_ref, dy_ref, *refs
):
    outs, (proj, down) = refs[:-2], refs[-2:]
    a = a_ref[...]
    proj[:, :D] = contract(a, dq_ref[...])
    proj[:, D : 3 * D] = contract(rn_ref[...].astype(f32), dkv_ref[...], precise)
    proj[:, 3 * D : 4 * D] = contract(o_ref[...], dy2_ref[...])
    proj[:, 4 * D :] = contract(b_ref[...], dh_ref[...])
    dr = dr_ref[...]
    for k, cell in enumerate(cells_of(a)):
        down[k * D : (k + 1) * D, :D] = contract(cell, dr)
    down[:, D:] = contract(g_ref[...], dy_ref[...])
    rows = D // n_dp
    sub = rows // subs
    wide = (4 * D + FF) // cols
    down_rows = FF // n_dp
    for c in range(cols):
        for d in range(n_dp):
            for n, out in enumerate(outs):
                for j in range(subs) if len(outs) == 1 else (None,):
                    if j is None:
                        k = core_ref[0] if n == 0 else 1 - core_ref[0]
                        at = (c ^ core_ref[1], lax.rem(d + n_dp - core_ref[2], n_dp))
                    else:
                        k = j
                        at = (c, j, d)
                    start = d * rows + k * sub
                    low = d * down_rows + (c * subs + k) * (down_rows // (cols * subs))
                    if j is None:
                        start = pl.multiple_of(start, 8)
                        low = pl.multiple_of(low, 8)
                    out[(*at, slice(0, sub))] = proj[pl.ds(start, sub), c * wide : (c + 1) * wide]
                    out[(*at, slice(sub, 2 * sub))] = down[pl.ds(low, sub), :]


def moments(w, g, m, v):
    m2 = beta_one * m + (1.0 - beta_one) * g
    v2 = beta_two * v + (1.0 - beta_two) * g * g
    u = (
        m2 / (1.0 - beta_one**STEP) / (jnp.sqrt(v2 / (1.0 - beta_two**STEP)) + lamb_eps)
        + decay_rate * w
    )
    return m2, v2, u


def update_body(
    cols, subs, late, factor_ref, early_ref, late_ref, wp, mp, vp, wd, md, vd, mp2, vp2, up, md2, vd2, ud, sums
):
    factor = factor_ref[0]
    layer = pl.program_id(0)
    sub = wp.shape[1] // subs
    wide = wp.shape[2] // cols

    def go(g_ref):
        squares = [0.0, 0.0]

        def put(n, at, refs, outs, g):
            new = moments(refs[0][at], g * factor, refs[1][at], refs[2][at])
            for out, value in zip(outs, new):
                out[at] = value
            squares[n] = squares[n] + jnp.sum(new[2] * new[2], 0, keepdims=True)

        for c in range(cols):
            for k in range(subs):
                g = g_ref[c * subs + k].astype(f32).reshape(2 * sub, wide)
                at = (0, slice(k * sub, (k + 1) * sub), slice(c * wide, (c + 1) * wide))
                put(0, at, (wp, mp, vp), (mp2, vp2, up), g[:sub])
                rows = slice((c * subs + k) * sub, (c * subs + k + 1) * sub)
                for half in range(2):
                    at = (0, half, rows, slice(0, D))
                    put(1, at, (wd, md, vd), (md2, vd2, ud), g[sub:, half * D : (half + 1) * D])
        for n in range(2):
            sums[0, n : n + 1, :] = jnp.broadcast_to(jnp.sum(squares[n], 1, keepdims=True), (1, LANES))

    pl.when(layer >= late)(lambda: go(early_ref))
    pl.when(layer < late)(lambda: go(late_ref))


def group_sums(arrs, layered=None):
    embed, proj, downs, taps, head, gains, biases = arrs
    if layered is None:
        layered = [jnp.sum(a.reshape(a.shape[0], -1), 1) for a in (proj, downs)]
    layered = [*layered, jnp.sum(taps.reshape(taps.shape[0], -1), 1)]
    slot = jnp.arange(4 + 3 * LAYERS)
    total = jnp.zeros((4 + 3 * LAYERS,), f32)
    for n, a in enumerate((embed, head, gains, biases)):
        total = jnp.where(slot == n, jnp.sum(a), total)
    for n, a in enumerate(layered):
        total = total + jnp.pad(a, (4 + LAYERS * n, LAYERS * (2 - n)))
    return total


def spread_ratio(ratio):
    return (
        ratio[0],
        ratio[4 : 4 + LAYERS].reshape(LAYERS, 1, 1),
        ratio[4 + LAYERS : 4 + 2 * LAYERS].reshape(LAYERS, 1, 1, 1),
        ratio[4 + 2 * LAYERS : 4 + 3 * LAYERS].reshape(LAYERS, 1, 1),
        ratio[1],
        ratio[2],
        ratio[3],
    )


def per_device(
    patches,
    valid,
    labels,
    partners,
    mix,
    embed_w,
    in_proj,
    down_proj,
    dw_kernel,
    head_w,
    norm_gain,
    norm_bias,
    m_embed,
    m_proj,
    m_down,
    m_taps,
    m_head,
    m_gain,
    m_bias,
    v_embed,
    v_proj,
    v_down,
    v_taps,
    v_head,
    v_gain,
    v_bias,
):
    masters = (embed_w, in_proj, down_proj, dw_kernel, head_w, norm_gain, norm_bias)
    firsts = (m_embed, m_proj, m_down, m_taps, m_head, m_gain, m_bias)
    seconds = (v_embed, v_proj, v_down, v_taps, v_head, v_gain, v_bias)
    n_seq = lax.axis_size("seq")
    n_dp = lax.axis_size("dp")
    seq_pos = lax.axis_index("seq")
    img_dev, rows = (patches.shape[0], patches.shape[1])
    images = img_dev * n_dp

    team = n_seq
    while team * img_dev > n_seq:
        team //= 2
    blocks = n_seq // team
    rows_own = rows * blocks
    tok = rows_own * W
    keys_own = tok // 4
    image = jnp.minimum(seq_pos // team, img_dev - 1)
    busy = seq_pos // team < img_dev
    place = seq_pos % team

    def between(shift, wrap):
        pairs = []
        for base in range(0, n_seq, team):
            for h in range(team):
                if wrap or 0 <= h + shift < team:
                    pairs.append((base + (h + shift) % team, base + h))
        return pairs

    ends = jnp.stack([place > 0, place < team - 1]).astype(jnp.int32)

    def edges(v, edge):
        if team == 2:
            other = lax.ppermute(edge, "seq", between(1, True))
            return other, other
        low = lax.ppermute(v[-W:], "seq", between(-1, False))
        high = lax.ppermute(v[:W], "seq", between(1, False))
        return low, high

    def all_keys(v):
        return jnp.concatenate(
            [v] + [lax.ppermute(v, "seq", between(j, True)) for j in range(1, team)], 0
        )

    def own_keys(v):
        total = v[:keys_own]
        for j in range(1, team):
            part = v[j * keys_own : (j + 1) * keys_own]
            total = total + lax.ppermute(part, "seq", between(-j, True))
        return total

    back_block = seq_pos % blocks
    routes = [
        [
            (blocks * h + (i + r) % blocks, team * i + h)
            for i in range(img_dev)
            for h in range(team)
        ]
        for r in range(blocks)
    ]

    def to_team(v):
        got = []
        for r, pairs in enumerate(routes):
            send = lax.dynamic_index_in_dim(
                v, jnp.minimum((back_block - r) % blocks, img_dev - 1), 0, keepdims=False
            )
            got.append(lax.ppermute(send, "seq", pairs))
        twice = jnp.stack(got + got)
        own = lax.dynamic_slice_in_dim(twice, (blocks - image) % blocks, blocks, 0)
        return own.reshape(tok, -1)

    cols = 4
    subs = n_seq // cols
    row_in = D // n_dp
    sub_in = row_in // subs
    wide = in_proj.shape[2] // cols
    down_rows = down_proj.shape[2] // n_seq
    core = seq_pos % subs

    def part_of(flat):
        size = -(-flat.shape[0] // (wide * n_seq)) * wide * n_seq
        flat = jnp.pad(flat, (0, size - flat.shape[0])).reshape(n_seq, -1, wide)
        return lax.dynamic_index_in_dim(flat, seq_pos, 0, keepdims=False)

    def layer_part(l):
        block = lax.dynamic_slice(
            in_proj[l], (core * sub_in, (seq_pos // subs) * wide), (sub_in, wide)
        )
        lower = lax.dynamic_slice_in_dim(down_proj[l], seq_pos * down_rows, down_rows, 1)
        return [to_bf(block), to_bf(jnp.concatenate([lower[0], lower[1]], 1))]

    def gathered(parts):
        sizes = [p.shape[0] for p in parts]
        got = lax.all_gather(jnp.concatenate(parts, 0), ("dp", "seq"), axis=0, tiled=False)
        return got, sizes

    def cut(got, sizes):
        got = got.reshape(n_dp, n_seq, sum(sizes), wide)
        starts = [sum(sizes[:i]) for i in range(len(sizes))]
        return [got[:, :, a : a + n] for a, n in zip(starts, sizes)]

    def proj_of(got):
        got = got.reshape(n_dp, cols, subs, sub_in, wide).transpose(0, 2, 3, 1, 4)
        return got.reshape(D, cols * wide)

    dp_pos = lax.axis_index("dp")

    def over_dp(v):
        got = [v] + [
            lax.ppermute(v, "dp", [((d + j) % n_dp, d) for d in range(n_dp)])
            for j in range(1, n_dp)
        ]
        return lax.dynamic_slice_in_dim(jnp.stack(got + got), (n_dp - dp_pos) % n_dp, n_dp, 0)

    embed16 = over_dp(to_bf(embed_w)).reshape(-1, D)
    taps16 = over_dp(to_bf(dw_kernel).reshape(LAYERS * 9, -1))
    norms16 = over_dp(to_bf(jnp.stack([norm_gain, norm_bias])))
    taps32 = taps16.transpose(1, 0, 2).reshape(LAYERS, 9, FF).astype(f32)
    norms32 = norms16.transpose(1, 2, 0, 3).reshape(2, -1, D).astype(f32)
    gain32, bias32 = norms32[0], norms32[1]
    groups = [[0, 1, 2], [3, 4, 5]]
    extra = [[], [part_of(to_bf(head_w).reshape(-1))]]

    def layers_of(got, count):
        return [(proj_of(got[2 * i]), got[2 * i + 1].reshape(FF, 2 * D)) for i in range(count)]

    raw = [
        gathered(more + [p for l in members for p in layer_part(l)])
        for members, more in zip(groups, extra)
    ]
    first_late = groups[1][0]

    def own(v):
        return lax.dynamic_index_in_dim(v, image, 0, keepdims=False)

    wanted = own(partners)
    partner_label = jnp.zeros((), jnp.int32)
    for j in range(n_dp):
        other = labels
        if j:
            other = lax.ppermute(labels, "dp", [((d + j) % n_dp, d) for d in range(n_dp)])
        index = ((dp_pos + j) % n_dp) * img_dev + jnp.arange(img_dev)
        partner_label = partner_label + jnp.sum(jnp.where(index == wanted, other, 0))
    valid_own = own(valid)
    tid = lax.broadcasted_iota(jnp.int32, (tok, 1), 0)
    within = tid % W
    row_id = place * rows_own + tid // W
    col_id = 2 * (within % HALF) + within // HALF
    okay = ((row_id < valid_own[0]) & (col_id < valid_own[1]) & busy).astype(f32)
    kid = lax.broadcasted_iota(jnp.int32, (team * keys_own, 1), 0)
    segment = (place + kid // keys_own) % team
    key_row = segment * (rows_own // 2) + (kid % keys_own) // HALF
    key_ok = (2 * key_row < valid_own[0]) & (2 * (kid % HALF) < valid_own[1])
    shut = jnp.where(key_ok, 0.0, big_neg).astype(f32)
    count = (valid_own[0] * valid_own[1]).astype(f32).reshape(1, 1)
    classes = lax.broadcasted_iota(jnp.int32, (1, CLS), 1)
    mix_own = own(mix)
    target = mix_own * (classes == own(labels)).astype(f32) + (1.0 - mix_own) * (
        classes == partner_label
    ).astype(f32)

    def weights(l, layer):
        base = 1 + 3 * l
        return dict(
            wq=layer[0][:, :D],
            wkv=layer[0][:, D : 3 * D],
            wo=layer[0][:, 3 * D : 4 * D],
            w1=layer[0][:, 4 * D :],
            wsr=layer[1][:, :D],
            w2=layer[1][:, D:],
            taps=taps32[l],
            gain=gain32[base : base + 3],
            bias=bias32[base : base + 3],
        )

    wts = [weights(l, layer) for l, layer in zip(groups[0], layers_of(cut(*raw[0]), len(groups[0])))]
    ln_first = jnp.stack([gain32[0], bias32[0]])
    ln_last = jnp.stack([gain32[-1], bias32[-1]])

    full = ((tok, D), f32)
    half = ((tok, D), bf16)
    wide16 = ((tok, FF), bf16)
    input_outs = [half, half, ((keys_own, D), f32), ((keys_own, D), bf16), ((keys_own, 2 * D), bf16)]
    ln_out = ((2, D), f32)
    row16 = ((W, FF), bf16)

    spread = patches.reshape(img_dev, rows, HALF, 2, -1).transpose(0, 1, 3, 2, 4)
    patch_own = to_team(spread.reshape(img_dev, rows * W, -1))
    e, x = run(2, embed_body, [full, full], patch_own, embed16, ln_first)
    w = wts[0]
    a16, q16, r, rn16, kv16 = run(
        2, first_body, input_outs, x, w["gain"], w["bias"], w["wq"], w["wsr"], w["wkv"]
    )
    kept = []
    for l in range(LAYERS):
        w = wts[l]
        kv_all = all_keys(kv16)
        o16, lse, x2, b16, h16, edge = run(
            4,
            middle_body,
            [half, ((HEADS, tok), f32), full, half, wide16, row16],
            q16,
            kv_all,
            shut,
            x,
            w["gain"],
            w["bias"],
            w["wo"],
            w["w1"],
            place=ends,
        )
        hlow, hhigh = edges(h16, edge)
        keep = dict(
            x=x, a16=a16, q16=q16, r=r, rn16=rn16, kv=kv_all, o16=o16, lse=lse, x2=x2, b16=b16,
            h16=h16, hlow=hlow, hhigh=hhigh,
        )
        shared = (h16, hlow, hhigh, w["taps"], x2, w["w2"])
        if l + 1 == first_late:
            got, _ = lax.optimization_barrier((raw[1][0], kv_all))
            got = cut(got, raw[1][1])
            head16 = got[0].reshape(n_dp, -1)[:, : head_w.size].reshape(D, CLS)
            wts += [weights(m, layer) for m, layer in zip(groups[1], layers_of(got[1:], len(groups[1])))]
        if l + 1 < LAYERS:
            n = wts[l + 1]
            keep["g16"], keep["slope"], x, a16, q16, r, rn16, kv16 = run(
                8,
                join_body,
                [wide16, ((tok, FF), f32), full] + input_outs,
                *shared,
                n["gain"],
                n["bias"],
                n["wq"],
                n["wsr"],
                n["wkv"],
                place=ends,
            )
        else:
            keep["g16"], keep["slope"], x, pool = run(
                7,
                last_body,
                [wide16, ((tok, FF), f32), full, ((1, D), f32)],
                *shared,
                ln_last,
                okay,
                place=ends,
            )
        kept.append(keep)

    whole = pool
    for j in range(1, team):
        whole = whole + lax.ppermute(pool, "seq", between(j, True))
    loss_own, pooled16, dlog16, dln_last, dx, dy16, dz16, edge = run(
        4,
        functools.partial(head_body, images),
        [((1, 1), f32), ((1, D), bf16), ((1, CLS), bf16), ln_out, full, half, wide16, row16],
        whole,
        count,
        head16,
        target,
        x,
        ln_last,
        okay,
        wts[-1]["w2"],
        kept[-1]["slope"],
        place=ends,
    )
    chosen = ((place == 0) & busy).astype(f32)
    d_head = pooled16.astype(f32).reshape(D, 1) * dlog16.astype(f32) * chosen
    loss_local = loss_own[0, 0] * busy.astype(f32)
    teams = n_seq // team
    loss_parts = jnp.zeros((teams,), f32)
    for j in range(teams):
        other = loss_local
        if j:
            other = lax.ppermute(
                loss_local, "seq", [((d + j * team) % n_seq, d) for d in range(n_seq)]
            )
        loss_parts = jnp.where(jnp.arange(teams) == (seq_pos // team + j) % teams, other, loss_parts)
    loss_seq = jnp.sum(loss_parts)

    piece = ((cols, n_dp, 2 * sub_in, wide), f32)
    paired = subs == 2 and cols == 4
    chip = seq_pos // subs
    where = jnp.stack([core, chip, dp_pos]).astype(jnp.int32)

    def weight_grads(*args):
        vm = pl.BlockSpec(memory_space=pltpu.VMEM)
        outs = [piece] * 2 if paired else [((cols, subs) + piece[0][1:], f32)]
        return pl.pallas_call(
            functools.partial(weight_grads_body, n_dp, cols, subs),
            out_shape=[jax.ShapeDtypeStruct(s, d) for s, d in outs],
            in_specs=[pl.BlockSpec(memory_space=pltpu.SMEM)] + [vm] * len(args),
            out_specs=[vm] * len(outs),
            scratch_shapes=[pltpu.VMEM((D, cols * wide), f32), pltpu.VMEM((FF, 2 * D), f32)],
            compiler_params=pltpu.CompilerParams(vmem_limit_bytes=48 << 20),
            cost_estimate=cost(6),
        )(where, *args)

    def padded_rest(parts):
        flat = jnp.concatenate(parts, 1)
        size = -(-flat.shape[1] // (16 * wide * n_seq)) * 16 * wide * n_seq
        flat = jnp.pad(flat, ((0, 0), (0, size - flat.shape[1])))
        flat = flat.reshape(n_dp, cols, subs, -1, wide).transpose(1, 2, 0, 3, 4)
        if not paired:
            return [flat]
        flat = jnp.stack([lax.dynamic_index_in_dim(flat, chip ^ j, 0, False) for j in range(cols)])
        twice = jnp.concatenate([flat, flat], 2)
        flat = lax.dynamic_slice_in_dim(twice, dp_pos, n_dp, 2)
        return [lax.dynamic_index_in_dim(flat, k, 1, False) for k in (core, 1 - core)]

    def pair_sum(parts):
        mine, send = parts
        return mine + lax.ppermute(send, "seq", [(d ^ 1, d) for d in range(n_seq)])

    def over_chips(v, bit):
        return lax.ppermute(v, "seq", [(d ^ (bit * subs), d) for d in range(n_seq)])

    def plane_first(y):
        cut = y.shape[2] // 2
        one, two = y[:, :, :cut], y[:, :, cut:]
        moved = (to_bf(jnp.stack([one[1], one[3]])), to_bf(jnp.stack([two[2], two[3]])))
        got = (over_chips(moved[0], 1).astype(f32), over_chips(moved[1], 2).astype(f32))
        return [one[0] + got[0][0], one[2] + got[0][1], two[0] + got[1][0], two[1] + got[1][1]]

    def plane_second(parts):
        one = parts[0] + over_chips(parts[1], 2)
        two = parts[2] + over_chips(parts[3], 1)
        return jnp.concatenate([one, two], 1)

    def dp_sum(y):
        total = y[0]
        for j in range(1, n_dp):
            pairs = [(d, (d + j) % n_dp) for d in range(n_dp)]
            total = total + lax.ppermute(to_bf(y[j]), "dp", pairs).astype(f32)
        return total

    def whole_sum(parts):
        y = jnp.concatenate([p[0] for p in parts], -2)
        y = lax.psum_scatter(y.reshape(-1, wide), "seq", scatter_dimension=0, tiled=True)
        return lax.psum_scatter(y, "dp", scatter_dimension=0, tiled=True)

    def tied(value, others):
        return lax.optimization_barrier((value, others))

    same = lambda v: v
    stages = [pair_sum, plane_first, same, plane_second, same, dp_sum]
    even, odd = ((0, 2, 4, 6), (1, 3, 5))
    pieces = []

    def advance(now, which):
        if not paired:
            return now
        ready = [p for p in pieces if p[0] in which]
        now, values = tied(now, [p[1] for p in ready])
        for p, v in zip(ready, values):
            p[1] = stages[p[0]](v) if p[0] < len(stages) else v
            p[0] += 1
        return now

    grads = [None] * LAYERS
    pieces.append([0, padded_rest([d_head.reshape(n_dp, -1)])])
    waiting = None
    for l in reversed(range(LAYERS)):
        w, k = wts[l], kept[l]
        zlow, zhigh = edges(dz16, edge)
        if waiting is not None:
            pieces.append([0, weight_grads(*waiting)])
        upper = dy16
        dz16 = advance(dz16, even)
        dh16, d_taps, dln2, dx2, dy2, dq16, dkv = run(
            11,
            block_back_body,
            [wide16, ((9, FF), f32), ln_out, full, half, half, ((team * keys_own, 2 * D), f32)],
            k["h16"], k["hlow"], k["hhigh"], dz16, zlow, zhigh, w["taps"], w["w1"], k["x2"], w["gain"], dx,
            w["wo"], k["q16"], k["kv"], shut, k["lse"],
            place=ends,
        )
        dkv_own = own_keys(dkv)
        dq16 = advance(dq16, odd)
        shared = (dkv_own, w["wkv"], k["r"], w["gain"], dq16, w["wq"], w["wsr"], k["x"], dx2)
        if l:
            dr16, dln, dx, dy16, dz16, edge = run(
                6,
                join_back_body,
                [((keys_own, D), bf16), ((4, D), f32), full, half, wide16, row16],
                *shared,
                wts[l - 1]["w2"],
                kept[l - 1]["slope"],
                place=ends,
            )
        else:
            dr16, dln, de16, dln_first = run(
                3,
                first_back_body,
                [((keys_own, D), bf16), ((4, D), f32), half, ln_out],
                *shared,
                e,
                ln_first,
            )
        waiting = (k["a16"], dq16, k["rn16"], dkv_own, k["o16"], dy2, k["b16"], dh16, dr16, k["g16"], upper)
        grads[l] = (
            d_taps,
            jnp.concatenate([dln[0:2], dln2[0:1]], 0),
            jnp.concatenate([dln[2:4], dln2[1:2]], 0),
        )
    pieces.append([0, weight_grads(*waiting)])
    de16 = advance(de16, even)
    (d_embed,) = run(3, embed_back_body, [((embed16.shape[0], D), f32)], patch_own, de16)
    d_embed = advance(d_embed, odd)
    d_gain = jnp.concatenate([dln_first[0:1]] + [g[1] for g in grads] + [dln_last[0:1]], 0)
    d_bias = jnp.concatenate([dln_first[1:2]] + [g[2] for g in grads] + [dln_last[1:2]], 0)
    d_taps = jnp.stack([g[0] for g in grads])
    rest = [
        d_embed.reshape(n_dp, -1),
        d_taps.reshape(LAYERS * 9, n_dp, -1).transpose(1, 0, 2).reshape(n_dp, -1),
        d_gain.reshape(-1, n_dp, row_in).transpose(1, 0, 2).reshape(n_dp, -1),
        d_bias.reshape(-1, n_dp, row_in).transpose(1, 0, 2).reshape(n_dp, -1),
    ]
    cuts = [0]
    for part in rest:
        cuts.append(cuts[-1] + part.shape[1])
    rest = padded_rest(rest)

    late = 3

    def together(parts):
        return to_bf(jnp.concatenate(parts, 0))

    if paired:
        assert all(p[0] > len(stages) for p in pieces[: LAYERS + 1 - late])
        early = together([p[1] for p in pieces[1 : LAYERS + 1 - late] + pieces[:1]])
        rest, early = tied(rest, early)
        rest = advance(rest, even)
        rest = advance(rest, odd)
        last = plane_second(plane_first(pair_sum(rest)))
        last = dp_sum(jnp.concatenate([pieces[-1][1], last], 1))
        sums = [None] * (LAYERS + 1 - late) + [p[1] for p in pieces[LAYERS + 1 - late : -1]] + [last]
    else:
        sums = [whole_sum([p[1]]) for p in pieces + [[0, rest]]]
        early = together(sums[1 : LAYERS + 1 - late] + sums[:1])
    early_got = lax.all_gather(early, "seq", axis=0, tiled=False)
    late_part, early_got = tied(together(sums[LAYERS + 1 - late :]), early_got)
    late_got = lax.all_gather(late_part, "seq", axis=0, tiled=False)
    head_start = (LAYERS - late) * 2 * sub_in
    g_head = early_got[:, head_start:].reshape(-1)[: head_w.size].reshape(head_w.shape).astype(f32)
    flat = late_got[:, late * 2 * sub_in :].reshape(-1).astype(f32)
    flat = [flat[a:b] for a, b in zip(cuts, cuts[1:])]
    shards = (
        flat[0].reshape(embed_w.shape),
        None,
        None,
        flat[1].reshape(dw_kernel.shape),
        g_head,
        flat[2].reshape(norm_gain.shape),
        flat[3].reshape(norm_bias.shape),
    )

    gsq_local = sum(jnp.sum(jnp.square(g.astype(f32))) for g in (early_got, late_got))
    wsq_local = group_sums(tuple((w * w for w in masters)))
    gsq, wsq, loss = lax.psum((gsq_local, wsq_local, loss_seq), "dp")
    grad_norm = jnp.sqrt(gsq)
    factor = jnp.minimum(1.0, clip_limit / grad_norm)

    proj_spec = pl.BlockSpec((1,) + in_proj.shape[1:], lambda l: (l, 0, 0))
    down_spec = pl.BlockSpec((1,) + down_proj.shape[1:], lambda l: (l, 0, 0, 0))
    block = (n_seq, 2 * sub_in, wide)
    blocks_of = [early_got, late_got]
    if 2 * sub_in % 8:
        block = (n_seq, 1, 2 * sub_in, wide)
        counts = (LAYERS - late, late)
        blocks_of = [
            g[:, : n * 2 * sub_in].reshape(n_seq, n, 2 * sub_in, wide)
            for g, n in zip(blocks_of, counts)
        ]
    tail = (0,) * (len(block) - 2)
    got = pl.pallas_call(
        functools.partial(update_body, cols, subs, late),
        grid=(LAYERS,),
        out_shape=[jax.ShapeDtypeStruct(in_proj.shape, f32)] * 3
        + [jax.ShapeDtypeStruct(down_proj.shape, f32)] * 3
        + [jax.ShapeDtypeStruct((LAYERS, 2, LANES), f32)],
        in_specs=[
            pl.BlockSpec(memory_space=pltpu.SMEM),
            pl.BlockSpec(block, lambda l: (0, jnp.minimum(LAYERS - 1 - l, LAYERS - 1 - late), *tail)),
            pl.BlockSpec(block, lambda l: (0, jnp.maximum(late - 1 - l, 0), *tail)),
        ]
        + [proj_spec] * 3
        + [down_spec] * 3,
        out_specs=[proj_spec] * 3 + [down_spec] * 3 + [pl.BlockSpec((1, 2, LANES), lambda l: (l, 0, 0))],
        compiler_params=pltpu.CompilerParams(vmem_limit_bytes=56 << 20),
        cost_estimate=cost(25),
    )(factor.reshape(1), *blocks_of, in_proj, m_proj, v_proj, down_proj, m_down, v_down)
    big = {1: got[0:3], 2: got[3:6]}
    new_m, new_v, updates = ([], [], [])
    for n, (w, g, m, v) in enumerate(zip(masters, shards, firsts, seconds)):
        m2, v2, u = big[n] if n in big else moments(w, g * factor, m, v)
        new_m.append(m2)
        new_v.append(v2)
        updates.append(u)
    usq = lax.psum(
        group_sums(tuple((u * u for u in updates)), [got[6][:, 0, 0], got[6][:, 1, 0]]), "dp"
    )
    wnorm = jnp.sqrt(wsq)
    unorm = jnp.sqrt(usq)
    ratio = wnorm / unorm
    spreads = spread_ratio(ratio)
    new_w = [w - learn_rate * r * u for w, r, u in zip(masters, spreads, updates)]
    stats = jnp.stack([wnorm, unorm])
    return (loss, grad_norm, stats, ratio, *new_w, *new_m, *new_v)


def solution(mesh):
    placed = (
        P("dp", None),
        P(None, "dp", None),
        P(None, None, "dp", None),
        P(None, None, "dp"),
        P("dp", None),
        P(None, "dp"),
        P(None, "dp"),
    )
    in_specs = (
        P("dp", "seq", None, None),
        P("dp", None),
        P("dp"),
        P("dp"),
        P("dp"),
    ) + placed * 3
    out_specs = (P(), P(), P(), P()) + placed * 3
    return jax.shard_map(
        per_device, mesh=mesh, in_specs=in_specs, out_specs=out_specs, check_vma=False
    )
```

```python
import functools

import jax
import jax.numpy as jnp
from jax import lax
from jax.experimental import pallas as pl
from jax.experimental.pallas import tpu as pltpu
from jax.sharding import PartitionSpec as P

D = 320
HEADS = 5
HD = 64
FF = 1280
CLS = 1000
W = 64
HALF = W // 2
LAYERS = 6
STEP = 5
LANES = 128


norm_eps = 1e-06
scale_qk = 0.125
big_neg = -1e30
beta_one = 0.9
beta_two = 0.999
lamb_eps = 1e-06
decay_rate = 0.01
learn_rate = 0.3
clip_limit = 0.1
root_half = 0.7071067811865476
root_two_pi = 0.3989422804014327
precise = lax.Precision.HIGHEST

f32 = jnp.float32
bf16 = jnp.bfloat16


def to_bf(v):
    return v.astype(bf16)


def dot(a, b):
    return jnp.dot(a, b, preferred_element_type=f32)


def dot_nt(a, b, precision=None):
    return lax.dot_general(
        a, b, (((1,), (1,)), ((), ())), precision=precision, preferred_element_type=f32
    )


def contract(a, b, precision=None):
    return lax.dot_general(
        a, b, (((0,), (0,)), ((), ())), precision=precision, preferred_element_type=f32
    )


def norm_parts(v):
    center = v - jnp.mean(v, -1, keepdims=True)
    spread = jnp.mean(center * center, -1, keepdims=True)
    scale = lax.rsqrt(spread + norm_eps)
    return center * scale, scale


def layer_norm(v, gain, bias):
    return norm_parts(v)[0] * gain + bias


def norm_back(v, gain, grad):
    unit, scale = norm_parts(v)
    dgain = jnp.sum(grad * unit, 0, keepdims=True)
    dbias = jnp.sum(grad, 0, keepdims=True)
    t = grad * gain
    dv = scale * (
        t - jnp.mean(t, -1, keepdims=True) - unit * jnp.mean(t * unit, -1, keepdims=True)
    )
    return dv, dgain, dbias


def cost(us):
    return pl.CostEstimate(flops=int(us * 1e8), bytes_accessed=int(us * 1e5), transcendentals=0)


def run(us, body, outs, *args, place=None):
    vm = pl.BlockSpec(memory_space=pltpu.VMEM)
    scalars = [] if place is None else [place]
    return pl.pallas_call(
        body,
        out_shape=[jax.ShapeDtypeStruct(s, d) for s, d in outs],
        in_specs=[pl.BlockSpec(memory_space=pltpu.SMEM)] * len(scalars) + [vm] * len(args),
        out_specs=[vm] * len(outs),
        compiler_params=pltpu.CompilerParams(vmem_limit_bytes=48 << 20),
        cost_estimate=cost(us),
    )(*scalars, *args)


def cells_of(v):
    rows = v.shape[0] // W
    split = v.reshape(rows // 2, 2, 2, HALF, v.shape[1])
    return [split[:, k // 2, k % 2].reshape(-1, v.shape[1]) for k in range(4)]


def attention_inputs(x, gain, bias, wq, wsr, wkv, a_ref, q_ref, r_ref, rn_ref, kv_ref):
    a = to_bf(layer_norm(x, gain[0:1], bias[0:1]))
    a_ref[...] = a
    q_ref[...] = to_bf(dot(a, wq[...]))
    total = None
    for k, cell in enumerate(cells_of(a)):
        part = dot(cell, wsr[k * D : (k + 1) * D, :])
        total = part if total is None else total + part
    r_ref[...] = total
    rn = to_bf(layer_norm(total, gain[1:2], bias[1:2]))
    rn_ref[...] = rn
    kv_ref[...] = to_bf(dot(rn, wkv[...]))


def embed_body(p_ref, w_ref, ln_ref, e_ref, x_ref):
    e = dot(p_ref[...], w_ref[...])
    e_ref[...] = e
    x_ref[...] = layer_norm(e, ln_ref[0:1], ln_ref[1:2])


def embed_back_body(p_ref, de_ref, dw_ref):
    dw_ref[...] = contract(p_ref[...], de_ref[...])


def first_body(x_ref, gain, bias, wq, wsr, wkv, *outs):
    attention_inputs(x_ref[...], gain, bias, wq, wsr, wkv, *outs)


def middle_body(
    place, q_ref, kv_ref, ok_ref, x_ref, gain, bias, wo, w1, o_ref, lse_ref, x2_ref, b_ref, h_ref, edge_ref
):
    q = q_ref[...] * jnp.asarray(scale_qk, bf16)
    keys = kv_ref.shape[0]
    kv = kv_ref[...]
    shut = jnp.broadcast_to(ok_ref[...], (keys, q.shape[0]))
    q_t = q.T
    v_t = kv[:, D:].T
    parts = []
    for head in range(HEADS):
        low, high = head * HD, (head + 1) * HD
        s = dot(kv[:, low:high], q_t[low:high, :]) + shut
        top = jnp.max(s, 0, keepdims=True)
        expo = jnp.exp(s - top)
        total = jnp.sum(expo, 0, keepdims=True)
        lse_ref[head : head + 1, :] = top + jnp.log(total)
        p = to_bf(expo * (1.0 / total))
        parts.append(dot(v_t[low:high, :], p))
    o = to_bf(jnp.concatenate(parts, 0).T)
    o_ref[...] = o
    x2 = x_ref[...] + dot(o, wo[...])
    x2_ref[...] = x2
    b = to_bf(layer_norm(x2, gain[2:3], bias[2:3]))
    b_ref[...] = b
    h_ref[...] = to_bf(dot(b, w1[...]))
    send_edge(place, h_ref, edge_ref)


def shift_down(v):
    index = lax.broadcasted_iota(jnp.int32, v.shape, 0)
    return jnp.where(index == 0, 0.0, pltpu.roll(v, 1, 0))


def shift_up(v):
    index = lax.broadcasted_iota(jnp.int32, v.shape, 0)
    return jnp.where(index == v.shape[0] - 1, 0.0, pltpu.roll(v, v.shape[0] - 1, 0))


def from_left(v):
    return jnp.concatenate([shift_down(v[HALF:]), v[:HALF]], 0)


def from_right(v):
    return jnp.concatenate([v[HALF:], shift_up(v[:HALF])], 0)


def row_of(main, near, i, rows, lanes):
    place, low, high = near
    if i < 0:
        return jnp.where(place[0] > 0, low[:, lanes].astype(f32), 0.0)
    if i >= rows:
        return jnp.where(place[1] > 0, high[:, lanes].astype(f32), 0.0)
    return main[i * W : (i + 1) * W, lanes].astype(f32)


def send_edge(place, main, edge_ref):
    start = pl.multiple_of(jnp.where(place[0] > 0, 0, main.shape[0] - W), W)
    edge_ref[...] = main[pl.ds(start, W), :]


def conv_gelu(h_ref, ends, taps_ref, g_ref, slope_ref):
    rows = h_ref.shape[0] // W

    def chunk(c, carry):
        lanes = pl.ds(pl.multiple_of(c * LANES, LANES), LANES)
        taps = [taps_ref[k : k + 1, lanes] for k in range(9)]
        near = [row_of(h_ref, ends, i, rows, lanes) for i in (-1, 0)]
        for i in range(rows):
            near.append(row_of(h_ref, ends, i + 1, rows, lanes))
            sums = [
                taps[j] * near[0] + taps[3 + j] * near[1] + taps[6 + j] * near[2] for j in range(3)
            ]
            z = sums[1] + from_left(sums[0]) + from_right(sums[2])
            phi = 0.5 + 0.5 * lax.erf(z * root_half)
            here = slice(i * W, (i + 1) * W)
            g_ref[here, lanes] = to_bf(z * phi)
            slope_ref[here, lanes] = phi + z * (jnp.exp(-0.5 * z * z) * root_two_pi)
            near = near[1:]
        return carry

    lax.fori_loop(0, FF // LANES, chunk, 0)


def last_body(place, h_ref, low_ref, high_ref, taps_ref, x2_ref, w2, ln_ref, ok_ref, g_ref, slope_ref, x_ref, sum_ref):
    conv_gelu(h_ref, (place, low_ref, high_ref), taps_ref, g_ref, slope_ref)
    x = x2_ref[...] + dot(g_ref[...], w2[...])
    x_ref[...] = x
    fin = layer_norm(x, ln_ref[0:1], ln_ref[1:2])
    sum_ref[...] = jnp.sum(fin * ok_ref[...], 0, keepdims=True)


def join_body(
    place, h_ref, low_ref, high_ref, taps_ref, x2_ref, w2, gain, bias, wq, wsr, wkv, g_ref, slope_ref, x_ref, *outs
):
    conv_gelu(h_ref, (place, low_ref, high_ref), taps_ref, g_ref, slope_ref)
    x = x2_ref[...] + dot(g_ref[...], w2[...])
    x_ref[...] = x
    attention_inputs(x, gain, bias, wq, wsr, wkv, *outs)


def gelu_back(place, dx, w2, slope_ref, dy_ref, dz_ref, edge_ref):
    dy = to_bf(dx)
    dy_ref[...] = dy
    dg = to_bf(dot_nt(dy, w2[...])).astype(f32)
    dz_ref[...] = to_bf(dg * slope_ref[...])
    send_edge(place, dz_ref, edge_ref)


def head_body(
    images,
    place,
    pool_ref,
    count_ref,
    head_ref,
    target_ref,
    x_ref,
    ln_ref,
    ok_ref,
    w2,
    slope_ref,
    loss_ref,
    pooled_ref,
    dlog_ref,
    dln_ref,
    dx_ref,
    dy_ref,
    dz_ref,
    edge_ref,
):
    count = count_ref[...]
    pooled = to_bf(pool_ref[...] / count)
    pooled_ref[...] = pooled
    logits = dot(jnp.broadcast_to(pooled.astype(f32), (16, D)).astype(bf16), head_ref[...])[0:1]
    shifted = logits - jnp.max(logits, -1, keepdims=True)
    logp = shifted - jnp.log(jnp.sum(jnp.exp(shifted), -1, keepdims=True))
    target = target_ref[...]
    loss_ref[...] = jnp.sum(target * logp, -1, keepdims=True) * (-1.0 / images)
    dlog = to_bf((jnp.exp(logp) - target) * (1.0 / images))
    dlog_ref[...] = dlog
    wide = jnp.broadcast_to(dlog.astype(f32), (16, CLS)).astype(bf16)
    dpool = dot_nt(wide, head_ref[...])[0:1] / count
    dx, dgain, dbias = norm_back(x_ref[...], ln_ref[0:1], ok_ref[...] * dpool)
    dln_ref[0:1, :] = dgain
    dln_ref[1:2, :] = dbias
    dx_ref[...] = dx
    gelu_back(place, dx, w2, slope_ref, dy_ref, dz_ref, edge_ref)


def conv_back(h_ref, hends, dz_ref, zends, taps_ref, dh_ref, dtaps_ref):
    rows = h_ref.shape[0] // W

    def chunk(c, carry):
        lanes = pl.ds(pl.multiple_of(c * LANES, LANES), LANES)
        taps = [taps_ref[k : k + 1, lanes] for k in range(9)]
        acc = [jnp.zeros((8, LANES), f32) for _ in range(9)]

        def views(i):
            v = row_of(dz_ref, zends, i, rows, lanes)
            return [from_right(v), v, from_left(v)]

        near = [views(-1), views(0)]
        hear = [row_of(h_ref, hends, i, rows, lanes) for i in (-1, 0)]
        for i in range(rows):
            near.append(views(i + 1))
            hear.append(row_of(h_ref, hends, i + 1, rows, lanes))
            dh = None
            for di in range(3):
                for dj in range(3):
                    part = taps[3 * di + dj] * near[2 - di][dj]
                    dh = part if dh is None else dh + part
            dh_ref[i * W : (i + 1) * W, lanes] = to_bf(dh)
            for di in range(3):
                for dj in range(3):
                    prod = (hear[di] * near[1][dj]).reshape(W // 8, 8, LANES)
                    acc[3 * di + dj] = acc[3 * di + dj] + jnp.sum(prod, 0)
            near = near[1:]
            hear = hear[1:]
        for k in range(9):
            dtaps_ref[k : k + 1, lanes] = jnp.sum(acc[k], 0, keepdims=True)
        return carry

    lax.fori_loop(0, FF // LANES, chunk, 0)


def block_back_body(
    place,
    h_ref,
    hlow_ref,
    hhigh_ref,
    dz_ref,
    zlow_ref,
    zhigh_ref,
    taps_ref,
    w1,
    x2_ref,
    gain,
    dx_ref,
    wo,
    q_ref,
    kv_ref,
    ok_ref,
    lse_ref,
    dh_ref,
    dtaps_ref,
    dln_ref,
    dx2_ref,
    dy_ref,
    dq_ref,
    dkv_ref,
):
    conv_back(
        h_ref, (place, hlow_ref, hhigh_ref), dz_ref, (place, zlow_ref, zhigh_ref), taps_ref, dh_ref, dtaps_ref
    )
    db = dot_nt(dh_ref[...], w1[...])
    dln, dgain, dbias = norm_back(x2_ref[...], gain[2:3], db)
    dln_ref[0:1, :] = dgain
    dln_ref[1:2, :] = dbias
    dx2 = dx_ref[...] + dln
    dx2_ref[...] = dx2
    dy = to_bf(dx2)
    dy_ref[...] = dy
    do_t = to_bf(dot_nt(wo[...], dy))
    q = q_ref[...] * jnp.asarray(scale_qk, bf16)
    q_t = q.T
    keys = kv_ref.shape[0]
    kv = kv_ref[...]
    k_t = (kv[:, :D] * jnp.asarray(scale_qk, bf16)).T
    shut = jnp.broadcast_to(ok_ref[...], (keys, q.shape[0]))
    dq_parts, dk_parts, dv_parts = ([], [], [])
    for head in range(HEADS):
        low, high = head * HD, (head + 1) * HD
        s = dot(kv[:, low:high], q_t[low:high, :]) + shut
        p = jnp.exp(s - lse_ref[head : head + 1, :])
        dp = dot(kv[:, D + low : D + high], do_t[low:high, :])
        dv_parts.append(dot_nt(do_t[low:high, :], to_bf(p)))
        ds = to_bf(p * (dp - jnp.sum(p * dp, 0, keepdims=True)))
        dq_parts.append(dot(k_t[low:high, :], ds))
        dk_parts.append(dot_nt(q_t[low:high, :], ds))
    dq_ref[...] = to_bf(jnp.concatenate(dq_parts, 0).T)
    dkv_ref[...] = jnp.concatenate(dk_parts + dv_parts, 0).T


def inputs_back(dkv, wkv, r_ref, gain, dq_ref, wq, wsr, x_ref, dx2_ref, dr_ref, dln_ref):
    w_kv = wkv[...].astype(f32)
    drn = dot_nt(dkv, w_kv, precise)
    dr, dgain1, dbias1 = norm_back(r_ref[...], gain[1:2], drn)
    dr = to_bf(dr)
    dr_ref[...] = dr
    rows = x_ref.shape[0] // W
    cells = [
        dot_nt(dr, wsr[k * D : (k + 1) * D, :]).reshape(rows // 2, 1, 1, HALF, D) for k in range(4)
    ]
    placed = jnp.concatenate(
        [jnp.concatenate(cells[0:2], 2), jnp.concatenate(cells[2:4], 2)], 1
    ).reshape(rows * W, D)
    da = dot_nt(dq_ref[...], wq[...]) + placed
    dln, dgain0, dbias0 = norm_back(x_ref[...], gain[0:1], da)
    for k, row in enumerate((dgain0, dgain1, dbias0, dbias1)):
        dln_ref[k : k + 1, :] = row
    return dx2_ref[...] + dln


def join_back_body(
    place, dkv_ref, wkv, r_ref, gain, dq_ref, wq, wsr, x_ref, dx2_ref, w2, slope_ref,
    dr_ref, dln_ref, dx_ref, dy_ref, dz_ref, edge_ref
):
    dx = inputs_back(dkv_ref[...], wkv, r_ref, gain, dq_ref, wq, wsr, x_ref, dx2_ref, dr_ref, dln_ref)
    dx_ref[...] = dx
    gelu_back(place, dx, w2, slope_ref, dy_ref, dz_ref, edge_ref)


def first_back_body(
    dkv_ref, wkv, r_ref, gain, dq_ref, wq, wsr, x_ref, dx2_ref, e_ref, ln_ref, dr_ref, dln_ref, de_ref, dle_ref
):
    dx = inputs_back(dkv_ref[...], wkv, r_ref, gain, dq_ref, wq, wsr, x_ref, dx2_ref, dr_ref, dln_ref)
    de, dgain, dbias = norm_back(e_ref[...], ln_ref[0:1], dx)
    de_ref[...] = to_bf(de)
    dle_ref[0:1, :] = dgain
    dle_ref[1:2, :] = dbias


def weight_grads_body(
    n_dp, cols, subs, core_ref, a_ref, dq_ref, rn_ref, dkv_ref, o_ref, dy2_ref, b_ref, dh_ref, dr_ref, g_ref, dy_ref, *refs
):
    outs, (proj, down) = refs[:-2], refs[-2:]
    a = a_ref[...]
    proj[:, :D] = contract(a, dq_ref[...])
    proj[:, D : 3 * D] = contract(rn_ref[...].astype(f32), dkv_ref[...], precise)
    proj[:, 3 * D : 4 * D] = contract(o_ref[...], dy2_ref[...])
    proj[:, 4 * D :] = contract(b_ref[...], dh_ref[...])
    dr = dr_ref[...]
    for k, cell in enumerate(cells_of(a)):
        down[k * D : (k + 1) * D, :D] = contract(cell, dr)
    down[:, D:] = contract(g_ref[...], dy_ref[...])
    rows = D // n_dp
    sub = rows // subs
    wide = (4 * D + FF) // cols
    down_rows = FF // n_dp
    for c in range(cols):
        for d in range(n_dp):
            for n, out in enumerate(outs):
                for j in range(subs) if len(outs) == 1 else (None,):
                    if j is None:
                        k = core_ref[0] if n == 0 else 1 - core_ref[0]
                        at = (c ^ core_ref[1], d)
                    else:
                        k = j
                        at = (c, j, d)
                    start = d * rows + k * sub
                    low = d * down_rows + (c * subs + k) * (down_rows // (cols * subs))
                    if j is None:
                        start = pl.multiple_of(start, 8)
                        low = pl.multiple_of(low, 8)
                    out[(*at, slice(0, sub))] = proj[pl.ds(start, sub), c * wide : (c + 1) * wide]
                    out[(*at, slice(sub, 2 * sub))] = down[pl.ds(low, sub), :]


def moments(w, g, m, v):
    m2 = beta_one * m + (1.0 - beta_one) * g
    v2 = beta_two * v + (1.0 - beta_two) * g * g
    u = (
        m2 / (1.0 - beta_one**STEP) / (jnp.sqrt(v2 / (1.0 - beta_two**STEP)) + lamb_eps)
        + decay_rate * w
    )
    return m2, v2, u


def update_body(
    cols, subs, late, factor_ref, early_ref, late_ref, wp, mp, vp, wd, md, vd, mp2, vp2, up, md2, vd2, ud, sums
):
    factor = factor_ref[0]
    layer = pl.program_id(0)
    sub = wp.shape[1] // subs
    wide = wp.shape[2] // cols

    def go(g_ref):
        squares = [0.0, 0.0]

        def put(n, at, refs, outs, g):
            new = moments(refs[0][at], g * factor, refs[1][at], refs[2][at])
            for out, value in zip(outs, new):
                out[at] = value
            squares[n] = squares[n] + jnp.sum(new[2] * new[2], 0, keepdims=True)

        for c in range(cols):
            for k in range(subs):
                g = g_ref[c * subs + k].astype(f32).reshape(2 * sub, wide)
                at = (0, slice(k * sub, (k + 1) * sub), slice(c * wide, (c + 1) * wide))
                put(0, at, (wp, mp, vp), (mp2, vp2, up), g[:sub])
                rows = slice((c * subs + k) * sub, (c * subs + k + 1) * sub)
                for half in range(2):
                    at = (0, half, rows, slice(0, D))
                    put(1, at, (wd, md, vd), (md2, vd2, ud), g[sub:, half * D : (half + 1) * D])
        for n in range(2):
            sums[0, n : n + 1, :] = jnp.broadcast_to(jnp.sum(squares[n], 1, keepdims=True), (1, LANES))

    pl.when(layer >= late)(lambda: go(early_ref))
    pl.when(layer < late)(lambda: go(late_ref))


def group_sums(arrs, layered=None):
    embed, proj, downs, taps, head, gains, biases = arrs
    if layered is None:
        layered = [jnp.sum(a.reshape(a.shape[0], -1), 1) for a in (proj, downs)]
    layered = [*layered, jnp.sum(taps.reshape(taps.shape[0], -1), 1)]
    slot = jnp.arange(4 + 3 * LAYERS)
    total = jnp.zeros((4 + 3 * LAYERS,), f32)
    for n, a in enumerate((embed, head, gains, biases)):
        total = jnp.where(slot == n, jnp.sum(a), total)
    for n, a in enumerate(layered):
        total = total + jnp.pad(a, (4 + LAYERS * n, LAYERS * (2 - n)))
    return total


def spread_ratio(ratio):
    return (
        ratio[0],
        ratio[4 : 4 + LAYERS].reshape(LAYERS, 1, 1),
        ratio[4 + LAYERS : 4 + 2 * LAYERS].reshape(LAYERS, 1, 1, 1),
        ratio[4 + 2 * LAYERS : 4 + 3 * LAYERS].reshape(LAYERS, 1, 1),
        ratio[1],
        ratio[2],
        ratio[3],
    )


def per_device(
    patches,
    valid,
    labels,
    partners,
    mix,
    embed_w,
    in_proj,
    down_proj,
    dw_kernel,
    head_w,
    norm_gain,
    norm_bias,
    m_embed,
    m_proj,
    m_down,
    m_taps,
    m_head,
    m_gain,
    m_bias,
    v_embed,
    v_proj,
    v_down,
    v_taps,
    v_head,
    v_gain,
    v_bias,
):
    masters = (embed_w, in_proj, down_proj, dw_kernel, head_w, norm_gain, norm_bias)
    firsts = (m_embed, m_proj, m_down, m_taps, m_head, m_gain, m_bias)
    seconds = (v_embed, v_proj, v_down, v_taps, v_head, v_gain, v_bias)
    n_seq = lax.axis_size("seq")
    n_dp = lax.axis_size("dp")
    seq_pos = lax.axis_index("seq")
    img_dev, rows = (patches.shape[0], patches.shape[1])
    images = img_dev * n_dp

    team = n_seq
    while team * img_dev > n_seq:
        team //= 2
    blocks = n_seq // team
    rows_own = rows * blocks
    tok = rows_own * W
    keys_own = tok // 4
    image = jnp.minimum(seq_pos // team, img_dev - 1)
    busy = seq_pos // team < img_dev
    place = seq_pos % team

    def between(shift, wrap):
        pairs = []
        for base in range(0, n_seq, team):
            for h in range(team):
                if wrap or 0 <= h + shift < team:
                    pairs.append((base + (h + shift) % team, base + h))
        return pairs

    ends = jnp.stack([place > 0, place < team - 1]).astype(jnp.int32)

    def edges(v, edge):
        if team == 2:
            other = lax.ppermute(edge, "seq", between(1, True))
            return other, other
        low = lax.ppermute(v[-W:], "seq", between(-1, False))
        high = lax.ppermute(v[:W], "seq", between(1, False))
        return low, high

    def all_keys(v):
        return jnp.concatenate(
            [v] + [lax.ppermute(v, "seq", between(j, True)) for j in range(1, team)], 0
        )

    def own_keys(v):
        total = v[:keys_own]
        for j in range(1, team):
            part = v[j * keys_own : (j + 1) * keys_own]
            total = total + lax.ppermute(part, "seq", between(-j, True))
        return total

    back_block = seq_pos % blocks
    routes = [
        [
            (blocks * h + (i + r) % blocks, team * i + h)
            for i in range(img_dev)
            for h in range(team)
        ]
        for r in range(blocks)
    ]

    def to_team(v):
        got = []
        for r, pairs in enumerate(routes):
            send = lax.dynamic_index_in_dim(
                v, jnp.minimum((back_block - r) % blocks, img_dev - 1), 0, keepdims=False
            )
            got.append(lax.ppermute(send, "seq", pairs))
        twice = jnp.stack(got + got)
        own = lax.dynamic_slice_in_dim(twice, (blocks - image) % blocks, blocks, 0)
        return own.reshape(tok, -1)

    cols = 4
    subs = n_seq // cols
    row_in = D // n_dp
    sub_in = row_in // subs
    wide = in_proj.shape[2] // cols
    down_rows = down_proj.shape[2] // n_seq
    core = seq_pos % subs

    def part_of(flat):
        size = -(-flat.shape[0] // (wide * n_seq)) * wide * n_seq
        flat = jnp.pad(flat, (0, size - flat.shape[0])).reshape(n_seq, -1, wide)
        return lax.dynamic_index_in_dim(flat, seq_pos, 0, keepdims=False)

    def layer_part(l):
        block = lax.dynamic_slice(
            in_proj[l], (core * sub_in, (seq_pos // subs) * wide), (sub_in, wide)
        )
        lower = lax.dynamic_slice_in_dim(down_proj[l], seq_pos * down_rows, down_rows, 1)
        return [to_bf(block), to_bf(jnp.concatenate([lower[0], lower[1]], 1))]

    def gathered(parts):
        sizes = [p.shape[0] for p in parts]
        got = lax.all_gather(jnp.concatenate(parts, 0), ("dp", "seq"), axis=0, tiled=False)
        return got, sizes

    def cut(got, sizes):
        got = got.reshape(n_dp, n_seq, sum(sizes), wide)
        starts = [sum(sizes[:i]) for i in range(len(sizes))]
        return [got[:, :, a : a + n] for a, n in zip(starts, sizes)]

    def proj_of(got):
        got = got.reshape(n_dp, cols, subs, sub_in, wide).transpose(0, 2, 3, 1, 4)
        return got.reshape(D, cols * wide)

    dp_pos = lax.axis_index("dp")

    def over_dp(v):
        got = [v] + [
            lax.ppermute(v, "dp", [((d + j) % n_dp, d) for d in range(n_dp)])
            for j in range(1, n_dp)
        ]
        return lax.dynamic_slice_in_dim(jnp.stack(got + got), (n_dp - dp_pos) % n_dp, n_dp, 0)

    embed16 = over_dp(to_bf(embed_w)).reshape(-1, D)
    taps16 = over_dp(to_bf(dw_kernel).reshape(LAYERS * 9, -1))
    norms16 = over_dp(to_bf(jnp.stack([norm_gain, norm_bias])))
    taps32 = taps16.transpose(1, 0, 2).reshape(LAYERS, 9, FF).astype(f32)
    norms32 = norms16.transpose(1, 2, 0, 3).reshape(2, -1, D).astype(f32)
    gain32, bias32 = norms32[0], norms32[1]
    groups = [[0, 1, 2], [3, 4, 5]]
    extra = [[], [part_of(to_bf(head_w).reshape(-1))]]

    def layers_of(got, count):
        return [(proj_of(got[2 * i]), got[2 * i + 1].reshape(FF, 2 * D)) for i in range(count)]

    parts_of = [more + [p for l in members for p in layer_part(l)] for members, more in zip(groups, extra)]
    raw = [gathered(parts_of[0])]
    first_late = groups[1][0]

    def own(v):
        return lax.dynamic_index_in_dim(v, image, 0, keepdims=False)

    wanted = own(partners)
    partner_label = jnp.zeros((), jnp.int32)
    for j in range(n_dp):
        other = labels
        if j:
            other = lax.ppermute(labels, "dp", [((d + j) % n_dp, d) for d in range(n_dp)])
        index = ((dp_pos + j) % n_dp) * img_dev + jnp.arange(img_dev)
        partner_label = partner_label + jnp.sum(jnp.where(index == wanted, other, 0))
    valid_own = own(valid)
    tid = lax.broadcasted_iota(jnp.int32, (tok, 1), 0)
    within = tid % W
    row_id = place * rows_own + tid // W
    col_id = 2 * (within % HALF) + within // HALF
    okay = ((row_id < valid_own[0]) & (col_id < valid_own[1]) & busy).astype(f32)
    kid = lax.broadcasted_iota(jnp.int32, (team * keys_own, 1), 0)
    segment = (place + kid // keys_own) % team
    key_row = segment * (rows_own // 2) + (kid % keys_own) // HALF
    key_ok = (2 * key_row < valid_own[0]) & (2 * (kid % HALF) < valid_own[1])
    shut = jnp.where(key_ok, 0.0, big_neg).astype(f32)
    count = (valid_own[0] * valid_own[1]).astype(f32).reshape(1, 1)
    classes = lax.broadcasted_iota(jnp.int32, (1, CLS), 1)
    mix_own = own(mix)
    target = mix_own * (classes == own(labels)).astype(f32) + (1.0 - mix_own) * (
        classes == partner_label
    ).astype(f32)

    def weights(l, layer):
        base = 1 + 3 * l
        return dict(
            wq=layer[0][:, :D],
            wkv=layer[0][:, D : 3 * D],
            wo=layer[0][:, 3 * D : 4 * D],
            w1=layer[0][:, 4 * D :],
            wsr=layer[1][:, :D],
            w2=layer[1][:, D:],
            taps=taps32[l],
            gain=gain32[base : base + 3],
            bias=bias32[base : base + 3],
        )

    full = ((tok, D), f32)
    ln_first = jnp.stack([gain32[0], bias32[0]])
    spread = patches.reshape(img_dev, rows, HALF, 2, -1).transpose(0, 1, 3, 2, 4)
    patch_own = to_team(spread.reshape(img_dev, rows * W, -1))
    e, x = run(2, embed_body, [full, full], patch_own, embed16, ln_first)
    second, x = lax.optimization_barrier((parts_of[1], x))
    raw.append(gathered(second))
    wts = [weights(l, layer) for l, layer in zip(groups[0], layers_of(cut(*raw[0]), len(groups[0])))]
    ln_last = jnp.stack([gain32[-1], bias32[-1]])

    half = ((tok, D), bf16)
    wide16 = ((tok, FF), bf16)
    input_outs = [half, half, ((keys_own, D), f32), ((keys_own, D), bf16), ((keys_own, 2 * D), bf16)]
    ln_out = ((2, D), f32)
    row16 = ((W, FF), bf16)

    w = wts[0]
    a16, q16, r, rn16, kv16 = run(
        2, first_body, input_outs, x, w["gain"], w["bias"], w["wq"], w["wsr"], w["wkv"]
    )
    kept = []
    for l in range(LAYERS):
        w = wts[l]
        kv_all = all_keys(kv16)
        o16, lse, x2, b16, h16, edge = run(
            4,
            middle_body,
            [half, ((HEADS, tok), f32), full, half, wide16, row16],
            q16,
            kv_all,
            shut,
            x,
            w["gain"],
            w["bias"],
            w["wo"],
            w["w1"],
            place=ends,
        )
        hlow, hhigh = edges(h16, edge)
        keep = dict(
            x=x, a16=a16, q16=q16, r=r, rn16=rn16, kv=kv_all, o16=o16, lse=lse, x2=x2, b16=b16,
            h16=h16, hlow=hlow, hhigh=hhigh,
        )
        shared = (h16, hlow, hhigh, w["taps"], x2, w["w2"])
        if l + 1 == first_late:
            got, _ = lax.optimization_barrier((raw[1][0], kv_all))
            got = cut(got, raw[1][1])
            head16 = got[0].reshape(n_dp, -1)[:, : head_w.size].reshape(D, CLS)
            wts += [weights(m, layer) for m, layer in zip(groups[1], layers_of(got[1:], len(groups[1])))]
        if l + 1 < LAYERS:
            n = wts[l + 1]
            keep["g16"], keep["slope"], x, a16, q16, r, rn16, kv16 = run(
                8,
                join_body,
                [wide16, ((tok, FF), f32), full] + input_outs,
                *shared,
                n["gain"],
                n["bias"],
                n["wq"],
                n["wsr"],
                n["wkv"],
                place=ends,
            )
        else:
            keep["g16"], keep["slope"], x, pool = run(
                7,
                last_body,
                [wide16, ((tok, FF), f32), full, ((1, D), f32)],
                *shared,
                ln_last,
                okay,
                place=ends,
            )
        kept.append(keep)

    whole = pool
    for j in range(1, team):
        whole = whole + lax.ppermute(pool, "seq", between(j, True))
    loss_own, pooled16, dlog16, dln_last, dx, dy16, dz16, edge = run(
        4,
        functools.partial(head_body, images),
        [((1, 1), f32), ((1, D), bf16), ((1, CLS), bf16), ln_out, full, half, wide16, row16],
        whole,
        count,
        head16,
        target,
        x,
        ln_last,
        okay,
        wts[-1]["w2"],
        kept[-1]["slope"],
        place=ends,
    )
    chosen = ((place == 0) & busy).astype(f32)
    d_head = pooled16.astype(f32).reshape(D, 1) * dlog16.astype(f32) * chosen
    loss_local = loss_own[0, 0] * busy.astype(f32)
    teams = n_seq // team
    loss_parts = jnp.zeros((teams,), f32)
    for j in range(teams):
        other = loss_local
        if j:
            other = lax.ppermute(
                loss_local, "seq", [((d + j * team) % n_seq, d) for d in range(n_seq)]
            )
        loss_parts = jnp.where(jnp.arange(teams) == (seq_pos // team + j) % teams, other, loss_parts)
    loss_seq = jnp.sum(loss_parts)

    piece = ((cols, n_dp, 2 * sub_in, wide), f32)
    paired = subs == 2 and cols == 4
    chip = seq_pos // subs
    where = jnp.stack([core, chip]).astype(jnp.int32)

    def weight_grads(*args):
        vm = pl.BlockSpec(memory_space=pltpu.VMEM)
        outs = [piece] * 2 if paired else [((cols, subs) + piece[0][1:], f32)]
        return pl.pallas_call(
            functools.partial(weight_grads_body, n_dp, cols, subs),
            out_shape=[jax.ShapeDtypeStruct(s, d) for s, d in outs],
            in_specs=[pl.BlockSpec(memory_space=pltpu.SMEM)] + [vm] * len(args),
            out_specs=[vm] * len(outs),
            scratch_shapes=[pltpu.VMEM((D, cols * wide), f32), pltpu.VMEM((FF, 2 * D), f32)],
            compiler_params=pltpu.CompilerParams(vmem_limit_bytes=48 << 20),
            cost_estimate=cost(6),
        )(where, *args)

    def padded_rest(parts):
        flat = jnp.concatenate(parts, 1)
        size = -(-flat.shape[1] // (16 * wide * n_seq)) * 16 * wide * n_seq
        flat = jnp.pad(flat, ((0, 0), (0, size - flat.shape[1])))
        flat = flat.reshape(n_dp, cols, subs, -1, wide).transpose(1, 2, 0, 3, 4)
        if not paired:
            return [flat]
        flat = jnp.stack([lax.dynamic_index_in_dim(flat, chip ^ j, 0, False) for j in range(cols)])
        return [lax.dynamic_index_in_dim(flat, k, 1, False) for k in (core, 1 - core)]

    def pair_sum(parts):
        mine, send = parts
        return mine + lax.ppermute(send, "seq", [(d ^ 1, d) for d in range(n_seq)])

    def over_chips(v, bit):
        return lax.ppermute(v, "seq", [(d ^ (bit * subs), d) for d in range(n_seq)])

    def plane_first(y):
        cut = y.shape[2] // 2
        one, two = y[:, :, :cut], y[:, :, cut:]
        moved = (to_bf(jnp.stack([one[1], one[3]])), to_bf(jnp.stack([two[2], two[3]])))
        got = (over_chips(moved[0], 1).astype(f32), over_chips(moved[1], 2).astype(f32))
        return [one[0] + got[0][0], one[2] + got[0][1], two[0] + got[1][0], two[1] + got[1][1]]

    def plane_second(parts):
        one = parts[0] + over_chips(parts[1], 2)
        two = parts[2] + over_chips(parts[3], 1)
        return jnp.concatenate([one, two], 1)

    def dp_sum(y, dtype=f32):
        def of(j):
            return lax.dynamic_index_in_dim(y, (dp_pos + j) % n_dp, 0, keepdims=False)

        total = of(0)
        for j in range(1, n_dp):
            pairs = [(d, (d + j) % n_dp) for d in range(n_dp)]
            total = total + lax.ppermute(of(j).astype(dtype), "dp", pairs).astype(f32)
        return total

    def whole_sum(parts):
        y = jnp.concatenate([p[0] for p in parts], -2)
        y = lax.psum_scatter(y.reshape(-1, wide), "seq", scatter_dimension=0, tiled=True)
        return lax.psum_scatter(y, "dp", scatter_dimension=0, tiled=True)

    def tied(value, others):
        return lax.optimization_barrier((value, others))

    stages = [pair_sum, plane_first, plane_second]
    pieces = []

    def advance(now):
        if not paired:
            return now
        ready = [p for p in pieces if p[0] <= len(stages) + 1]
        now, values = tied(now, [p[1] for p in ready])
        for n, (p, v) in enumerate(zip(ready, values)):
            if p[0] < len(stages):
                p[1] = stages[p[0]](v)
            elif p[0] > len(stages) or p is pieces[0]:
                p[1] = v
            elif p is pieces[1]:
                p[1] = dp_sum(jnp.concatenate([v, pieces[0][1]], 1))
            else:
                p[1] = dp_sum(v)
            p[0] += 1
        return now

    grads = [None] * LAYERS
    pieces.append([0, padded_rest([d_head.reshape(n_dp, -1)])])
    waiting = None
    for l in reversed(range(LAYERS)):
        w, k = wts[l], kept[l]
        zlow, zhigh = edges(dz16, edge)
        upper = dy16
        dz16 = advance(dz16)
        dh16, d_taps, dln2, dx2, dy2, dq16, dkv = run(
            11,
            block_back_body,
            [wide16, ((9, FF), f32), ln_out, full, half, half, ((team * keys_own, 2 * D), f32)],
            k["h16"], k["hlow"], k["hhigh"], dz16, zlow, zhigh, w["taps"], w["w1"], k["x2"], w["gain"], dx,
            w["wo"], k["q16"], k["kv"], shut, k["lse"],
            place=ends,
        )
        if waiting is not None:
            first, _ = tied(waiting[0], dkv)
            pieces.append([0, weight_grads(first, *waiting[1:])])
        dkv_own = own_keys(dkv)
        dq16 = advance(dq16)
        shared = (dkv_own, w["wkv"], k["r"], w["gain"], dq16, w["wq"], w["wsr"], k["x"], dx2)
        if l:
            dr16, dln, dx, dy16, dz16, edge = run(
                6,
                join_back_body,
                [((keys_own, D), bf16), ((4, D), f32), full, half, wide16, row16],
                *shared,
                wts[l - 1]["w2"],
                kept[l - 1]["slope"],
                place=ends,
            )
        else:
            dr16, dln, de16, dln_first = run(
                3,
                first_back_body,
                [((keys_own, D), bf16), ((4, D), f32), half, ln_out],
                *shared,
                e,
                ln_first,
            )
        waiting = (k["a16"], dq16, k["rn16"], dkv_own, k["o16"], dy2, k["b16"], dh16, dr16, k["g16"], upper)
        grads[l] = (
            d_taps,
            jnp.concatenate([dln[0:2], dln2[0:1]], 0),
            jnp.concatenate([dln[2:4], dln2[1:2]], 0),
        )
    pieces.append([0, weight_grads(*waiting)])
    de16 = advance(de16)
    (d_embed,) = run(3, embed_back_body, [((embed16.shape[0], D), f32)], patch_own, de16)
    d_embed = advance(d_embed)
    d_gain = jnp.concatenate([dln_first[0:1]] + [g[1] for g in grads] + [dln_last[0:1]], 0)
    d_bias = jnp.concatenate([dln_first[1:2]] + [g[2] for g in grads] + [dln_last[1:2]], 0)
    d_taps = jnp.stack([g[0] for g in grads])
    rest = [
        d_embed.reshape(n_dp, -1),
        d_taps.reshape(LAYERS * 9, n_dp, -1).transpose(1, 0, 2).reshape(n_dp, -1),
        d_gain.reshape(-1, n_dp, row_in).transpose(1, 0, 2).reshape(n_dp, -1),
        d_bias.reshape(-1, n_dp, row_in).transpose(1, 0, 2).reshape(n_dp, -1),
    ]
    cuts = [0]
    for part in rest:
        cuts.append(cuts[-1] + part.shape[1])
    rest = padded_rest(rest)

    late = 3

    def together(parts):
        return to_bf(jnp.concatenate(parts, 0))

    if paired:
        assert all(p[0] > len(stages) + 1 for p in pieces[: LAYERS + 1 - late])
        own_rows = 2 * sub_in
        parts = [p[1] for p in pieces[1 : LAYERS + 1 - late]]
        early = together([parts[0][:own_rows], *parts[1:], parts[0][own_rows:]])
        rest, early = tied(rest, early)
        rest = advance(rest)
        last = plane_second(plane_first(pair_sum(rest)))
        last = dp_sum(jnp.concatenate([pieces[-1][1], last], 1), bf16)
        sums = [None] * (LAYERS + 1 - late) + [p[1] for p in pieces[LAYERS + 1 - late : -1]] + [last]
    else:
        sums = [whole_sum([p[1]]) for p in pieces + [[0, rest]]]
        early = together(sums[1 : LAYERS + 1 - late] + sums[:1])
    early_got = lax.all_gather(early, "seq", axis=0, tiled=False)
    late_part, early_got = tied(together(sums[LAYERS + 1 - late :]), early_got)
    late_got = lax.all_gather(late_part, "seq", axis=0, tiled=False)
    head_start = (LAYERS - late) * 2 * sub_in
    g_head = early_got[:, head_start:].reshape(-1)[: head_w.size].reshape(head_w.shape).astype(f32)
    flat = late_got[:, late * 2 * sub_in :].reshape(-1).astype(f32)
    flat = [flat[a:b] for a, b in zip(cuts, cuts[1:])]
    shards = (
        flat[0].reshape(embed_w.shape),
        None,
        None,
        flat[1].reshape(dw_kernel.shape),
        g_head,
        flat[2].reshape(norm_gain.shape),
        flat[3].reshape(norm_bias.shape),
    )

    gsq_local = sum(jnp.sum(jnp.square(g.astype(f32))) for g in (early_got, late_got))
    wsq_local = group_sums(tuple((w * w for w in masters)))
    gsq, wsq, loss = lax.psum((gsq_local, wsq_local, loss_seq), "dp")
    grad_norm = jnp.sqrt(gsq)
    factor = jnp.minimum(1.0, clip_limit / grad_norm)

    proj_spec = pl.BlockSpec((1,) + in_proj.shape[1:], lambda l: (l, 0, 0))
    down_spec = pl.BlockSpec((1,) + down_proj.shape[1:], lambda l: (l, 0, 0, 0))
    block = (n_seq, 2 * sub_in, wide)
    blocks_of = [early_got, late_got]
    if 2 * sub_in % 8:
        block = (n_seq, 1, 2 * sub_in, wide)
        counts = (LAYERS - late, late)
        blocks_of = [
            g[:, : n * 2 * sub_in].reshape(n_seq, n, 2 * sub_in, wide)
            for g, n in zip(blocks_of, counts)
        ]
    tail = (0,) * (len(block) - 2)
    got = pl.pallas_call(
        functools.partial(update_body, cols, subs, late),
        grid=(LAYERS,),
        out_shape=[jax.ShapeDtypeStruct(in_proj.shape, f32)] * 3
        + [jax.ShapeDtypeStruct(down_proj.shape, f32)] * 3
        + [jax.ShapeDtypeStruct((LAYERS, 2, LANES), f32)],
        in_specs=[
            pl.BlockSpec(memory_space=pltpu.SMEM),
            pl.BlockSpec(block, lambda l: (0, jnp.minimum(LAYERS - 1 - l, LAYERS - 1 - late), *tail)),
            pl.BlockSpec(block, lambda l: (0, jnp.maximum(late - 1 - l, 0), *tail)),
        ]
        + [proj_spec] * 3
        + [down_spec] * 3,
        out_specs=[proj_spec] * 3 + [down_spec] * 3 + [pl.BlockSpec((1, 2, LANES), lambda l: (l, 0, 0))],
        compiler_params=pltpu.CompilerParams(vmem_limit_bytes=56 << 20),
        cost_estimate=cost(25),
    )(factor.reshape(1), *blocks_of, in_proj, m_proj, v_proj, down_proj, m_down, v_down)
    big = {1: got[0:3], 2: got[3:6]}
    new_m, new_v, updates = ([], [], [])
    for n, (w, g, m, v) in enumerate(zip(masters, shards, firsts, seconds)):
        m2, v2, u = big[n] if n in big else moments(w, g * factor, m, v)
        new_m.append(m2)
        new_v.append(v2)
        updates.append(u)
    usq = lax.psum(
        group_sums(tuple((u * u for u in updates)), [got[6][:, 0, 0], got[6][:, 1, 0]]), "dp"
    )
    wnorm = jnp.sqrt(wsq)
    unorm = jnp.sqrt(usq)
    ratio = wnorm / unorm
    spreads = spread_ratio(ratio)
    new_w = [w - learn_rate * r * u for w, r, u in zip(masters, spreads, updates)]
    stats = jnp.stack([wnorm, unorm])
    return (loss, grad_norm, stats, ratio, *new_w, *new_m, *new_v)


def solution(mesh):
    placed = (
        P("dp", None),
        P(None, "dp", None),
        P(None, None, "dp", None),
        P(None, None, "dp"),
        P("dp", None),
        P(None, "dp"),
        P(None, "dp"),
    )
    in_specs = (
        P("dp", "seq", None, None),
        P("dp", None),
        P("dp"),
        P("dp"),
        P("dp"),
    ) + placed * 3
    out_specs = (P(), P(), P(), P()) + placed * 3
    return jax.shard_map(
        per_device, mesh=mesh, in_specs=in_specs, out_specs=out_specs, check_vma=False
    )
```

```python
import functools

import jax
import jax.numpy as jnp
from jax import lax
from jax.experimental import pallas as pl
from jax.experimental.pallas import tpu as pltpu
from jax.sharding import PartitionSpec as P

D = 320
HEADS = 5
HD = 64
FF = 1280
CLS = 1000
W = 64
HALF = W // 2
LAYERS = 6
STEP = 5
LANES = 128


norm_eps = 1e-06
scale_qk = 0.125
big_neg = -1e30
beta_one = 0.9
beta_two = 0.999
lamb_eps = 1e-06
decay_rate = 0.01
learn_rate = 0.3
clip_limit = 0.1
root_half = 0.7071067811865476
root_two_pi = 0.3989422804014327
precise = lax.Precision.HIGHEST

f32 = jnp.float32
bf16 = jnp.bfloat16


def to_bf(v):
    return v.astype(bf16)


def dot(a, b):
    return jnp.dot(a, b, preferred_element_type=f32)


def dot_nt(a, b, precision=None):
    return lax.dot_general(
        a, b, (((1,), (1,)), ((), ())), precision=precision, preferred_element_type=f32
    )


def contract(a, b, precision=None):
    return lax.dot_general(
        a, b, (((0,), (0,)), ((), ())), precision=precision, preferred_element_type=f32
    )


def norm_parts(v):
    center = v - jnp.mean(v, -1, keepdims=True)
    spread = jnp.mean(center * center, -1, keepdims=True)
    scale = lax.rsqrt(spread + norm_eps)
    return center * scale, scale


def layer_norm(v, gain, bias):
    return norm_parts(v)[0] * gain + bias


def norm_back(v, gain, grad):
    unit, scale = norm_parts(v)
    dgain = jnp.sum(grad * unit, 0, keepdims=True)
    dbias = jnp.sum(grad, 0, keepdims=True)
    t = grad * gain
    dv = scale * (
        t - jnp.mean(t, -1, keepdims=True) - unit * jnp.mean(t * unit, -1, keepdims=True)
    )
    return dv, dgain, dbias


def cost(us):
    return pl.CostEstimate(flops=int(us * 1e8), bytes_accessed=int(us * 1e5), transcendentals=0)


def run(us, body, outs, *args, place=None):
    vm = pl.BlockSpec(memory_space=pltpu.VMEM)
    scalars = [] if place is None else [place]
    return pl.pallas_call(
        body,
        out_shape=[jax.ShapeDtypeStruct(s, d) for s, d in outs],
        in_specs=[pl.BlockSpec(memory_space=pltpu.SMEM)] * len(scalars) + [vm] * len(args),
        out_specs=[vm] * len(outs),
        compiler_params=pltpu.CompilerParams(vmem_limit_bytes=48 << 20),
        cost_estimate=cost(us),
    )(*scalars, *args)


def cells_of(v):
    rows = v.shape[0] // W
    split = v.reshape(rows // 2, 2, 2, HALF, v.shape[1])
    return [split[:, k // 2, k % 2].reshape(-1, v.shape[1]) for k in range(4)]


def attention_inputs(x, gain, bias, wq, wsr, wkv, a_ref, q_ref, r_ref, rn_ref, kv_ref):
    a = to_bf(layer_norm(x, gain[0:1], bias[0:1]))
    a_ref[...] = a
    q_ref[...] = to_bf(dot(a, wq[...]))
    total = None
    for k, cell in enumerate(cells_of(a)):
        part = dot(cell, wsr[k * D : (k + 1) * D, :])
        total = part if total is None else total + part
    r_ref[...] = total
    rn = to_bf(layer_norm(total, gain[1:2], bias[1:2]))
    rn_ref[...] = rn
    kv_ref[...] = to_bf(dot(rn, wkv[...]))


def embed_body(p_ref, w_ref, ln_ref, e_ref, x_ref):
    e = dot(p_ref[...], w_ref[...])
    e_ref[...] = e
    x_ref[...] = layer_norm(e, ln_ref[0:1], ln_ref[1:2])


def embed_back_body(p_ref, de_ref, dw_ref):
    dw_ref[...] = contract(p_ref[...], de_ref[...])


def first_body(x_ref, gain, bias, wq, wsr, wkv, *outs):
    attention_inputs(x_ref[...], gain, bias, wq, wsr, wkv, *outs)


def middle_body(
    place, q_ref, kv_ref, ok_ref, x_ref, gain, bias, wo, w1, o_ref, lse_ref, x2_ref, b_ref, h_ref, edge_ref
):
    q = q_ref[...] * jnp.asarray(scale_qk, bf16)
    keys = kv_ref.shape[0]
    kv = kv_ref[...]
    shut = jnp.broadcast_to(ok_ref[...], (keys, q.shape[0]))
    q_t = q.T
    v_t = kv[:, D:].T
    parts = []
    for head in range(HEADS):
        low, high = head * HD, (head + 1) * HD
        s = dot(kv[:, low:high], q_t[low:high, :]) + shut
        top = jnp.max(s, 0, keepdims=True)
        expo = jnp.exp(s - top)
        total = jnp.sum(expo, 0, keepdims=True)
        lse_ref[head : head + 1, :] = top + jnp.log(total)
        p = to_bf(expo * (1.0 / total))
        parts.append(dot(v_t[low:high, :], p))
    o = to_bf(jnp.concatenate(parts, 0).T)
    o_ref[...] = o
    x2 = x_ref[...] + dot(o, wo[...])
    x2_ref[...] = x2
    b = to_bf(layer_norm(x2, gain[2:3], bias[2:3]))
    b_ref[...] = b
    h_ref[...] = to_bf(dot(b, w1[...]))
    send_edge(place, h_ref, edge_ref)


def shift_down(v):
    index = lax.broadcasted_iota(jnp.int32, v.shape, 0)
    return jnp.where(index == 0, 0.0, pltpu.roll(v, 1, 0))


def shift_up(v):
    index = lax.broadcasted_iota(jnp.int32, v.shape, 0)
    return jnp.where(index == v.shape[0] - 1, 0.0, pltpu.roll(v, v.shape[0] - 1, 0))


def from_left(v):
    return jnp.concatenate([shift_down(v[HALF:]), v[:HALF]], 0)


def from_right(v):
    return jnp.concatenate([v[HALF:], shift_up(v[:HALF])], 0)


def row_of(main, near, i, rows, lanes):
    place, low, high = near
    if i < 0:
        return jnp.where(place[0] > 0, low[:, lanes].astype(f32), 0.0)
    if i >= rows:
        return jnp.where(place[1] > 0, high[:, lanes].astype(f32), 0.0)
    return main[i * W : (i + 1) * W, lanes].astype(f32)


def send_edge(place, main, edge_ref):
    start = pl.multiple_of(jnp.where(place[0] > 0, 0, main.shape[0] - W), W)
    edge_ref[...] = main[pl.ds(start, W), :]


def conv_gelu(h_ref, ends, taps_ref, g_ref, slope_ref):
    rows = h_ref.shape[0] // W

    def chunk(c, carry):
        lanes = pl.ds(pl.multiple_of(c * LANES, LANES), LANES)
        taps = [taps_ref[k : k + 1, lanes] for k in range(9)]
        near = [row_of(h_ref, ends, i, rows, lanes) for i in (-1, 0)]
        for i in range(rows):
            near.append(row_of(h_ref, ends, i + 1, rows, lanes))
            sums = [
                taps[j] * near[0] + taps[3 + j] * near[1] + taps[6 + j] * near[2] for j in range(3)
            ]
            z = sums[1] + from_left(sums[0]) + from_right(sums[2])
            phi = 0.5 + 0.5 * lax.erf(z * root_half)
            here = slice(i * W, (i + 1) * W)
            g_ref[here, lanes] = to_bf(z * phi)
            slope_ref[here, lanes] = phi + z * (jnp.exp(-0.5 * z * z) * root_two_pi)
            near = near[1:]
        return carry

    lax.fori_loop(0, FF // LANES, chunk, 0)


def last_body(place, h_ref, low_ref, high_ref, taps_ref, x2_ref, w2, ln_ref, ok_ref, g_ref, slope_ref, x_ref, sum_ref):
    conv_gelu(h_ref, (place, low_ref, high_ref), taps_ref, g_ref, slope_ref)
    x = x2_ref[...] + dot(g_ref[...], w2[...])
    x_ref[...] = x
    fin = layer_norm(x, ln_ref[0:1], ln_ref[1:2])
    sum_ref[...] = jnp.sum(fin * ok_ref[...], 0, keepdims=True)


def join_body(
    place, h_ref, low_ref, high_ref, taps_ref, x2_ref, w2, gain, bias, wq, wsr, wkv, g_ref, slope_ref, x_ref, *outs
):
    conv_gelu(h_ref, (place, low_ref, high_ref), taps_ref, g_ref, slope_ref)
    x = x2_ref[...] + dot(g_ref[...], w2[...])
    x_ref[...] = x
    attention_inputs(x, gain, bias, wq, wsr, wkv, *outs)


def gelu_back(place, dx, w2, slope_ref, dy_ref, dz_ref, edge_ref):
    dy = to_bf(dx)
    dy_ref[...] = dy
    dg = to_bf(dot_nt(dy, w2[...])).astype(f32)
    dz_ref[...] = to_bf(dg * slope_ref[...])
    send_edge(place, dz_ref, edge_ref)


def head_body(
    images,
    place,
    pool_ref,
    count_ref,
    head_ref,
    target_ref,
    x_ref,
    ln_ref,
    ok_ref,
    w2,
    slope_ref,
    loss_ref,
    pooled_ref,
    dlog_ref,
    dln_ref,
    dx_ref,
    dy_ref,
    dz_ref,
    edge_ref,
):
    count = count_ref[...]
    pooled = to_bf(pool_ref[...] / count)
    pooled_ref[...] = pooled
    logits = dot(jnp.broadcast_to(pooled.astype(f32), (16, D)).astype(bf16), head_ref[...])[0:1]
    shifted = logits - jnp.max(logits, -1, keepdims=True)
    logp = shifted - jnp.log(jnp.sum(jnp.exp(shifted), -1, keepdims=True))
    target = target_ref[...]
    loss_ref[...] = jnp.sum(target * logp, -1, keepdims=True) * (-1.0 / images)
    dlog = to_bf((jnp.exp(logp) - target) * (1.0 / images))
    dlog_ref[...] = dlog
    wide = jnp.broadcast_to(dlog.astype(f32), (16, CLS)).astype(bf16)
    dpool = dot_nt(wide, head_ref[...])[0:1] / count
    dx, dgain, dbias = norm_back(x_ref[...], ln_ref[0:1], ok_ref[...] * dpool)
    dln_ref[0:1, :] = dgain
    dln_ref[1:2, :] = dbias
    dx_ref[...] = dx
    gelu_back(place, dx, w2, slope_ref, dy_ref, dz_ref, edge_ref)


def conv_back(h_ref, hends, dz_ref, zends, taps_ref, dh_ref, dtaps_ref):
    rows = h_ref.shape[0] // W

    def chunk(c, carry):
        lanes = pl.ds(pl.multiple_of(c * LANES, LANES), LANES)
        taps = [taps_ref[k : k + 1, lanes] for k in range(9)]
        acc = [jnp.zeros((8, LANES), f32) for _ in range(9)]

        def views(i):
            v = row_of(dz_ref, zends, i, rows, lanes)
            return [from_right(v), v, from_left(v)]

        near = [views(-1), views(0)]
        hear = [row_of(h_ref, hends, i, rows, lanes) for i in (-1, 0)]
        for i in range(rows):
            near.append(views(i + 1))
            hear.append(row_of(h_ref, hends, i + 1, rows, lanes))
            dh = None
            for di in range(3):
                for dj in range(3):
                    part = taps[3 * di + dj] * near[2 - di][dj]
                    dh = part if dh is None else dh + part
            dh_ref[i * W : (i + 1) * W, lanes] = to_bf(dh)
            for di in range(3):
                for dj in range(3):
                    prod = (hear[di] * near[1][dj]).reshape(W // 8, 8, LANES)
                    acc[3 * di + dj] = acc[3 * di + dj] + jnp.sum(prod, 0)
            near = near[1:]
            hear = hear[1:]
        for k in range(9):
            dtaps_ref[k : k + 1, lanes] = jnp.sum(acc[k], 0, keepdims=True)
        return carry

    lax.fori_loop(0, FF // LANES, chunk, 0)


def block_back_body(
    place,
    h_ref,
    hlow_ref,
    hhigh_ref,
    dz_ref,
    zlow_ref,
    zhigh_ref,
    taps_ref,
    w1,
    x2_ref,
    gain,
    dx_ref,
    wo,
    q_ref,
    kv_ref,
    ok_ref,
    lse_ref,
    dh_ref,
    dtaps_ref,
    dln_ref,
    dx2_ref,
    dy_ref,
    dq_ref,
    dkv_ref,
):
    conv_back(
        h_ref, (place, hlow_ref, hhigh_ref), dz_ref, (place, zlow_ref, zhigh_ref), taps_ref, dh_ref, dtaps_ref
    )
    db = dot_nt(dh_ref[...], w1[...])
    dln, dgain, dbias = norm_back(x2_ref[...], gain[2:3], db)
    dln_ref[0:1, :] = dgain
    dln_ref[1:2, :] = dbias
    dx2 = dx_ref[...] + dln
    dx2_ref[...] = dx2
    dy = to_bf(dx2)
    dy_ref[...] = dy
    do_t = to_bf(dot_nt(wo[...], dy))
    q = q_ref[...] * jnp.asarray(scale_qk, bf16)
    q_t = q.T
    keys = kv_ref.shape[0]
    kv = kv_ref[...]
    k_t = (kv[:, :D] * jnp.asarray(scale_qk, bf16)).T
    shut = jnp.broadcast_to(ok_ref[...], (keys, q.shape[0]))
    dq_parts, dk_parts, dv_parts = ([], [], [])
    for head in range(HEADS):
        low, high = head * HD, (head + 1) * HD
        s = dot(kv[:, low:high], q_t[low:high, :]) + shut
        p = jnp.exp(s - lse_ref[head : head + 1, :])
        dp = dot(kv[:, D + low : D + high], do_t[low:high, :])
        dv_parts.append(dot_nt(do_t[low:high, :], to_bf(p)))
        ds = to_bf(p * (dp - jnp.sum(p * dp, 0, keepdims=True)))
        dq_parts.append(dot(k_t[low:high, :], ds))
        dk_parts.append(dot_nt(q_t[low:high, :], ds))
    dq_ref[...] = to_bf(jnp.concatenate(dq_parts, 0).T)
    dkv_ref[...] = jnp.concatenate(dk_parts + dv_parts, 0).T


def inputs_back(dkv, wkv, r_ref, gain, dq_ref, wq, wsr, x_ref, dx2_ref, dr_ref, dln_ref):
    w_kv = wkv[...].astype(f32)
    drn = dot_nt(dkv, w_kv, precise)
    dr, dgain1, dbias1 = norm_back(r_ref[...], gain[1:2], drn)
    dr = to_bf(dr)
    dr_ref[...] = dr
    rows = x_ref.shape[0] // W
    cells = [
        dot_nt(dr, wsr[k * D : (k + 1) * D, :]).reshape(rows // 2, 1, 1, HALF, D) for k in range(4)
    ]
    placed = jnp.concatenate(
        [jnp.concatenate(cells[0:2], 2), jnp.concatenate(cells[2:4], 2)], 1
    ).reshape(rows * W, D)
    da = dot_nt(dq_ref[...], wq[...]) + placed
    dln, dgain0, dbias0 = norm_back(x_ref[...], gain[0:1], da)
    for k, row in enumerate((dgain0, dgain1, dbias0, dbias1)):
        dln_ref[k : k + 1, :] = row
    return dx2_ref[...] + dln


def join_back_body(
    place, dkv_ref, wkv, r_ref, gain, dq_ref, wq, wsr, x_ref, dx2_ref, w2, slope_ref,
    dr_ref, dln_ref, dx_ref, dy_ref, dz_ref, edge_ref
):
    dx = inputs_back(dkv_ref[...], wkv, r_ref, gain, dq_ref, wq, wsr, x_ref, dx2_ref, dr_ref, dln_ref)
    dx_ref[...] = dx
    gelu_back(place, dx, w2, slope_ref, dy_ref, dz_ref, edge_ref)


def first_back_body(
    dkv_ref, wkv, r_ref, gain, dq_ref, wq, wsr, x_ref, dx2_ref, e_ref, ln_ref, dr_ref, dln_ref, de_ref, dle_ref
):
    dx = inputs_back(dkv_ref[...], wkv, r_ref, gain, dq_ref, wq, wsr, x_ref, dx2_ref, dr_ref, dln_ref)
    de, dgain, dbias = norm_back(e_ref[...], ln_ref[0:1], dx)
    de_ref[...] = to_bf(de)
    dle_ref[0:1, :] = dgain
    dle_ref[1:2, :] = dbias


def weight_grads_body(
    n_dp, cols, subs, core_ref, a_ref, dq_ref, rn_ref, dkv_ref, o_ref, dy2_ref, b_ref, dh_ref, dr_ref, g_ref, dy_ref, *refs
):
    outs, (proj, down) = refs[:-2], refs[-2:]
    a = a_ref[...]
    proj[:, :D] = contract(a, dq_ref[...])
    proj[:, D : 3 * D] = contract(rn_ref[...].astype(f32), dkv_ref[...], precise)
    proj[:, 3 * D : 4 * D] = contract(o_ref[...], dy2_ref[...])
    proj[:, 4 * D :] = contract(b_ref[...], dh_ref[...])
    dr = dr_ref[...]
    for k, cell in enumerate(cells_of(a)):
        down[k * D : (k + 1) * D, :D] = contract(cell, dr)
    down[:, D:] = contract(g_ref[...], dy_ref[...])
    rows = D // n_dp
    sub = rows // subs
    wide = (4 * D + FF) // cols
    down_rows = FF // n_dp
    for c in range(cols):
        for d in range(n_dp):
            for n, out in enumerate(outs):
                for j in range(subs) if len(outs) == 1 else (None,):
                    if j is None:
                        k = core_ref[0] if n == 0 else 1 - core_ref[0]
                        at = (c ^ core_ref[1], d)
                    else:
                        k = j
                        at = (c, j, d)
                    start = d * rows + k * sub
                    low = d * down_rows + (c * subs + k) * (down_rows // (cols * subs))
                    if j is None:
                        start = pl.multiple_of(start, 8)
                        low = pl.multiple_of(low, 8)
                    out[(*at, slice(0, sub))] = proj[pl.ds(start, sub), c * wide : (c + 1) * wide]
                    out[(*at, slice(sub, 2 * sub))] = down[pl.ds(low, sub), :]


def moments(w, g, m, v):
    m2 = beta_one * m + (1.0 - beta_one) * g
    v2 = beta_two * v + (1.0 - beta_two) * g * g
    u = (
        m2 / (1.0 - beta_one**STEP) / (jnp.sqrt(v2 / (1.0 - beta_two**STEP)) + lamb_eps)
        + decay_rate * w
    )
    return m2, v2, u


def update_body(
    cols, subs, late, factor_ref, early_ref, late_ref, wp, mp, vp, wd, md, vd, mp2, vp2, up, md2, vd2, ud, sums
):
    factor = factor_ref[0]
    layer = pl.program_id(0)
    sub = wp.shape[1] // subs
    wide = wp.shape[2] // cols

    def go(g_ref):
        squares = [0.0, 0.0]

        def put(n, at, refs, outs, g):
            new = moments(refs[0][at], g * factor, refs[1][at], refs[2][at])
            for out, value in zip(outs, new):
                out[at] = value
            squares[n] = squares[n] + jnp.sum(new[2] * new[2], 0, keepdims=True)

        for c in range(cols):
            for k in range(subs):
                g = g_ref[c * subs + k].astype(f32).reshape(2 * sub, wide)
                at = (0, slice(k * sub, (k + 1) * sub), slice(c * wide, (c + 1) * wide))
                put(0, at, (wp, mp, vp), (mp2, vp2, up), g[:sub])
                rows = slice((c * subs + k) * sub, (c * subs + k + 1) * sub)
                for half in range(2):
                    at = (0, half, rows, slice(0, D))
                    put(1, at, (wd, md, vd), (md2, vd2, ud), g[sub:, half * D : (half + 1) * D])
        lane = lax.broadcasted_iota(jnp.int32, (1, LANES), 1)
        total = jnp.zeros((1, LANES), f32)
        for n in range(2):
            value = jnp.broadcast_to(jnp.sum(squares[n], 1, keepdims=True), (1, LANES))
            total = jnp.where(lane == 4 + n * LAYERS + layer, value, total)
        sums[0] = jnp.broadcast_to(total, sums.shape[1:])

    pl.when(layer >= late)(lambda: go(early_ref))
    pl.when(layer < late)(lambda: go(late_ref))


def group_sums(arrs, layered=None):
    embed, proj, downs, taps, head, gains, biases = arrs
    slot = lax.broadcasted_iota(jnp.int32, (1, 4 + 3 * LAYERS), 1)

    def placed(values, start):
        at = lax.broadcasted_iota(jnp.int32, (values.shape[0], 1), 0) + start
        return jnp.sum(jnp.where(at == slot, values[:, None], 0.0), 0)

    total = placed(jnp.sum(taps, (1, 2)), 4 + 2 * LAYERS)
    for n, a in enumerate((embed, head, gains, biases)):
        total = total + jnp.where(slot[0] == n, jnp.sum(a), 0.0)
    if layered is not None:
        return total + layered
    for n, a in enumerate((proj, downs)):
        total = total + placed(jnp.sum(a.reshape(a.shape[0], -1), 1), 4 + n * LAYERS)
    return total


def spread_ratio(ratio):
    return (
        ratio[0],
        ratio[4 : 4 + LAYERS].reshape(LAYERS, 1, 1),
        ratio[4 + LAYERS : 4 + 2 * LAYERS].reshape(LAYERS, 1, 1, 1),
        ratio[4 + 2 * LAYERS : 4 + 3 * LAYERS].reshape(LAYERS, 1, 1),
        ratio[1],
        ratio[2],
        ratio[3],
    )


def per_device(
    patches,
    valid,
    labels,
    partners,
    mix,
    embed_w,
    in_proj,
    down_proj,
    dw_kernel,
    head_w,
    norm_gain,
    norm_bias,
    m_embed,
    m_proj,
    m_down,
    m_taps,
    m_head,
    m_gain,
    m_bias,
    v_embed,
    v_proj,
    v_down,
    v_taps,
    v_head,
    v_gain,
    v_bias,
):
    masters = (embed_w, in_proj, down_proj, dw_kernel, head_w, norm_gain, norm_bias)
    firsts = (m_embed, m_proj, m_down, m_taps, m_head, m_gain, m_bias)
    seconds = (v_embed, v_proj, v_down, v_taps, v_head, v_gain, v_bias)
    n_seq = lax.axis_size("seq")
    n_dp = lax.axis_size("dp")
    seq_pos = lax.axis_index("seq")
    img_dev, rows = (patches.shape[0], patches.shape[1])
    images = img_dev * n_dp

    team = n_seq
    while team * img_dev > n_seq:
        team //= 2
    blocks = n_seq // team
    rows_own = rows * blocks
    tok = rows_own * W
    keys_own = tok // 4
    image = jnp.minimum(seq_pos // team, img_dev - 1)
    busy = seq_pos // team < img_dev
    place = seq_pos % team

    def between(shift, wrap):
        pairs = []
        for base in range(0, n_seq, team):
            for h in range(team):
                if wrap or 0 <= h + shift < team:
                    pairs.append((base + (h + shift) % team, base + h))
        return pairs

    ends = jnp.stack([place > 0, place < team - 1]).astype(jnp.int32)

    def edges(v, edge):
        if team == 2:
            other = lax.ppermute(edge, "seq", between(1, True))
            return other, other
        low = lax.ppermute(v[-W:], "seq", between(-1, False))
        high = lax.ppermute(v[:W], "seq", between(1, False))
        return low, high

    def all_keys(v):
        return jnp.concatenate(
            [v] + [lax.ppermute(v, "seq", between(j, True)) for j in range(1, team)], 0
        )

    def own_keys(v):
        total = v[:keys_own]
        for j in range(1, team):
            part = v[j * keys_own : (j + 1) * keys_own]
            total = total + lax.ppermute(part, "seq", between(-j, True))
        return total

    back_block = seq_pos % blocks
    routes = [
        [
            (blocks * h + (i + r) % blocks, team * i + h)
            for i in range(img_dev)
            for h in range(team)
        ]
        for r in range(blocks)
    ]

    def to_team(v):
        got = []
        for r, pairs in enumerate(routes):
            send = lax.dynamic_index_in_dim(
                v, jnp.minimum((back_block - r) % blocks, img_dev - 1), 0, keepdims=False
            )
            got.append(lax.ppermute(send, "seq", pairs))
        twice = jnp.stack(got + got)
        own = lax.dynamic_slice_in_dim(twice, (blocks - image) % blocks, blocks, 0)
        return own.reshape(tok, -1)

    cols = 4
    subs = n_seq // cols
    row_in = D // n_dp
    sub_in = row_in // subs
    wide = in_proj.shape[2] // cols
    down_rows = down_proj.shape[2] // n_seq
    core = seq_pos % subs

    def part_of(flat):
        size = -(-flat.shape[0] // (wide * n_seq)) * wide * n_seq
        flat = jnp.pad(flat, (0, size - flat.shape[0])).reshape(n_seq, -1, wide)
        return lax.dynamic_index_in_dim(flat, seq_pos, 0, keepdims=False)

    def layer_part(l):
        block = lax.dynamic_slice(
            in_proj[l], (core * sub_in, (seq_pos // subs) * wide), (sub_in, wide)
        )
        lower = lax.dynamic_slice_in_dim(down_proj[l], seq_pos * down_rows, down_rows, 1)
        return [to_bf(block), to_bf(jnp.concatenate([lower[0], lower[1]], 1))]

    def gathered(parts):
        sizes = [p.shape[0] for p in parts]
        got = lax.all_gather(jnp.concatenate(parts, 0), ("dp", "seq"), axis=0, tiled=False)
        return got, sizes

    def cut(got, sizes):
        got = got.reshape(n_dp, n_seq, sum(sizes), wide)
        starts = [sum(sizes[:i]) for i in range(len(sizes))]
        return [got[:, :, a : a + n] for a, n in zip(starts, sizes)]

    def proj_of(got):
        got = got.reshape(n_dp, cols, subs, sub_in, wide).transpose(0, 2, 3, 1, 4)
        return got.reshape(D, cols * wide)

    dp_pos = lax.axis_index("dp")

    def over_dp(v):
        got = [v] + [
            lax.ppermute(v, "dp", [((d + j) % n_dp, d) for d in range(n_dp)])
            for j in range(1, n_dp)
        ]
        return lax.dynamic_slice_in_dim(jnp.stack(got + got), (n_dp - dp_pos) % n_dp, n_dp, 0)

    embed16 = over_dp(to_bf(embed_w)).reshape(-1, D)
    taps16 = over_dp(to_bf(dw_kernel).reshape(LAYERS * 9, -1))
    norms16 = over_dp(to_bf(jnp.stack([norm_gain, norm_bias])))
    taps32 = taps16.transpose(1, 0, 2).reshape(LAYERS, 9, FF).astype(f32)
    norms32 = norms16.transpose(1, 2, 0, 3).reshape(2, -1, D).astype(f32)
    gain32, bias32 = norms32[0], norms32[1]
    groups = [[0, 1, 2, 3], [4, 5]]
    extra = [[], [part_of(to_bf(head_w).reshape(-1))]]

    def layers_of(got, count):
        return [(proj_of(got[2 * i]), got[2 * i + 1].reshape(FF, 2 * D)) for i in range(count)]

    parts_of = [more + [p for l in members for p in layer_part(l)] for members, more in zip(groups, extra)]
    raw = [gathered(parts_of[0])]
    first_late = groups[1][0]

    def own(v):
        return lax.dynamic_index_in_dim(v, image, 0, keepdims=False)

    wanted = own(partners)
    partner_label = jnp.zeros((), jnp.int32)
    for j in range(n_dp):
        other = labels
        if j:
            other = lax.ppermute(labels, "dp", [((d + j) % n_dp, d) for d in range(n_dp)])
        index = ((dp_pos + j) % n_dp) * img_dev + jnp.arange(img_dev)
        partner_label = partner_label + jnp.sum(jnp.where(index == wanted, other, 0))
    valid_own = own(valid)
    tid = lax.broadcasted_iota(jnp.int32, (tok, 1), 0)
    within = tid % W
    row_id = place * rows_own + tid // W
    col_id = 2 * (within % HALF) + within // HALF
    okay = ((row_id < valid_own[0]) & (col_id < valid_own[1]) & busy).astype(f32)
    kid = lax.broadcasted_iota(jnp.int32, (team * keys_own, 1), 0)
    segment = (place + kid // keys_own) % team
    key_row = segment * (rows_own // 2) + (kid % keys_own) // HALF
    key_ok = (2 * key_row < valid_own[0]) & (2 * (kid % HALF) < valid_own[1])
    shut = jnp.where(key_ok, 0.0, big_neg).astype(f32)
    count = (valid_own[0] * valid_own[1]).astype(f32).reshape(1, 1)
    classes = lax.broadcasted_iota(jnp.int32, (1, CLS), 1)
    mix_own = own(mix)
    target = mix_own * (classes == own(labels)).astype(f32) + (1.0 - mix_own) * (
        classes == partner_label
    ).astype(f32)

    def weights(l, layer):
        base = 1 + 3 * l
        return dict(
            wq=layer[0][:, :D],
            wkv=layer[0][:, D : 3 * D],
            wo=layer[0][:, 3 * D : 4 * D],
            w1=layer[0][:, 4 * D :],
            wsr=layer[1][:, :D],
            w2=layer[1][:, D:],
            taps=taps32[l],
            gain=gain32[base : base + 3],
            bias=bias32[base : base + 3],
        )

    full = ((tok, D), f32)
    ln_first = jnp.stack([gain32[0], bias32[0]])
    spread = patches.reshape(img_dev, rows, HALF, 2, -1).transpose(0, 1, 3, 2, 4)
    patch_own = to_team(spread.reshape(img_dev, rows * W, -1))
    e, x = run(2, embed_body, [full, full], patch_own, embed16, ln_first)
    second, x = lax.optimization_barrier((parts_of[1], x))
    raw.append(gathered(second))
    wts = [weights(l, layer) for l, layer in zip(groups[0], layers_of(cut(*raw[0]), len(groups[0])))]
    ln_last = jnp.stack([gain32[-1], bias32[-1]])

    half = ((tok, D), bf16)
    wide16 = ((tok, FF), bf16)
    input_outs = [half, half, ((keys_own, D), f32), ((keys_own, D), bf16), ((keys_own, 2 * D), bf16)]
    ln_out = ((2, D), f32)
    row16 = ((W, FF), bf16)

    w = wts[0]
    a16, q16, r, rn16, kv16 = run(
        2, first_body, input_outs, x, w["gain"], w["bias"], w["wq"], w["wsr"], w["wkv"]
    )
    kept = []
    for l in range(LAYERS):
        w = wts[l]
        kv_all = all_keys(kv16)
        o16, lse, x2, b16, h16, edge = run(
            4,
            middle_body,
            [half, ((HEADS, tok), f32), full, half, wide16, row16],
            q16,
            kv_all,
            shut,
            x,
            w["gain"],
            w["bias"],
            w["wo"],
            w["w1"],
            place=ends,
        )
        hlow, hhigh = edges(h16, edge)
        keep = dict(
            x=x, a16=a16, q16=q16, r=r, rn16=rn16, kv=kv_all, o16=o16, lse=lse, x2=x2, b16=b16,
            h16=h16, hlow=hlow, hhigh=hhigh,
        )
        shared = (h16, hlow, hhigh, w["taps"], x2, w["w2"])
        if l + 1 == first_late:
            got, _ = lax.optimization_barrier((raw[1][0], kv_all))
            got = cut(got, raw[1][1])
            head16 = got[0].reshape(n_dp, -1)[:, : head_w.size].reshape(D, CLS)
            wts += [weights(m, layer) for m, layer in zip(groups[1], layers_of(got[1:], len(groups[1])))]
        if l + 1 < LAYERS:
            n = wts[l + 1]
            keep["g16"], keep["slope"], x, a16, q16, r, rn16, kv16 = run(
                8,
                join_body,
                [wide16, ((tok, FF), f32), full] + input_outs,
                *shared,
                n["gain"],
                n["bias"],
                n["wq"],
                n["wsr"],
                n["wkv"],
                place=ends,
            )
        else:
            keep["g16"], keep["slope"], x, pool = run(
                7,
                last_body,
                [wide16, ((tok, FF), f32), full, ((1, D), f32)],
                *shared,
                ln_last,
                okay,
                place=ends,
            )
        kept.append(keep)

    whole = pool
    for j in range(1, team):
        whole = whole + lax.ppermute(pool, "seq", between(j, True))
    loss_own, pooled16, dlog16, dln_last, dx, dy16, dz16, edge = run(
        4,
        functools.partial(head_body, images),
        [((1, 1), f32), ((1, D), bf16), ((1, CLS), bf16), ln_out, full, half, wide16, row16],
        whole,
        count,
        head16,
        target,
        x,
        ln_last,
        okay,
        wts[-1]["w2"],
        kept[-1]["slope"],
        place=ends,
    )
    chosen = ((place == 0) & busy).astype(f32)
    d_head = pooled16.astype(f32).reshape(D, 1) * dlog16.astype(f32) * chosen
    loss_local = loss_own[0, 0] * busy.astype(f32)
    teams = n_seq // team
    loss_parts = jnp.zeros((teams,), f32)
    for j in range(teams):
        other = loss_local
        if j:
            other = lax.ppermute(
                loss_local, "seq", [((d + j * team) % n_seq, d) for d in range(n_seq)]
            )
        loss_parts = jnp.where(jnp.arange(teams) == (seq_pos // team + j) % teams, other, loss_parts)
    loss_seq = jnp.sum(loss_parts)

    piece = ((cols, n_dp, 2 * sub_in, wide), f32)
    paired = subs == 2 and cols == 4
    chip = seq_pos // subs
    where = jnp.stack([core, chip]).astype(jnp.int32)

    def weight_grads(*args):
        vm = pl.BlockSpec(memory_space=pltpu.VMEM)
        outs = [piece] * 2 if paired else [((cols, subs) + piece[0][1:], f32)]
        return pl.pallas_call(
            functools.partial(weight_grads_body, n_dp, cols, subs),
            out_shape=[jax.ShapeDtypeStruct(s, d) for s, d in outs],
            in_specs=[pl.BlockSpec(memory_space=pltpu.SMEM)] + [vm] * len(args),
            out_specs=[vm] * len(outs),
            scratch_shapes=[pltpu.VMEM((D, cols * wide), f32), pltpu.VMEM((FF, 2 * D), f32)],
            compiler_params=pltpu.CompilerParams(vmem_limit_bytes=48 << 20),
            cost_estimate=cost(6),
        )(where, *args)

    def padded_rest(parts):
        flat = jnp.concatenate(parts, 1)
        size = -(-flat.shape[1] // (16 * wide * n_seq)) * 16 * wide * n_seq
        flat = jnp.pad(flat, ((0, 0), (0, size - flat.shape[1])))
        flat = flat.reshape(n_dp, cols, subs, -1, wide).transpose(1, 2, 0, 3, 4)
        if not paired:
            return [flat]
        flat = jnp.stack([lax.dynamic_index_in_dim(flat, chip ^ j, 0, False) for j in range(cols)])
        return [lax.dynamic_index_in_dim(flat, k, 1, False) for k in (core, 1 - core)]

    def pair_sum(parts):
        mine, send = parts
        return mine + lax.ppermute(send, "seq", [(d ^ 1, d) for d in range(n_seq)])

    def over_chips(v, bit):
        return lax.ppermute(v, "seq", [(d ^ (bit * subs), d) for d in range(n_seq)])

    def plane_first(y):
        cut = y.shape[2] // 2
        one, two = y[:, :, :cut], y[:, :, cut:]
        moved = (to_bf(jnp.stack([one[1], one[3]])), to_bf(jnp.stack([two[2], two[3]])))
        got = (over_chips(moved[0], 1).astype(f32), over_chips(moved[1], 2).astype(f32))
        return [one[0] + got[0][0], one[2] + got[0][1], two[0] + got[1][0], two[1] + got[1][1]]

    def plane_second(parts):
        one = parts[0] + over_chips(parts[1].astype(wire[0]), 2).astype(f32)
        two = parts[2] + over_chips(parts[3].astype(wire[0]), 1).astype(f32)
        return jnp.concatenate([one, two], 1)

    def dp_sum(y):
        def of(j):
            return lax.dynamic_index_in_dim(y, (dp_pos + j) % n_dp, 0, keepdims=False)

        total = of(0)
        for j in range(1, n_dp):
            pairs = [(d, (d + j) % n_dp) for d in range(n_dp)]
            total = total + lax.ppermute(of(j).astype(wire[0]), "dp", pairs).astype(f32)
        return total

    def whole_sum(parts):
        y = jnp.concatenate([p[0] for p in parts], -2)
        y = lax.psum_scatter(y.reshape(-1, wide), "seq", scatter_dimension=0, tiled=True)
        return lax.psum_scatter(y, "dp", scatter_dimension=0, tiled=True)

    def tied(value, others):
        return lax.optimization_barrier((value, others))

    wire = [f32]
    stages = [pair_sum, plane_first, plane_second]
    pieces = []

    def advance(now):
        if not paired:
            return now
        ready = [p for p in pieces if p[0] <= len(stages) + 1]
        now, values = tied(now, [p[1] for p in ready])
        for n, (p, v) in enumerate(zip(ready, values)):
            if p[0] < len(stages):
                p[1] = stages[p[0]](v)
            elif p[0] > len(stages) or p is pieces[0]:
                p[1] = v
            elif p is pieces[1]:
                p[1] = dp_sum(jnp.concatenate([v, pieces[0][1]], 1))
            else:
                p[1] = dp_sum(v)
            p[0] += 1
        return now

    grads = [None] * LAYERS
    pieces.append([0, padded_rest([d_head.reshape(n_dp, -1)])])
    waiting = None
    for l in reversed(range(LAYERS)):
        w, k = wts[l], kept[l]
        zlow, zhigh = edges(dz16, edge)
        upper = dy16
        dz16 = advance(dz16)
        dh16, d_taps, dln2, dx2, dy2, dq16, dkv = run(
            11,
            block_back_body,
            [wide16, ((9, FF), f32), ln_out, full, half, half, ((team * keys_own, 2 * D), f32)],
            k["h16"], k["hlow"], k["hhigh"], dz16, zlow, zhigh, w["taps"], w["w1"], k["x2"], w["gain"], dx,
            w["wo"], k["q16"], k["kv"], shut, k["lse"],
            place=ends,
        )
        if waiting is not None:
            first, _ = tied(waiting[0], dkv)
            pieces.append([0, weight_grads(first, *waiting[1:])])
        dkv_own = own_keys(dkv)
        dq16 = advance(dq16)
        shared = (dkv_own, w["wkv"], k["r"], w["gain"], dq16, w["wq"], w["wsr"], k["x"], dx2)
        if l:
            dr16, dln, dx, dy16, dz16, edge = run(
                6,
                join_back_body,
                [((keys_own, D), bf16), ((4, D), f32), full, half, wide16, row16],
                *shared,
                wts[l - 1]["w2"],
                kept[l - 1]["slope"],
                place=ends,
            )
        else:
            dr16, dln, de16, dln_first = run(
                3,
                first_back_body,
                [((keys_own, D), bf16), ((4, D), f32), half, ln_out],
                *shared,
                e,
                ln_first,
            )
        waiting = (k["a16"], dq16, k["rn16"], dkv_own, k["o16"], dy2, k["b16"], dh16, dr16, k["g16"], upper)
        grads[l] = (
            d_taps,
            jnp.concatenate([dln[0:2], dln2[0:1]], 0),
            jnp.concatenate([dln[2:4], dln2[1:2]], 0),
        )
    wire[0] = bf16
    pieces.append([0, weight_grads(*waiting)])
    de16 = advance(de16)
    (d_embed,) = run(3, embed_back_body, [((embed16.shape[0], D), f32)], patch_own, de16)
    d_embed = advance(d_embed)
    d_gain = jnp.concatenate([dln_first[0:1]] + [g[1] for g in grads] + [dln_last[0:1]], 0)
    d_bias = jnp.concatenate([dln_first[1:2]] + [g[2] for g in grads] + [dln_last[1:2]], 0)
    d_taps = jnp.stack([g[0] for g in grads])
    rest = [
        d_embed.reshape(n_dp, -1),
        d_taps.reshape(LAYERS * 9, n_dp, -1).transpose(1, 0, 2).reshape(n_dp, -1),
        d_gain.reshape(-1, n_dp, row_in).transpose(1, 0, 2).reshape(n_dp, -1),
        d_bias.reshape(-1, n_dp, row_in).transpose(1, 0, 2).reshape(n_dp, -1),
    ]
    cuts = [0]
    for part in rest:
        cuts.append(cuts[-1] + part.shape[1])
    rest = padded_rest(rest)

    late = 3

    def together(parts):
        return to_bf(jnp.concatenate(parts, 0))

    if paired:
        assert all(p[0] > len(stages) + 1 for p in pieces[: LAYERS + 1 - late])
        own_rows = 2 * sub_in
        parts = [p[1] for p in pieces[1 : LAYERS + 1 - late]]
        early = together([parts[0][:own_rows], *parts[1:], parts[0][own_rows:]])
        rest, early = tied(rest, early)
        rest = advance(rest)
        last = plane_second(plane_first(pair_sum(rest)))
        last = dp_sum(jnp.concatenate([pieces[-1][1], last], 1))
        sums = [None] * (LAYERS + 1 - late) + [p[1] for p in pieces[LAYERS + 1 - late : -1]] + [last]
    else:
        sums = [whole_sum([p[1]]) for p in pieces + [[0, rest]]]
        early = together(sums[1 : LAYERS + 1 - late] + sums[:1])
    early_got = lax.all_gather(early, "seq", axis=0, tiled=False)
    late_part, early_got = tied(together(sums[LAYERS + 1 - late :]), early_got)
    late_got = lax.all_gather(late_part, "seq", axis=0, tiled=False)
    head_start = (LAYERS - late) * 2 * sub_in
    g_head = early_got[:, head_start:].reshape(-1)[: head_w.size].reshape(head_w.shape).astype(f32)
    flat = late_got[:, late * 2 * sub_in :].reshape(-1).astype(f32)
    flat = [flat[a:b] for a, b in zip(cuts, cuts[1:])]
    shards = (
        flat[0].reshape(embed_w.shape),
        None,
        None,
        flat[1].reshape(dw_kernel.shape),
        g_head,
        flat[2].reshape(norm_gain.shape),
        flat[3].reshape(norm_bias.shape),
    )

    gsq_local = sum(jnp.sum(jnp.square(g.astype(f32))) for g in (early_got, late_got))
    wsq_local = group_sums(tuple((w * w for w in masters)))
    gsq, wsq, loss = lax.psum((gsq_local, wsq_local, loss_seq), "dp")
    grad_norm = jnp.sqrt(gsq)
    factor = jnp.minimum(1.0, clip_limit / grad_norm)

    proj_spec = pl.BlockSpec((1,) + in_proj.shape[1:], lambda l: (l, 0, 0))
    down_spec = pl.BlockSpec((1,) + down_proj.shape[1:], lambda l: (l, 0, 0, 0))
    block = (n_seq, 2 * sub_in, wide)
    blocks_of = [early_got, late_got]
    if 2 * sub_in % 8:
        block = (n_seq, 1, 2 * sub_in, wide)
        counts = (LAYERS - late, late)
        blocks_of = [
            g[:, : n * 2 * sub_in].reshape(n_seq, n, 2 * sub_in, wide)
            for g, n in zip(blocks_of, counts)
        ]
    tail = (0,) * (len(block) - 2)
    got = pl.pallas_call(
        functools.partial(update_body, cols, subs, late),
        grid=(LAYERS,),
        out_shape=[jax.ShapeDtypeStruct(in_proj.shape, f32)] * 3
        + [jax.ShapeDtypeStruct(down_proj.shape, f32)] * 3
        + [jax.ShapeDtypeStruct((LAYERS, 8, LANES), f32)],
        in_specs=[
            pl.BlockSpec(memory_space=pltpu.SMEM),
            pl.BlockSpec(block, lambda l: (0, jnp.minimum(LAYERS - 1 - l, LAYERS - 1 - late), *tail)),
            pl.BlockSpec(block, lambda l: (0, jnp.maximum(late - 1 - l, 0), *tail)),
        ]
        + [proj_spec] * 3
        + [down_spec] * 3,
        out_specs=[proj_spec] * 3 + [down_spec] * 3 + [pl.BlockSpec((1, 8, LANES), lambda l: (l, 0, 0))],
        compiler_params=pltpu.CompilerParams(vmem_limit_bytes=56 << 20),
        cost_estimate=cost(25),
    )(factor.reshape(1), *blocks_of, in_proj, m_proj, v_proj, down_proj, m_down, v_down)
    big = {1: got[0:3], 2: got[3:6]}
    new_m, new_v, updates = ([], [], [])
    for n, (w, g, m, v) in enumerate(zip(masters, shards, firsts, seconds)):
        m2, v2, u = big[n] if n in big else moments(w, g * factor, m, v)
        new_m.append(m2)
        new_v.append(v2)
        updates.append(u)
    usq = lax.psum(
        group_sums(
            tuple((u * u for u in updates)), jnp.sum(got[6][:, 0, : 4 + 3 * LAYERS], 0)
        ),
        "dp",
    )
    wnorm = jnp.sqrt(wsq)
    unorm = jnp.sqrt(usq)
    ratio = wnorm / unorm
    spreads = spread_ratio(ratio)
    new_w = [w - learn_rate * r * u for w, r, u in zip(masters, spreads, updates)]
    stats = jnp.stack([wnorm, unorm])
    return (loss, grad_norm, stats, ratio, *new_w, *new_m, *new_v)


def solution(mesh):
    placed = (
        P("dp", None),
        P(None, "dp", None),
        P(None, None, "dp", None),
        P(None, None, "dp"),
        P("dp", None),
        P(None, "dp"),
        P(None, "dp"),
    )
    in_specs = (
        P("dp", "seq", None, None),
        P("dp", None),
        P("dp"),
        P("dp"),
        P("dp"),
    ) + placed * 3
    out_specs = (P(), P(), P(), P()) + placed * 3
    return jax.shard_map(
        per_device, mesh=mesh, in_specs=in_specs, out_specs=out_specs, check_vma=False
    )
```

```python
import functools

import jax
import jax.numpy as jnp
from jax import lax
from jax.experimental import pallas as pl
from jax.experimental.pallas import tpu as pltpu
from jax.sharding import PartitionSpec as P

D = 320
HEADS = 5
HD = 64
FF = 1280
CLS = 1000
W = 64
HALF = W // 2
LAYERS = 6
STEP = 5
LANES = 128


norm_eps = 1e-06
scale_qk = 0.125
big_neg = -1e30
beta_one = 0.9
beta_two = 0.999
lamb_eps = 1e-06
decay_rate = 0.01
learn_rate = 0.3
clip_limit = 0.1
root_half = 0.7071067811865476
root_two_pi = 0.3989422804014327
precise = lax.Precision.HIGHEST

f32 = jnp.float32
bf16 = jnp.bfloat16


def to_bf(v):
    return v.astype(bf16)


def dot(a, b):
    return jnp.dot(a, b, preferred_element_type=f32)


def dot_nt(a, b, precision=None):
    return lax.dot_general(
        a, b, (((1,), (1,)), ((), ())), precision=precision, preferred_element_type=f32
    )


def contract(a, b, precision=None):
    return lax.dot_general(
        a, b, (((0,), (0,)), ((), ())), precision=precision, preferred_element_type=f32
    )


def norm_parts(v):
    center = v - jnp.mean(v, -1, keepdims=True)
    spread = jnp.mean(center * center, -1, keepdims=True)
    scale = lax.rsqrt(spread + norm_eps)
    return center * scale, scale


def layer_norm(v, gain, bias):
    return norm_parts(v)[0] * gain + bias


def norm_back(v, gain, grad):
    unit, scale = norm_parts(v)
    dgain = jnp.sum(grad * unit, 0, keepdims=True)
    dbias = jnp.sum(grad, 0, keepdims=True)
    t = grad * gain
    dv = scale * (
        t - jnp.mean(t, -1, keepdims=True) - unit * jnp.mean(t * unit, -1, keepdims=True)
    )
    return dv, dgain, dbias


def cost(us):
    return pl.CostEstimate(flops=int(us * 1e8), bytes_accessed=int(us * 1e5), transcendentals=0)


def run(us, body, outs, *args, place=None):
    vm = pl.BlockSpec(memory_space=pltpu.VMEM)
    scalars = [] if place is None else [place]
    return pl.pallas_call(
        body,
        out_shape=[jax.ShapeDtypeStruct(s, d) for s, d in outs],
        in_specs=[pl.BlockSpec(memory_space=pltpu.SMEM)] * len(scalars) + [vm] * len(args),
        out_specs=[vm] * len(outs),
        compiler_params=pltpu.CompilerParams(vmem_limit_bytes=48 << 20),
        cost_estimate=cost(us),
    )(*scalars, *args)


def cells_of(v):
    rows = v.shape[0] // W
    split = v.reshape(rows // 2, 2, 2, HALF, v.shape[1])
    return [split[:, k // 2, k % 2].reshape(-1, v.shape[1]) for k in range(4)]


def attention_inputs(x, gain, bias, wq, wsr, wkv, a_ref, q_ref, r_ref, rn_ref, kv_ref):
    a = to_bf(layer_norm(x, gain[0:1], bias[0:1]))
    a_ref[...] = a
    q_ref[...] = to_bf(dot(a, wq[...]))
    total = None
    for k, cell in enumerate(cells_of(a)):
        part = dot(cell, wsr[k * D : (k + 1) * D, :])
        total = part if total is None else total + part
    r_ref[...] = total
    rn = to_bf(layer_norm(total, gain[1:2], bias[1:2]))
    rn_ref[...] = rn
    kv_ref[...] = to_bf(dot(rn, wkv[...]))


def embed_body(p_ref, w_ref, ln_ref, e_ref, x_ref):
    e = dot(p_ref[...], w_ref[...])
    e_ref[...] = e
    x_ref[...] = layer_norm(e, ln_ref[0:1], ln_ref[1:2])


def embed_back_body(p_ref, de_ref, dw_ref):
    dw_ref[...] = contract(p_ref[...], de_ref[...])


def first_body(x_ref, gain, bias, wq, wsr, wkv, *outs):
    attention_inputs(x_ref[...], gain, bias, wq, wsr, wkv, *outs)


def middle_body(
    place, q_ref, kv_ref, ok_ref, x_ref, gain, bias, wo, w1, o_ref, lse_ref, x2_ref, b_ref, h_ref, edge_ref
):
    q = q_ref[...] * jnp.asarray(scale_qk, bf16)
    keys = kv_ref.shape[0]
    kv = kv_ref[...]
    shut = jnp.broadcast_to(ok_ref[...], (keys, q.shape[0]))
    q_t = q.T
    v_t = kv[:, D:].T
    parts = []
    for head in range(HEADS):
        low, high = head * HD, (head + 1) * HD
        s = dot(kv[:, low:high], q_t[low:high, :]) + shut
        top = jnp.max(s, 0, keepdims=True)
        expo = jnp.exp(s - top)
        total = jnp.sum(expo, 0, keepdims=True)
        lse_ref[head : head + 1, :] = top + jnp.log(total)
        p = to_bf(expo * (1.0 / total))
        parts.append(dot(v_t[low:high, :], p))
    o = to_bf(jnp.concatenate(parts, 0).T)
    o_ref[...] = o
    x2 = x_ref[...] + dot(o, wo[...])
    x2_ref[...] = x2
    b = to_bf(layer_norm(x2, gain[2:3], bias[2:3]))
    b_ref[...] = b
    h_ref[...] = to_bf(dot(b, w1[...]))
    send_edge(place, h_ref, edge_ref)


def shift_down(v):
    index = lax.broadcasted_iota(jnp.int32, v.shape, 0)
    return jnp.where(index == 0, 0.0, pltpu.roll(v, 1, 0))


def shift_up(v):
    index = lax.broadcasted_iota(jnp.int32, v.shape, 0)
    return jnp.where(index == v.shape[0] - 1, 0.0, pltpu.roll(v, v.shape[0] - 1, 0))


def from_left(v):
    return jnp.concatenate([shift_down(v[HALF:]), v[:HALF]], 0)


def from_right(v):
    return jnp.concatenate([v[HALF:], shift_up(v[:HALF])], 0)


def row_of(main, near, i, rows, lanes):
    place, low, high = near
    if i < 0:
        return jnp.where(place[0] > 0, low[:, lanes].astype(f32), 0.0)
    if i >= rows:
        return jnp.where(place[1] > 0, high[:, lanes].astype(f32), 0.0)
    return main[i * W : (i + 1) * W, lanes].astype(f32)


def send_edge(place, main, edge_ref):
    start = pl.multiple_of(jnp.where(place[0] > 0, 0, main.shape[0] - W), W)
    edge_ref[...] = main[pl.ds(start, W), :]


def conv_gelu(h_ref, ends, taps_ref, g_ref, slope_ref):
    rows = h_ref.shape[0] // W

    def chunk(c, carry):
        lanes = pl.ds(pl.multiple_of(c * LANES, LANES), LANES)
        taps = [taps_ref[k : k + 1, lanes] for k in range(9)]
        near = [row_of(h_ref, ends, i, rows, lanes) for i in (-1, 0)]
        for i in range(rows):
            near.append(row_of(h_ref, ends, i + 1, rows, lanes))
            sums = [
                taps[j] * near[0] + taps[3 + j] * near[1] + taps[6 + j] * near[2] for j in range(3)
            ]
            z = sums[1] + from_left(sums[0]) + from_right(sums[2])
            phi = 0.5 + 0.5 * lax.erf(z * root_half)
            here = slice(i * W, (i + 1) * W)
            g_ref[here, lanes] = to_bf(z * phi)
            slope_ref[here, lanes] = phi + z * (jnp.exp(-0.5 * z * z) * root_two_pi)
            near = near[1:]
        return carry

    lax.fori_loop(0, FF // LANES, chunk, 0)


def last_body(place, h_ref, low_ref, high_ref, taps_ref, x2_ref, w2, ln_ref, ok_ref, g_ref, slope_ref, x_ref, sum_ref):
    conv_gelu(h_ref, (place, low_ref, high_ref), taps_ref, g_ref, slope_ref)
    x = x2_ref[...] + dot(g_ref[...], w2[...])
    x_ref[...] = x
    fin = layer_norm(x, ln_ref[0:1], ln_ref[1:2])
    sum_ref[...] = jnp.sum(fin * ok_ref[...], 0, keepdims=True)


def join_body(
    place, h_ref, low_ref, high_ref, taps_ref, x2_ref, w2, gain, bias, wq, wsr, wkv, g_ref, slope_ref, x_ref, *outs
):
    conv_gelu(h_ref, (place, low_ref, high_ref), taps_ref, g_ref, slope_ref)
    x = x2_ref[...] + dot(g_ref[...], w2[...])
    x_ref[...] = x
    attention_inputs(x, gain, bias, wq, wsr, wkv, *outs)


def gelu_back(place, dx, w2, slope_ref, dy_ref, dz_ref, edge_ref):
    dy = to_bf(dx)
    dy_ref[...] = dy
    dg = to_bf(dot_nt(dy, w2[...])).astype(f32)
    dz_ref[...] = to_bf(dg * slope_ref[...])
    send_edge(place, dz_ref, edge_ref)


def head_body(
    images,
    place,
    pool_ref,
    count_ref,
    head_ref,
    target_ref,
    x_ref,
    ln_ref,
    ok_ref,
    w2,
    slope_ref,
    loss_ref,
    pooled_ref,
    dlog_ref,
    dln_ref,
    dx_ref,
    dy_ref,
    dz_ref,
    edge_ref,
):
    count = count_ref[...]
    pooled = to_bf(pool_ref[...] / count)
    pooled_ref[...] = pooled
    logits = dot(jnp.broadcast_to(pooled.astype(f32), (16, D)).astype(bf16), head_ref[...])[0:1]
    shifted = logits - jnp.max(logits, -1, keepdims=True)
    logp = shifted - jnp.log(jnp.sum(jnp.exp(shifted), -1, keepdims=True))
    target = target_ref[...]
    loss_ref[...] = jnp.sum(target * logp, -1, keepdims=True) * (-1.0 / images)
    dlog = to_bf((jnp.exp(logp) - target) * (1.0 / images))
    dlog_ref[...] = dlog
    wide = jnp.broadcast_to(dlog.astype(f32), (16, CLS)).astype(bf16)
    dpool = dot_nt(wide, head_ref[...])[0:1] / count
    dx, dgain, dbias = norm_back(x_ref[...], ln_ref[0:1], ok_ref[...] * dpool)
    dln_ref[0:1, :] = dgain
    dln_ref[1:2, :] = dbias
    dx_ref[...] = dx
    gelu_back(place, dx, w2, slope_ref, dy_ref, dz_ref, edge_ref)


def conv_back(h_ref, hends, dz_ref, zends, taps_ref, dh_ref, dtaps_ref):
    rows = h_ref.shape[0] // W

    def chunk(c, carry):
        lanes = pl.ds(pl.multiple_of(c * LANES, LANES), LANES)
        taps = [taps_ref[k : k + 1, lanes] for k in range(9)]
        acc = [jnp.zeros((8, LANES), f32) for _ in range(9)]

        def views(i):
            v = row_of(dz_ref, zends, i, rows, lanes)
            return [from_right(v), v, from_left(v)]

        near = [views(-1), views(0)]
        hear = [row_of(h_ref, hends, i, rows, lanes) for i in (-1, 0)]
        for i in range(rows):
            near.append(views(i + 1))
            hear.append(row_of(h_ref, hends, i + 1, rows, lanes))
            dh = None
            for di in range(3):
                for dj in range(3):
                    part = taps[3 * di + dj] * near[2 - di][dj]
                    dh = part if dh is None else dh + part
            dh_ref[i * W : (i + 1) * W, lanes] = to_bf(dh)
            for di in range(3):
                for dj in range(3):
                    prod = (hear[di] * near[1][dj]).reshape(W // 8, 8, LANES)
                    acc[3 * di + dj] = acc[3 * di + dj] + jnp.sum(prod, 0)
            near = near[1:]
            hear = hear[1:]
        for k in range(9):
            dtaps_ref[k : k + 1, lanes] = jnp.sum(acc[k], 0, keepdims=True)
        return carry

    lax.fori_loop(0, FF // LANES, chunk, 0)


def block_back_body(
    place,
    h_ref,
    hlow_ref,
    hhigh_ref,
    dz_ref,
    zlow_ref,
    zhigh_ref,
    taps_ref,
    w1,
    x2_ref,
    gain,
    dx_ref,
    wo,
    q_ref,
    kv_ref,
    ok_ref,
    lse_ref,
    dh_ref,
    dtaps_ref,
    dln_ref,
    dx2_ref,
    dy_ref,
    dq_ref,
    dkv_ref,
):
    conv_back(
        h_ref, (place, hlow_ref, hhigh_ref), dz_ref, (place, zlow_ref, zhigh_ref), taps_ref, dh_ref, dtaps_ref
    )
    db = dot_nt(dh_ref[...], w1[...])
    dln, dgain, dbias = norm_back(x2_ref[...], gain[2:3], db)
    dln_ref[0:1, :] = dgain
    dln_ref[1:2, :] = dbias
    dx2 = dx_ref[...] + dln
    dx2_ref[...] = dx2
    dy = to_bf(dx2)
    dy_ref[...] = dy
    do_t = to_bf(dot_nt(wo[...], dy))
    q = q_ref[...] * jnp.asarray(scale_qk, bf16)
    q_t = q.T
    keys = kv_ref.shape[0]
    kv = kv_ref[...]
    k_t = (kv[:, :D] * jnp.asarray(scale_qk, bf16)).T
    shut = jnp.broadcast_to(ok_ref[...], (keys, q.shape[0]))
    dq_parts, dk_parts, dv_parts = ([], [], [])
    for head in range(HEADS):
        low, high = head * HD, (head + 1) * HD
        s = dot(kv[:, low:high], q_t[low:high, :]) + shut
        p = jnp.exp(s - lse_ref[head : head + 1, :])
        dp = dot(kv[:, D + low : D + high], do_t[low:high, :])
        dv_parts.append(dot_nt(do_t[low:high, :], to_bf(p)))
        ds = to_bf(p * (dp - jnp.sum(p * dp, 0, keepdims=True)))
        dq_parts.append(dot(k_t[low:high, :], ds))
        dk_parts.append(dot_nt(q_t[low:high, :], ds))
    dq_ref[...] = to_bf(jnp.concatenate(dq_parts, 0).T)
    dkv_ref[...] = jnp.concatenate(dk_parts + dv_parts, 0).T


def inputs_back(dkv, wkv, r_ref, gain, dq_ref, wq, wsr, x_ref, dx2_ref, dr_ref, dln_ref):
    w_kv = wkv[...].astype(f32)
    drn = dot_nt(dkv, w_kv, precise)
    dr, dgain1, dbias1 = norm_back(r_ref[...], gain[1:2], drn)
    dr = to_bf(dr)
    dr_ref[...] = dr
    rows = x_ref.shape[0] // W
    cells = [
        dot_nt(dr, wsr[k * D : (k + 1) * D, :]).reshape(rows // 2, 1, 1, HALF, D) for k in range(4)
    ]
    placed = jnp.concatenate(
        [jnp.concatenate(cells[0:2], 2), jnp.concatenate(cells[2:4], 2)], 1
    ).reshape(rows * W, D)
    da = dot_nt(dq_ref[...], wq[...]) + placed
    dln, dgain0, dbias0 = norm_back(x_ref[...], gain[0:1], da)
    for k, row in enumerate((dgain0, dgain1, dbias0, dbias1)):
        dln_ref[k : k + 1, :] = row
    return dx2_ref[...] + dln


def join_back_body(
    place, dkv_ref, wkv, r_ref, gain, dq_ref, wq, wsr, x_ref, dx2_ref, w2, slope_ref,
    dr_ref, dln_ref, dx_ref, dy_ref, dz_ref, edge_ref
):
    dx = inputs_back(dkv_ref[...], wkv, r_ref, gain, dq_ref, wq, wsr, x_ref, dx2_ref, dr_ref, dln_ref)
    dx_ref[...] = dx
    gelu_back(place, dx, w2, slope_ref, dy_ref, dz_ref, edge_ref)


def first_back_body(
    dkv_ref, wkv, r_ref, gain, dq_ref, wq, wsr, x_ref, dx2_ref, e_ref, ln_ref, dr_ref, dln_ref, de_ref, dle_ref
):
    dx = inputs_back(dkv_ref[...], wkv, r_ref, gain, dq_ref, wq, wsr, x_ref, dx2_ref, dr_ref, dln_ref)
    de, dgain, dbias = norm_back(e_ref[...], ln_ref[0:1], dx)
    de_ref[...] = to_bf(de)
    dle_ref[0:1, :] = dgain
    dle_ref[1:2, :] = dbias


def weight_grads_body(
    n_dp, cols, subs, core_ref, a_ref, dq_ref, rn_ref, dkv_ref, o_ref, dy2_ref, b_ref, dh_ref, dr_ref, g_ref, dy_ref, *refs
):
    outs, (proj, down) = refs[:-2], refs[-2:]
    a = a_ref[...]
    proj[:, :D] = contract(a, dq_ref[...])
    proj[:, D : 3 * D] = contract(rn_ref[...].astype(f32), dkv_ref[...], precise)
    proj[:, 3 * D : 4 * D] = contract(o_ref[...], dy2_ref[...])
    proj[:, 4 * D :] = contract(b_ref[...], dh_ref[...])
    dr = dr_ref[...]
    for k, cell in enumerate(cells_of(a)):
        down[k * D : (k + 1) * D, :D] = contract(cell, dr)
    down[:, D:] = contract(g_ref[...], dy_ref[...])
    rows = D // n_dp
    sub = rows // subs
    wide = (4 * D + FF) // cols
    down_rows = FF // n_dp
    for c in range(cols):
        for d in range(n_dp):
            for n, out in enumerate(outs):
                for j in range(subs) if len(outs) == 1 else (None,):
                    if j is None:
                        k = core_ref[0] if n == 0 else 1 - core_ref[0]
                        at = (c ^ core_ref[1], d)
                    else:
                        k = j
                        at = (c, j, d)
                    start = d * rows + k * sub
                    low = d * down_rows + (c * subs + k) * (down_rows // (cols * subs))
                    if j is None:
                        start = pl.multiple_of(start, 8)
                        low = pl.multiple_of(low, 8)
                    out[(*at, slice(0, sub))] = proj[pl.ds(start, sub), c * wide : (c + 1) * wide]
                    out[(*at, slice(sub, 2 * sub))] = down[pl.ds(low, sub), :]


def moments(w, g, m, v):
    m2 = beta_one * m + (1.0 - beta_one) * g
    v2 = beta_two * v + (1.0 - beta_two) * g * g
    u = (
        m2 / (1.0 - beta_one**STEP) / (jnp.sqrt(v2 / (1.0 - beta_two**STEP)) + lamb_eps)
        + decay_rate * w
    )
    return m2, v2, u


def update_body(
    cols, subs, late, factor_ref, early_ref, late_ref, wp, mp, vp, wd, md, vd, mp2, vp2, up, md2, vd2, ud, sums
):
    factor = factor_ref[0]
    layer = pl.program_id(0)
    sub = wp.shape[1] // subs
    wide = wp.shape[2] // cols

    def go(g_ref):
        squares = [0.0, 0.0]

        def put(n, at, refs, outs, g):
            new = moments(refs[0][at], g * factor, refs[1][at], refs[2][at])
            for out, value in zip(outs, new):
                out[at] = value
            squares[n] = squares[n] + jnp.sum(new[2] * new[2], 0, keepdims=True)

        for c in range(cols):
            for k in range(subs):
                g = g_ref[c * subs + k].astype(f32).reshape(2 * sub, wide)
                at = (0, slice(k * sub, (k + 1) * sub), slice(c * wide, (c + 1) * wide))
                put(0, at, (wp, mp, vp), (mp2, vp2, up), g[:sub])
                rows = slice((c * subs + k) * sub, (c * subs + k + 1) * sub)
                for half in range(2):
                    at = (0, half, rows, slice(0, D))
                    put(1, at, (wd, md, vd), (md2, vd2, ud), g[sub:, half * D : (half + 1) * D])
        lane = lax.broadcasted_iota(jnp.int32, (1, LANES), 1)
        total = jnp.zeros((1, LANES), f32)
        for n in range(2):
            value = jnp.broadcast_to(jnp.sum(squares[n], 1, keepdims=True), (1, LANES))
            total = jnp.where(lane == 4 + n * LAYERS + layer, value, total)
        sums[0] = jnp.broadcast_to(total, sums.shape[1:])

    pl.when(layer >= late)(lambda: go(early_ref))
    pl.when(layer < late)(lambda: go(late_ref))


def group_sums(arrs, layered=None):
    embed, proj, downs, taps, head, gains, biases = arrs
    slot = lax.broadcasted_iota(jnp.int32, (1, 4 + 3 * LAYERS), 1)

    def placed(values, start):
        at = lax.broadcasted_iota(jnp.int32, (values.shape[0], 1), 0) + start
        return jnp.sum(jnp.where(at == slot, values[:, None], 0.0), 0)

    total = placed(jnp.sum(taps, (1, 2)), 4 + 2 * LAYERS)
    for n, a in enumerate((embed, head, gains, biases)):
        total = total + jnp.where(slot[0] == n, jnp.sum(a), 0.0)
    if layered is not None:
        return total + layered
    for n, a in enumerate((proj, downs)):
        total = total + placed(jnp.sum(a.reshape(a.shape[0], -1), 1), 4 + n * LAYERS)
    return total


def spread_ratio(ratio):
    return (
        ratio[0],
        ratio[4 : 4 + LAYERS].reshape(LAYERS, 1, 1),
        ratio[4 + LAYERS : 4 + 2 * LAYERS].reshape(LAYERS, 1, 1, 1),
        ratio[4 + 2 * LAYERS : 4 + 3 * LAYERS].reshape(LAYERS, 1, 1),
        ratio[1],
        ratio[2],
        ratio[3],
    )


def per_device(
    patches,
    valid,
    labels,
    partners,
    mix,
    embed_w,
    in_proj,
    down_proj,
    dw_kernel,
    head_w,
    norm_gain,
    norm_bias,
    m_embed,
    m_proj,
    m_down,
    m_taps,
    m_head,
    m_gain,
    m_bias,
    v_embed,
    v_proj,
    v_down,
    v_taps,
    v_head,
    v_gain,
    v_bias,
):
    masters = (embed_w, in_proj, down_proj, dw_kernel, head_w, norm_gain, norm_bias)
    firsts = (m_embed, m_proj, m_down, m_taps, m_head, m_gain, m_bias)
    seconds = (v_embed, v_proj, v_down, v_taps, v_head, v_gain, v_bias)
    n_seq = lax.axis_size("seq")
    n_dp = lax.axis_size("dp")
    seq_pos = lax.axis_index("seq")
    img_dev, rows = (patches.shape[0], patches.shape[1])
    images = img_dev * n_dp

    team = n_seq
    while team * img_dev > n_seq:
        team //= 2
    blocks = n_seq // team
    rows_own = rows * blocks
    tok = rows_own * W
    keys_own = tok // 4
    image = jnp.minimum(seq_pos // team, img_dev - 1)
    busy = seq_pos // team < img_dev
    place = seq_pos % team

    def between(shift, wrap):
        pairs = []
        for base in range(0, n_seq, team):
            for h in range(team):
                if wrap or 0 <= h + shift < team:
                    pairs.append((base + (h + shift) % team, base + h))
        return pairs

    ends = jnp.stack([place > 0, place < team - 1]).astype(jnp.int32)

    def edges(v, edge):
        if team == 2:
            other = lax.ppermute(edge, "seq", between(1, True))
            return other, other
        low = lax.ppermute(v[-W:], "seq", between(-1, False))
        high = lax.ppermute(v[:W], "seq", between(1, False))
        return low, high

    def all_keys(v):
        return jnp.concatenate(
            [v] + [lax.ppermute(v, "seq", between(j, True)) for j in range(1, team)], 0
        )

    def own_keys(v):
        total = v[:keys_own]
        for j in range(1, team):
            part = v[j * keys_own : (j + 1) * keys_own]
            total = total + lax.ppermute(part, "seq", between(-j, True))
        return total

    back_block = seq_pos % blocks
    routes = [
        [
            (blocks * h + (i + r) % blocks, team * i + h)
            for i in range(img_dev)
            for h in range(team)
        ]
        for r in range(blocks)
    ]

    def to_team(v):
        got = []
        for r, pairs in enumerate(routes):
            send = lax.dynamic_index_in_dim(
                v, jnp.minimum((back_block - r) % blocks, img_dev - 1), 0, keepdims=False
            )
            got.append(lax.ppermute(send, "seq", pairs))
        twice = jnp.stack(got + got)
        own = lax.dynamic_slice_in_dim(twice, (blocks - image) % blocks, blocks, 0)
        return own.reshape(tok, -1)

    cols = 4
    subs = n_seq // cols
    row_in = D // n_dp
    sub_in = row_in // subs
    wide = in_proj.shape[2] // cols
    down_rows = down_proj.shape[2] // n_seq
    core = seq_pos % subs

    def part_of(flat):
        size = -(-flat.shape[0] // (wide * n_seq)) * wide * n_seq
        flat = jnp.pad(flat, (0, size - flat.shape[0])).reshape(n_seq, -1, wide)
        return lax.dynamic_index_in_dim(flat, seq_pos, 0, keepdims=False)

    def layer_part(l):
        block = lax.dynamic_slice(
            in_proj[l], (core * sub_in, (seq_pos // subs) * wide), (sub_in, wide)
        )
        lower = lax.dynamic_slice_in_dim(down_proj[l], seq_pos * down_rows, down_rows, 1)
        return [to_bf(block), to_bf(jnp.concatenate([lower[0], lower[1]], 1))]

    def gathered(part):
        return lax.all_gather(part.reshape(-1, wide), "seq", axis=0, tiled=False)

    def cut(got, sizes):
        got = got.reshape(n_seq, n_dp, sum(sizes), wide).transpose(1, 0, 2, 3)
        starts = [sum(sizes[:i]) for i in range(len(sizes))]
        return [got[:, :, a : a + n] for a, n in zip(starts, sizes)]

    def proj_of(got):
        got = got.reshape(n_dp, cols, subs, sub_in, wide).transpose(0, 2, 3, 1, 4)
        return got.reshape(D, cols * wide)

    dp_pos = lax.axis_index("dp")

    def over_dp(v):
        got = [v] + [
            lax.ppermute(v, "dp", [((d + j) % n_dp, d) for d in range(n_dp)])
            for j in range(1, n_dp)
        ]
        return lax.dynamic_slice_in_dim(jnp.stack(got + got), (n_dp - dp_pos) % n_dp, n_dp, 0)

    taps16 = over_dp(to_bf(dw_kernel).reshape(LAYERS * 9, -1))
    norms16 = over_dp(to_bf(jnp.stack([norm_gain, norm_bias])))
    taps32 = taps16.transpose(1, 0, 2).reshape(LAYERS, 9, FF).astype(f32)
    norms32 = norms16.transpose(1, 2, 0, 3).reshape(2, -1, D).astype(f32)
    gain32, bias32 = norms32[0], norms32[1]
    groups = [[0], [1, 2], [3, 4], [5]]
    extra = [[], [], [], [part_of(to_bf(head_w).reshape(-1))]]

    def layers_of(got, count):
        return [(proj_of(got[2 * i]), got[2 * i + 1].reshape(FF, 2 * D)) for i in range(count)]

    parts_of = [more + [p for l in members for p in layer_part(l)] for members, more in zip(groups, extra)]
    sizes_of = [[p.shape[0] for p in parts] for parts in parts_of]
    lines = [over_dp(jnp.concatenate(parts, 0)) for parts in parts_of]
    behind, lines[0] = lax.optimization_barrier((to_bf(embed_w), lines[0]))
    embed16 = over_dp(behind).reshape(-1, D)
    raw = [gathered(lines[0])]
    first_of = {members[0]: n for n, members in enumerate(groups)}

    def own(v):
        return lax.dynamic_index_in_dim(v, image, 0, keepdims=False)

    wanted = own(partners)
    partner_label = jnp.zeros((), jnp.int32)
    for j in range(n_dp):
        other = labels
        if j:
            other = lax.ppermute(labels, "dp", [((d + j) % n_dp, d) for d in range(n_dp)])
        index = ((dp_pos + j) % n_dp) * img_dev + jnp.arange(img_dev)
        partner_label = partner_label + jnp.sum(jnp.where(index == wanted, other, 0))
    valid_own = own(valid)
    tid = lax.broadcasted_iota(jnp.int32, (tok, 1), 0)
    within = tid % W
    row_id = place * rows_own + tid // W
    col_id = 2 * (within % HALF) + within // HALF
    okay = ((row_id < valid_own[0]) & (col_id < valid_own[1]) & busy).astype(f32)
    kid = lax.broadcasted_iota(jnp.int32, (team * keys_own, 1), 0)
    segment = (place + kid // keys_own) % team
    key_row = segment * (rows_own // 2) + (kid % keys_own) // HALF
    key_ok = (2 * key_row < valid_own[0]) & (2 * (kid % HALF) < valid_own[1])
    shut = jnp.where(key_ok, 0.0, big_neg).astype(f32)
    count = (valid_own[0] * valid_own[1]).astype(f32).reshape(1, 1)
    classes = lax.broadcasted_iota(jnp.int32, (1, CLS), 1)
    mix_own = own(mix)
    target = mix_own * (classes == own(labels)).astype(f32) + (1.0 - mix_own) * (
        classes == partner_label
    ).astype(f32)

    def weights(l, layer):
        base = 1 + 3 * l
        return dict(
            wq=layer[0][:, :D],
            wkv=layer[0][:, D : 3 * D],
            wo=layer[0][:, 3 * D : 4 * D],
            w1=layer[0][:, 4 * D :],
            wsr=layer[1][:, :D],
            w2=layer[1][:, D:],
            taps=taps32[l],
            gain=gain32[base : base + 3],
            bias=bias32[base : base + 3],
        )

    full = ((tok, D), f32)
    ln_first = jnp.stack([gain32[0], bias32[0]])
    spread = patches.reshape(img_dev, rows, HALF, 2, -1).transpose(0, 1, 3, 2, 4)
    patch_own = to_team(spread.reshape(img_dev, rows * W, -1))
    e, x = run(2, embed_body, [full, full], patch_own, embed16, ln_first)
    lines[1], x = lax.optimization_barrier((lines[1], x))
    raw += [gathered(line) for line in lines[1:]]
    wts = [weights(l, layer) for l, layer in zip(groups[0], layers_of(cut(raw[0], sizes_of[0]), len(groups[0])))]
    ln_last = jnp.stack([gain32[-1], bias32[-1]])

    half = ((tok, D), bf16)
    wide16 = ((tok, FF), bf16)
    input_outs = [half, half, ((keys_own, D), f32), ((keys_own, D), bf16), ((keys_own, 2 * D), bf16)]
    ln_out = ((2, D), f32)
    row16 = ((W, FF), bf16)

    w = wts[0]
    a16, q16, r, rn16, kv16 = run(
        2, first_body, input_outs, x, w["gain"], w["bias"], w["wq"], w["wsr"], w["wkv"]
    )
    kept = []
    for l in range(LAYERS):
        w = wts[l]
        kv_all = all_keys(kv16)
        o16, lse, x2, b16, h16, edge = run(
            4,
            middle_body,
            [half, ((HEADS, tok), f32), full, half, wide16, row16],
            q16,
            kv_all,
            shut,
            x,
            w["gain"],
            w["bias"],
            w["wo"],
            w["w1"],
            place=ends,
        )
        hlow, hhigh = edges(h16, edge)
        keep = dict(
            x=x, a16=a16, q16=q16, r=r, rn16=rn16, kv=kv_all, o16=o16, lse=lse, x2=x2, b16=b16,
            h16=h16, hlow=hlow, hhigh=hhigh,
        )
        shared = (h16, hlow, hhigh, w["taps"], x2, w["w2"])
        if l + 1 in first_of:
            n = first_of[l + 1]
            got, _ = lax.optimization_barrier((raw[n], kv_all))
            got = cut(got, sizes_of[n])
            if extra[n]:
                head16 = got.pop(0).reshape(n_dp, -1)[:, : head_w.size].reshape(D, CLS)
            wts += [weights(m, layer) for m, layer in zip(groups[n], layers_of(got, len(groups[n])))]
        if l + 1 < LAYERS:
            n = wts[l + 1]
            keep["g16"], keep["slope"], x, a16, q16, r, rn16, kv16 = run(
                8,
                join_body,
                [wide16, ((tok, FF), f32), full] + input_outs,
                *shared,
                n["gain"],
                n["bias"],
                n["wq"],
                n["wsr"],
                n["wkv"],
                place=ends,
            )
        else:
            keep["g16"], keep["slope"], x, pool = run(
                7,
                last_body,
                [wide16, ((tok, FF), f32), full, ((1, D), f32)],
                *shared,
                ln_last,
                okay,
                place=ends,
            )
        kept.append(keep)

    whole = pool
    for j in range(1, team):
        whole = whole + lax.ppermute(pool, "seq", between(j, True))
    loss_own, pooled16, dlog16, dln_last, dx, dy16, dz16, edge = run(
        4,
        functools.partial(head_body, images),
        [((1, 1), f32), ((1, D), bf16), ((1, CLS), bf16), ln_out, full, half, wide16, row16],
        whole,
        count,
        head16,
        target,
        x,
        ln_last,
        okay,
        wts[-1]["w2"],
        kept[-1]["slope"],
        place=ends,
    )
    chosen = ((place == 0) & busy).astype(f32)
    d_head = pooled16.astype(f32).reshape(D, 1) * dlog16.astype(f32) * chosen
    loss_local = loss_own[0, 0] * busy.astype(f32)
    teams = n_seq // team
    loss_parts = jnp.zeros((teams,), f32)
    for j in range(teams):
        other = loss_local
        if j:
            other = lax.ppermute(
                loss_local, "seq", [((d + j * team) % n_seq, d) for d in range(n_seq)]
            )
        loss_parts = jnp.where(jnp.arange(teams) == (seq_pos // team + j) % teams, other, loss_parts)
    loss_seq = jnp.sum(loss_parts)

    piece = ((cols, n_dp, 2 * sub_in, wide), f32)
    paired = subs == 2 and cols == 4
    chip = seq_pos // subs
    where = jnp.stack([core, chip]).astype(jnp.int32)

    def weight_grads(*args):
        vm = pl.BlockSpec(memory_space=pltpu.VMEM)
        outs = [piece] * 2 if paired else [((cols, subs) + piece[0][1:], f32)]
        return pl.pallas_call(
            functools.partial(weight_grads_body, n_dp, cols, subs),
            out_shape=[jax.ShapeDtypeStruct(s, d) for s, d in outs],
            in_specs=[pl.BlockSpec(memory_space=pltpu.SMEM)] + [vm] * len(args),
            out_specs=[vm] * len(outs),
            scratch_shapes=[pltpu.VMEM((D, cols * wide), f32), pltpu.VMEM((FF, 2 * D), f32)],
            compiler_params=pltpu.CompilerParams(vmem_limit_bytes=48 << 20),
            cost_estimate=cost(6),
        )(where, *args)

    def padded_rest(parts):
        flat = jnp.concatenate(parts, 1)
        size = -(-flat.shape[1] // (16 * wide * n_seq)) * 16 * wide * n_seq
        flat = jnp.pad(flat, ((0, 0), (0, size - flat.shape[1])))
        flat = flat.reshape(n_dp, cols, subs, -1, wide).transpose(1, 2, 0, 3, 4)
        if not paired:
            return [flat]
        flat = jnp.stack([lax.dynamic_index_in_dim(flat, chip ^ j, 0, False) for j in range(cols)])
        return [lax.dynamic_index_in_dim(flat, k, 1, False) for k in (core, 1 - core)]

    def pair_sum(parts):
        mine, send = parts
        return mine + lax.ppermute(send, "seq", [(d ^ 1, d) for d in range(n_seq)])

    def over_chips(v, bit):
        return lax.ppermute(v, "seq", [(d ^ (bit * subs), d) for d in range(n_seq)])

    def plane_first(y):
        cut = y.shape[2] // 2
        one, two = y[:, :, :cut], y[:, :, cut:]
        moved = (to_bf(jnp.stack([one[1], one[3]])), to_bf(jnp.stack([two[2], two[3]])))
        got = (over_chips(moved[0], 1).astype(f32), over_chips(moved[1], 2).astype(f32))
        return [one[0] + got[0][0], one[2] + got[0][1], two[0] + got[1][0], two[1] + got[1][1]]

    def plane_second(parts):
        one = parts[0] + over_chips(parts[1].astype(wire[0]), 2).astype(f32)
        two = parts[2] + over_chips(parts[3].astype(wire[0]), 1).astype(f32)
        return jnp.concatenate([one, two], 1)

    def dp_sum(y):
        def of(j):
            return lax.dynamic_index_in_dim(y, (dp_pos + j) % n_dp, 0, keepdims=False)

        total = of(0)
        for j in range(1, n_dp):
            pairs = [(d, (d + j) % n_dp) for d in range(n_dp)]
            total = total + lax.ppermute(of(j).astype(wire[0]), "dp", pairs).astype(f32)
        return total

    def whole_sum(parts):
        y = jnp.concatenate([p[0] for p in parts], -2)
        y = lax.psum_scatter(y.reshape(-1, wide), "seq", scatter_dimension=0, tiled=True)
        return lax.psum_scatter(y, "dp", scatter_dimension=0, tiled=True)

    def tied(value, others):
        return lax.optimization_barrier((value, others))

    wire = [f32]
    stages = [pair_sum, plane_first, plane_second]
    pieces = []

    def advance(now):
        if not paired:
            return now
        ready = [p for p in pieces if p[0] <= len(stages) + 1]
        now, values = tied(now, [p[1] for p in ready])
        for n, (p, v) in enumerate(zip(ready, values)):
            if p[0] < len(stages):
                p[1] = stages[p[0]](v)
            elif p[0] > len(stages) or p is pieces[0]:
                p[1] = v
            elif p is pieces[1]:
                p[1] = dp_sum(jnp.concatenate([v, pieces[0][1]], 1))
            else:
                p[1] = dp_sum(v)
            p[0] += 1
        return now

    grads = [None] * LAYERS
    pieces.append([0, padded_rest([d_head.reshape(n_dp, -1)])])
    waiting = None
    for l in reversed(range(LAYERS)):
        w, k = wts[l], kept[l]
        zlow, zhigh = edges(dz16, edge)
        upper = dy16
        dz16 = advance(dz16)
        dh16, d_taps, dln2, dx2, dy2, dq16, dkv = run(
            11,
            block_back_body,
            [wide16, ((9, FF), f32), ln_out, full, half, half, ((team * keys_own, 2 * D), f32)],
            k["h16"], k["hlow"], k["hhigh"], dz16, zlow, zhigh, w["taps"], w["w1"], k["x2"], w["gain"], dx,
            w["wo"], k["q16"], k["kv"], shut, k["lse"],
            place=ends,
        )
        if waiting is not None:
            first, _ = tied(waiting[0], dkv)
            pieces.append([0, weight_grads(first, *waiting[1:])])
        dkv_own = own_keys(dkv)
        dq16 = advance(dq16)
        shared = (dkv_own, w["wkv"], k["r"], w["gain"], dq16, w["wq"], w["wsr"], k["x"], dx2)
        if l:
            dr16, dln, dx, dy16, dz16, edge = run(
                6,
                join_back_body,
                [((keys_own, D), bf16), ((4, D), f32), full, half, wide16, row16],
                *shared,
                wts[l - 1]["w2"],
                kept[l - 1]["slope"],
                place=ends,
            )
        else:
            dr16, dln, de16, dln_first = run(
                3,
                first_back_body,
                [((keys_own, D), bf16), ((4, D), f32), half, ln_out],
                *shared,
                e,
                ln_first,
            )
        waiting = (k["a16"], dq16, k["rn16"], dkv_own, k["o16"], dy2, k["b16"], dh16, dr16, k["g16"], upper)
        grads[l] = (
            d_taps,
            jnp.concatenate([dln[0:2], dln2[0:1]], 0),
            jnp.concatenate([dln[2:4], dln2[1:2]], 0),
        )
    wire[0] = bf16
    pieces.append([0, weight_grads(*waiting)])
    de16 = advance(de16)
    (d_embed,) = run(3, embed_back_body, [((embed16.shape[0], D), f32)], patch_own, de16)
    d_embed = advance(d_embed)
    d_gain = jnp.concatenate([dln_first[0:1]] + [g[1] for g in grads] + [dln_last[0:1]], 0)
    d_bias = jnp.concatenate([dln_first[1:2]] + [g[2] for g in grads] + [dln_last[1:2]], 0)
    d_taps = jnp.stack([g[0] for g in grads])
    rest = [
        d_embed.reshape(n_dp, -1),
        d_taps.reshape(LAYERS * 9, n_dp, -1).transpose(1, 0, 2).reshape(n_dp, -1),
        d_gain.reshape(-1, n_dp, row_in).transpose(1, 0, 2).reshape(n_dp, -1),
        d_bias.reshape(-1, n_dp, row_in).transpose(1, 0, 2).reshape(n_dp, -1),
    ]
    cuts = [0]
    for part in rest:
        cuts.append(cuts[-1] + part.shape[1])
    rest = padded_rest(rest)

    late = 3

    def together(parts):
        return to_bf(jnp.concatenate(parts, 0))

    if paired:
        assert all(p[0] > len(stages) + 1 for p in pieces[: LAYERS + 1 - late])
        own_rows = 2 * sub_in
        parts = [p[1] for p in pieces[1 : LAYERS + 1 - late]]
        early = together([parts[0][:own_rows], *parts[1:], parts[0][own_rows:]])
        rest, early = tied(rest, early)
        rest = advance(rest)
        last = plane_second(plane_first(pair_sum(rest)))
        last = dp_sum(jnp.concatenate([pieces[-1][1], last], 1))
        sums = [None] * (LAYERS + 1 - late) + [p[1] for p in pieces[LAYERS + 1 - late : -1]] + [last]
    else:
        sums = [whole_sum([p[1]]) for p in pieces + [[0, rest]]]
        early = together(sums[1 : LAYERS + 1 - late] + sums[:1])
    early_got = lax.all_gather(early, "seq", axis=0, tiled=False)
    late_part, early_got = tied(together(sums[LAYERS + 1 - late :]), early_got)
    late_got = lax.all_gather(late_part, "seq", axis=0, tiled=False)
    head_start = (LAYERS - late) * 2 * sub_in
    g_head = early_got[:, head_start:].reshape(-1)[: head_w.size].reshape(head_w.shape).astype(f32)
    flat = late_got[:, late * 2 * sub_in :].reshape(-1).astype(f32)
    flat = [flat[a:b] for a, b in zip(cuts, cuts[1:])]
    shards = (
        flat[0].reshape(embed_w.shape),
        None,
        None,
        flat[1].reshape(dw_kernel.shape),
        g_head,
        flat[2].reshape(norm_gain.shape),
        flat[3].reshape(norm_bias.shape),
    )

    gsq_local = sum(jnp.sum(jnp.square(g.astype(f32))) for g in (early_got, late_got))
    wsq_local = group_sums(tuple((w * w for w in masters)))
    gsq, wsq, loss = lax.psum((gsq_local, wsq_local, loss_seq), "dp")
    grad_norm = jnp.sqrt(gsq)
    factor = jnp.minimum(1.0, clip_limit / grad_norm)

    proj_spec = pl.BlockSpec((1,) + in_proj.shape[1:], lambda l: (l, 0, 0))
    down_spec = pl.BlockSpec((1,) + down_proj.shape[1:], lambda l: (l, 0, 0, 0))
    block = (n_seq, 2 * sub_in, wide)
    blocks_of = [early_got, late_got]
    if 2 * sub_in % 8:
        block = (n_seq, 1, 2 * sub_in, wide)
        counts = (LAYERS - late, late)
        blocks_of = [
            g[:, : n * 2 * sub_in].reshape(n_seq, n, 2 * sub_in, wide)
            for g, n in zip(blocks_of, counts)
        ]
    tail = (0,) * (len(block) - 2)
    got = pl.pallas_call(
        functools.partial(update_body, cols, subs, late),
        grid=(LAYERS,),
        out_shape=[jax.ShapeDtypeStruct(in_proj.shape, f32)] * 3
        + [jax.ShapeDtypeStruct(down_proj.shape, f32)] * 3
        + [jax.ShapeDtypeStruct((LAYERS, 8, LANES), f32)],
        in_specs=[
            pl.BlockSpec(memory_space=pltpu.SMEM),
            pl.BlockSpec(block, lambda l: (0, jnp.minimum(LAYERS - 1 - l, LAYERS - 1 - late), *tail)),
            pl.BlockSpec(block, lambda l: (0, jnp.maximum(late - 1 - l, 0), *tail)),
        ]
        + [proj_spec] * 3
        + [down_spec] * 3,
        out_specs=[proj_spec] * 3 + [down_spec] * 3 + [pl.BlockSpec((1, 8, LANES), lambda l: (l, 0, 0))],
        compiler_params=pltpu.CompilerParams(vmem_limit_bytes=56 << 20),
        cost_estimate=cost(25),
    )(factor.reshape(1), *blocks_of, in_proj, m_proj, v_proj, down_proj, m_down, v_down)
    big = {1: got[0:3], 2: got[3:6]}
    new_m, new_v, updates = ([], [], [])
    for n, (w, g, m, v) in enumerate(zip(masters, shards, firsts, seconds)):
        m2, v2, u = big[n] if n in big else moments(w, g * factor, m, v)
        new_m.append(m2)
        new_v.append(v2)
        updates.append(u)
    usq = lax.psum(
        group_sums(
            tuple((u * u for u in updates)), jnp.sum(got[6][:, 0, : 4 + 3 * LAYERS], 0)
        ),
        "dp",
    )
    wnorm = jnp.sqrt(wsq)
    unorm = jnp.sqrt(usq)
    ratio = wnorm / unorm
    spreads = spread_ratio(ratio)
    new_w = [w - learn_rate * r * u for w, r, u in zip(masters, spreads, updates)]
    stats = jnp.stack([wnorm, unorm])
    return (loss, grad_norm, stats, ratio, *new_w, *new_m, *new_v)


def solution(mesh):
    placed = (
        P("dp", None),
        P(None, "dp", None),
        P(None, None, "dp", None),
        P(None, None, "dp"),
        P("dp", None),
        P(None, "dp"),
        P(None, "dp"),
    )
    in_specs = (
        P("dp", "seq", None, None),
        P("dp", None),
        P("dp"),
        P("dp"),
        P("dp"),
    ) + placed * 3
    out_specs = (P(), P(), P(), P()) + placed * 3
    return jax.shard_map(
        per_device, mesh=mesh, in_specs=in_specs, out_specs=out_specs, check_vma=False
    )
```

```python
import functools

import jax
import jax.numpy as jnp
from jax import lax
from jax.experimental import pallas as pl
from jax.experimental.pallas import tpu as pltpu
from jax.sharding import PartitionSpec as P

D = 320
HEADS = 5
HD = 64
FF = 1280
CLS = 1000
W = 64
HALF = W // 2
LAYERS = 6
STEP = 5
LANES = 128


norm_eps = 1e-06
scale_qk = 0.125
big_neg = -1e30
beta_one = 0.9
beta_two = 0.999
lamb_eps = 1e-06
decay_rate = 0.01
learn_rate = 0.3
clip_limit = 0.1
root_half = 0.7071067811865476
root_two_pi = 0.3989422804014327
precise = lax.Precision.HIGHEST

f32 = jnp.float32
bf16 = jnp.bfloat16


def to_bf(v):
    return v.astype(bf16)


def dot(a, b):
    return jnp.dot(a, b, preferred_element_type=f32)


def dot_nt(a, b, precision=None):
    return lax.dot_general(
        a, b, (((1,), (1,)), ((), ())), precision=precision, preferred_element_type=f32
    )


def contract(a, b, precision=None):
    return lax.dot_general(
        a, b, (((0,), (0,)), ((), ())), precision=precision, preferred_element_type=f32
    )


def norm_parts(v):
    center = v - jnp.mean(v, -1, keepdims=True)
    spread = jnp.mean(center * center, -1, keepdims=True)
    scale = lax.rsqrt(spread + norm_eps)
    return center * scale, scale


def layer_norm(v, gain, bias):
    return norm_parts(v)[0] * gain + bias


def norm_back(v, gain, grad):
    unit, scale = norm_parts(v)
    dgain = jnp.sum(grad * unit, 0, keepdims=True)
    dbias = jnp.sum(grad, 0, keepdims=True)
    t = grad * gain
    dv = scale * (
        t - jnp.mean(t, -1, keepdims=True) - unit * jnp.mean(t * unit, -1, keepdims=True)
    )
    return dv, dgain, dbias


def cost(us):
    return pl.CostEstimate(flops=int(us * 1e8), bytes_accessed=int(us * 1e5), transcendentals=0)


def run(us, body, outs, *args, place=None):
    vm = pl.BlockSpec(memory_space=pltpu.VMEM)
    scalars = [] if place is None else [place]
    return pl.pallas_call(
        body,
        out_shape=[jax.ShapeDtypeStruct(s, d) for s, d in outs],
        in_specs=[pl.BlockSpec(memory_space=pltpu.SMEM)] * len(scalars) + [vm] * len(args),
        out_specs=[vm] * len(outs),
        compiler_params=pltpu.CompilerParams(vmem_limit_bytes=48 << 20),
        cost_estimate=cost(us),
    )(*scalars, *args)


def cells_of(v):
    rows = v.shape[0] // W
    split = v.reshape(rows // 2, 2, 2, HALF, v.shape[1])
    return [split[:, k // 2, k % 2].reshape(-1, v.shape[1]) for k in range(4)]


def attention_inputs(x, gain, bias, wq, wsr, wkv, a_ref, q_ref, r_ref, rn_ref, kv_ref):
    a = to_bf(layer_norm(x, gain[0:1], bias[0:1]))
    a_ref[...] = a
    q_ref[...] = to_bf(dot(a, wq[...]))
    total = None
    for k, cell in enumerate(cells_of(a)):
        part = dot(cell, wsr[k * D : (k + 1) * D, :])
        total = part if total is None else total + part
    r_ref[...] = total
    rn = to_bf(layer_norm(total, gain[1:2], bias[1:2]))
    rn_ref[...] = rn
    kv_ref[...] = to_bf(dot(rn, wkv[...]))


def embed_body(p_ref, w_ref, ln_ref, e_ref, x_ref):
    e = dot(p_ref[...], w_ref[...])
    e_ref[...] = e
    x_ref[...] = layer_norm(e, ln_ref[0:1], ln_ref[1:2])


def embed_back_body(p_ref, de_ref, dw_ref):
    dw_ref[...] = contract(p_ref[...], de_ref[...])


def first_body(x_ref, gain, bias, wq, wsr, wkv, *outs):
    attention_inputs(x_ref[...], gain, bias, wq, wsr, wkv, *outs)


def middle_body(
    place, q_ref, kv_ref, ok_ref, x_ref, gain, bias, wo, w1, o_ref, lse_ref, x2_ref, b_ref, h_ref, edge_ref
):
    q = q_ref[...] * jnp.asarray(scale_qk, bf16)
    keys = kv_ref.shape[0]
    kv = kv_ref[...]
    shut = jnp.broadcast_to(ok_ref[...], (keys, q.shape[0]))
    q_t = q.T
    v_t = kv[:, D:].T
    parts = []
    for head in range(HEADS):
        low, high = head * HD, (head + 1) * HD
        s = dot(kv[:, low:high], q_t[low:high, :]) + shut
        top = jnp.max(s, 0, keepdims=True)
        expo = jnp.exp(s - top)
        total = jnp.sum(expo, 0, keepdims=True)
        lse_ref[head : head + 1, :] = top + jnp.log(total)
        p = to_bf(expo * (1.0 / total))
        parts.append(dot(v_t[low:high, :], p))
    o = to_bf(jnp.concatenate(parts, 0).T)
    o_ref[...] = o
    x2 = x_ref[...] + dot(o, wo[...])
    x2_ref[...] = x2
    b = to_bf(layer_norm(x2, gain[2:3], bias[2:3]))
    b_ref[...] = b
    h_ref[...] = to_bf(dot(b, w1[...]))
    send_edge(place, h_ref, edge_ref)


def shift_down(v):
    index = lax.broadcasted_iota(jnp.int32, v.shape, 0)
    return jnp.where(index == 0, 0.0, pltpu.roll(v, 1, 0))


def shift_up(v):
    index = lax.broadcasted_iota(jnp.int32, v.shape, 0)
    return jnp.where(index == v.shape[0] - 1, 0.0, pltpu.roll(v, v.shape[0] - 1, 0))


def from_left(v):
    return jnp.concatenate([shift_down(v[HALF:]), v[:HALF]], 0)


def from_right(v):
    return jnp.concatenate([v[HALF:], shift_up(v[:HALF])], 0)


def row_of(main, near, i, rows, lanes):
    place, low, high = near
    if i < 0:
        return jnp.where(place[0] > 0, low[:, lanes].astype(f32), 0.0)
    if i >= rows:
        return jnp.where(place[1] > 0, high[:, lanes].astype(f32), 0.0)
    return main[i * W : (i + 1) * W, lanes].astype(f32)


def send_edge(place, main, edge_ref):
    start = pl.multiple_of(jnp.where(place[0] > 0, 0, main.shape[0] - W), W)
    edge_ref[...] = main[pl.ds(start, W), :]


def conv_gelu(h_ref, ends, taps_ref, g_ref, slope_ref):
    rows = h_ref.shape[0] // W

    def chunk(c, carry):
        lanes = pl.ds(pl.multiple_of(c * LANES, LANES), LANES)
        taps = [taps_ref[k : k + 1, lanes] for k in range(9)]
        near = [row_of(h_ref, ends, i, rows, lanes) for i in (-1, 0)]
        for i in range(rows):
            near.append(row_of(h_ref, ends, i + 1, rows, lanes))
            sums = [
                taps[j] * near[0] + taps[3 + j] * near[1] + taps[6 + j] * near[2] for j in range(3)
            ]
            z = sums[1] + from_left(sums[0]) + from_right(sums[2])
            phi = 0.5 + 0.5 * lax.erf(z * root_half)
            here = slice(i * W, (i + 1) * W)
            g_ref[here, lanes] = to_bf(z * phi)
            slope_ref[here, lanes] = phi + z * (jnp.exp(-0.5 * z * z) * root_two_pi)
            near = near[1:]
        return carry

    lax.fori_loop(0, FF // LANES, chunk, 0)


def last_body(place, h_ref, low_ref, high_ref, taps_ref, x2_ref, w2, ln_ref, ok_ref, g_ref, slope_ref, x_ref, sum_ref):
    conv_gelu(h_ref, (place, low_ref, high_ref), taps_ref, g_ref, slope_ref)
    x = x2_ref[...] + dot(g_ref[...], w2[...])
    x_ref[...] = x
    fin = layer_norm(x, ln_ref[0:1], ln_ref[1:2])
    sum_ref[...] = jnp.sum(fin * ok_ref[...], 0, keepdims=True)


def join_body(
    place, h_ref, low_ref, high_ref, taps_ref, x2_ref, w2, gain, bias, wq, wsr, wkv, g_ref, slope_ref, x_ref, *outs
):
    conv_gelu(h_ref, (place, low_ref, high_ref), taps_ref, g_ref, slope_ref)
    x = x2_ref[...] + dot(g_ref[...], w2[...])
    x_ref[...] = x
    attention_inputs(x, gain, bias, wq, wsr, wkv, *outs)


def gelu_back(place, dx, w2, slope_ref, dy_ref, dz_ref, edge_ref):
    dy = to_bf(dx)
    dy_ref[...] = dy
    dg = to_bf(dot_nt(dy, w2[...])).astype(f32)
    dz_ref[...] = to_bf(dg * slope_ref[...])
    send_edge(place, dz_ref, edge_ref)


def head_body(
    images,
    place,
    pool_ref,
    count_ref,
    head_ref,
    target_ref,
    x_ref,
    ln_ref,
    ok_ref,
    w2,
    slope_ref,
    loss_ref,
    pooled_ref,
    dlog_ref,
    dln_ref,
    dx_ref,
    dy_ref,
    dz_ref,
    edge_ref,
):
    count = count_ref[...]
    pooled = to_bf(pool_ref[...] / count)
    pooled_ref[...] = pooled
    logits = dot(jnp.broadcast_to(pooled.astype(f32), (16, D)).astype(bf16), head_ref[...])[0:1]
    shifted = logits - jnp.max(logits, -1, keepdims=True)
    logp = shifted - jnp.log(jnp.sum(jnp.exp(shifted), -1, keepdims=True))
    target = target_ref[...]
    loss_ref[...] = jnp.sum(target * logp, -1, keepdims=True) * (-1.0 / images)
    dlog = to_bf((jnp.exp(logp) - target) * (1.0 / images))
    dlog_ref[...] = dlog
    wide = jnp.broadcast_to(dlog.astype(f32), (16, CLS)).astype(bf16)
    dpool = dot_nt(wide, head_ref[...])[0:1] / count
    dx, dgain, dbias = norm_back(x_ref[...], ln_ref[0:1], ok_ref[...] * dpool)
    dln_ref[0:1, :] = dgain
    dln_ref[1:2, :] = dbias
    dx_ref[...] = dx
    gelu_back(place, dx, w2, slope_ref, dy_ref, dz_ref, edge_ref)


def conv_back(h_ref, hends, dz_ref, zends, taps_ref, dh_ref, dtaps_ref):
    rows = h_ref.shape[0] // W

    def chunk(c, carry):
        lanes = pl.ds(pl.multiple_of(c * LANES, LANES), LANES)
        taps = [taps_ref[k : k + 1, lanes] for k in range(9)]
        acc = [jnp.zeros((8, LANES), f32) for _ in range(9)]

        def views(i):
            v = row_of(dz_ref, zends, i, rows, lanes)
            return [from_right(v), v, from_left(v)]

        near = [views(-1), views(0)]
        hear = [row_of(h_ref, hends, i, rows, lanes) for i in (-1, 0)]
        for i in range(rows):
            near.append(views(i + 1))
            hear.append(row_of(h_ref, hends, i + 1, rows, lanes))
            dh = None
            for di in range(3):
                for dj in range(3):
                    part = taps[3 * di + dj] * near[2 - di][dj]
                    dh = part if dh is None else dh + part
            dh_ref[i * W : (i + 1) * W, lanes] = to_bf(dh)
            for di in range(3):
                for dj in range(3):
                    prod = (hear[di] * near[1][dj]).reshape(W // 8, 8, LANES)
                    acc[3 * di + dj] = acc[3 * di + dj] + jnp.sum(prod, 0)
            near = near[1:]
            hear = hear[1:]
        for k in range(9):
            dtaps_ref[k : k + 1, lanes] = jnp.sum(acc[k], 0, keepdims=True)
        return carry

    lax.fori_loop(0, FF // LANES, chunk, 0)


def block_back_body(
    place,
    h_ref,
    hlow_ref,
    hhigh_ref,
    dz_ref,
    zlow_ref,
    zhigh_ref,
    taps_ref,
    w1,
    x2_ref,
    gain,
    dx_ref,
    wo,
    q_ref,
    kv_ref,
    ok_ref,
    lse_ref,
    dh_ref,
    dtaps_ref,
    dln_ref,
    dx2_ref,
    dy_ref,
    dq_ref,
    dkv_ref,
):
    conv_back(
        h_ref, (place, hlow_ref, hhigh_ref), dz_ref, (place, zlow_ref, zhigh_ref), taps_ref, dh_ref, dtaps_ref
    )
    db = dot_nt(dh_ref[...], w1[...])
    dln, dgain, dbias = norm_back(x2_ref[...], gain[2:3], db)
    dln_ref[0:1, :] = dgain
    dln_ref[1:2, :] = dbias
    dx2 = dx_ref[...] + dln
    dx2_ref[...] = dx2
    dy = to_bf(dx2)
    dy_ref[...] = dy
    do_t = to_bf(dot_nt(wo[...], dy))
    q = q_ref[...] * jnp.asarray(scale_qk, bf16)
    q_t = q.T
    keys = kv_ref.shape[0]
    kv = kv_ref[...]
    k_t = (kv[:, :D] * jnp.asarray(scale_qk, bf16)).T
    shut = jnp.broadcast_to(ok_ref[...], (keys, q.shape[0]))
    dq_parts, dk_parts, dv_parts = ([], [], [])
    for head in range(HEADS):
        low, high = head * HD, (head + 1) * HD
        s = dot(kv[:, low:high], q_t[low:high, :]) + shut
        p = jnp.exp(s - lse_ref[head : head + 1, :])
        dp = dot(kv[:, D + low : D + high], do_t[low:high, :])
        dv_parts.append(dot_nt(do_t[low:high, :], to_bf(p)))
        ds = to_bf(p * (dp - jnp.sum(p * dp, 0, keepdims=True)))
        dq_parts.append(dot(k_t[low:high, :], ds))
        dk_parts.append(dot_nt(q_t[low:high, :], ds))
    dq_ref[...] = to_bf(jnp.concatenate(dq_parts, 0).T)
    dkv_ref[...] = jnp.concatenate(dk_parts + dv_parts, 0).T


def inputs_back(dkv, wkv, r_ref, gain, dq_ref, wq, wsr, x_ref, dx2_ref, dr_ref, dln_ref):
    w_kv = wkv[...].astype(f32)
    drn = dot_nt(dkv, w_kv, precise)
    dr, dgain1, dbias1 = norm_back(r_ref[...], gain[1:2], drn)
    dr = to_bf(dr)
    dr_ref[...] = dr
    rows = x_ref.shape[0] // W
    cells = [
        dot_nt(dr, wsr[k * D : (k + 1) * D, :]).reshape(rows // 2, 1, 1, HALF, D) for k in range(4)
    ]
    placed = jnp.concatenate(
        [jnp.concatenate(cells[0:2], 2), jnp.concatenate(cells[2:4], 2)], 1
    ).reshape(rows * W, D)
    da = dot_nt(dq_ref[...], wq[...]) + placed
    dln, dgain0, dbias0 = norm_back(x_ref[...], gain[0:1], da)
    for k, row in enumerate((dgain0, dgain1, dbias0, dbias1)):
        dln_ref[k : k + 1, :] = row
    return dx2_ref[...] + dln


def join_back_body(
    place, dkv_ref, wkv, r_ref, gain, dq_ref, wq, wsr, x_ref, dx2_ref, w2, slope_ref,
    dr_ref, dln_ref, dx_ref, dy_ref, dz_ref, edge_ref
):
    dx = inputs_back(dkv_ref[...], wkv, r_ref, gain, dq_ref, wq, wsr, x_ref, dx2_ref, dr_ref, dln_ref)
    dx_ref[...] = dx
    gelu_back(place, dx, w2, slope_ref, dy_ref, dz_ref, edge_ref)


def first_back_body(
    dkv_ref, wkv, r_ref, gain, dq_ref, wq, wsr, x_ref, dx2_ref, e_ref, ln_ref, dr_ref, dln_ref, de_ref, dle_ref
):
    dx = inputs_back(dkv_ref[...], wkv, r_ref, gain, dq_ref, wq, wsr, x_ref, dx2_ref, dr_ref, dln_ref)
    de, dgain, dbias = norm_back(e_ref[...], ln_ref[0:1], dx)
    de_ref[...] = to_bf(de)
    dle_ref[0:1, :] = dgain
    dle_ref[1:2, :] = dbias


def weight_grads_body(
    n_dp, cols, subs, core_ref, a_ref, dq_ref, rn_ref, dkv_ref, o_ref, dy2_ref, b_ref, dh_ref, dr_ref, g_ref, dy_ref, *refs
):
    outs, (proj, down) = refs[:-2], refs[-2:]
    a = a_ref[...]
    proj[:, :D] = contract(a, dq_ref[...])
    proj[:, D : 3 * D] = contract(rn_ref[...].astype(f32), dkv_ref[...], precise)
    proj[:, 3 * D : 4 * D] = contract(o_ref[...], dy2_ref[...])
    proj[:, 4 * D :] = contract(b_ref[...], dh_ref[...])
    dr = dr_ref[...]
    for k, cell in enumerate(cells_of(a)):
        down[k * D : (k + 1) * D, :D] = contract(cell, dr)
    down[:, D:] = contract(g_ref[...], dy_ref[...])
    rows = D // n_dp
    sub = rows // subs
    wide = (4 * D + FF) // cols
    down_rows = FF // n_dp
    for c in range(cols):
        for d in range(n_dp):
            for n, out in enumerate(outs):
                for j in range(subs) if len(outs) == 1 else (None,):
                    if j is None:
                        k = core_ref[0] if n == 0 else 1 - core_ref[0]
                        at = (c ^ core_ref[1], d)
                    else:
                        k = j
                        at = (c, j, d)
                    start = d * rows + k * sub
                    low = d * down_rows + (c * subs + k) * (down_rows // (cols * subs))
                    if j is None:
                        start = pl.multiple_of(start, 8)
                        low = pl.multiple_of(low, 8)
                    out[(*at, slice(0, sub))] = proj[pl.ds(start, sub), c * wide : (c + 1) * wide]
                    out[(*at, slice(sub, 2 * sub))] = down[pl.ds(low, sub), :]


def moments(w, g, m, v):
    m2 = beta_one * m + (1.0 - beta_one) * g
    v2 = beta_two * v + (1.0 - beta_two) * g * g
    u = (
        m2 / (1.0 - beta_one**STEP) / (jnp.sqrt(v2 / (1.0 - beta_two**STEP)) + lamb_eps)
        + decay_rate * w
    )
    return m2, v2, u


def update_body(
    cols, subs, late, factor_ref, early_ref, late_ref, wp, mp, vp, wd, md, vd, mp2, vp2, up, md2, vd2, ud, sums
):
    factor = factor_ref[0]
    layer = pl.program_id(0)
    sub = wp.shape[1] // subs
    wide = wp.shape[2] // cols

    def go(g_ref):
        squares = [0.0, 0.0]

        def put(n, at, refs, outs, g):
            new = moments(refs[0][at], g * factor, refs[1][at], refs[2][at])
            for out, value in zip(outs, new):
                out[at] = value
            squares[n] = squares[n] + jnp.sum(new[2] * new[2], 0, keepdims=True)

        for c in range(cols):
            for k in range(subs):
                g = g_ref[c * subs + k].astype(f32).reshape(2 * sub, wide)
                at = (0, slice(k * sub, (k + 1) * sub), slice(c * wide, (c + 1) * wide))
                put(0, at, (wp, mp, vp), (mp2, vp2, up), g[:sub])
                rows = slice((c * subs + k) * sub, (c * subs + k + 1) * sub)
                for half in range(2):
                    at = (0, half, rows, slice(0, D))
                    put(1, at, (wd, md, vd), (md2, vd2, ud), g[sub:, half * D : (half + 1) * D])
        lane = lax.broadcasted_iota(jnp.int32, (1, LANES), 1)
        total = jnp.zeros((1, LANES), f32)
        for n in range(2):
            value = jnp.broadcast_to(jnp.sum(squares[n], 1, keepdims=True), (1, LANES))
            total = jnp.where(lane == 4 + n * LAYERS + layer, value, total)
        sums[0] = jnp.broadcast_to(total, sums.shape[1:])

    pl.when(layer >= late)(lambda: go(early_ref))
    pl.when(layer < late)(lambda: go(late_ref))


def group_sums(arrs, layered=None):
    embed, proj, downs, taps, head, gains, biases = arrs
    slot = lax.broadcasted_iota(jnp.int32, (1, 4 + 3 * LAYERS), 1)

    def placed(values, start):
        at = lax.broadcasted_iota(jnp.int32, (values.shape[0], 1), 0) + start
        return jnp.sum(jnp.where(at == slot, values[:, None], 0.0), 0)

    total = placed(jnp.sum(taps, (1, 2)), 4 + 2 * LAYERS)
    for n, a in enumerate((embed, head, gains, biases)):
        total = total + jnp.where(slot[0] == n, jnp.sum(a), 0.0)
    if layered is not None:
        return total + layered
    for n, a in enumerate((proj, downs)):
        total = total + placed(jnp.sum(a.reshape(a.shape[0], -1), 1), 4 + n * LAYERS)
    return total


def spread_ratio(ratio):
    return (
        ratio[0],
        ratio[4 : 4 + LAYERS].reshape(LAYERS, 1, 1),
        ratio[4 + LAYERS : 4 + 2 * LAYERS].reshape(LAYERS, 1, 1, 1),
        ratio[4 + 2 * LAYERS : 4 + 3 * LAYERS].reshape(LAYERS, 1, 1),
        ratio[1],
        ratio[2],
        ratio[3],
    )


def per_device(
    patches,
    valid,
    labels,
    partners,
    mix,
    embed_w,
    in_proj,
    down_proj,
    dw_kernel,
    head_w,
    norm_gain,
    norm_bias,
    m_embed,
    m_proj,
    m_down,
    m_taps,
    m_head,
    m_gain,
    m_bias,
    v_embed,
    v_proj,
    v_down,
    v_taps,
    v_head,
    v_gain,
    v_bias,
):
    masters = (embed_w, in_proj, down_proj, dw_kernel, head_w, norm_gain, norm_bias)
    firsts = (m_embed, m_proj, m_down, m_taps, m_head, m_gain, m_bias)
    seconds = (v_embed, v_proj, v_down, v_taps, v_head, v_gain, v_bias)
    n_seq = lax.axis_size("seq")
    n_dp = lax.axis_size("dp")
    seq_pos = lax.axis_index("seq")
    img_dev, rows = (patches.shape[0], patches.shape[1])
    images = img_dev * n_dp

    team = n_seq
    while team * img_dev > n_seq:
        team //= 2
    blocks = n_seq // team
    rows_own = rows * blocks
    tok = rows_own * W
    keys_own = tok // 4
    image = jnp.minimum(seq_pos // team, img_dev - 1)
    busy = seq_pos // team < img_dev
    place = seq_pos % team

    def between(shift, wrap):
        pairs = []
        for base in range(0, n_seq, team):
            for h in range(team):
                if wrap or 0 <= h + shift < team:
                    pairs.append((base + (h + shift) % team, base + h))
        return pairs

    ends = jnp.stack([place > 0, place < team - 1]).astype(jnp.int32)

    def edges(v, edge):
        if team == 2:
            other = lax.ppermute(edge, "seq", between(1, True))
            return other, other
        low = lax.ppermute(v[-W:], "seq", between(-1, False))
        high = lax.ppermute(v[:W], "seq", between(1, False))
        return low, high

    def all_keys(v):
        return jnp.concatenate(
            [v] + [lax.ppermute(v, "seq", between(j, True)) for j in range(1, team)], 0
        )

    def own_keys(v):
        total = v[:keys_own]
        for j in range(1, team):
            part = v[j * keys_own : (j + 1) * keys_own]
            total = total + lax.ppermute(part, "seq", between(-j, True))
        return total

    back_block = seq_pos % blocks
    routes = [
        [
            (blocks * h + (i + r) % blocks, team * i + h)
            for i in range(img_dev)
            for h in range(team)
        ]
        for r in range(blocks)
    ]

    def to_team(v):
        got = []
        for r, pairs in enumerate(routes):
            send = lax.dynamic_index_in_dim(
                v, jnp.minimum((back_block - r) % blocks, img_dev - 1), 0, keepdims=False
            )
            got.append(lax.ppermute(send, "seq", pairs))
        twice = jnp.stack(got + got)
        own = lax.dynamic_slice_in_dim(twice, (blocks - image) % blocks, blocks, 0)
        return own.reshape(tok, -1)

    cols = 4
    subs = n_seq // cols
    row_in = D // n_dp
    sub_in = row_in // subs
    wide = in_proj.shape[2] // cols
    down_rows = down_proj.shape[2] // n_seq
    core = seq_pos % subs

    def part_of(flat):
        size = -(-flat.shape[0] // (wide * n_seq)) * wide * n_seq
        flat = jnp.pad(flat, (0, size - flat.shape[0])).reshape(n_seq, -1, wide)
        return lax.dynamic_index_in_dim(flat, seq_pos, 0, keepdims=False)

    def layer_part(l):
        block = lax.dynamic_slice(
            in_proj[l], (core * sub_in, (seq_pos // subs) * wide), (sub_in, wide)
        )
        lower = lax.dynamic_slice_in_dim(down_proj[l], seq_pos * down_rows, down_rows, 1)
        return [to_bf(block), to_bf(jnp.concatenate([lower[0], lower[1]], 1))]

    def gathered(part):
        return lax.all_gather(part.reshape(-1, wide), "seq", axis=0, tiled=False)

    def cut(got, sizes):
        got = got.reshape(n_seq, n_dp, sum(sizes), wide).transpose(1, 0, 2, 3)
        starts = [sum(sizes[:i]) for i in range(len(sizes))]
        return [got[:, :, a : a + n] for a, n in zip(starts, sizes)]

    def proj_of(got):
        got = got.reshape(n_dp, cols, subs, sub_in, wide).transpose(0, 2, 3, 1, 4)
        return got.reshape(D, cols * wide)

    dp_pos = lax.axis_index("dp")

    def over_dp(v):
        got = [v] + [
            lax.ppermute(v, "dp", [((d + j) % n_dp, d) for d in range(n_dp)])
            for j in range(1, n_dp)
        ]
        return lax.dynamic_slice_in_dim(jnp.stack(got + got), (n_dp - dp_pos) % n_dp, n_dp, 0)

    groups = [[0], [1, 2], [3, 4], [5]]
    extra = [[], [], [], [part_of(to_bf(head_w).reshape(-1))]]

    def layers_of(got, count):
        return [(proj_of(got[2 * i]), got[2 * i + 1].reshape(FF, 2 * D)) for i in range(count)]

    parts_of = [more + [p for l in members for p in layer_part(l)] for members, more in zip(groups, extra)]
    sizes_of = [[p.shape[0] for p in parts] for parts in parts_of]
    lines = [over_dp(jnp.concatenate(parts, 0)) for parts in parts_of[:2]]
    norms = jnp.stack([norm_gain, norm_bias])
    small = jnp.concatenate([to_bf(v).reshape(-1, D) for v in (embed_w, dw_kernel, norms)], 0)
    small, lines[0] = lax.optimization_barrier((small, lines[0]))
    small = over_dp(small)
    marks = (embed_w.shape[0], embed_w.shape[0] + dw_kernel.size // D)
    embed16 = small[:, : marks[0]].reshape(-1, D)
    taps32 = small[:, marks[0] : marks[1]].reshape(n_dp, LAYERS * 9, -1).transpose(1, 0, 2)
    taps32 = taps32.reshape(LAYERS, 9, FF).astype(f32)
    norms32 = small[:, marks[1] :].reshape(n_dp, 2, -1, row_in).transpose(1, 2, 0, 3)
    norms32 = norms32.reshape(2, -1, D).astype(f32)
    gain32, bias32 = norms32[0], norms32[1]

    def total_over_dp(v):
        got = [v] + [
            lax.ppermute(v, "dp", [((d + j) % n_dp, d) for d in range(n_dp)])
            for j in range(1, n_dp)
        ]
        index = lax.broadcasted_iota(jnp.int32, (n_dp, 1), 0)
        rows_of = [jnp.where(index == (dp_pos + j) % n_dp, g, 0.0) for j, g in enumerate(got)]
        return jnp.sum(sum(rows_of), 0)
    raw = [gathered(lines[0])]
    first_of = {members[0]: n for n, members in enumerate(groups)}

    def own(v):
        return lax.dynamic_index_in_dim(v, image, 0, keepdims=False)

    wanted = own(partners)
    partner_label = jnp.zeros((), jnp.int32)
    for j in range(n_dp):
        other = labels
        if j:
            other = lax.ppermute(labels, "dp", [((d + j) % n_dp, d) for d in range(n_dp)])
        index = ((dp_pos + j) % n_dp) * img_dev + jnp.arange(img_dev)
        partner_label = partner_label + jnp.sum(jnp.where(index == wanted, other, 0))
    valid_own = own(valid)
    tid = lax.broadcasted_iota(jnp.int32, (tok, 1), 0)
    within = tid % W
    row_id = place * rows_own + tid // W
    col_id = 2 * (within % HALF) + within // HALF
    okay = ((row_id < valid_own[0]) & (col_id < valid_own[1]) & busy).astype(f32)
    kid = lax.broadcasted_iota(jnp.int32, (team * keys_own, 1), 0)
    segment = (place + kid // keys_own) % team
    key_row = segment * (rows_own // 2) + (kid % keys_own) // HALF
    key_ok = (2 * key_row < valid_own[0]) & (2 * (kid % HALF) < valid_own[1])
    shut = jnp.where(key_ok, 0.0, big_neg).astype(f32)
    count = (valid_own[0] * valid_own[1]).astype(f32).reshape(1, 1)
    classes = lax.broadcasted_iota(jnp.int32, (1, CLS), 1)
    mix_own = own(mix)
    target = mix_own * (classes == own(labels)).astype(f32) + (1.0 - mix_own) * (
        classes == partner_label
    ).astype(f32)

    def weights(l, layer):
        base = 1 + 3 * l
        return dict(
            wq=layer[0][:, :D],
            wkv=layer[0][:, D : 3 * D],
            wo=layer[0][:, 3 * D : 4 * D],
            w1=layer[0][:, 4 * D :],
            wsr=layer[1][:, :D],
            w2=layer[1][:, D:],
            taps=taps32[l],
            gain=gain32[base : base + 3],
            bias=bias32[base : base + 3],
        )

    full = ((tok, D), f32)
    ln_first = jnp.stack([gain32[0], bias32[0]])
    spread = patches.reshape(img_dev, rows, HALF, 2, -1).transpose(0, 1, 3, 2, 4)
    patch_own = to_team(spread.reshape(img_dev, rows * W, -1))
    e, x = run(2, embed_body, [full, full], patch_own, embed16, ln_first)
    lines[1], x = lax.optimization_barrier((lines[1], x))
    raw.append(gathered(lines[1]))
    wts = [weights(l, layer) for l, layer in zip(groups[0], layers_of(cut(raw[0], sizes_of[0]), len(groups[0])))]
    ln_last = jnp.stack([gain32[-1], bias32[-1]])

    half = ((tok, D), bf16)
    wide16 = ((tok, FF), bf16)
    input_outs = [half, half, ((keys_own, D), f32), ((keys_own, D), bf16), ((keys_own, 2 * D), bf16)]
    ln_out = ((2, D), f32)
    row16 = ((W, FF), bf16)

    w = wts[0]
    a16, q16, r, rn16, kv16 = run(
        2, first_body, input_outs, x, w["gain"], w["bias"], w["wq"], w["wsr"], w["wkv"]
    )
    kept = []
    for l in range(LAYERS):
        w = wts[l]
        if l + 2 < len(groups):
            parts, kv16 = lax.optimization_barrier((parts_of[l + 2], kv16))
            raw.append(gathered(over_dp(jnp.concatenate(parts, 0))))
        kv_all = all_keys(kv16)
        o16, lse, x2, b16, h16, edge = run(
            4,
            middle_body,
            [half, ((HEADS, tok), f32), full, half, wide16, row16],
            q16,
            kv_all,
            shut,
            x,
            w["gain"],
            w["bias"],
            w["wo"],
            w["w1"],
            place=ends,
        )
        hlow, hhigh = edges(h16, edge)
        keep = dict(
            x=x, a16=a16, q16=q16, r=r, rn16=rn16, kv=kv_all, o16=o16, lse=lse, x2=x2, b16=b16,
            h16=h16, hlow=hlow, hhigh=hhigh,
        )
        shared = (h16, hlow, hhigh, w["taps"], x2, w["w2"])
        if l + 1 in first_of:
            n = first_of[l + 1]
            got, _ = lax.optimization_barrier((raw[n], kv_all))
            got = cut(got, sizes_of[n])
            if extra[n]:
                head16 = got.pop(0).reshape(n_dp, -1)[:, : head_w.size].reshape(D, CLS)
            wts += [weights(m, layer) for m, layer in zip(groups[n], layers_of(got, len(groups[n])))]
        if l + 1 < LAYERS:
            n = wts[l + 1]
            keep["g16"], keep["slope"], x, a16, q16, r, rn16, kv16 = run(
                8,
                join_body,
                [wide16, ((tok, FF), f32), full] + input_outs,
                *shared,
                n["gain"],
                n["bias"],
                n["wq"],
                n["wsr"],
                n["wkv"],
                place=ends,
            )
        else:
            keep["g16"], keep["slope"], x, pool = run(
                7,
                last_body,
                [wide16, ((tok, FF), f32), full, ((1, D), f32)],
                *shared,
                ln_last,
                okay,
                place=ends,
            )
        kept.append(keep)

    whole = pool
    for j in range(1, team):
        whole = whole + lax.ppermute(pool, "seq", between(j, True))
    loss_own, pooled16, dlog16, dln_last, dx, dy16, dz16, edge = run(
        4,
        functools.partial(head_body, images),
        [((1, 1), f32), ((1, D), bf16), ((1, CLS), bf16), ln_out, full, half, wide16, row16],
        whole,
        count,
        head16,
        target,
        x,
        ln_last,
        okay,
        wts[-1]["w2"],
        kept[-1]["slope"],
        place=ends,
    )
    chosen = ((place == 0) & busy).astype(f32)
    d_head = pooled16.astype(f32).reshape(D, 1) * dlog16.astype(f32) * chosen
    loss_local = loss_own[0, 0] * busy.astype(f32)
    teams = n_seq // team
    loss_parts = jnp.zeros((teams,), f32)
    for j in range(teams):
        other = loss_local
        if j:
            other = lax.ppermute(
                loss_local, "seq", [((d + j * team) % n_seq, d) for d in range(n_seq)]
            )
        loss_parts = jnp.where(jnp.arange(teams) == (seq_pos // team + j) % teams, other, loss_parts)
    loss_seq = jnp.sum(loss_parts)

    piece = ((cols, n_dp, 2 * sub_in, wide), f32)
    paired = subs == 2 and cols == 4
    chip = seq_pos // subs
    where = jnp.stack([core, chip]).astype(jnp.int32)

    def weight_grads(*args):
        vm = pl.BlockSpec(memory_space=pltpu.VMEM)
        outs = [piece] * 2 if paired else [((cols, subs) + piece[0][1:], f32)]
        return pl.pallas_call(
            functools.partial(weight_grads_body, n_dp, cols, subs),
            out_shape=[jax.ShapeDtypeStruct(s, d) for s, d in outs],
            in_specs=[pl.BlockSpec(memory_space=pltpu.SMEM)] + [vm] * len(args),
            out_specs=[vm] * len(outs),
            scratch_shapes=[pltpu.VMEM((D, cols * wide), f32), pltpu.VMEM((FF, 2 * D), f32)],
            compiler_params=pltpu.CompilerParams(vmem_limit_bytes=48 << 20),
            cost_estimate=cost(6),
        )(where, *args)

    def padded_rest(parts):
        flat = jnp.concatenate(parts, 1)
        size = -(-flat.shape[1] // (16 * wide * n_seq)) * 16 * wide * n_seq
        flat = jnp.pad(flat, ((0, 0), (0, size - flat.shape[1])))
        flat = flat.reshape(n_dp, cols, subs, -1, wide).transpose(1, 2, 0, 3, 4)
        if not paired:
            return [flat]
        flat = jnp.stack([lax.dynamic_index_in_dim(flat, chip ^ j, 0, False) for j in range(cols)])
        return [lax.dynamic_index_in_dim(flat, k, 1, False) for k in (core, 1 - core)]

    def pair_sum(parts):
        mine, send = parts
        return mine + lax.ppermute(send, "seq", [(d ^ 1, d) for d in range(n_seq)])

    def over_chips(v, bit):
        return lax.ppermute(v, "seq", [(d ^ (bit * subs), d) for d in range(n_seq)])

    def plane_first(y):
        cut = y.shape[2] // 2
        one, two = y[:, :, :cut], y[:, :, cut:]
        moved = (to_bf(jnp.stack([one[1], one[3]])), to_bf(jnp.stack([two[2], two[3]])))
        got = (over_chips(moved[0], 1).astype(f32), over_chips(moved[1], 2).astype(f32))
        return [one[0] + got[0][0], one[2] + got[0][1], two[0] + got[1][0], two[1] + got[1][1]]

    def plane_second(parts):
        one = parts[0] + over_chips(parts[1].astype(wire[0]), 2).astype(f32)
        two = parts[2] + over_chips(parts[3].astype(wire[0]), 1).astype(f32)
        return jnp.concatenate([one, two], 1)

    def dp_sum(y):
        def of(j):
            return lax.dynamic_index_in_dim(y, (dp_pos + j) % n_dp, 0, keepdims=False)

        total = of(0)
        for j in range(1, n_dp):
            pairs = [(d, (d + j) % n_dp) for d in range(n_dp)]
            total = total + lax.ppermute(of(j).astype(wire[0]), "dp", pairs).astype(f32)
        return total

    def whole_sum(parts):
        y = jnp.concatenate([p[0] for p in parts], -2)
        y = lax.psum_scatter(y.reshape(-1, wide), "seq", scatter_dimension=0, tiled=True)
        return lax.psum_scatter(y, "dp", scatter_dimension=0, tiled=True)

    def tied(value, others):
        return lax.optimization_barrier((value, others))

    wire = [f32]
    stages = [pair_sum, plane_first, plane_second]
    pieces = []

    def advance(now):
        if not paired:
            return now
        ready = [p for p in pieces if p[0] <= len(stages) + 1]
        now, values = tied(now, [p[1] for p in ready])
        if wire[0] == bf16:
            values = [v if p[0] else p[1] for p, v in zip(ready, values)]
        for p, v in zip(ready, values):
            if p[0] < len(stages):
                p[1] = stages[p[0]](v)
            elif p[0] > len(stages) or p is pieces[0]:
                p[1] = v
            elif p is pieces[1]:
                p[1] = dp_sum(jnp.concatenate([v, pieces[0][1]], 1))
            else:
                p[1] = dp_sum(v)
            p[0] += 1
        return now

    grads = [None] * LAYERS
    pieces.append([0, padded_rest([d_head.reshape(n_dp, -1)])])
    waiting = None
    for l in reversed(range(LAYERS)):
        w, k = wts[l], kept[l]
        zlow, zhigh = edges(dz16, edge)
        upper = dy16
        dz16 = advance(dz16)
        dh16, d_taps, dln2, dx2, dy2, dq16, dkv = run(
            11,
            block_back_body,
            [wide16, ((9, FF), f32), ln_out, full, half, half, ((team * keys_own, 2 * D), f32)],
            k["h16"], k["hlow"], k["hhigh"], dz16, zlow, zhigh, w["taps"], w["w1"], k["x2"], w["gain"], dx,
            w["wo"], k["q16"], k["kv"], shut, k["lse"],
            place=ends,
        )
        if waiting is not None:
            first, _ = tied(waiting[0], dkv)
            pieces.append([0, weight_grads(first, *waiting[1:])])
        dkv_own = own_keys(dkv)
        dq16 = advance(dq16)
        shared = (dkv_own, w["wkv"], k["r"], w["gain"], dq16, w["wq"], w["wsr"], k["x"], dx2)
        if l:
            dr16, dln, dx, dy16, dz16, edge = run(
                6,
                join_back_body,
                [((keys_own, D), bf16), ((4, D), f32), full, half, wide16, row16],
                *shared,
                wts[l - 1]["w2"],
                kept[l - 1]["slope"],
                place=ends,
            )
        else:
            dr16, dln, de16, dln_first = run(
                3,
                first_back_body,
                [((keys_own, D), bf16), ((4, D), f32), half, ln_out],
                *shared,
                e,
                ln_first,
            )
        waiting = (k["a16"], dq16, k["rn16"], dkv_own, k["o16"], dy2, k["b16"], dh16, dr16, k["g16"], upper)
        grads[l] = (
            d_taps,
            jnp.concatenate([dln[0:2], dln2[0:1]], 0),
            jnp.concatenate([dln[2:4], dln2[1:2]], 0),
        )
    wire[0] = bf16
    pieces.append([0, weight_grads(*waiting)])
    de16 = advance(de16)
    (d_embed,) = run(3, embed_back_body, [((embed16.shape[0], D), f32)], patch_own, de16)
    d_embed = advance(d_embed)
    d_gain = jnp.concatenate([dln_first[0:1]] + [g[1] for g in grads] + [dln_last[0:1]], 0)
    d_bias = jnp.concatenate([dln_first[1:2]] + [g[2] for g in grads] + [dln_last[1:2]], 0)
    d_taps = jnp.stack([g[0] for g in grads])
    rest = [
        d_embed.reshape(n_dp, -1),
        d_taps.reshape(LAYERS * 9, n_dp, -1).transpose(1, 0, 2).reshape(n_dp, -1),
        d_gain.reshape(-1, n_dp, row_in).transpose(1, 0, 2).reshape(n_dp, -1),
        d_bias.reshape(-1, n_dp, row_in).transpose(1, 0, 2).reshape(n_dp, -1),
    ]
    cuts = [0]
    for part in rest:
        cuts.append(cuts[-1] + part.shape[1])
    rest = padded_rest(rest)

    late = 3

    def together(parts):
        return to_bf(jnp.concatenate(parts, 0))

    if paired:
        assert all(p[0] > len(stages) + 1 for p in pieces[: LAYERS + 1 - late])
        own_rows = 2 * sub_in
        parts = [p[1] for p in pieces[1 : LAYERS + 1 - late]]
        early = together([parts[0][:own_rows], *parts[1:], parts[0][own_rows:]])
        rest, early = tied(rest, early)
        rest = advance(rest)
        last = plane_second(plane_first(pair_sum(rest)))
        last = dp_sum(jnp.concatenate([pieces[-1][1], last], 1))
        sums = [None] * (LAYERS + 1 - late) + [p[1] for p in pieces[LAYERS + 1 - late : -1]] + [last]
    else:
        sums = [whole_sum([p[1]]) for p in pieces + [[0, rest]]]
        early = together(sums[1 : LAYERS + 1 - late] + sums[:1])
    early_got = lax.all_gather(early, "seq", axis=0, tiled=False)
    late_part, early_got = tied(together(sums[LAYERS + 1 - late :]), early_got)
    late_got = lax.all_gather(late_part, "seq", axis=0, tiled=False)
    head_start = (LAYERS - late) * 2 * sub_in
    g_head = early_got[:, head_start:].reshape(-1)[: head_w.size].reshape(head_w.shape).astype(f32)
    flat = late_got[:, late * 2 * sub_in :].reshape(-1).astype(f32)
    flat = [flat[a:b] for a, b in zip(cuts, cuts[1:])]
    shards = (
        flat[0].reshape(embed_w.shape),
        None,
        None,
        flat[1].reshape(dw_kernel.shape),
        g_head,
        flat[2].reshape(norm_gain.shape),
        flat[3].reshape(norm_bias.shape),
    )

    gsq_local = sum(jnp.sum(jnp.square(g.astype(f32))) for g in (early_got, late_got))
    wsq_local = group_sums(tuple((w * w for w in masters)))
    ends_of = jnp.where(jnp.arange(LANES) == LANES - 1, loss_seq, 0.0)
    first_sums = total_over_dp(
        jnp.where(jnp.arange(LANES) == LANES - 2, gsq_local, ends_of)
        + jnp.pad(wsq_local, (0, LANES - wsq_local.shape[0]))
    )
    gsq, wsq, loss = first_sums[LANES - 2], first_sums[: 4 + 3 * LAYERS], first_sums[LANES - 1]
    grad_norm = jnp.sqrt(gsq)
    factor = jnp.minimum(1.0, clip_limit / grad_norm)

    proj_spec = pl.BlockSpec((1,) + in_proj.shape[1:], lambda l: (l, 0, 0))
    down_spec = pl.BlockSpec((1,) + down_proj.shape[1:], lambda l: (l, 0, 0, 0))
    block = (n_seq, 2 * sub_in, wide)
    blocks_of = [early_got, late_got]
    if 2 * sub_in % 8:
        block = (n_seq, 1, 2 * sub_in, wide)
        counts = (LAYERS - late, late)
        blocks_of = [
            g[:, : n * 2 * sub_in].reshape(n_seq, n, 2 * sub_in, wide)
            for g, n in zip(blocks_of, counts)
        ]
    tail = (0,) * (len(block) - 2)
    got = pl.pallas_call(
        functools.partial(update_body, cols, subs, late),
        grid=(LAYERS,),
        out_shape=[jax.ShapeDtypeStruct(in_proj.shape, f32)] * 3
        + [jax.ShapeDtypeStruct(down_proj.shape, f32)] * 3
        + [jax.ShapeDtypeStruct((LAYERS, 8, LANES), f32)],
        in_specs=[
            pl.BlockSpec(memory_space=pltpu.SMEM),
            pl.BlockSpec(block, lambda l: (0, jnp.minimum(LAYERS - 1 - l, LAYERS - 1 - late), *tail)),
            pl.BlockSpec(block, lambda l: (0, jnp.maximum(late - 1 - l, 0), *tail)),
        ]
        + [proj_spec] * 3
        + [down_spec] * 3,
        out_specs=[proj_spec] * 3 + [down_spec] * 3 + [pl.BlockSpec((1, 8, LANES), lambda l: (l, 0, 0))],
        compiler_params=pltpu.CompilerParams(vmem_limit_bytes=56 << 20),
        cost_estimate=cost(25),
    )(factor.reshape(1), *blocks_of, in_proj, m_proj, v_proj, down_proj, m_down, v_down)
    big = {1: got[0:3], 2: got[3:6]}
    new_m, new_v, updates = ([], [], [])
    for n, (w, g, m, v) in enumerate(zip(masters, shards, firsts, seconds)):
        m2, v2, u = big[n] if n in big else moments(w, g * factor, m, v)
        new_m.append(m2)
        new_v.append(v2)
        updates.append(u)
    usq = total_over_dp(
        group_sums(tuple((u * u for u in updates)), jnp.sum(got[6][:, 0, : 4 + 3 * LAYERS], 0))
    )
    wnorm = jnp.sqrt(wsq)
    unorm = jnp.sqrt(usq)
    ratio = wnorm / unorm
    spreads = spread_ratio(ratio)
    new_w = [w - learn_rate * r * u for w, r, u in zip(masters, spreads, updates)]
    stats = jnp.stack([wnorm, unorm])
    return (loss, grad_norm, stats, ratio, *new_w, *new_m, *new_v)


def solution(mesh):
    placed = (
        P("dp", None),
        P(None, "dp", None),
        P(None, None, "dp", None),
        P(None, None, "dp"),
        P("dp", None),
        P(None, "dp"),
        P(None, "dp"),
    )
    in_specs = (
        P("dp", "seq", None, None),
        P("dp", None),
        P("dp"),
        P("dp"),
        P("dp"),
    ) + placed * 3
    out_specs = (P(), P(), P(), P()) + placed * 3
    return jax.shard_map(
        per_device, mesh=mesh, in_specs=in_specs, out_specs=out_specs, check_vma=False
    )
```

```python
import functools

import jax
import jax.numpy as jnp
from jax import lax
from jax.experimental import pallas as pl
from jax.experimental.pallas import tpu as pltpu
from jax.sharding import PartitionSpec as P

D = 320
HEADS = 5
HD = 64
FF = 1280
CLS = 1000
W = 64
HALF = W // 2
LAYERS = 6
STEP = 5
LANES = 128


norm_eps = 1e-06
scale_qk = 0.125
big_neg = -1e30
beta_one = 0.9
beta_two = 0.999
lamb_eps = 1e-06
decay_rate = 0.01
learn_rate = 0.3
clip_limit = 0.1
root_half = 0.7071067811865476
root_two_pi = 0.3989422804014327
precise = lax.Precision.HIGHEST

f32 = jnp.float32
bf16 = jnp.bfloat16


def to_bf(v):
    return v.astype(bf16)


def dot(a, b):
    return jnp.dot(a, b, preferred_element_type=f32)


def dot_nt(a, b, precision=None):
    return lax.dot_general(
        a, b, (((1,), (1,)), ((), ())), precision=precision, preferred_element_type=f32
    )


def contract(a, b, precision=None):
    return lax.dot_general(
        a, b, (((0,), (0,)), ((), ())), precision=precision, preferred_element_type=f32
    )


def norm_parts(v):
    center = v - jnp.mean(v, -1, keepdims=True)
    spread = jnp.mean(center * center, -1, keepdims=True)
    scale = lax.rsqrt(spread + norm_eps)
    return center * scale, scale


def layer_norm(v, gain, bias):
    return norm_parts(v)[0] * gain + bias


def norm_back(v, gain, grad):
    unit, scale = norm_parts(v)
    dgain = jnp.sum(grad * unit, 0, keepdims=True)
    dbias = jnp.sum(grad, 0, keepdims=True)
    t = grad * gain
    dv = scale * (
        t - jnp.mean(t, -1, keepdims=True) - unit * jnp.mean(t * unit, -1, keepdims=True)
    )
    return dv, dgain, dbias


def cost(us):
    return pl.CostEstimate(flops=int(us * 1e8), bytes_accessed=int(us * 1e5), transcendentals=0)


def run(us, body, outs, *args, place=None):
    vm = pl.BlockSpec(memory_space=pltpu.VMEM)
    scalars = [] if place is None else [place]
    return pl.pallas_call(
        body,
        out_shape=[jax.ShapeDtypeStruct(s, d) for s, d in outs],
        in_specs=[pl.BlockSpec(memory_space=pltpu.SMEM)] * len(scalars) + [vm] * len(args),
        out_specs=[vm] * len(outs),
        compiler_params=pltpu.CompilerParams(vmem_limit_bytes=48 << 20),
        cost_estimate=cost(us),
    )(*scalars, *args)


class Rows:
    def __init__(self, ref, start):
        self.ref, self.start = ref, start

    def __getitem__(self, at):
        rows, *rest = at if isinstance(at, tuple) else (at,)
        return self.ref[(slice(self.start + rows.start, self.start + rows.stop), *rest)]


def shifted(body, starts):
    def call(*refs):
        return body(*[Rows(r, starts[n]) if n in starts else r for n, r in enumerate(refs)])

    return call


def cells_of(v):
    rows = v.shape[0] // W
    split = v.reshape(rows // 2, 2, 2, HALF, v.shape[1])
    return [split[:, k // 2, k % 2].reshape(-1, v.shape[1]) for k in range(4)]


def attention_inputs(x, gain, bias, wq, wsr, wkv, a_ref, q_ref, r_ref, rn_ref, kv_ref):
    a = to_bf(layer_norm(x, gain[0:1], bias[0:1]))
    a_ref[...] = a
    q_ref[...] = to_bf(dot(a, wq[...]))
    total = None
    for k, cell in enumerate(cells_of(a)):
        part = dot(cell, wsr[k * D : (k + 1) * D, :])
        total = part if total is None else total + part
    r_ref[...] = total
    rn = to_bf(layer_norm(total, gain[1:2], bias[1:2]))
    rn_ref[...] = rn
    kv_ref[...] = to_bf(dot(rn, wkv[...]))


def embed_body(p_ref, w_ref, ln_ref, e_ref, x_ref):
    e = dot(p_ref[...], w_ref[...])
    e_ref[...] = e
    x_ref[...] = layer_norm(e, ln_ref[0:1], ln_ref[1:2])


def embed_back_body(p_ref, de_ref, dw_ref):
    dw_ref[...] = contract(p_ref[...], de_ref[...])


def first_body(x_ref, gain, bias, wq, wsr, wkv, *outs):
    attention_inputs(x_ref[...], gain, bias, wq, wsr, wkv, *outs)


def middle_body(
    place, q_ref, kv_ref, ok_ref, x_ref, gain, bias, wo, w1, o_ref, lse_ref, x2_ref, b_ref, h_ref, edge_ref
):
    q = q_ref[...] * jnp.asarray(scale_qk, bf16)
    keys = kv_ref.shape[0]
    kv = kv_ref[...]
    shut = jnp.broadcast_to(ok_ref[...], (keys, q.shape[0]))
    q_t = q.T
    v_t = kv[:, D:].T
    parts = []
    for head in range(HEADS):
        low, high = head * HD, (head + 1) * HD
        s = dot(kv[:, low:high], q_t[low:high, :]) + shut
        top = jnp.max(s, 0, keepdims=True)
        expo = jnp.exp(s - top)
        total = jnp.sum(expo, 0, keepdims=True)
        lse_ref[head : head + 1, :] = top + jnp.log(total)
        p = to_bf(expo * (1.0 / total))
        parts.append(dot(v_t[low:high, :], p))
    o = to_bf(jnp.concatenate(parts, 0).T)
    o_ref[...] = o
    x2 = x_ref[...] + dot(o, wo[...])
    x2_ref[...] = x2
    b = to_bf(layer_norm(x2, gain[2:3], bias[2:3]))
    b_ref[...] = b
    h_ref[...] = to_bf(dot(b, w1[...]))
    send_edge(place, h_ref, edge_ref)


def shift_down(v):
    index = lax.broadcasted_iota(jnp.int32, v.shape, 0)
    return jnp.where(index == 0, 0.0, pltpu.roll(v, 1, 0))


def shift_up(v):
    index = lax.broadcasted_iota(jnp.int32, v.shape, 0)
    return jnp.where(index == v.shape[0] - 1, 0.0, pltpu.roll(v, v.shape[0] - 1, 0))


def from_left(v):
    return jnp.concatenate([shift_down(v[HALF:]), v[:HALF]], 0)


def from_right(v):
    return jnp.concatenate([v[HALF:], shift_up(v[:HALF])], 0)


def row_of(main, near, i, rows, lanes):
    place, low, high = near
    if i < 0:
        return jnp.where(place[0] > 0, low[:, lanes].astype(f32), 0.0)
    if i >= rows:
        return jnp.where(place[1] > 0, high[:, lanes].astype(f32), 0.0)
    return main[i * W : (i + 1) * W, lanes].astype(f32)


def send_edge(place, main, edge_ref):
    start = pl.multiple_of(jnp.where(place[0] > 0, 0, main.shape[0] - W), W)
    edge_ref[...] = main[pl.ds(start, W), :]


def conv_gelu(h_ref, ends, taps_ref, g_ref, slope_ref):
    rows = h_ref.shape[0] // W

    def chunk(c, carry):
        lanes = pl.ds(pl.multiple_of(c * LANES, LANES), LANES)
        taps = [taps_ref[k : k + 1, lanes] for k in range(9)]
        near = [row_of(h_ref, ends, i, rows, lanes) for i in (-1, 0)]
        for i in range(rows):
            near.append(row_of(h_ref, ends, i + 1, rows, lanes))
            sums = [
                taps[j] * near[0] + taps[3 + j] * near[1] + taps[6 + j] * near[2] for j in range(3)
            ]
            z = sums[1] + from_left(sums[0]) + from_right(sums[2])
            phi = 0.5 + 0.5 * lax.erf(z * root_half)
            here = slice(i * W, (i + 1) * W)
            g_ref[here, lanes] = to_bf(z * phi)
            slope_ref[here, lanes] = phi + z * (jnp.exp(-0.5 * z * z) * root_two_pi)
            near = near[1:]
        return carry

    lax.fori_loop(0, FF // LANES, chunk, 0)


def last_body(place, h_ref, low_ref, high_ref, taps_ref, x2_ref, w2, ln_ref, ok_ref, g_ref, slope_ref, x_ref, sum_ref):
    conv_gelu(h_ref, (place, low_ref, high_ref), taps_ref, g_ref, slope_ref)
    x = x2_ref[...] + dot(g_ref[...], w2[...])
    x_ref[...] = x
    fin = layer_norm(x, ln_ref[0:1], ln_ref[1:2])
    sum_ref[...] = jnp.sum(fin * ok_ref[...], 0, keepdims=True)


def join_body(
    place, h_ref, low_ref, high_ref, taps_ref, x2_ref, w2, gain, bias, wq, wsr, wkv, g_ref, slope_ref, x_ref, *outs
):
    conv_gelu(h_ref, (place, low_ref, high_ref), taps_ref, g_ref, slope_ref)
    x = x2_ref[...] + dot(g_ref[...], w2[...])
    x_ref[...] = x
    attention_inputs(x, gain, bias, wq, wsr, wkv, *outs)


def gelu_back(place, dx, w2, slope_ref, dy_ref, dz_ref, edge_ref):
    dy = to_bf(dx)
    dy_ref[...] = dy
    dg = to_bf(dot_nt(dy, w2[...])).astype(f32)
    dz_ref[...] = to_bf(dg * slope_ref[...])
    send_edge(place, dz_ref, edge_ref)


def head_body(
    images,
    place,
    pool_ref,
    count_ref,
    head_ref,
    target_ref,
    x_ref,
    ln_ref,
    ok_ref,
    w2,
    slope_ref,
    loss_ref,
    pooled_ref,
    dlog_ref,
    dln_ref,
    dx_ref,
    dy_ref,
    dz_ref,
    edge_ref,
):
    count = count_ref[...]
    pooled = to_bf(pool_ref[...] / count)
    pooled_ref[...] = pooled
    logits = dot(jnp.broadcast_to(pooled.astype(f32), (16, D)).astype(bf16), head_ref[...])[0:1]
    shifted = logits - jnp.max(logits, -1, keepdims=True)
    logp = shifted - jnp.log(jnp.sum(jnp.exp(shifted), -1, keepdims=True))
    target = target_ref[...]
    loss_ref[...] = jnp.sum(target * logp, -1, keepdims=True) * (-1.0 / images)
    dlog = to_bf((jnp.exp(logp) - target) * (1.0 / images))
    dlog_ref[...] = dlog
    wide = jnp.broadcast_to(dlog.astype(f32), (16, CLS)).astype(bf16)
    dpool = dot_nt(wide, head_ref[...])[0:1] / count
    dx, dgain, dbias = norm_back(x_ref[...], ln_ref[0:1], ok_ref[...] * dpool)
    dln_ref[0:1, :] = dgain
    dln_ref[1:2, :] = dbias
    dx_ref[...] = dx
    gelu_back(place, dx, w2, slope_ref, dy_ref, dz_ref, edge_ref)


def conv_back(h_ref, hends, dz_ref, zends, taps_ref, dh_ref, dtaps_ref):
    rows = h_ref.shape[0] // W

    def chunk(c, carry):
        lanes = pl.ds(pl.multiple_of(c * LANES, LANES), LANES)
        taps = [taps_ref[k : k + 1, lanes] for k in range(9)]
        acc = [jnp.zeros((8, LANES), f32) for _ in range(9)]

        def views(i):
            v = row_of(dz_ref, zends, i, rows, lanes)
            return [from_right(v), v, from_left(v)]

        near = [views(-1), views(0)]
        hear = [row_of(h_ref, hends, i, rows, lanes) for i in (-1, 0)]
        for i in range(rows):
            near.append(views(i + 1))
            hear.append(row_of(h_ref, hends, i + 1, rows, lanes))
            dh = None
            for di in range(3):
                for dj in range(3):
                    part = taps[3 * di + dj] * near[2 - di][dj]
                    dh = part if dh is None else dh + part
            dh_ref[i * W : (i + 1) * W, lanes] = to_bf(dh)
            for di in range(3):
                for dj in range(3):
                    prod = (hear[di] * near[1][dj]).reshape(W // 8, 8, LANES)
                    acc[3 * di + dj] = acc[3 * di + dj] + jnp.sum(prod, 0)
            near = near[1:]
            hear = hear[1:]
        for k in range(9):
            dtaps_ref[k : k + 1, lanes] = jnp.sum(acc[k], 0, keepdims=True)
        return carry

    lax.fori_loop(0, FF // LANES, chunk, 0)


def block_back_body(
    place,
    h_ref,
    hlow_ref,
    hhigh_ref,
    dz_ref,
    zlow_ref,
    zhigh_ref,
    taps_ref,
    w1,
    x2_ref,
    gain,
    dx_ref,
    wo,
    q_ref,
    kv_ref,
    ok_ref,
    lse_ref,
    dh_ref,
    dtaps_ref,
    dln_ref,
    dx2_ref,
    dy_ref,
    dq_ref,
    dkv_ref,
):
    conv_back(
        h_ref, (place, hlow_ref, hhigh_ref), dz_ref, (place, zlow_ref, zhigh_ref), taps_ref, dh_ref, dtaps_ref
    )
    db = dot_nt(dh_ref[...], w1[...])
    dln, dgain, dbias = norm_back(x2_ref[...], gain[2:3], db)
    dln_ref[0:1, :] = dgain
    dln_ref[1:2, :] = dbias
    dx2 = dx_ref[...] + dln
    dx2_ref[...] = dx2
    dy = to_bf(dx2)
    dy_ref[...] = dy
    do_t = to_bf(dot_nt(wo[...], dy))
    q = q_ref[...] * jnp.asarray(scale_qk, bf16)
    q_t = q.T
    keys = kv_ref.shape[0]
    kv = kv_ref[...]
    k_t = (kv[:, :D] * jnp.asarray(scale_qk, bf16)).T
    shut = jnp.broadcast_to(ok_ref[...], (keys, q.shape[0]))
    dq_parts, dk_parts, dv_parts = ([], [], [])
    for head in range(HEADS):
        low, high = head * HD, (head + 1) * HD
        s = dot(kv[:, low:high], q_t[low:high, :]) + shut
        p = jnp.exp(s - lse_ref[head : head + 1, :])
        dp = dot(kv[:, D + low : D + high], do_t[low:high, :])
        dv_parts.append(dot_nt(do_t[low:high, :], to_bf(p)))
        ds = to_bf(p * (dp - jnp.sum(p * dp, 0, keepdims=True)))
        dq_parts.append(dot(k_t[low:high, :], ds))
        dk_parts.append(dot_nt(q_t[low:high, :], ds))
    dq_ref[...] = to_bf(jnp.concatenate(dq_parts, 0).T)
    dkv_ref[...] = jnp.concatenate(dk_parts + dv_parts, 0).T


def inputs_back(dkv, wkv, r_ref, gain, dq_ref, wq, wsr, x_ref, dx2_ref, dr_ref, dln_ref):
    w_kv = wkv[...].astype(f32)
    drn = dot_nt(dkv, w_kv, precise)
    dr, dgain1, dbias1 = norm_back(r_ref[...], gain[1:2], drn)
    dr = to_bf(dr)
    dr_ref[...] = dr
    rows = x_ref.shape[0] // W
    cells = [
        dot_nt(dr, wsr[k * D : (k + 1) * D, :]).reshape(rows // 2, 1, 1, HALF, D) for k in range(4)
    ]
    placed = jnp.concatenate(
        [jnp.concatenate(cells[0:2], 2), jnp.concatenate(cells[2:4], 2)], 1
    ).reshape(rows * W, D)
    da = dot_nt(dq_ref[...], wq[...]) + placed
    dln, dgain0, dbias0 = norm_back(x_ref[...], gain[0:1], da)
    for k, row in enumerate((dgain0, dgain1, dbias0, dbias1)):
        dln_ref[k : k + 1, :] = row
    return dx2_ref[...] + dln


def join_back_body(
    place, dkv_ref, wkv, r_ref, gain, dq_ref, wq, wsr, x_ref, dx2_ref, w2, slope_ref,
    dr_ref, dln_ref, dx_ref, dy_ref, dz_ref, edge_ref
):
    dx = inputs_back(dkv_ref[...], wkv, r_ref, gain, dq_ref, wq, wsr, x_ref, dx2_ref, dr_ref, dln_ref)
    dx_ref[...] = dx
    gelu_back(place, dx, w2, slope_ref, dy_ref, dz_ref, edge_ref)


def first_back_body(
    dkv_ref, wkv, r_ref, gain, dq_ref, wq, wsr, x_ref, dx2_ref, e_ref, ln_ref, dr_ref, dln_ref, de_ref, dle_ref
):
    dx = inputs_back(dkv_ref[...], wkv, r_ref, gain, dq_ref, wq, wsr, x_ref, dx2_ref, dr_ref, dln_ref)
    de, dgain, dbias = norm_back(e_ref[...], ln_ref[0:1], dx)
    de_ref[...] = to_bf(de)
    dle_ref[0:1, :] = dgain
    dle_ref[1:2, :] = dbias


def weight_grads_body(
    n_dp, cols, subs, core_ref, a_ref, dq_ref, rn_ref, dkv_ref, o_ref, dy2_ref, b_ref, dh_ref, dr_ref, g_ref, dy_ref, *refs
):
    outs, (proj, down) = refs[:-2], refs[-2:]
    a = a_ref[...]
    proj[:, :D] = contract(a, dq_ref[...])
    proj[:, D : 3 * D] = contract(rn_ref[...].astype(f32), dkv_ref[...], precise)
    proj[:, 3 * D : 4 * D] = contract(o_ref[...], dy2_ref[...])
    proj[:, 4 * D :] = contract(b_ref[...], dh_ref[...])
    dr = dr_ref[...]
    for k, cell in enumerate(cells_of(a)):
        down[k * D : (k + 1) * D, :D] = contract(cell, dr)
    down[:, D:] = contract(g_ref[...], dy_ref[...])
    rows = D // n_dp
    sub = rows // subs
    wide = (4 * D + FF) // cols
    down_rows = FF // n_dp
    for c in range(cols):
        for d in range(n_dp):
            for n, out in enumerate(outs):
                for j in range(subs) if len(outs) == 1 else (None,):
                    if j is None:
                        k = core_ref[0] if n == 0 else 1 - core_ref[0]
                        at = (c ^ core_ref[1], d)
                    else:
                        k = j
                        at = (c, j, d)
                    start = d * rows + k * sub
                    low = d * down_rows + (c * subs + k) * (down_rows // (cols * subs))
                    if j is None:
                        start = pl.multiple_of(start, 8)
                        low = pl.multiple_of(low, 8)
                    out[(*at, slice(0, sub))] = proj[pl.ds(start, sub), c * wide : (c + 1) * wide]
                    out[(*at, slice(sub, 2 * sub))] = down[pl.ds(low, sub), :]


def moments(w, g, m, v):
    m2 = beta_one * m + (1.0 - beta_one) * g
    v2 = beta_two * v + (1.0 - beta_two) * g * g
    u = (
        m2 / (1.0 - beta_one**STEP) / (jnp.sqrt(v2 / (1.0 - beta_two**STEP)) + lamb_eps)
        + decay_rate * w
    )
    return m2, v2, u


def update_body(
    cols, subs, late, factor_ref, early_ref, late_ref, wp, mp, vp, wd, md, vd, mp2, vp2, up, md2, vd2, ud, sums
):
    factor = factor_ref[0]
    layer = pl.program_id(0)
    sub = wp.shape[1] // subs
    wide = wp.shape[2] // cols

    def go(g_ref):
        squares = [0.0, 0.0]

        def put(n, at, refs, outs, g):
            new = moments(refs[0][at], g * factor, refs[1][at], refs[2][at])
            for out, value in zip(outs, new):
                out[at] = value
            squares[n] = squares[n] + jnp.sum(new[2] * new[2], 0, keepdims=True)

        for c in range(cols):
            for k in range(subs):
                g = g_ref[c * subs + k].astype(f32).reshape(2 * sub, wide)
                at = (0, slice(k * sub, (k + 1) * sub), slice(c * wide, (c + 1) * wide))
                put(0, at, (wp, mp, vp), (mp2, vp2, up), g[:sub])
                rows = slice((c * subs + k) * sub, (c * subs + k + 1) * sub)
                for half in range(2):
                    at = (0, half, rows, slice(0, D))
                    put(1, at, (wd, md, vd), (md2, vd2, ud), g[sub:, half * D : (half + 1) * D])
        lane = lax.broadcasted_iota(jnp.int32, (1, LANES), 1)
        total = jnp.zeros((1, LANES), f32)
        for n in range(2):
            value = jnp.broadcast_to(jnp.sum(squares[n], 1, keepdims=True), (1, LANES))
            total = jnp.where(lane == 4 + n * LAYERS + layer, value, total)
        sums[0] = jnp.broadcast_to(total, sums.shape[1:])

    pl.when(layer >= late)(lambda: go(early_ref))
    pl.when(layer < late)(lambda: go(late_ref))


def group_sums(arrs, layered=None):
    embed, proj, downs, taps, head, gains, biases = arrs
    slot = lax.broadcasted_iota(jnp.int32, (1, 4 + 3 * LAYERS), 1)

    def placed(values, start):
        at = lax.broadcasted_iota(jnp.int32, (values.shape[0], 1), 0) + start
        return jnp.sum(jnp.where(at == slot, values[:, None], 0.0), 0)

    total = placed(jnp.sum(taps, (1, 2)), 4 + 2 * LAYERS)
    for n, a in enumerate((embed, head, gains, biases)):
        total = total + jnp.where(slot[0] == n, jnp.sum(a), 0.0)
    if layered is not None:
        return total + layered
    for n, a in enumerate((proj, downs)):
        total = total + placed(jnp.sum(a.reshape(a.shape[0], -1), 1), 4 + n * LAYERS)
    return total


def spread_ratio(ratio):
    return (
        ratio[0],
        ratio[4 : 4 + LAYERS].reshape(LAYERS, 1, 1),
        ratio[4 + LAYERS : 4 + 2 * LAYERS].reshape(LAYERS, 1, 1, 1),
        ratio[4 + 2 * LAYERS : 4 + 3 * LAYERS].reshape(LAYERS, 1, 1),
        ratio[1],
        ratio[2],
        ratio[3],
    )


def per_device(
    patches,
    valid,
    labels,
    partners,
    mix,
    embed_w,
    in_proj,
    down_proj,
    dw_kernel,
    head_w,
    norm_gain,
    norm_bias,
    m_embed,
    m_proj,
    m_down,
    m_taps,
    m_head,
    m_gain,
    m_bias,
    v_embed,
    v_proj,
    v_down,
    v_taps,
    v_head,
    v_gain,
    v_bias,
):
    masters = (embed_w, in_proj, down_proj, dw_kernel, head_w, norm_gain, norm_bias)
    firsts = (m_embed, m_proj, m_down, m_taps, m_head, m_gain, m_bias)
    seconds = (v_embed, v_proj, v_down, v_taps, v_head, v_gain, v_bias)
    n_seq = lax.axis_size("seq")
    n_dp = lax.axis_size("dp")
    seq_pos = lax.axis_index("seq")
    img_dev, rows = (patches.shape[0], patches.shape[1])
    images = img_dev * n_dp

    team = n_seq
    while team * img_dev > n_seq:
        team //= 2
    blocks = n_seq // team
    rows_own = rows * blocks
    tok = rows_own * W
    keys_own = tok // 4
    image = jnp.minimum(seq_pos // team, img_dev - 1)
    busy = seq_pos // team < img_dev
    place = seq_pos % team

    def between(shift, wrap):
        pairs = []
        for base in range(0, n_seq, team):
            for h in range(team):
                if wrap or 0 <= h + shift < team:
                    pairs.append((base + (h + shift) % team, base + h))
        return pairs

    ends = jnp.stack([place > 0, place < team - 1]).astype(jnp.int32)

    def edges(v, edge):
        if team == 2:
            other = lax.ppermute(edge, "seq", between(1, True))
            return other, other
        low = lax.ppermute(v[-W:], "seq", between(-1, False))
        high = lax.ppermute(v[:W], "seq", between(1, False))
        return low, high

    def all_keys(v):
        return jnp.concatenate(
            [v] + [lax.ppermute(v, "seq", between(j, True)) for j in range(1, team)], 0
        )

    def own_keys(v):
        total = v[:keys_own]
        for j in range(1, team):
            part = v[j * keys_own : (j + 1) * keys_own]
            total = total + lax.ppermute(part, "seq", between(-j, True))
        return total

    back_block = seq_pos % blocks
    routes = [
        [
            (blocks * h + (i + r) % blocks, team * i + h)
            for i in range(img_dev)
            for h in range(team)
        ]
        for r in range(blocks)
    ]

    def to_team(v):
        got = []
        for r, pairs in enumerate(routes):
            send = lax.dynamic_index_in_dim(
                v, jnp.minimum((back_block - r) % blocks, img_dev - 1), 0, keepdims=False
            )
            got.append(lax.ppermute(send, "seq", pairs))
        twice = jnp.stack(got + got)
        own = lax.dynamic_slice_in_dim(twice, (blocks - image) % blocks, blocks, 0)
        return own.reshape(tok, -1)

    cols = 4
    subs = n_seq // cols
    row_in = D // n_dp
    sub_in = row_in // subs
    wide = in_proj.shape[2] // cols
    down_rows = down_proj.shape[2] // n_seq
    core = seq_pos % subs

    def part_of(flat):
        size = -(-flat.shape[0] // (wide * n_seq)) * wide * n_seq
        flat = jnp.pad(flat, (0, size - flat.shape[0])).reshape(n_seq, -1, wide)
        return lax.dynamic_index_in_dim(flat, seq_pos, 0, keepdims=False)

    def layer_part(l):
        block = lax.dynamic_slice(
            in_proj[l], (core * sub_in, (seq_pos // subs) * wide), (sub_in, wide)
        )
        lower = lax.dynamic_slice_in_dim(down_proj[l], seq_pos * down_rows, down_rows, 1)
        return [to_bf(block), to_bf(jnp.concatenate([lower[0], lower[1]], 1))]

    def gathered(part):
        return lax.all_gather(part, ("dp", "seq"), axis=0, tiled=False)

    def cut(got, sizes):
        got = got.reshape(n_dp, n_seq, sum(sizes), wide)
        starts = [sum(sizes[:i]) for i in range(len(sizes))]
        return [got[:, :, a : a + n] for a, n in zip(starts, sizes)]

    def proj_of(got):
        got = got.reshape(n_dp, cols, subs, sub_in, wide).transpose(0, 2, 3, 1, 4)
        return got.reshape(D, cols * wide)

    dp_pos = lax.axis_index("dp")

    def over_dp(v):
        got = [v] + [
            lax.ppermute(v, "dp", [((d + j) % n_dp, d) for d in range(n_dp)])
            for j in range(1, n_dp)
        ]
        return lax.dynamic_slice_in_dim(jnp.stack(got + got), (n_dp - dp_pos) % n_dp, n_dp, 0)

    groups = [[0, 1, 2], [3, 4, 5]]
    extra = [[], [part_of(to_bf(head_w).reshape(-1))]]

    def layers_of(got, count):
        return [(proj_of(got[2 * i]), got[2 * i + 1].reshape(FF, 2 * D)) for i in range(count)]

    parts_of = [more + [p for l in members for p in layer_part(l)] for members, more in zip(groups, extra)]
    sizes_of = [[p.shape[0] for p in parts] for parts in parts_of]
    lines = [jnp.concatenate(parts, 0) for parts in parts_of]
    norms = jnp.stack([norm_gain, norm_bias])
    small = jnp.concatenate([to_bf(v).reshape(-1, D) for v in (embed_w, dw_kernel, norms)], 0)
    small = over_dp(small)
    marks = (embed_w.shape[0], embed_w.shape[0] + dw_kernel.size // D)
    embed16 = small[:, : marks[0]].reshape(-1, D)
    taps32 = small[:, marks[0] : marks[1]].reshape(n_dp, LAYERS * 9, -1).transpose(1, 0, 2)
    taps32 = taps32.reshape(LAYERS * 9, FF).astype(f32)
    norms32 = small[:, marks[1] :].reshape(n_dp, 2, -1, row_in).transpose(1, 2, 0, 3)
    norms32 = norms32.reshape(2, -1, D).astype(f32)
    gain32, bias32 = norms32[0], norms32[1]

    def total_over_dp(v):
        got = [v] + [
            lax.ppermute(v, "dp", [((d + j) % n_dp, d) for d in range(n_dp)])
            for j in range(1, n_dp)
        ]
        index = lax.broadcasted_iota(jnp.int32, (n_dp, 1), 0)
        rows_of = [jnp.where(index == (dp_pos + j) % n_dp, g, 0.0) for j, g in enumerate(got)]
        return jnp.sum(sum(rows_of), 0)
    raw = [gathered(lines[0])]
    first_of = {members[0]: n for n, members in enumerate(groups)}

    def own(v):
        return lax.dynamic_index_in_dim(v, image, 0, keepdims=False)

    wanted = own(partners)
    partner_label = jnp.zeros((), jnp.int32)
    for j in range(n_dp):
        other = labels
        if j:
            other = lax.ppermute(labels, "dp", [((d + j) % n_dp, d) for d in range(n_dp)])
        index = ((dp_pos + j) % n_dp) * img_dev + jnp.arange(img_dev)
        partner_label = partner_label + jnp.sum(jnp.where(index == wanted, other, 0))
    valid_own = own(valid)
    tid = lax.broadcasted_iota(jnp.int32, (tok, 1), 0)
    within = tid % W
    row_id = place * rows_own + tid // W
    col_id = 2 * (within % HALF) + within // HALF
    okay = ((row_id < valid_own[0]) & (col_id < valid_own[1]) & busy).astype(f32)
    kid = lax.broadcasted_iota(jnp.int32, (team * keys_own, 1), 0)
    segment = (place + kid // keys_own) % team
    key_row = segment * (rows_own // 2) + (kid % keys_own) // HALF
    key_ok = (2 * key_row < valid_own[0]) & (2 * (kid % HALF) < valid_own[1])
    shut = jnp.where(key_ok, 0.0, big_neg).astype(f32)
    count = (valid_own[0] * valid_own[1]).astype(f32).reshape(1, 1)
    classes = lax.broadcasted_iota(jnp.int32, (1, CLS), 1)
    mix_own = own(mix)
    target = mix_own * (classes == own(labels)).astype(f32) + (1.0 - mix_own) * (
        classes == partner_label
    ).astype(f32)

    def weights(l, layer):
        return dict(
            wq=layer[0][:, :D],
            wkv=layer[0][:, D : 3 * D],
            wo=layer[0][:, 3 * D : 4 * D],
            w1=layer[0][:, 4 * D :],
            wsr=layer[1][:, :D],
            w2=layer[1][:, D:],
            taps=taps32,
            gain=gain32,
            bias=bias32,
        )

    full = ((tok, D), f32)
    ln_first = jnp.stack([gain32[0], bias32[0]])
    spread = patches.reshape(img_dev, rows, HALF, 2, -1).transpose(0, 1, 3, 2, 4)
    patch_own = to_team(spread.reshape(img_dev, rows * W, -1))
    e, x = run(2, embed_body, [full, full], patch_own, embed16, ln_first)
    lines[1], x = lax.optimization_barrier((lines[1], x))
    raw.append(gathered(lines[1]))
    wts = [weights(l, layer) for l, layer in zip(groups[0], layers_of(cut(raw[0], sizes_of[0]), len(groups[0])))]
    ln_last = jnp.stack([gain32[-1], bias32[-1]])

    half = ((tok, D), bf16)
    wide16 = ((tok, FF), bf16)
    input_outs = [half, half, ((keys_own, D), f32), ((keys_own, D), bf16), ((keys_own, 2 * D), bf16)]
    ln_out = ((2, D), f32)
    row16 = ((W, FF), bf16)

    w = wts[0]
    a16, q16, r, rn16, kv16 = run(
        2, shifted(first_body, {1: 1, 2: 1}), input_outs, x, w["gain"], w["bias"], w["wq"], w["wsr"], w["wkv"]
    )
    kept = []
    for l in range(LAYERS):
        w = wts[l]
        kv_all = all_keys(kv16)
        o16, lse, x2, b16, h16, edge = run(
            4,
            shifted(middle_body, {5: 1 + 3 * l, 6: 1 + 3 * l}),
            [half, ((HEADS, tok), f32), full, half, wide16, row16],
            q16,
            kv_all,
            shut,
            x,
            w["gain"],
            w["bias"],
            w["wo"],
            w["w1"],
            place=ends,
        )
        hlow, hhigh = edges(h16, edge)
        keep = dict(
            x=x, a16=a16, q16=q16, r=r, rn16=rn16, kv=kv_all, o16=o16, lse=lse, x2=x2, b16=b16,
            h16=h16, hlow=hlow, hhigh=hhigh,
        )
        shared = (h16, hlow, hhigh, w["taps"], x2, w["w2"])
        if l + 1 in first_of:
            n = first_of[l + 1]
            got, _ = lax.optimization_barrier((raw[n], kv_all))
            got = cut(got, sizes_of[n])
            if extra[n]:
                head16 = got.pop(0).reshape(n_dp, -1)[:, : head_w.size].reshape(D, CLS)
            wts += [weights(m, layer) for m, layer in zip(groups[n], layers_of(got, len(groups[n])))]
        if l + 1 < LAYERS:
            n = wts[l + 1]
            keep["g16"], keep["slope"], x, a16, q16, r, rn16, kv16 = run(
                8,
                shifted(join_body, {4: 9 * l, 7: 4 + 3 * l, 8: 4 + 3 * l}),
                [wide16, ((tok, FF), f32), full] + input_outs,
                *shared,
                n["gain"],
                n["bias"],
                n["wq"],
                n["wsr"],
                n["wkv"],
                place=ends,
            )
        else:
            keep["g16"], keep["slope"], x, pool = run(
                7,
                shifted(last_body, {4: 9 * l}),
                [wide16, ((tok, FF), f32), full, ((1, D), f32)],
                *shared,
                ln_last,
                okay,
                place=ends,
            )
        kept.append(keep)

    whole = pool
    for j in range(1, team):
        whole = whole + lax.ppermute(pool, "seq", between(j, True))
    loss_own, pooled16, dlog16, dln_last, dx, dy16, dz16, edge = run(
        4,
        functools.partial(head_body, images),
        [((1, 1), f32), ((1, D), bf16), ((1, CLS), bf16), ln_out, full, half, wide16, row16],
        whole,
        count,
        head16,
        target,
        x,
        ln_last,
        okay,
        wts[-1]["w2"],
        kept[-1]["slope"],
        place=ends,
    )
    chosen = ((place == 0) & busy).astype(f32)
    d_head = pooled16.astype(f32).reshape(D, 1) * dlog16.astype(f32) * chosen
    loss_local = loss_own[0, 0] * busy.astype(f32)
    teams = n_seq // team
    loss_parts = jnp.zeros((teams,), f32)
    for j in range(teams):
        other = loss_local
        if j:
            other = lax.ppermute(
                loss_local, "seq", [((d + j * team) % n_seq, d) for d in range(n_seq)]
            )
        loss_parts = jnp.where(jnp.arange(teams) == (seq_pos // team + j) % teams, other, loss_parts)
    loss_seq = jnp.sum(loss_parts)

    piece = ((cols, n_dp, 2 * sub_in, wide), f32)
    paired = subs == 2 and cols == 4
    chip = seq_pos // subs
    where = jnp.stack([core, chip]).astype(jnp.int32)

    def weight_grads(*args):
        vm = pl.BlockSpec(memory_space=pltpu.VMEM)
        outs = [piece] * 2 if paired else [((cols, subs) + piece[0][1:], f32)]
        return pl.pallas_call(
            functools.partial(weight_grads_body, n_dp, cols, subs),
            out_shape=[jax.ShapeDtypeStruct(s, d) for s, d in outs],
            in_specs=[pl.BlockSpec(memory_space=pltpu.SMEM)] + [vm] * len(args),
            out_specs=[vm] * len(outs),
            scratch_shapes=[pltpu.VMEM((D, cols * wide), f32), pltpu.VMEM((FF, 2 * D), f32)],
            compiler_params=pltpu.CompilerParams(vmem_limit_bytes=48 << 20),
            cost_estimate=cost(6),
        )(where, *args)

    def padded_rest(parts):
        flat = jnp.concatenate(parts, 1)
        size = -(-flat.shape[1] // (16 * wide * n_seq)) * 16 * wide * n_seq
        flat = jnp.pad(flat, ((0, 0), (0, size - flat.shape[1])))
        flat = flat.reshape(n_dp, cols, subs, -1, wide).transpose(1, 2, 0, 3, 4)
        if not paired:
            return [flat]
        flat = jnp.stack([lax.dynamic_index_in_dim(flat, chip ^ j, 0, False) for j in range(cols)])
        return [lax.dynamic_index_in_dim(flat, k, 1, False) for k in (core, 1 - core)]

    def pair_sum(parts):
        mine, send = parts
        return mine + lax.ppermute(send, "seq", [(d ^ 1, d) for d in range(n_seq)])

    def over_chips(v, bit):
        return lax.ppermute(v, "seq", [(d ^ (bit * subs), d) for d in range(n_seq)])

    def plane_first(y):
        cut = y.shape[2] // 2
        one, two = y[:, :, :cut], y[:, :, cut:]
        moved = (to_bf(jnp.stack([one[1], one[3]])), to_bf(jnp.stack([two[2], two[3]])))
        got = (over_chips(moved[0], 1).astype(f32), over_chips(moved[1], 2).astype(f32))
        return [one[0] + got[0][0], one[2] + got[0][1], two[0] + got[1][0], two[1] + got[1][1]]

    def plane_second(parts):
        one = parts[0] + over_chips(parts[1].astype(wire[0]), 2).astype(f32)
        two = parts[2] + over_chips(parts[3].astype(wire[0]), 1).astype(f32)
        return jnp.concatenate([one, two], 1)

    def dp_sum(y):
        def of(j):
            return lax.dynamic_index_in_dim(y, (dp_pos + j) % n_dp, 0, keepdims=False)

        total = of(0)
        for j in range(1, n_dp):
            pairs = [(d, (d + j) % n_dp) for d in range(n_dp)]
            total = total + lax.ppermute(of(j).astype(wire[0]), "dp", pairs).astype(f32)
        return total

    def whole_sum(parts):
        y = jnp.concatenate([p[0] for p in parts], -2)
        y = lax.psum_scatter(y.reshape(-1, wide), "seq", scatter_dimension=0, tiled=True)
        return lax.psum_scatter(y, "dp", scatter_dimension=0, tiled=True)

    def tied(value, others):
        return lax.optimization_barrier((value, others))

    wire = [f32]
    stages = [pair_sum, plane_first, plane_second]
    pieces = []

    def advance(now):
        if not paired:
            return now
        ready = [p for p in pieces if p[0] <= len(stages) + 1]
        now, values = tied(now, [p[1] for p in ready])
        if wire[0] == bf16:
            values = [v if p[0] else p[1] for p, v in zip(ready, values)]
        for p, v in zip(ready, values):
            if p[0] < len(stages):
                p[1] = stages[p[0]](v)
            elif p[0] > len(stages) or p is pieces[0]:
                p[1] = v
            elif p is pieces[1]:
                p[1] = dp_sum(jnp.concatenate([v, pieces[0][1]], 1))
            else:
                p[1] = dp_sum(v)
            p[0] += 1
        return now

    grads = [None] * LAYERS
    pieces.append([0, padded_rest([d_head.reshape(n_dp, -1)])])
    waiting = None
    for l in reversed(range(LAYERS)):
        w, k = wts[l], kept[l]
        zlow, zhigh = edges(dz16, edge)
        upper = dy16
        dz16 = advance(dz16)
        dh16, d_taps, dln2, dx2, dy2, dq16, dkv = run(
            11,
            shifted(block_back_body, {7: 9 * l, 10: 1 + 3 * l}),
            [wide16, ((9, FF), f32), ln_out, full, half, half, ((team * keys_own, 2 * D), f32)],
            k["h16"], k["hlow"], k["hhigh"], dz16, zlow, zhigh, w["taps"], w["w1"], k["x2"], w["gain"], dx,
            w["wo"], k["q16"], k["kv"], shut, k["lse"],
            place=ends,
        )
        if waiting is not None:
            first, _ = tied(waiting[0], dkv)
            pieces.append([0, weight_grads(first, *waiting[1:])])
        dkv_own = own_keys(dkv)
        dq16 = advance(dq16)
        shared = (dkv_own, w["wkv"], k["r"], w["gain"], dq16, w["wq"], w["wsr"], k["x"], dx2)
        if l:
            dr16, dln, dx, dy16, dz16, edge = run(
                6,
                shifted(join_back_body, {4: 1 + 3 * l}),
                [((keys_own, D), bf16), ((4, D), f32), full, half, wide16, row16],
                *shared,
                wts[l - 1]["w2"],
                kept[l - 1]["slope"],
                place=ends,
            )
        else:
            dr16, dln, de16, dln_first = run(
                3,
                shifted(first_back_body, {3: 1}),
                [((keys_own, D), bf16), ((4, D), f32), half, ln_out],
                *shared,
                e,
                ln_first,
            )
        waiting = (k["a16"], dq16, k["rn16"], dkv_own, k["o16"], dy2, k["b16"], dh16, dr16, k["g16"], upper)
        grads[l] = (
            d_taps,
            jnp.concatenate([dln[0:2], dln2[0:1]], 0),
            jnp.concatenate([dln[2:4], dln2[1:2]], 0),
        )
    wire[0] = bf16
    pieces.append([0, weight_grads(*waiting)])
    de16 = advance(de16)
    (d_embed,) = run(3, embed_back_body, [((embed16.shape[0], D), f32)], patch_own, de16)
    d_embed = advance(d_embed)
    d_gain = jnp.concatenate([dln_first[0:1]] + [g[1] for g in grads] + [dln_last[0:1]], 0)
    d_bias = jnp.concatenate([dln_first[1:2]] + [g[2] for g in grads] + [dln_last[1:2]], 0)
    d_taps = jnp.stack([g[0] for g in grads])
    rest = [
        d_embed.reshape(n_dp, -1),
        d_taps.reshape(LAYERS * 9, n_dp, -1).transpose(1, 0, 2).reshape(n_dp, -1),
        d_gain.reshape(-1, n_dp, row_in).transpose(1, 0, 2).reshape(n_dp, -1),
        d_bias.reshape(-1, n_dp, row_in).transpose(1, 0, 2).reshape(n_dp, -1),
    ]
    cuts = [0]
    for part in rest:
        cuts.append(cuts[-1] + part.shape[1])
    rest = padded_rest(rest)

    late = 3

    def together(parts):
        return to_bf(jnp.concatenate(parts, 0))

    if paired:
        assert all(p[0] > len(stages) + 1 for p in pieces[: LAYERS + 1 - late])
        own_rows = 2 * sub_in
        parts = [p[1] for p in pieces[1 : LAYERS + 1 - late]]
        early = together([parts[0][:own_rows], *parts[1:], parts[0][own_rows:]])
        rest, early = tied(rest, early)
        rest = advance(rest)
        last = plane_second(plane_first(pair_sum(rest)))
        last = dp_sum(jnp.concatenate([pieces[-1][1], last], 1))
        sums = [None] * (LAYERS + 1 - late) + [p[1] for p in pieces[LAYERS + 1 - late : -1]] + [last]
    else:
        sums = [whole_sum([p[1]]) for p in pieces + [[0, rest]]]
        early = together(sums[1 : LAYERS + 1 - late] + sums[:1])
    early_got = lax.all_gather(early, "seq", axis=0, tiled=False)
    late_part, early_got = tied(together(sums[LAYERS + 1 - late :]), early_got)
    late_got = lax.all_gather(late_part, "seq", axis=0, tiled=False)
    head_start = (LAYERS - late) * 2 * sub_in
    g_head = early_got[:, head_start:].reshape(-1)[: head_w.size].reshape(head_w.shape).astype(f32)
    flat = late_got[:, late * 2 * sub_in :].reshape(-1).astype(f32)
    flat = [flat[a:b] for a, b in zip(cuts, cuts[1:])]
    shards = (
        flat[0].reshape(embed_w.shape),
        None,
        None,
        flat[1].reshape(dw_kernel.shape),
        g_head,
        flat[2].reshape(norm_gain.shape),
        flat[3].reshape(norm_bias.shape),
    )

    gsq_local = sum(jnp.sum(jnp.square(g.astype(f32))) for g in (early_got, late_got))
    wsq_local = group_sums(tuple((w * w for w in masters)))
    ends_of = jnp.where(jnp.arange(LANES) == LANES - 1, loss_seq, 0.0)
    first_sums = total_over_dp(
        jnp.where(jnp.arange(LANES) == LANES - 2, gsq_local, ends_of)
        + jnp.pad(wsq_local, (0, LANES - wsq_local.shape[0]))
    )
    gsq, wsq, loss = first_sums[LANES - 2], first_sums[: 4 + 3 * LAYERS], first_sums[LANES - 1]
    grad_norm = jnp.sqrt(gsq)
    factor = jnp.minimum(1.0, clip_limit / grad_norm)

    proj_spec = pl.BlockSpec((1,) + in_proj.shape[1:], lambda l: (l, 0, 0))
    down_spec = pl.BlockSpec((1,) + down_proj.shape[1:], lambda l: (l, 0, 0, 0))
    block = (n_seq, 2 * sub_in, wide)
    blocks_of = [early_got, late_got]
    if 2 * sub_in % 8:
        block = (n_seq, 1, 2 * sub_in, wide)
        counts = (LAYERS - late, late)
        blocks_of = [
            g[:, : n * 2 * sub_in].reshape(n_seq, n, 2 * sub_in, wide)
            for g, n in zip(blocks_of, counts)
        ]
    tail = (0,) * (len(block) - 2)
    got = pl.pallas_call(
        functools.partial(update_body, cols, subs, late),
        grid=(LAYERS,),
        out_shape=[jax.ShapeDtypeStruct(in_proj.shape, f32)] * 3
        + [jax.ShapeDtypeStruct(down_proj.shape, f32)] * 3
        + [jax.ShapeDtypeStruct((LAYERS, 8, LANES), f32)],
        in_specs=[
            pl.BlockSpec(memory_space=pltpu.SMEM),
            pl.BlockSpec(block, lambda l: (0, jnp.minimum(LAYERS - 1 - l, LAYERS - 1 - late), *tail)),
            pl.BlockSpec(block, lambda l: (0, jnp.maximum(late - 1 - l, 0), *tail)),
        ]
        + [proj_spec] * 3
        + [down_spec] * 3,
        out_specs=[proj_spec] * 3 + [down_spec] * 3 + [pl.BlockSpec((1, 8, LANES), lambda l: (l, 0, 0))],
        compiler_params=pltpu.CompilerParams(vmem_limit_bytes=56 << 20),
        cost_estimate=cost(25),
    )(factor.reshape(1), *blocks_of, in_proj, m_proj, v_proj, down_proj, m_down, v_down)
    big = {1: got[0:3], 2: got[3:6]}
    new_m, new_v, updates = ([], [], [])
    for n, (w, g, m, v) in enumerate(zip(masters, shards, firsts, seconds)):
        m2, v2, u = big[n] if n in big else moments(w, g * factor, m, v)
        new_m.append(m2)
        new_v.append(v2)
        updates.append(u)
    usq = total_over_dp(
        group_sums(tuple((u * u for u in updates)), jnp.sum(got[6][:, 0, : 4 + 3 * LAYERS], 0))
    )
    wnorm = jnp.sqrt(wsq)
    unorm = jnp.sqrt(usq)
    ratio = wnorm / unorm
    spreads = spread_ratio(ratio)
    new_w = [w - learn_rate * r * u for w, r, u in zip(masters, spreads, updates)]
    stats = jnp.stack([wnorm, unorm])
    return (loss, grad_norm, stats, ratio, *new_w, *new_m, *new_v)


def solution(mesh):
    placed = (
        P("dp", None),
        P(None, "dp", None),
        P(None, None, "dp", None),
        P(None, None, "dp"),
        P("dp", None),
        P(None, "dp"),
        P(None, "dp"),
    )
    in_specs = (
        P("dp", "seq", None, None),
        P("dp", None),
        P("dp"),
        P("dp"),
        P("dp"),
    ) + placed * 3
    out_specs = (P(), P(), P(), P()) + placed * 3
    return jax.shard_map(
        per_device, mesh=mesh, in_specs=in_specs, out_specs=out_specs, check_vma=False
    )
```

```python
import functools

import jax
import jax.numpy as jnp
from jax import lax
from jax.experimental import pallas as pl
from jax.experimental.pallas import tpu as pltpu
from jax.sharding import PartitionSpec as P

D = 320
HEADS = 5
HD = 64
FF = 1280
CLS = 1000
W = 64
HALF = W // 2
LAYERS = 6
STEP = 5
LANES = 128


norm_eps = 1e-06
scale_qk = 0.125
big_neg = -1e30
beta_one = 0.9
beta_two = 0.999
lamb_eps = 1e-06
decay_rate = 0.01
learn_rate = 0.3
clip_limit = 0.1
root_half = 0.7071067811865476
root_two_pi = 0.3989422804014327
precise = lax.Precision.HIGHEST

f32 = jnp.float32
bf16 = jnp.bfloat16


def to_bf(v):
    return v.astype(bf16)


def dot(a, b):
    return jnp.dot(a, b, preferred_element_type=f32)


def dot_nt(a, b, precision=None):
    return lax.dot_general(
        a, b, (((1,), (1,)), ((), ())), precision=precision, preferred_element_type=f32
    )


def contract(a, b, precision=None):
    return lax.dot_general(
        a, b, (((0,), (0,)), ((), ())), precision=precision, preferred_element_type=f32
    )


def norm_parts(v):
    center = v - jnp.mean(v, -1, keepdims=True)
    spread = jnp.mean(center * center, -1, keepdims=True)
    scale = lax.rsqrt(spread + norm_eps)
    return center * scale, scale


def layer_norm(v, gain, bias):
    return norm_parts(v)[0] * gain + bias


def norm_back(v, gain, grad):
    unit, scale = norm_parts(v)
    dgain = jnp.sum(grad * unit, 0, keepdims=True)
    dbias = jnp.sum(grad, 0, keepdims=True)
    t = grad * gain
    dv = scale * (
        t - jnp.mean(t, -1, keepdims=True) - unit * jnp.mean(t * unit, -1, keepdims=True)
    )
    return dv, dgain, dbias


def cost(us):
    return pl.CostEstimate(flops=int(us * 1e8), bytes_accessed=int(us * 1e5), transcendentals=0)


def run(us, body, outs, *args, place=None):
    vm = pl.BlockSpec(memory_space=pltpu.VMEM)
    scalars = [] if place is None else [place]
    return pl.pallas_call(
        body,
        out_shape=[jax.ShapeDtypeStruct(s, d) for s, d in outs],
        in_specs=[pl.BlockSpec(memory_space=pltpu.SMEM)] * len(scalars) + [vm] * len(args),
        out_specs=[vm] * len(outs),
        compiler_params=pltpu.CompilerParams(vmem_limit_bytes=48 << 20),
        cost_estimate=cost(us),
    )(*scalars, *args)


class Rows:
    def __init__(self, ref, start):
        self.ref, self.start = ref, start

    def __getitem__(self, at):
        rows, *rest = at if isinstance(at, tuple) else (at,)
        return self.ref[(slice(self.start + rows.start, self.start + rows.stop), *rest)]


def shifted(body, starts):
    def call(*refs):
        return body(*[Rows(r, starts[n]) if n in starts else r for n, r in enumerate(refs)])

    return call


def cells_of(v):
    rows = v.shape[0] // W
    split = v.reshape(rows // 2, 2, 2, HALF, v.shape[1])
    return [split[:, k // 2, k % 2].reshape(-1, v.shape[1]) for k in range(4)]


def attention_inputs(x, gain, bias, wq, wsr, wkv, a_ref, q_ref, r_ref, rn_ref, kv_ref):
    a = to_bf(layer_norm(x, gain[0:1], bias[0:1]))
    a_ref[...] = a
    q_ref[...] = to_bf(dot(a, wq[...]))
    total = None
    for k, cell in enumerate(cells_of(a)):
        part = dot(cell, wsr[k * D : (k + 1) * D, :])
        total = part if total is None else total + part
    r_ref[...] = total
    rn = to_bf(layer_norm(total, gain[1:2], bias[1:2]))
    rn_ref[...] = rn
    kv_ref[...] = to_bf(dot(rn, wkv[...]))


def embed_body(p_ref, w_ref, ln_ref, e_ref, x_ref):
    e = dot(p_ref[...], w_ref[...])
    e_ref[...] = e
    x_ref[...] = layer_norm(e, ln_ref[0:1], ln_ref[1:2])


def embed_back_body(p_ref, de_ref, dw_ref):
    dw_ref[...] = contract(p_ref[...], de_ref[...])


def first_body(x_ref, gain, bias, wq, wsr, wkv, *outs):
    attention_inputs(x_ref[...], gain, bias, wq, wsr, wkv, *outs)


def middle_body(
    place, q_ref, kv_ref, ok_ref, x_ref, gain, bias, wo, w1, o_ref, lse_ref, x2_ref, b_ref, h_ref, edge_ref
):
    q = q_ref[...] * jnp.asarray(scale_qk, bf16)
    keys = kv_ref.shape[0]
    kv = kv_ref[...]
    shut = jnp.broadcast_to(ok_ref[...], (keys, q.shape[0]))
    q_t = q.T
    v_t = kv[:, D:].T
    parts = []
    for head in range(HEADS):
        low, high = head * HD, (head + 1) * HD
        s = dot(kv[:, low:high], q_t[low:high, :]) + shut
        top = jnp.max(s, 0, keepdims=True)
        expo = jnp.exp(s - top)
        total = jnp.sum(expo, 0, keepdims=True)
        lse_ref[head : head + 1, :] = top + jnp.log(total)
        p = to_bf(expo * (1.0 / total))
        parts.append(dot(v_t[low:high, :], p))
    o = to_bf(jnp.concatenate(parts, 0).T)
    o_ref[...] = o
    x2 = x_ref[...] + dot(o, wo[...])
    x2_ref[...] = x2
    b = to_bf(layer_norm(x2, gain[2:3], bias[2:3]))
    b_ref[...] = b
    h_ref[...] = to_bf(dot(b, w1[...]))
    send_edge(place, h_ref, edge_ref)


def shift_down(v):
    index = lax.broadcasted_iota(jnp.int32, v.shape, 0)
    return jnp.where(index == 0, 0.0, pltpu.roll(v, 1, 0))


def shift_up(v):
    index = lax.broadcasted_iota(jnp.int32, v.shape, 0)
    return jnp.where(index == v.shape[0] - 1, 0.0, pltpu.roll(v, v.shape[0] - 1, 0))


def from_left(v):
    return jnp.concatenate([shift_down(v[HALF:]), v[:HALF]], 0)


def from_right(v):
    return jnp.concatenate([v[HALF:], shift_up(v[:HALF])], 0)


def row_of(main, near, i, rows, lanes):
    place, low, high = near
    if i < 0:
        return jnp.where(place[0] > 0, low[:, lanes].astype(f32), 0.0)
    if i >= rows:
        return jnp.where(place[1] > 0, high[:, lanes].astype(f32), 0.0)
    return main[i * W : (i + 1) * W, lanes].astype(f32)


def send_edge(place, main, edge_ref):
    start = pl.multiple_of(jnp.where(place[0] > 0, 0, main.shape[0] - W), W)
    edge_ref[...] = main[pl.ds(start, W), :]


def conv_gelu(h_ref, ends, taps_ref, g_ref, slope_ref):
    rows = h_ref.shape[0] // W

    def chunk(c, carry):
        lanes = pl.ds(pl.multiple_of(c * LANES, LANES), LANES)
        taps = [taps_ref[k : k + 1, lanes] for k in range(9)]
        near = [row_of(h_ref, ends, i, rows, lanes) for i in (-1, 0)]
        for i in range(rows):
            near.append(row_of(h_ref, ends, i + 1, rows, lanes))
            sums = [
                taps[j] * near[0] + taps[3 + j] * near[1] + taps[6 + j] * near[2] for j in range(3)
            ]
            z = sums[1] + from_left(sums[0]) + from_right(sums[2])
            phi = 0.5 + 0.5 * lax.erf(z * root_half)
            here = slice(i * W, (i + 1) * W)
            g_ref[here, lanes] = to_bf(z * phi)
            slope_ref[here, lanes] = phi + z * (jnp.exp(-0.5 * z * z) * root_two_pi)
            near = near[1:]
        return carry

    lax.fori_loop(0, FF // LANES, chunk, 0)


def last_body(place, h_ref, low_ref, high_ref, taps_ref, x2_ref, w2, ln_ref, ok_ref, g_ref, slope_ref, x_ref, sum_ref):
    conv_gelu(h_ref, (place, low_ref, high_ref), taps_ref, g_ref, slope_ref)
    x = x2_ref[...] + dot(g_ref[...], w2[...])
    x_ref[...] = x
    fin = layer_norm(x, ln_ref[0:1], ln_ref[1:2])
    sum_ref[...] = jnp.sum(fin * ok_ref[...], 0, keepdims=True)


def join_body(
    place, h_ref, low_ref, high_ref, taps_ref, x2_ref, w2, gain, bias, wq, wsr, wkv, g_ref, slope_ref, x_ref, *outs
):
    conv_gelu(h_ref, (place, low_ref, high_ref), taps_ref, g_ref, slope_ref)
    x = x2_ref[...] + dot(g_ref[...], w2[...])
    x_ref[...] = x
    attention_inputs(x, gain, bias, wq, wsr, wkv, *outs)


def gelu_back(place, dx, w2, slope_ref, dy_ref, dz_ref, edge_ref):
    dy = to_bf(dx)
    dy_ref[...] = dy
    dg = to_bf(dot_nt(dy, w2[...])).astype(f32)
    dz_ref[...] = to_bf(dg * slope_ref[...])
    send_edge(place, dz_ref, edge_ref)


def head_body(
    images,
    place,
    pool_ref,
    count_ref,
    head_ref,
    target_ref,
    x_ref,
    ln_ref,
    ok_ref,
    w2,
    slope_ref,
    loss_ref,
    pooled_ref,
    dlog_ref,
    dln_ref,
    dx_ref,
    dy_ref,
    dz_ref,
    edge_ref,
):
    count = count_ref[...]
    pooled = to_bf(pool_ref[...] / count)
    pooled_ref[...] = pooled
    logits = dot(jnp.broadcast_to(pooled.astype(f32), (16, D)).astype(bf16), head_ref[...])[0:1]
    shifted = logits - jnp.max(logits, -1, keepdims=True)
    logp = shifted - jnp.log(jnp.sum(jnp.exp(shifted), -1, keepdims=True))
    target = target_ref[...]
    loss_ref[...] = jnp.sum(target * logp, -1, keepdims=True) * (-1.0 / images)
    dlog = to_bf((jnp.exp(logp) - target) * (1.0 / images))
    dlog_ref[...] = dlog
    wide = jnp.broadcast_to(dlog.astype(f32), (16, CLS)).astype(bf16)
    dpool = dot_nt(wide, head_ref[...])[0:1] / count
    dx, dgain, dbias = norm_back(x_ref[...], ln_ref[0:1], ok_ref[...] * dpool)
    dln_ref[0:1, :] = dgain
    dln_ref[1:2, :] = dbias
    dx_ref[...] = dx
    gelu_back(place, dx, w2, slope_ref, dy_ref, dz_ref, edge_ref)


def conv_back(h_ref, hends, dz_ref, zends, taps_ref, dh_ref, dtaps_ref):
    rows = h_ref.shape[0] // W

    def chunk(c, carry):
        lanes = pl.ds(pl.multiple_of(c * LANES, LANES), LANES)
        taps = [taps_ref[k : k + 1, lanes] for k in range(9)]
        acc = [jnp.zeros((8, LANES), f32) for _ in range(9)]

        def views(i):
            v = row_of(dz_ref, zends, i, rows, lanes)
            return [from_right(v), v, from_left(v)]

        near = [views(-1), views(0)]
        hear = [row_of(h_ref, hends, i, rows, lanes) for i in (-1, 0)]
        for i in range(rows):
            near.append(views(i + 1))
            hear.append(row_of(h_ref, hends, i + 1, rows, lanes))
            dh = None
            for di in range(3):
                for dj in range(3):
                    part = taps[3 * di + dj] * near[2 - di][dj]
                    dh = part if dh is None else dh + part
            dh_ref[i * W : (i + 1) * W, lanes] = to_bf(dh)
            for di in range(3):
                for dj in range(3):
                    prod = (hear[di] * near[1][dj]).reshape(W // 8, 8, LANES)
                    acc[3 * di + dj] = acc[3 * di + dj] + jnp.sum(prod, 0)
            near = near[1:]
            hear = hear[1:]
        for k in range(9):
            dtaps_ref[k : k + 1, lanes] = jnp.sum(acc[k], 0, keepdims=True)
        return carry

    lax.fori_loop(0, FF // LANES, chunk, 0)


def block_back_body(
    place,
    h_ref,
    hlow_ref,
    hhigh_ref,
    dz_ref,
    zlow_ref,
    zhigh_ref,
    taps_ref,
    w1,
    x2_ref,
    gain,
    dx_ref,
    wo,
    q_ref,
    kv_ref,
    ok_ref,
    lse_ref,
    dh_ref,
    dtaps_ref,
    dln_ref,
    dx2_ref,
    dy_ref,
    dq_ref,
    dkv_ref,
):
    conv_back(
        h_ref, (place, hlow_ref, hhigh_ref), dz_ref, (place, zlow_ref, zhigh_ref), taps_ref, dh_ref, dtaps_ref
    )
    db = dot_nt(dh_ref[...], w1[...])
    dln, dgain, dbias = norm_back(x2_ref[...], gain[2:3], db)
    dln_ref[0:1, :] = dgain
    dln_ref[1:2, :] = dbias
    dx2 = dx_ref[...] + dln
    dx2_ref[...] = dx2
    dy = to_bf(dx2)
    dy_ref[...] = dy
    do_t = to_bf(dot_nt(wo[...], dy))
    q = q_ref[...] * jnp.asarray(scale_qk, bf16)
    q_t = q.T
    keys = kv_ref.shape[0]
    kv = kv_ref[...]
    k_t = (kv[:, :D] * jnp.asarray(scale_qk, bf16)).T
    shut = jnp.broadcast_to(ok_ref[...], (keys, q.shape[0]))
    dq_parts, dk_parts, dv_parts = ([], [], [])
    for head in range(HEADS):
        low, high = head * HD, (head + 1) * HD
        s = dot(kv[:, low:high], q_t[low:high, :]) + shut
        p = jnp.exp(s - lse_ref[head : head + 1, :])
        dp = dot(kv[:, D + low : D + high], do_t[low:high, :])
        dv_parts.append(dot_nt(do_t[low:high, :], to_bf(p)))
        ds = to_bf(p * (dp - jnp.sum(p * dp, 0, keepdims=True)))
        dq_parts.append(dot(k_t[low:high, :], ds))
        dk_parts.append(dot_nt(q_t[low:high, :], ds))
    dq_ref[...] = to_bf(jnp.concatenate(dq_parts, 0).T)
    dkv_ref[...] = jnp.concatenate(dk_parts + dv_parts, 0).T


def inputs_back(dkv, wkv, r_ref, gain, dq_ref, wq, wsr, x_ref, dx2_ref, dr_ref, dln_ref):
    w_kv = wkv[...].astype(f32)
    drn = dot_nt(dkv, w_kv, precise)
    dr, dgain1, dbias1 = norm_back(r_ref[...], gain[1:2], drn)
    dr = to_bf(dr)
    dr_ref[...] = dr
    rows = x_ref.shape[0] // W
    cells = [
        dot_nt(dr, wsr[k * D : (k + 1) * D, :]).reshape(rows // 2, 1, 1, HALF, D) for k in range(4)
    ]
    placed = jnp.concatenate(
        [jnp.concatenate(cells[0:2], 2), jnp.concatenate(cells[2:4], 2)], 1
    ).reshape(rows * W, D)
    da = dot_nt(dq_ref[...], wq[...]) + placed
    dln, dgain0, dbias0 = norm_back(x_ref[...], gain[0:1], da)
    for k, row in enumerate((dgain0, dgain1, dbias0, dbias1)):
        dln_ref[k : k + 1, :] = row
    return dx2_ref[...] + dln


def join_back_body(
    place, dkv_ref, wkv, r_ref, gain, dq_ref, wq, wsr, x_ref, dx2_ref, w2, slope_ref,
    dr_ref, dln_ref, dx_ref, dy_ref, dz_ref, edge_ref
):
    dx = inputs_back(dkv_ref[...], wkv, r_ref, gain, dq_ref, wq, wsr, x_ref, dx2_ref, dr_ref, dln_ref)
    dx_ref[...] = dx
    gelu_back(place, dx, w2, slope_ref, dy_ref, dz_ref, edge_ref)


def first_back_body(
    dkv_ref, wkv, r_ref, gain, dq_ref, wq, wsr, x_ref, dx2_ref, e_ref, ln_ref, dr_ref, dln_ref, de_ref, dle_ref
):
    dx = inputs_back(dkv_ref[...], wkv, r_ref, gain, dq_ref, wq, wsr, x_ref, dx2_ref, dr_ref, dln_ref)
    de, dgain, dbias = norm_back(e_ref[...], ln_ref[0:1], dx)
    de_ref[...] = to_bf(de)
    dle_ref[0:1, :] = dgain
    dle_ref[1:2, :] = dbias


def weight_grads_body(
    n_dp, cols, subs, core_ref, a_ref, dq_ref, rn_ref, dkv_ref, o_ref, dy2_ref, b_ref, dh_ref, dr_ref, g_ref, dy_ref, *refs
):
    outs, (proj, down) = refs[:-2], refs[-2:]
    a = a_ref[...]
    proj[:, :D] = contract(a, dq_ref[...])
    proj[:, D : 3 * D] = contract(rn_ref[...].astype(f32), dkv_ref[...], precise)
    proj[:, 3 * D : 4 * D] = contract(o_ref[...], dy2_ref[...])
    proj[:, 4 * D :] = contract(b_ref[...], dh_ref[...])
    dr = dr_ref[...]
    for k, cell in enumerate(cells_of(a)):
        down[k * D : (k + 1) * D, :D] = contract(cell, dr)
    down[:, D:] = contract(g_ref[...], dy_ref[...])
    rows = D // n_dp
    sub = rows // subs
    wide = (4 * D + FF) // cols
    down_rows = FF // n_dp
    for c in range(cols):
        for d in range(n_dp):
            for n, out in enumerate(outs):
                for j in range(subs) if len(outs) == 1 else (None,):
                    if j is None:
                        k = core_ref[0] if n == 0 else 1 - core_ref[0]
                        at = (c ^ core_ref[1], d)
                    else:
                        k = j
                        at = (c, j, d)
                    start = d * rows + k * sub
                    low = d * down_rows + (c * subs + k) * (down_rows // (cols * subs))
                    if j is None:
                        start = pl.multiple_of(start, 8)
                        low = pl.multiple_of(low, 8)
                    out[(*at, slice(0, sub))] = proj[pl.ds(start, sub), c * wide : (c + 1) * wide]
                    out[(*at, slice(sub, 2 * sub))] = down[pl.ds(low, sub), :]


def moments(w, g, m, v):
    m2 = beta_one * m + (1.0 - beta_one) * g
    v2 = beta_two * v + (1.0 - beta_two) * g * g
    u = (
        m2 / (1.0 - beta_one**STEP) / (jnp.sqrt(v2 / (1.0 - beta_two**STEP)) + lamb_eps)
        + decay_rate * w
    )
    return m2, v2, u


def update_body(
    cols, subs, late, factor_ref, early_ref, late_ref, wp, mp, vp, wd, md, vd, mp2, vp2, up, md2, vd2, ud, sums
):
    factor = factor_ref[0]
    layer = pl.program_id(0)
    sub = wp.shape[1] // subs
    wide = wp.shape[2] // cols

    def go(g_ref):
        squares = [0.0, 0.0]

        def put(n, at, refs, outs, g):
            new = moments(refs[0][at], g * factor, refs[1][at], refs[2][at])
            for out, value in zip(outs, new):
                out[at] = value
            squares[n] = squares[n] + jnp.sum(new[2] * new[2], 0, keepdims=True)

        for c in range(cols):
            for k in range(subs):
                g = g_ref[c * subs + k].astype(f32).reshape(2 * sub, wide)
                at = (0, slice(k * sub, (k + 1) * sub), slice(c * wide, (c + 1) * wide))
                put(0, at, (wp, mp, vp), (mp2, vp2, up), g[:sub])
                rows = slice((c * subs + k) * sub, (c * subs + k + 1) * sub)
                for half in range(2):
                    at = (0, half, rows, slice(0, D))
                    put(1, at, (wd, md, vd), (md2, vd2, ud), g[sub:, half * D : (half + 1) * D])
        lane = lax.broadcasted_iota(jnp.int32, (1, LANES), 1)
        total = jnp.zeros((1, LANES), f32)
        for n in range(2):
            value = jnp.broadcast_to(jnp.sum(squares[n], 1, keepdims=True), (1, LANES))
            total = jnp.where(lane == 4 + n * LAYERS + layer, value, total)
        sums[0] = jnp.broadcast_to(total, sums.shape[1:])

    pl.when(layer >= late)(lambda: go(early_ref))
    pl.when(layer < late)(lambda: go(late_ref))


def group_sums(arrs, layered=None):
    embed, proj, downs, taps, head, gains, biases = arrs
    slot = lax.broadcasted_iota(jnp.int32, (1, 4 + 3 * LAYERS), 1)

    def placed(values, start):
        at = lax.broadcasted_iota(jnp.int32, (values.shape[0], 1), 0) + start
        return jnp.sum(jnp.where(at == slot, values[:, None], 0.0), 0)

    total = placed(jnp.sum(taps, (1, 2)), 4 + 2 * LAYERS)
    for n, a in enumerate((embed, head, gains, biases)):
        total = total + jnp.where(slot[0] == n, jnp.sum(a), 0.0)
    if layered is not None:
        return total + layered
    for n, a in enumerate((proj, downs)):
        total = total + placed(jnp.sum(a.reshape(a.shape[0], -1), 1), 4 + n * LAYERS)
    return total


def spread_ratio(ratio):
    return (
        ratio[0],
        ratio[4 : 4 + LAYERS].reshape(LAYERS, 1, 1),
        ratio[4 + LAYERS : 4 + 2 * LAYERS].reshape(LAYERS, 1, 1, 1),
        ratio[4 + 2 * LAYERS : 4 + 3 * LAYERS].reshape(LAYERS, 1, 1),
        ratio[1],
        ratio[2],
        ratio[3],
    )


def per_device(
    patches,
    valid,
    labels,
    partners,
    mix,
    embed_w,
    in_proj,
    down_proj,
    dw_kernel,
    head_w,
    norm_gain,
    norm_bias,
    m_embed,
    m_proj,
    m_down,
    m_taps,
    m_head,
    m_gain,
    m_bias,
    v_embed,
    v_proj,
    v_down,
    v_taps,
    v_head,
    v_gain,
    v_bias,
):
    masters = (embed_w, in_proj, down_proj, dw_kernel, head_w, norm_gain, norm_bias)
    firsts = (m_embed, m_proj, m_down, m_taps, m_head, m_gain, m_bias)
    seconds = (v_embed, v_proj, v_down, v_taps, v_head, v_gain, v_bias)
    n_seq = lax.axis_size("seq")
    n_dp = lax.axis_size("dp")
    seq_pos = lax.axis_index("seq")
    img_dev, rows = (patches.shape[0], patches.shape[1])
    images = img_dev * n_dp

    team = n_seq
    while team * img_dev > n_seq:
        team //= 2
    blocks = n_seq // team
    rows_own = rows * blocks
    tok = rows_own * W
    keys_own = tok // 4
    image = jnp.minimum(seq_pos // team, img_dev - 1)
    busy = seq_pos // team < img_dev
    place = seq_pos % team

    def between(shift, wrap):
        pairs = []
        for base in range(0, n_seq, team):
            for h in range(team):
                if wrap or 0 <= h + shift < team:
                    pairs.append((base + (h + shift) % team, base + h))
        return pairs

    ends = jnp.stack([place > 0, place < team - 1]).astype(jnp.int32)

    def edges(v, edge):
        if team == 2:
            other = lax.ppermute(edge, "seq", between(1, True))
            return other, other
        low = lax.ppermute(v[-W:], "seq", between(-1, False))
        high = lax.ppermute(v[:W], "seq", between(1, False))
        return low, high

    def all_keys(v):
        return jnp.concatenate(
            [v] + [lax.ppermute(v, "seq", between(j, True)) for j in range(1, team)], 0
        )

    def own_keys(v):
        total = v[:keys_own]
        for j in range(1, team):
            part = v[j * keys_own : (j + 1) * keys_own]
            total = total + lax.ppermute(part, "seq", between(-j, True))
        return total

    back_block = seq_pos % blocks
    routes = [
        [
            (blocks * h + (i + r) % blocks, team * i + h)
            for i in range(img_dev)
            for h in range(team)
        ]
        for r in range(blocks)
    ]

    def to_team(v):
        got = []
        for r, pairs in enumerate(routes):
            send = lax.dynamic_index_in_dim(
                v, jnp.minimum((back_block - r) % blocks, img_dev - 1), 0, keepdims=False
            )
            got.append(lax.ppermute(send, "seq", pairs))
        twice = jnp.stack(got + got)
        own = lax.dynamic_slice_in_dim(twice, (blocks - image) % blocks, blocks, 0)
        return own.reshape(tok, -1)

    cols = 4
    subs = n_seq // cols
    row_in = D // n_dp
    sub_in = row_in // subs
    wide = in_proj.shape[2] // cols
    down_rows = down_proj.shape[2] // n_seq
    core = seq_pos % subs

    def part_of(flat):
        size = -(-flat.shape[0] // (wide * n_seq)) * wide * n_seq
        flat = jnp.pad(flat, (0, size - flat.shape[0])).reshape(n_seq, -1, wide)
        return lax.dynamic_index_in_dim(flat, seq_pos, 0, keepdims=False)

    def layer_part(l):
        block = lax.dynamic_slice(
            in_proj[l], (core * sub_in, (seq_pos // subs) * wide), (sub_in, wide)
        )
        lower = lax.dynamic_slice_in_dim(down_proj[l], seq_pos * down_rows, down_rows, 1)
        return [to_bf(block), to_bf(jnp.concatenate([lower[0], lower[1]], 1))]

    def gathered(part):
        return lax.all_gather(part, ("dp", "seq"), axis=0, tiled=False)

    def cut(got, sizes):
        got = got.reshape(n_dp, n_seq, sum(sizes), wide)
        starts = [sum(sizes[:i]) for i in range(len(sizes))]
        return [got[:, :, a : a + n] for a, n in zip(starts, sizes)]

    def proj_of(got):
        got = got.reshape(n_dp, cols, subs, sub_in, wide).transpose(0, 2, 3, 1, 4)
        return got.reshape(D, cols * wide)

    dp_pos = lax.axis_index("dp")

    def over_dp(v):
        got = [v] + [
            lax.ppermute(v, "dp", [((d + j) % n_dp, d) for d in range(n_dp)])
            for j in range(1, n_dp)
        ]
        return lax.dynamic_slice_in_dim(jnp.stack(got + got), (n_dp - dp_pos) % n_dp, n_dp, 0)

    groups = [[0, 1, 2, 3], [4, 5]]
    extra = [[], [part_of(to_bf(head_w).reshape(-1))]]

    def layers_of(got, count):
        return [(proj_of(got[2 * i]), got[2 * i + 1].reshape(FF, 2 * D)) for i in range(count)]

    parts_of = [more + [p for l in members for p in layer_part(l)] for members, more in zip(groups, extra)]
    sizes_of = [[p.shape[0] for p in parts] for parts in parts_of]
    lines = [jnp.concatenate(parts, 0) for parts in parts_of]
    norms = jnp.stack([norm_gain, norm_bias])
    small = jnp.concatenate([to_bf(v).reshape(-1, D) for v in (embed_w, dw_kernel, norms)], 0)
    small = over_dp(small)
    marks = (embed_w.shape[0], embed_w.shape[0] + dw_kernel.size // D)
    embed16 = small[:, : marks[0]].reshape(-1, D)
    taps32 = small[:, marks[0] : marks[1]].reshape(n_dp, LAYERS * 9, -1).transpose(1, 0, 2)
    taps32 = taps32.reshape(LAYERS * 9, FF).astype(f32)
    norms32 = small[:, marks[1] :].reshape(n_dp, 2, -1, row_in).transpose(1, 2, 0, 3)
    norms32 = norms32.reshape(2, -1, D).astype(f32)
    gain32, bias32 = norms32[0], norms32[1]

    def total_over_dp(v):
        got = [v] + [
            lax.ppermute(v, "dp", [((d + j) % n_dp, d) for d in range(n_dp)])
            for j in range(1, n_dp)
        ]
        index = lax.broadcasted_iota(jnp.int32, (n_dp, 1), 0)
        rows_of = [jnp.where(index == (dp_pos + j) % n_dp, g, 0.0) for j, g in enumerate(got)]
        return jnp.sum(sum(rows_of), 0)
    raw = [gathered(lines[0])]
    first_of = {members[0]: n for n, members in enumerate(groups)}

    def own(v):
        return lax.dynamic_index_in_dim(v, image, 0, keepdims=False)

    wanted = own(partners)
    partner_label = jnp.zeros((), jnp.int32)
    for j in range(n_dp):
        other = labels
        if j:
            other = lax.ppermute(labels, "dp", [((d + j) % n_dp, d) for d in range(n_dp)])
        index = ((dp_pos + j) % n_dp) * img_dev + jnp.arange(img_dev)
        partner_label = partner_label + jnp.sum(jnp.where(index == wanted, other, 0))
    valid_own = own(valid)
    tid = lax.broadcasted_iota(jnp.int32, (tok, 1), 0)
    within = tid % W
    row_id = place * rows_own + tid // W
    col_id = 2 * (within % HALF) + within // HALF
    okay = ((row_id < valid_own[0]) & (col_id < valid_own[1]) & busy).astype(f32)
    kid = lax.broadcasted_iota(jnp.int32, (team * keys_own, 1), 0)
    segment = (place + kid // keys_own) % team
    key_row = segment * (rows_own // 2) + (kid % keys_own) // HALF
    key_ok = (2 * key_row < valid_own[0]) & (2 * (kid % HALF) < valid_own[1])
    shut = jnp.where(key_ok, 0.0, big_neg).astype(f32)
    count = (valid_own[0] * valid_own[1]).astype(f32).reshape(1, 1)
    classes = lax.broadcasted_iota(jnp.int32, (1, CLS), 1)
    mix_own = own(mix)
    target = mix_own * (classes == own(labels)).astype(f32) + (1.0 - mix_own) * (
        classes == partner_label
    ).astype(f32)

    def weights(l, layer):
        return dict(
            wq=layer[0][:, :D],
            wkv=layer[0][:, D : 3 * D],
            wo=layer[0][:, 3 * D : 4 * D],
            w1=layer[0][:, 4 * D :],
            wsr=layer[1][:, :D],
            w2=layer[1][:, D:],
            taps=taps32,
            gain=gain32,
            bias=bias32,
        )

    full = ((tok, D), f32)
    ln_first = jnp.stack([gain32[0], bias32[0]])
    spread = patches.reshape(img_dev, rows, HALF, 2, -1).transpose(0, 1, 3, 2, 4)
    patch_own = to_team(spread.reshape(img_dev, rows * W, -1))
    e, x = run(2, embed_body, [full, full], patch_own, embed16, ln_first)
    lines[1], x = lax.optimization_barrier((lines[1], x))
    raw.append(gathered(lines[1]))
    wts = [weights(l, layer) for l, layer in zip(groups[0], layers_of(cut(raw[0], sizes_of[0]), len(groups[0])))]
    ln_last = jnp.stack([gain32[-1], bias32[-1]])

    half = ((tok, D), bf16)
    wide16 = ((tok, FF), bf16)
    input_outs = [half, half, ((keys_own, D), f32), ((keys_own, D), bf16), ((keys_own, 2 * D), bf16)]
    ln_out = ((2, D), f32)
    row16 = ((W, FF), bf16)

    w = wts[0]
    a16, q16, r, rn16, kv16 = run(
        2, shifted(first_body, {1: 1, 2: 1}), input_outs, x, w["gain"], w["bias"], w["wq"], w["wsr"], w["wkv"]
    )
    kept = []
    for l in range(LAYERS):
        w = wts[l]
        kv_all = all_keys(kv16)
        o16, lse, x2, b16, h16, edge = run(
            4,
            shifted(middle_body, {5: 1 + 3 * l, 6: 1 + 3 * l}),
            [half, ((HEADS, tok), f32), full, half, wide16, row16],
            q16,
            kv_all,
            shut,
            x,
            w["gain"],
            w["bias"],
            w["wo"],
            w["w1"],
            place=ends,
        )
        hlow, hhigh = edges(h16, edge)
        keep = dict(
            x=x, a16=a16, q16=q16, r=r, rn16=rn16, kv=kv_all, o16=o16, lse=lse, x2=x2, b16=b16,
            h16=h16, hlow=hlow, hhigh=hhigh,
        )
        shared = (h16, hlow, hhigh, w["taps"], x2, w["w2"])
        if l + 1 in first_of:
            n = first_of[l + 1]
            got, _ = lax.optimization_barrier((raw[n], kv_all))
            got = cut(got, sizes_of[n])
            if extra[n]:
                head16 = got.pop(0).reshape(n_dp, -1)[:, : head_w.size].reshape(D, CLS)
            wts += [weights(m, layer) for m, layer in zip(groups[n], layers_of(got, len(groups[n])))]
        if l + 1 < LAYERS:
            n = wts[l + 1]
            keep["g16"], keep["slope"], x, a16, q16, r, rn16, kv16 = run(
                8,
                shifted(join_body, {4: 9 * l, 7: 4 + 3 * l, 8: 4 + 3 * l}),
                [wide16, ((tok, FF), f32), full] + input_outs,
                *shared,
                n["gain"],
                n["bias"],
                n["wq"],
                n["wsr"],
                n["wkv"],
                place=ends,
            )
        else:
            keep["g16"], keep["slope"], x, pool = run(
                7,
                shifted(last_body, {4: 9 * l}),
                [wide16, ((tok, FF), f32), full, ((1, D), f32)],
                *shared,
                ln_last,
                okay,
                place=ends,
            )
        kept.append(keep)

    whole = pool
    for j in range(1, team):
        whole = whole + lax.ppermute(pool, "seq", between(j, True))
    loss_own, pooled16, dlog16, dln_last, dx, dy16, dz16, edge = run(
        4,
        functools.partial(head_body, images),
        [((1, 1), f32), ((1, D), bf16), ((1, CLS), bf16), ln_out, full, half, wide16, row16],
        whole,
        count,
        head16,
        target,
        x,
        ln_last,
        okay,
        wts[-1]["w2"],
        kept[-1]["slope"],
        place=ends,
    )
    chosen = ((place == 0) & busy).astype(f32)
    d_head = pooled16.astype(f32).reshape(D, 1) * dlog16.astype(f32) * chosen
    loss_local = loss_own[0, 0] * busy.astype(f32)
    teams = n_seq // team
    loss_parts = jnp.zeros((teams,), f32)
    for j in range(teams):
        other = loss_local
        if j:
            other = lax.ppermute(
                loss_local, "seq", [((d + j * team) % n_seq, d) for d in range(n_seq)]
            )
        loss_parts = jnp.where(jnp.arange(teams) == (seq_pos // team + j) % teams, other, loss_parts)
    loss_seq = jnp.sum(loss_parts)

    piece = ((cols, n_dp, 2 * sub_in, wide), f32)
    paired = subs == 2 and cols == 4
    chip = seq_pos // subs
    where = jnp.stack([core, chip]).astype(jnp.int32)

    def weight_grads(*args):
        vm = pl.BlockSpec(memory_space=pltpu.VMEM)
        outs = [piece] * 2 if paired else [((cols, subs) + piece[0][1:], f32)]
        return pl.pallas_call(
            functools.partial(weight_grads_body, n_dp, cols, subs),
            out_shape=[jax.ShapeDtypeStruct(s, d) for s, d in outs],
            in_specs=[pl.BlockSpec(memory_space=pltpu.SMEM)] + [vm] * len(args),
            out_specs=[vm] * len(outs),
            scratch_shapes=[pltpu.VMEM((D, cols * wide), f32), pltpu.VMEM((FF, 2 * D), f32)],
            compiler_params=pltpu.CompilerParams(vmem_limit_bytes=48 << 20),
            cost_estimate=cost(6),
        )(where, *args)

    def padded_rest(parts):
        flat = jnp.concatenate(parts, 1)
        size = -(-flat.shape[1] // (16 * wide * n_seq)) * 16 * wide * n_seq
        flat = jnp.pad(flat, ((0, 0), (0, size - flat.shape[1])))
        flat = flat.reshape(n_dp, cols, subs, -1, wide).transpose(1, 2, 0, 3, 4)
        if not paired:
            return [flat]
        flat = jnp.stack([lax.dynamic_index_in_dim(flat, chip ^ j, 0, False) for j in range(cols)])
        return [lax.dynamic_index_in_dim(flat, k, 1, False) for k in (core, 1 - core)]

    def pair_sum(parts):
        mine, send = parts
        return mine + lax.ppermute(send, "seq", [(d ^ 1, d) for d in range(n_seq)])

    def over_chips(v, bit):
        return lax.ppermute(v, "seq", [(d ^ (bit * subs), d) for d in range(n_seq)])

    def plane_first(y):
        cut = y.shape[2] // 2
        one, two = y[:, :, :cut], y[:, :, cut:]
        moved = (to_bf(jnp.stack([one[1], one[3]])), to_bf(jnp.stack([two[2], two[3]])))
        got = (over_chips(moved[0], 1).astype(f32), over_chips(moved[1], 2).astype(f32))
        return [one[0] + got[0][0], one[2] + got[0][1], two[0] + got[1][0], two[1] + got[1][1]]

    def plane_second(parts):
        one = parts[0] + over_chips(parts[1].astype(wire[0]), 2).astype(f32)
        two = parts[2] + over_chips(parts[3].astype(wire[0]), 1).astype(f32)
        return jnp.concatenate([one, two], 1)

    def dp_sum(y):
        def of(j):
            return lax.dynamic_index_in_dim(y, (dp_pos + j) % n_dp, 0, keepdims=False)

        total = of(0)
        for j in range(1, n_dp):
            pairs = [(d, (d + j) % n_dp) for d in range(n_dp)]
            total = total + lax.ppermute(of(j).astype(wire[0]), "dp", pairs).astype(f32)
        return total

    def whole_sum(parts):
        y = jnp.concatenate([p[0] for p in parts], -2)
        y = lax.psum_scatter(y.reshape(-1, wide), "seq", scatter_dimension=0, tiled=True)
        return lax.psum_scatter(y, "dp", scatter_dimension=0, tiled=True)

    def tied(value, others):
        return lax.optimization_barrier((value, others))

    wire, free = ([f32], [False])
    stages = [pair_sum, plane_first, plane_second]
    pieces = []

    def advance(now):
        if not paired:
            return now
        ready = [p for p in pieces if p[0] <= len(stages) + 1]
        now, values = tied(now, [p[1] for p in ready])
        if free[0]:
            values = [v if p[0] else p[1] for p, v in zip(ready, values)]
        for p, v in zip(ready, values):
            if p[0] < len(stages):
                p[1] = stages[p[0]](v)
            elif p[0] > len(stages) or p is pieces[0]:
                p[1] = v
            elif p is pieces[1]:
                p[1] = dp_sum(jnp.concatenate([v, pieces[0][1]], 1))
            else:
                p[1] = dp_sum(v)
            p[0] += 1
        return now

    grads = [None] * LAYERS
    pieces.append([0, padded_rest([d_head.reshape(n_dp, -1)])])
    waiting = None
    for l in reversed(range(LAYERS)):
        w, k = wts[l], kept[l]
        zlow, zhigh = edges(dz16, edge)
        upper = dy16
        dz16 = advance(dz16)
        dh16, d_taps, dln2, dx2, dy2, dq16, dkv = run(
            11,
            shifted(block_back_body, {7: 9 * l, 10: 1 + 3 * l}),
            [wide16, ((9, FF), f32), ln_out, full, half, half, ((team * keys_own, 2 * D), f32)],
            k["h16"], k["hlow"], k["hhigh"], dz16, zlow, zhigh, w["taps"], w["w1"], k["x2"], w["gain"], dx,
            w["wo"], k["q16"], k["kv"], shut, k["lse"],
            place=ends,
        )
        if waiting is not None:
            first, _ = tied(waiting[0], dkv)
            pieces.append([0, weight_grads(first, *waiting[1:])])
        dkv_own = own_keys(dkv)
        if l == 0:
            wire[0] = bf16
        dq16 = advance(dq16)
        shared = (dkv_own, w["wkv"], k["r"], w["gain"], dq16, w["wq"], w["wsr"], k["x"], dx2)
        if l:
            dr16, dln, dx, dy16, dz16, edge = run(
                6,
                shifted(join_back_body, {4: 1 + 3 * l}),
                [((keys_own, D), bf16), ((4, D), f32), full, half, wide16, row16],
                *shared,
                wts[l - 1]["w2"],
                kept[l - 1]["slope"],
                place=ends,
            )
        else:
            dr16, dln, de16, dln_first = run(
                3,
                shifted(first_back_body, {3: 1}),
                [((keys_own, D), bf16), ((4, D), f32), half, ln_out],
                *shared,
                e,
                ln_first,
            )
        waiting = (k["a16"], dq16, k["rn16"], dkv_own, k["o16"], dy2, k["b16"], dh16, dr16, k["g16"], upper)
        grads[l] = (
            d_taps,
            jnp.concatenate([dln[0:2], dln2[0:1]], 0),
            jnp.concatenate([dln[2:4], dln2[1:2]], 0),
        )
    free[0] = True
    pieces.append([0, weight_grads(*waiting)])
    de16 = advance(de16)
    (d_embed,) = run(3, embed_back_body, [((embed16.shape[0], D), f32)], patch_own, de16)
    d_embed = advance(d_embed)
    d_gain = jnp.concatenate([dln_first[0:1]] + [g[1] for g in grads] + [dln_last[0:1]], 0)
    d_bias = jnp.concatenate([dln_first[1:2]] + [g[2] for g in grads] + [dln_last[1:2]], 0)
    d_taps = jnp.stack([g[0] for g in grads])
    rest = [
        d_embed.reshape(n_dp, -1),
        d_taps.reshape(LAYERS * 9, n_dp, -1).transpose(1, 0, 2).reshape(n_dp, -1),
        d_gain.reshape(-1, n_dp, row_in).transpose(1, 0, 2).reshape(n_dp, -1),
        d_bias.reshape(-1, n_dp, row_in).transpose(1, 0, 2).reshape(n_dp, -1),
    ]
    cuts = [0]
    for part in rest:
        cuts.append(cuts[-1] + part.shape[1])
    rest = padded_rest(rest)

    late = 3

    def together(parts):
        return to_bf(jnp.concatenate(parts, 0))

    if paired:
        assert all(p[0] > len(stages) + 1 for p in pieces[: LAYERS + 1 - late])
        own_rows = 2 * sub_in
        parts = [p[1] for p in pieces[1 : LAYERS + 1 - late]]
        early = together([parts[0][:own_rows], *parts[1:], parts[0][own_rows:]])
        rest, early = tied(rest, early)
        rest = advance(rest)
        last = plane_second(plane_first(pair_sum(rest)))
        last = dp_sum(jnp.concatenate([pieces[-1][1], last], 1))
        sums = [None] * (LAYERS + 1 - late) + [p[1] for p in pieces[LAYERS + 1 - late : -1]] + [last]
    else:
        sums = [whole_sum([p[1]]) for p in pieces + [[0, rest]]]
        early = together(sums[1 : LAYERS + 1 - late] + sums[:1])
    early_got = lax.all_gather(early, "seq", axis=0, tiled=False)
    late_part, early_got = tied(together(sums[LAYERS + 1 - late :]), early_got)
    late_got = lax.all_gather(late_part, "seq", axis=0, tiled=False)
    head_start = (LAYERS - late) * 2 * sub_in
    g_head = early_got[:, head_start:].reshape(-1)[: head_w.size].reshape(head_w.shape).astype(f32)
    flat = late_got[:, late * 2 * sub_in :].reshape(-1).astype(f32)
    flat = [flat[a:b] for a, b in zip(cuts, cuts[1:])]
    shards = (
        flat[0].reshape(embed_w.shape),
        None,
        None,
        flat[1].reshape(dw_kernel.shape),
        g_head,
        flat[2].reshape(norm_gain.shape),
        flat[3].reshape(norm_bias.shape),
    )

    gsq_local = sum(jnp.sum(jnp.square(g.astype(f32))) for g in (early_got, late_got))
    wsq_local = group_sums(tuple((w * w for w in masters)))
    ends_of = jnp.where(jnp.arange(LANES) == LANES - 1, loss_seq, 0.0)
    first_sums = total_over_dp(
        jnp.where(jnp.arange(LANES) == LANES - 2, gsq_local, ends_of)
        + jnp.pad(wsq_local, (0, LANES - wsq_local.shape[0]))
    )
    gsq, wsq, loss = first_sums[LANES - 2], first_sums[: 4 + 3 * LAYERS], first_sums[LANES - 1]
    grad_norm = jnp.sqrt(gsq)
    factor = jnp.minimum(1.0, clip_limit / grad_norm)

    proj_spec = pl.BlockSpec((1,) + in_proj.shape[1:], lambda l: (l, 0, 0))
    down_spec = pl.BlockSpec((1,) + down_proj.shape[1:], lambda l: (l, 0, 0, 0))
    block = (n_seq, 2 * sub_in, wide)
    blocks_of = [early_got, late_got]
    if 2 * sub_in % 8:
        block = (n_seq, 1, 2 * sub_in, wide)
        counts = (LAYERS - late, late)
        blocks_of = [
            g[:, : n * 2 * sub_in].reshape(n_seq, n, 2 * sub_in, wide)
            for g, n in zip(blocks_of, counts)
        ]
    tail = (0,) * (len(block) - 2)
    got = pl.pallas_call(
        functools.partial(update_body, cols, subs, late),
        grid=(LAYERS,),
        out_shape=[jax.ShapeDtypeStruct(in_proj.shape, f32)] * 3
        + [jax.ShapeDtypeStruct(down_proj.shape, f32)] * 3
        + [jax.ShapeDtypeStruct((LAYERS, 8, LANES), f32)],
        in_specs=[
            pl.BlockSpec(memory_space=pltpu.SMEM),
            pl.BlockSpec(block, lambda l: (0, jnp.minimum(LAYERS - 1 - l, LAYERS - 1 - late), *tail)),
            pl.BlockSpec(block, lambda l: (0, jnp.maximum(late - 1 - l, 0), *tail)),
        ]
        + [proj_spec] * 3
        + [down_spec] * 3,
        out_specs=[proj_spec] * 3 + [down_spec] * 3 + [pl.BlockSpec((1, 8, LANES), lambda l: (l, 0, 0))],
        compiler_params=pltpu.CompilerParams(vmem_limit_bytes=56 << 20),
        cost_estimate=cost(25),
    )(factor.reshape(1), *blocks_of, in_proj, m_proj, v_proj, down_proj, m_down, v_down)
    big = {1: got[0:3], 2: got[3:6]}
    new_m, new_v, updates = ([], [], [])
    for n, (w, g, m, v) in enumerate(zip(masters, shards, firsts, seconds)):
        m2, v2, u = big[n] if n in big else moments(w, g * factor, m, v)
        new_m.append(m2)
        new_v.append(v2)
        updates.append(u)
    usq = total_over_dp(
        group_sums(tuple((u * u for u in updates)), jnp.sum(got[6][:, 0, : 4 + 3 * LAYERS], 0))
    )
    wnorm = jnp.sqrt(wsq)
    unorm = jnp.sqrt(usq)
    ratio = wnorm / unorm
    spreads = spread_ratio(ratio)
    new_w = [w - learn_rate * r * u for w, r, u in zip(masters, spreads, updates)]
    stats = jnp.stack([wnorm, unorm])
    return (loss, grad_norm, stats, ratio, *new_w, *new_m, *new_v)


def solution(mesh):
    placed = (
        P("dp", None),
        P(None, "dp", None),
        P(None, None, "dp", None),
        P(None, None, "dp"),
        P("dp", None),
        P(None, "dp"),
        P(None, "dp"),
    )
    in_specs = (
        P("dp", "seq", None, None),
        P("dp", None),
        P("dp"),
        P("dp"),
        P("dp"),
    ) + placed * 3
    out_specs = (P(), P(), P(), P()) + placed * 3
    return jax.shard_map(
        per_device, mesh=mesh, in_specs=in_specs, out_specs=out_specs, check_vma=False
    )
```
